128 devices in a mesh: row: 4 (over y), col: 32 (over z, x, core).
Axes of the slice: x: 4, y: 4, z: 4, core: 2. Of those that a mesh axis runs over, the one named last changes fastest.
Arguments:
- hidden: bfloat16 [24576, 1536], P('col'), may hold values from -6 to 6
- w_zx: bfloat16 [1536, 4096], P('col', 'row'), may hold values from -0.15625 to 0.15625
- w_bc: bfloat16 [1536, 256], P('col'), may hold values from -0.15625 to 0.15625
- w_dt: bfloat16 [1536, 32], P('col', 'row'), may hold values from -0.15625 to 0.15625
- w_out: bfloat16 [1536, 2048], P('col', 'row'), may hold values from -0.125 to 0.125
- dt_bias: float32 [32], P('row'), may hold values from -4 to -1
- a_log: float32 [32], P('row'), may hold values from -3 to 1
- d_skip: float32 [32], P('row'), may hold values from 0.5 to 1.5
- conv_x_w: float32 [4, 2048], P(None, 'row'), may hold values from -2 to 2
- conv_x_b: float32 [2048], P('row'), may hold values from -1.5 to 1.5
- conv_bc_w: float32 [4, 256], replicated, may hold values from -2 to 2
- conv_bc_b: float32 [256], replicated, may hold values from -1.5 to 1.5
- norm_gain: float32 [2048], P('row'), may hold values from 0.1 to 1.9
- prev_state: bfloat16 [768, 32, 64, 128], P('col', 'row'), may hold values from -3 to 3
- prev_edge_x: bfloat16 [768, 3, 2048], P('col', None, 'row'), may hold values from -6 to 6
- prev_edge_bc: bfloat16 [768, 3, 256], P('col'), may hold values from -6 to 6
- holder: int32 [1536], replicated, may hold values from 0 to 31, as said below
- continued: int32 [1536], replicated, may hold values from 0 to 1, as said below
- owner: int32 [1536], replicated, may hold values from 0 to 31, as said below
- accepted: int32 [1536], replicated, may hold values from 0 to 16
Outputs:
- mixed: bfloat16 [24576, 1536], P('col', 'row')
- new_state: bfloat16 [1536, 32, 64, 128], P('col', 'row')
- new_edge_x: bfloat16 [1536, 3, 2048], P('col', None, 'row')
- new_edge_bc: bfloat16 [1536, 3, 256], P('col')
The draws below stay inside these ranges and needn't reach their ends.
Inputs may be any that keep to these rules, and one draw needn't show every extreme that they name: Only read where continued is 1. Each holder holds exactly 24 continued requests, in request order in its slots; one holder holds at most 2 continued requests of one aligned block of 48 requests, and some holder holds that many. Exactly 24 requests of each aligned block of 48 requests are continued. Where continued is 1, owner equals holder. Each owner receives exactly 48 requests; of one aligned block of 48 requests at most 2 continued and at most 2 others go to one owner, at most 4 in all, and that many in some block.
All inputs are finite; a program needn't handle non-finite values.
Results may differ from the reference program's by a relative error of at most 0.0072.
Values may be sent and summed in bfloat16 or wider, within the bound.
A program may use at most 192 MiB of HBM per device.

```python
import jax
import jax.numpy as jnp
from jax import lax

D = 1536
HEADS = 32
HEAD_DIM = 64
STATE = 128
KCONV = 4
LEN = 16
REQ_DEV = 48
HELD = 24
INNER = 2048
REQUESTS = 1536
CACHE = 768
TOKENS = 24576
N_COL = 32


def band_lists(key, count):
    key_one, key_two = jax.random.split(key)
    first = jax.random.permutation(key_one, N_COL).astype(jnp.int32)
    others = (jax.random.permutation(key_two, N_COL - 1) + 1).astype(jnp.int32)
    order = jnp.concatenate([jnp.zeros((1,), jnp.int32), others])
    second = first[order]
    index = jnp.arange(count, dtype=jnp.int32)
    begin = jnp.where((index % 2 == 0)[None, :], first[:, None], second[:, None])
    return ((begin + (index // 2)[None, :]) % N_COL).astype(jnp.int32)


def shuffled_ranks(key):
    keys = jax.random.split(key, N_COL)
    perms = jax.vmap(lambda single: jax.random.permutation(single, REQ_DEV))(keys).astype(jnp.int32)
    return jnp.argsort(perms, axis=1).astype(jnp.int32)


def holder_plan(key):
    base = jax.random.fold_in(key, 11)
    key_band, key_pos, key_fill = jax.random.split(base, 3)
    lists = band_lists(key_band, HELD)
    rank = shuffled_ranks(key_pos)
    live = rank < HELD
    picked = jnp.take_along_axis(lists, jnp.minimum(rank, HELD - 1), axis=1)
    others = jnp.take_along_axis(lists, jnp.clip(rank - HELD, 0, HELD - 1), axis=1)
    filler = jax.random.randint(key_fill, (N_COL, REQ_DEV), 0, N_COL).astype(jnp.int32)
    holders = jnp.where(live, picked, filler).astype(jnp.int32)
    owners = jnp.where(live, picked, others).astype(jnp.int32)
    return (holders.reshape(REQUESTS), live.astype(jnp.int32).reshape(REQUESTS), owners.reshape(REQUESTS))


def draw_holder(key, part):
    return holder_plan(key)[0]


def draw_continued(key, part):
    return holder_plan(key)[1]


def draw_owner(key, part):
    return holder_plan(key)[2]


def plant(entries, key, smallest, largest):
    longest = entries.shape.index(max(entries.shape))
    spots = []
    for shift in (0, 1):
        where = [jax.random.randint(jax.random.fold_in(key, axis), (), 0, length) for axis, length in enumerate(entries.shape)]
        where[longest] = (where[longest] + shift) % entries.shape[longest]
        spots.append(tuple(where))
    return entries.at[spots[0]].set(smallest).at[spots[1]].set(largest)


def levels(key, extent, cuts, smallest, top_value):
    loudness, own = 1.0, jax.random.fold_in(key, 6)
    for dim, blocks in cuts:
        draws = jnp.exp(jax.random.uniform(jax.random.fold_in(own, dim), (blocks,), jnp.float32, smallest / len(cuts), top_value / len(cuts)))
        loudness = loudness * jnp.repeat(draws, extent[dim] // blocks).reshape([-1 if axis == dim else 1 for axis in range(len(extent))])
    return loudness


def gaussian(key, extent, scale, reach, cuts=(), kind=jnp.bfloat16):
    level = levels(key, extent, cuts, -0.22, 0.18) if cuts else 1.0
    array = jax.random.normal(key, extent, jnp.float32) * scale * level
    return jnp.minimum(jnp.maximum(array, -reach), reach).astype(kind)


def setup_inputs(seed: int = 0) -> dict:
    seeds = jax.random.split(jax.random.key(seed), 21)
    hidden = gaussian(seeds[0], (TOKENS, D), 1.0, 6.0, ((0, 32),))
    w_zx = gaussian(seeds[1], (D, 2 * INNER), D ** -0.5, 0.15625, ((0, 32), (1, 4)))
    w_bc = gaussian(seeds[2], (D, 2 * STATE), D ** -0.5, 0.15625, ((0, 32),))
    w_dt = gaussian(seeds[3], (D, HEADS), D ** -0.5, 0.15625, ((0, 32), (1, 4)))
    w_out = gaussian(seeds[4], (D, INNER), INNER ** -0.5, 0.125, ((0, 32), (1, 4)))
    dt_bias = jnp.clip(-4.0 + 3.0 * jax.random.uniform(seeds[5], (HEADS,), jnp.float32) ** levels(seeds[5], (HEADS,), ((0, 4),), -0.2, 0.2), -4.0, -1.0)
    a_log = jnp.clip(-3.0 + 4.0 * jax.random.uniform(seeds[6], (HEADS,), jnp.float32) ** levels(seeds[6], (HEADS,), ((0, 4),), -0.2, 0.2), -3.0, 1.0)
    d_skip = jnp.clip(0.5 + 1.0 * jax.random.uniform(seeds[7], (HEADS,), jnp.float32) ** levels(seeds[7], (HEADS,), ((0, 4),), -0.2, 0.2), 0.5, 1.5)
    conv_x_w = gaussian(seeds[8], (KCONV, INNER), 0.4, 2.0, ((1, 4),), jnp.float32)
    conv_x_b = gaussian(seeds[9], (INNER,), 0.3, 1.5, ((0, 4),), jnp.float32)
    conv_bc_w = gaussian(seeds[10], (KCONV, 2 * STATE), 0.4, 2.0, (), jnp.float32)
    conv_bc_b = gaussian(seeds[11], (2 * STATE,), 0.3, 1.5, (), jnp.float32)
    norm_gain = jnp.clip(1.0 + 0.18 * jax.random.normal(seeds[12], (INNER,), jnp.float32), 0.1, 1.9)
    prev_state = gaussian(seeds[13], (CACHE, HEADS, HEAD_DIM, STATE), 0.5, 3.0, ((0, 32), (1, 4)))
    prev_edge_x = gaussian(seeds[14], (CACHE, KCONV - 1, INNER), 1.0, 6.0, ((0, 32), (2, 4)))
    prev_edge_bc = gaussian(seeds[15], (CACHE, KCONV - 1, 2 * STATE), 1.0, 6.0, ((0, 32),))
    holder = draw_holder(jax.random.fold_in(seeds[20], 71), 0)
    continued = draw_continued(jax.random.fold_in(seeds[20], 71), 0)
    owner = draw_owner(jax.random.fold_in(seeds[20], 71), 0)
    accepted = plant(jax.random.randint(seeds[19], (REQUESTS,), 0, LEN + 1), jax.random.fold_in(seeds[19], 1), 0, LEN).astype(jnp.int32)
    return dict(hidden=hidden, w_zx=w_zx, w_bc=w_bc, w_dt=w_dt, w_out=w_out, dt_bias=dt_bias, a_log=a_log, d_skip=d_skip, conv_x_w=conv_x_w, conv_x_b=conv_x_b, conv_bc_w=conv_bc_w, conv_bc_b=conv_bc_b, norm_gain=norm_gain, prev_state=prev_state, prev_edge_x=prev_edge_x, prev_edge_bc=prev_edge_bc, holder=holder, continued=continued, owner=owner, accepted=accepted)


def ranks_of(values, live, count):
    onehot = ((values[:, None] == jnp.arange(count, dtype=jnp.int32)[None, :]) & live[:, None]).astype(jnp.int32)
    before = jnp.cumsum(onehot, axis=0) - onehot
    return lax.optimization_barrier(jnp.sum(before * onehot, axis=1)).astype(jnp.int32)

def conv_silu(edge, fresh, weight, bias):
    length = fresh.shape[1]
    series = jnp.concatenate([edge, fresh], axis=1).astype(jnp.float32)
    total = bias + weight[0] * series[:, 0:length]
    for shift in range(1, weight.shape[0]):
        total = total + weight[shift] * series[:, shift:shift + length]
    return jax.nn.silu(total).astype(jnp.bfloat16)

def last_rows(edge, fresh, accepted):
    keep = edge.shape[1]
    series = jnp.concatenate([edge, fresh], axis=1)
    return jax.vmap(lambda rows, start: lax.dynamic_slice_in_dim(rows, start, keep, 0))(series, accepted)

def reference(hidden, w_zx, w_bc, w_dt, w_out, dt_bias, a_log, d_skip, conv_x_w, conv_x_b, conv_bc_w, conv_bc_b, norm_gain, prev_state, prev_edge_x, prev_edge_bc, holder, continued, owner, accepted):
    highest = lax.Precision.HIGHEST
    proj_zx = jnp.dot(hidden, w_zx, preferred_element_type=jnp.float32).astype(jnp.bfloat16)
    proj_zx = proj_zx.reshape(N_COL, REQ_DEV, LEN, HEADS, 2 * HEAD_DIM)
    gate_in = proj_zx[..., :HEAD_DIM]
    x_in = proj_zx[..., HEAD_DIM:].reshape(N_COL, REQ_DEV, LEN, INNER)
    proj_bc = jnp.dot(hidden, w_bc, preferred_element_type=jnp.float32).astype(jnp.bfloat16)
    proj_bc = proj_bc.reshape(N_COL, REQ_DEV, LEN, 2 * STATE)
    dt_raw = jnp.dot(hidden, w_dt, preferred_element_type=jnp.float32).reshape(N_COL, REQ_DEV, LEN, HEADS)
    live = continued == 1
    slot = jnp.where(live, holder * HELD + ranks_of(holder, live, N_COL), 0).astype(jnp.int32)
    decay_rate = -jnp.exp(a_log)

    def one_group(items):
        gate_g, x_g, bc_g, raw_g, slot_g, live_g, accepted_g = items
        edge_x = jnp.where(live_g[:, None, None], jnp.take(prev_edge_x, slot_g, axis=0), jnp.zeros((), jnp.bfloat16))
        edge_bc = jnp.where(live_g[:, None, None], jnp.take(prev_edge_bc, slot_g, axis=0), jnp.zeros((), jnp.bfloat16))
        start_state = jnp.where(live_g[:, None, None, None], jnp.take(prev_state, slot_g, axis=0).astype(jnp.float32), jnp.zeros((), jnp.float32))
        x_conv = conv_silu(edge_x, x_g, conv_x_w, conv_x_b).astype(jnp.float32).reshape(REQ_DEV, LEN, HEADS, HEAD_DIM)
        bc_conv = conv_silu(edge_bc, bc_g, conv_bc_w, conv_bc_b).astype(jnp.float32)
        b_in = bc_conv[..., :STATE]
        c_in = bc_conv[..., STATE:]
        step_size = jax.nn.softplus(raw_g + dt_bias)

        def advance(carry, token):
            state, chosen = carry
            x_token, b_token, c_token, size_token, index = token
            state = jnp.exp(size_token * decay_rate)[:, :, None, None] * state + size_token[:, :, None, None] * x_token[:, :, :, None] * b_token[:, None, None, :]
            out_token = jnp.einsum('rhpn,rn->rhp', state, c_token, precision=highest) + d_skip[None, :, None] * x_token
            chosen = jnp.where((accepted_g == index + 1)[:, None, None, None], state, chosen)
            return ((state, chosen), out_token)
        tokens_first = (x_conv.transpose(1, 0, 2, 3), b_in.transpose(1, 0, 2), c_in.transpose(1, 0, 2), step_size.transpose(1, 0, 2), jnp.arange(LEN, dtype=jnp.int32))
        (final, chosen), outs = lax.scan(advance, (start_state, start_state), tokens_first)
        scan_out = outs.transpose(1, 0, 2, 3)
        gated = (scan_out * jax.nn.silu(gate_g.astype(jnp.float32))).reshape(REQ_DEV * LEN, INNER)
        mean_sq = lax.optimization_barrier(jnp.mean(gated * gated, axis=1, keepdims=True))
        normed = (gated * lax.rsqrt(mean_sq + 1e-05) * norm_gain).astype(jnp.bfloat16)
        mixed_g = jnp.dot(normed, w_out.T, preferred_element_type=jnp.float32).astype(jnp.bfloat16)
        return (mixed_g, chosen.astype(jnp.bfloat16), last_rows(edge_x, x_g, accepted_g), last_rows(edge_bc, bc_g, accepted_g))
    items = (gate_in, x_in, proj_bc, dt_raw, slot.reshape(N_COL, REQ_DEV), live.reshape(N_COL, REQ_DEV), accepted.reshape(N_COL, REQ_DEV))
    mixed_all, states_all, edges_x_all, edges_bc_all = lax.map(one_group, items)
    mixed = mixed_all.reshape(TOKENS, D)
    everyone = jnp.ones((REQUESTS,), dtype=bool)
    out_slot = (owner * REQ_DEV + ranks_of(owner, everyone, N_COL)).astype(jnp.int32)
    new_state = jnp.zeros((REQUESTS, HEADS, HEAD_DIM, STATE), jnp.bfloat16).at[out_slot].set(states_all.reshape(REQUESTS, HEADS, HEAD_DIM, STATE))
    new_edge_x = jnp.zeros((REQUESTS, KCONV - 1, INNER), jnp.bfloat16).at[out_slot].set(edges_x_all.reshape(REQUESTS, KCONV - 1, INNER))
    new_edge_bc = jnp.zeros((REQUESTS, KCONV - 1, 2 * STATE), jnp.bfloat16).at[out_slot].set(edges_bc_all.reshape(REQUESTS, KCONV - 1, 2 * STATE))
    return (mixed, new_state, new_edge_x, new_edge_bc)
```

```python
import jax
import jax.numpy as jnp
from jax import lax
from jax.sharding import PartitionSpec as P

HEAD_DIM = 64
STATE = 128
KCONV = 4
LEN = 16
INNER = 2048


def routing(owner, accepted, continued, col_index, request_count, cap):
    total = owner.shape[0]
    groups = total // request_count
    local = jnp.arange(request_count, dtype=jnp.int32)
    slots = jnp.arange(groups * cap, dtype=jnp.int32)
    mine = lax.dynamic_slice_in_dim(owner, col_index * request_count, request_count)
    earlier = local[None, :] < local[:, None]
    rank = jnp.sum(((mine[None, :] == mine[:, None]) & earlier).astype(jnp.int32), axis=1)
    home_key = mine * cap + rank
    send_from = jnp.sum(jnp.where(home_key[None, :] == slots[:, None], local[None, :], 0), axis=1)
    owned = (owner == col_index).reshape(groups, request_count)
    owned_int = owned.astype(jnp.int32)
    in_group = jnp.sum(jnp.where(earlier[None], owned_int[:, None, :], 0), axis=2)
    counts = jnp.sum(owned_int, axis=1)
    group = jnp.arange(groups, dtype=jnp.int32)
    before = jnp.sum(jnp.where(group[None, :] < group[:, None], counts[None, :], 0), axis=1)
    slot = jnp.where(owned, in_group + before[:, None], -1)
    match = slot[None] == local[:, None, None]

    def picked(values):
        return jnp.sum(jnp.where(match, values[None], 0), axis=(1, 2))

    pick = picked(group[:, None] * cap + in_group)
    own_accepted = picked(accepted.reshape(groups, request_count))
    own_cont = picked((continued == 1).astype(jnp.int32).reshape(groups, request_count))
    own_prev = jnp.sum(jnp.where(earlier, own_cont[None, :], 0), axis=1)
    back_from = jnp.sum(jnp.where(pick[None, :] == slots[:, None], local[None, :], 0), axis=1)
    return home_key, send_from, pick, own_accepted, own_cont, own_prev, back_from


def rows_of(source, index, live=None):
    ids = jnp.arange(source.shape[0], dtype=jnp.int32)
    hot = index[:, None] == ids[None, :]
    if live is not None:
        hot = hot & live[:, None]
    flat = source.reshape(source.shape[0], -1)
    out = jnp.dot(hot.astype(source.dtype), flat, preferred_element_type=jnp.float32)
    return out.astype(source.dtype).reshape((index.shape[0],) + source.shape[1:])


def conv_silu(edge, fresh, weight, bias):
    length = fresh.shape[1]
    series = jnp.concatenate([edge, fresh], axis=1).astype(jnp.float32)
    total = bias + weight[0] * series[:, 0:length]
    for shift in range(1, weight.shape[0]):
        total = total + weight[shift] * series[:, shift : shift + length]
    return jax.nn.silu(total).astype(jnp.bfloat16)


def last_rows(edge, fresh, accepted):
    keep = edge.shape[1]
    series = jnp.concatenate([edge, fresh], axis=1)
    ids = jnp.arange(series.shape[1], dtype=jnp.int32)
    picks = []
    for row in range(keep):
        hot = (ids[None, :] == accepted[:, None] + row)[:, :, None]
        picks.append(jnp.sum(jnp.where(hot, series, 0).astype(jnp.float32), axis=1))
    return jnp.stack(picks, axis=1).astype(edge.dtype)


def per_device(
    hidden,
    w_zx,
    w_bc,
    w_dt,
    w_out,
    dt_bias,
    a_log,
    d_skip,
    conv_x_w,
    conv_x_b,
    conv_bc_w,
    conv_bc_b,
    norm_gain,
    prev_state,
    prev_edge_x,
    prev_edge_bc,
    holder,
    continued,
    owner,
    accepted,
):
    highest = lax.Precision.HIGHEST
    col_count = lax.axis_size("col")
    col_index = lax.axis_index("col")
    row_index = lax.axis_index("row")
    row_count = lax.axis_size("row")
    token_count = hidden.shape[0]
    request_count = token_count // LEN
    heads_here = dt_bias.shape[0]
    inner_here = heads_here * HEAD_DIM
    slice_width = hidden.shape[1] // row_count
    decay_rate = -jnp.exp(a_log)
    cap = 4 * ((request_count // 4 + col_count - 1) // col_count)
    home_key, send_from, pick, my_accepted, own_cont, own_prev, back_from = routing(
        owner, accepted, continued, col_index, request_count, cap
    )
    own_live = own_cont > 0
    my_slice = lax.dynamic_slice_in_dim(hidden, row_index * slice_width, slice_width, 1)
    packed = rows_of(my_slice.reshape(request_count, LEN, slice_width), send_from)
    packed = packed.reshape(col_count, cap, LEN, slice_width)
    got = lax.all_to_all(packed, "col", split_axis=0, concat_axis=0, tiled=True)
    own_slice = rows_of(got.reshape(col_count * cap, LEN, slice_width), pick)
    own_slice = own_slice.reshape(token_count, slice_width)
    hidden = lax.all_gather(own_slice, "row", axis=1, tiled=True)

    rest = jnp.concatenate(
        [w_out, w_bc, w_dt, jnp.zeros((w_dt.shape[0], 128 - w_dt.shape[1]), w_dt.dtype)], axis=1
    )
    full_zx = lax.all_gather(w_zx, "col", axis=0, tiled=True)
    full_rest = lax.all_gather(rest, "col", axis=0, tiled=True)
    full_out = full_rest[:, :inner_here]
    full_bc = full_rest[:, inner_here : inner_here + 2 * STATE]
    full_dt = full_rest[:, inner_here + 2 * STATE : inner_here + 2 * STATE + heads_here]
    proj_zx = jnp.dot(hidden, full_zx, preferred_element_type=jnp.float32).astype(jnp.bfloat16)
    proj_zx = proj_zx.reshape(request_count, LEN, heads_here, 2 * HEAD_DIM)
    gate_in = proj_zx[..., :HEAD_DIM]
    x_in = proj_zx[..., HEAD_DIM:].reshape(request_count, LEN, inner_here)
    bc_flat = jnp.dot(hidden, full_bc, preferred_element_type=jnp.float32).astype(jnp.bfloat16)
    proj_bc = bc_flat.reshape(request_count, LEN, 2 * STATE)
    dt_raw = jnp.dot(hidden, full_dt, preferred_element_type=jnp.float32).reshape(
        request_count, LEN, heads_here
    )
    start_state = rows_of(prev_state, own_prev, own_live).astype(jnp.float32)
    edge_x = rows_of(prev_edge_x, own_prev, own_live)
    edge_bc = rows_of(prev_edge_bc, own_prev, own_live)
    number = x_in.shape[0]
    x_conv = (
        conv_silu(edge_x, x_in, conv_x_w, conv_x_b)
        .astype(jnp.float32)
        .reshape(number, LEN, heads_here, HEAD_DIM)
    )
    bc_conv = conv_silu(edge_bc, proj_bc, conv_bc_w, conv_bc_b).astype(jnp.float32)
    b_in = bc_conv[..., :STATE]
    c_in = bc_conv[..., STATE:]
    step_size = jax.nn.softplus(dt_raw + dt_bias)
    log_decay = jnp.stack(
        [jnp.sum((step_size * decay_rate)[:, : t + 1], axis=1) for t in range(LEN)], axis=1
    )
    positions = jnp.arange(LEN, dtype=jnp.int32)
    later = positions[:, None] >= positions[None, :]
    spread = log_decay[:, :, None, :] - log_decay[:, None, :, :]
    within = jnp.where(later[None, :, :, None], jnp.exp(jnp.minimum(spread, 0.0)), 0.0)
    scores = jnp.einsum("rtn,rsn->rts", c_in, b_in, precision=highest)
    mixing = within * scores[..., None] * step_size[:, None, :, :]
    scan_out = jnp.einsum("rtsh,rshp->rthp", mixing, x_conv, precision=highest)
    scan_out = scan_out + jnp.exp(log_decay)[..., None] * jnp.einsum(
        "rhpn,rtn->rthp", start_state, c_in, precision=highest
    )
    scan_out = scan_out + d_skip[None, None, :, None] * x_conv
    padded_decay = jnp.concatenate(
        [jnp.zeros((number, 1, heads_here), jnp.float32), log_decay], axis=1
    )
    pick_mask = (jnp.arange(LEN + 1, dtype=jnp.int32)[None, :] == my_accepted[:, None]).astype(
        jnp.float32
    )
    reach = jnp.sum(pick_mask[:, :, None] * padded_decay, axis=1)
    before = positions[None, :] < my_accepted[:, None]
    weight_s = (
        jnp.where(before[:, :, None], jnp.exp(jnp.minimum(reach[:, None, :] - log_decay, 0.0)), 0.0)
        * step_size
    )
    chosen = jnp.exp(reach)[:, :, None, None] * start_state + jnp.einsum(
        "rsh,rshp,rsn->rhpn", weight_s, x_conv, b_in, precision=highest
    )
    new_state, new_edge_x, new_edge_bc = (
        chosen.astype(jnp.bfloat16),
        last_rows(edge_x, x_in, my_accepted),
        last_rows(edge_bc, proj_bc, my_accepted),
    )
    gated = (scan_out * jax.nn.silu(gate_in.astype(jnp.float32))).reshape(token_count, inner_here)
    totals = lax.psum(jnp.sum(gated * gated, axis=1), "row")
    normed = (gated * lax.rsqrt(totals / INNER + 1e-05)[:, None] * norm_gain).astype(jnp.bfloat16)
    partial_out = lax.dot_general(
        normed, full_out, (((1,), (1,)), ((), ())), preferred_element_type=jnp.float32
    )
    own_mixed = lax.psum_scatter(partial_out, "row", scatter_dimension=1, tiled=True).astype(
        jnp.bfloat16
    )
    back = rows_of(own_mixed.reshape(request_count, LEN, slice_width), back_from)
    back = back.reshape(col_count, cap, LEN, slice_width)
    came = lax.all_to_all(back, "col", split_axis=0, concat_axis=0, tiled=True)
    mixed = rows_of(came.reshape(col_count * cap, LEN, slice_width), home_key)
    return (mixed.reshape(token_count, slice_width), new_state, new_edge_x, new_edge_bc)


def solution(mesh):
    return jax.shard_map(
        per_device,
        mesh=mesh,
        in_specs=(
            P("col", None),
            P("col", "row"),
            P("col", None),
            P("col", "row"),
            P("col", "row"),
            P("row"),
            P("row"),
            P("row"),
            P(None, "row"),
            P("row"),
            P(),
            P(),
            P("row"),
            P("col", "row", None, None),
            P("col", None, "row"),
            P("col", None, None),
            P(),
            P(),
            P(),
            P(),
        ),
        out_specs=(
            P("col", "row"),
            P("col", "row", None, None),
            P("col", None, "row"),
            P("col", None, None),
        ),
        check_vma=False,
    )
```

```python
import jax
import jax.numpy as jnp
from jax import lax
from jax.experimental import pallas as pl
from jax.experimental.pallas import tpu as pltpu
from jax.sharding import PartitionSpec as P

HEAD_DIM = 64
STATE = 128
KCONV = 4
LEN = 16
INNER = 2048
SIDE = 4
GROUP = 8
TOK = GROUP * LEN
MESH = pl.DeviceIdType.MESH
HIGHEST = lax.Precision.HIGHEST


def routing(owner, accepted, continued, col_index, request_count, cap):
    total = owner.shape[0]
    groups = total // request_count
    local = jnp.arange(request_count, dtype=jnp.int32)
    slots = jnp.arange(groups * cap, dtype=jnp.int32)
    mine = lax.dynamic_slice_in_dim(owner, col_index * request_count, request_count)
    earlier = local[None, :] < local[:, None]
    rank = jnp.sum(((mine[None, :] == mine[:, None]) & earlier).astype(jnp.int32), axis=1)
    home_key = mine * cap + rank
    send_from = jnp.sum(jnp.where(home_key[None, :] == slots[:, None], local[None, :], 0), axis=1)
    owned = (owner == col_index).reshape(groups, request_count)
    owned_int = owned.astype(jnp.int32)
    in_group = jnp.sum(jnp.where(earlier[None], owned_int[:, None, :], 0), axis=2)
    counts = jnp.sum(owned_int, axis=1)
    group = jnp.arange(groups, dtype=jnp.int32)
    before = jnp.sum(jnp.where(group[None, :] < group[:, None], counts[None, :], 0), axis=1)
    slot = jnp.where(owned, in_group + before[:, None], -1)
    match = slot[None] == local[:, None, None]

    def picked(values):
        return jnp.sum(jnp.where(match, values[None], 0), axis=(1, 2))

    pick = picked(group[:, None] * cap + in_group)
    own_accepted = picked(accepted.reshape(groups, request_count))
    own_cont = picked((continued == 1).astype(jnp.int32).reshape(groups, request_count))
    own_prev = jnp.sum(jnp.where(earlier, own_cont[None, :], 0), axis=1)
    back_from = jnp.sum(jnp.where(pick[None, :] == slots[:, None], local[None, :], 0), axis=1)
    return home_key, send_from, pick, own_accepted, own_cont, own_prev, back_from


def greet(row, me, rows, cols):
    barrier = pltpu.get_barrier_semaphore()

    def along_col(d, carry):
        pl.semaphore_signal(
            barrier, inc=1, device_id=(row, (me + d) % cols), device_id_type=MESH
        )
        return carry

    lax.fori_loop(1, cols, along_col, 0)

    def along_row(d, carry):
        pl.semaphore_signal(
            barrier, inc=1, device_id=((row + d) % rows, me), device_id_type=MESH
        )
        return carry

    lax.fori_loop(1, rows, along_row, 0)
    return barrier


def gather_kernel(
    rows, cols, cap, send_from, pick, hidden, wa, wb, hid_full, fa, fb,
    sl, packed, got, own, loc, a2a_s, a2a_r, was, wbs, war, wbr, y_s, y_r,
):
    row, me = lax.axis_index("row"), lax.axis_index("col")
    barrier = greet(row, me, rows, cols)
    width = sl.shape[2]
    half = sl.shape[0] // 2
    depth = wa.shape[0]

    def cols_of(r):
        return pl.ds(pl.multiple_of(r * width, 128), width)

    def block(ref, c):
        return ref.at[pl.ds(pl.multiple_of(c * depth, 16), depth), :]

    load = pltpu.make_async_copy(hidden.at[:, :, cols_of(row)], sl, loc.at[0])
    load.start()
    keep_a = pltpu.make_async_copy(wa, block(fa, me), loc.at[1])
    keep_b = pltpu.make_async_copy(wb, block(fb, me), loc.at[2])
    keep_a.start()
    keep_b.start()
    load.wait()

    def pack(s, carry):
        packed[s] = sl[send_from[s]]
        return carry

    lax.fori_loop(0, cols * cap, pack, 0)
    pl.semaphore_wait(barrier, cols - 1 + rows - 1)

    def piece(ref, c):
        return ref.at[pl.ds(c * cap, cap)]

    def push(d, carry):
        peer = (me + d) % cols
        pltpu.make_async_remote_copy(
            piece(packed, peer), piece(got, me), a2a_s.at[peer], a2a_r.at[me],
            device_id=(row, peer), device_id_type=MESH,
        ).start()
        return carry

    lax.fori_loop(1, cols, push, 0)
    keep_m = pltpu.make_async_copy(piece(packed, me), piece(got, me), loc.at[3])
    keep_m.start()

    core = me % 2
    x = (me // 2) % SIDE
    z = me // (2 * SIDE)
    a = x + core * (z - x)
    b = z + core * (x - z)

    def at(pa, pb):
        pa, pb = (pa + SIDE) % SIDE, (pb + SIDE) % SIDE
        px = pa + core * (pb - pa)
        pz = pb + core * (pa - pb)
        return (pz * SIDE + px) * 2 + core

    sibling = me + 1 - 2 * core
    sent = [0, 0]

    def send(which, src, c, dest):
        full, ss, rs = ((fa, was, war), (fb, wbs, wbr))[which]
        k = sent[which]
        sent[which] += 1
        pltpu.make_async_remote_copy(
            src, block(full, c), ss.at[k], rs.at[c],
            device_id=(row, dest), device_id_type=MESH,
        ).start()

    def forward(which, c, dest):
        send(which, block((fa, fb)[which], c), c, dest)

    def arrived(which, c):
        full, rs = ((fa, war), (fb, wbr))[which]
        pltpu.make_async_copy(block(full, c), block(full, c), rs.at[c]).wait()

    up, down = at(a + 1, b), at(a - 1, b)
    far = at(a + 2, b)
    over, under = at(a, b + 1), at(a, b - 1)
    for dest in (up, down, over, under, sibling):
        for which, src in ((0, wa), (1, wb)):
            send(which, src, me, dest)
    arrived(0, down)
    forward(0, down, up)
    arrived(1, up)
    forward(1, up, down)
    arrived(1, down)
    arrived(0, up)
    for c in (down, up):
        for which in (0, 1):
            for dest in (over, under, sibling):
                forward(which, c, dest)
    keep_m.wait()

    def took(d, carry):
        peer = (me + d) % cols
        pltpu.make_async_copy(piece(got, peer), piece(got, peer), a2a_r.at[peer]).wait()
        return carry

    lax.fori_loop(1, cols, took, 0)

    def unpack(s, carry):
        own[s] = got[pick[s]]
        return carry

    lax.fori_loop(0, own.shape[0], unpack, 0)

    def part(ref, h, r):
        return ref.at[pl.ds(h * half, half), :, cols_of(r)]

    right, left = (row + 1) % rows, (row + rows - 1) % rows
    far_row = (row + 2) % rows
    for k, dest in ((0, right), (1, left)):
        for h in (0, 1):
            pltpu.make_async_remote_copy(
                own.at[pl.ds(h * half, half)], part(hid_full, h, row),
                y_s.at[2 * k + h], y_r.at[row, h],
                device_id=(dest, me), device_id_type=MESH,
            ).start()
    keep_y = pltpu.make_async_copy(own, hid_full.at[:, :, cols_of(row)], loc.at[4])
    keep_y.start()

    for which in (0, 1):
        arrived(which, far)
        for dest in (over, under, sibling):
            forward(which, far, dest)
    for k in (0, 1, -1, 2):
        low, high = at(a + k, b - 1), at(a + k, b + 1)
        arrived(0, low)
        forward(0, low, over)
        arrived(1, high)
        forward(1, high, under)
        arrived(1, low)
        arrived(0, high)
        for which in (0, 1):
            forward(which, low, sibling)
            forward(which, high, sibling)

    def y_here(h, r):
        pltpu.make_async_copy(part(hid_full, h, r), part(hid_full, h, r), y_r.at[r, h]).wait()

    y_here(0, left)
    pltpu.make_async_remote_copy(
        part(hid_full, 0, left), part(hid_full, 0, left), y_s.at[4], y_r.at[left, 0],
        device_id=(right, me), device_id_type=MESH,
    ).start()
    y_here(1, right)
    pltpu.make_async_remote_copy(
        part(hid_full, 1, right), part(hid_full, 1, right), y_s.at[5], y_r.at[right, 1],
        device_id=(left, me), device_id_type=MESH,
    ).start()
    y_here(1, left)
    y_here(0, right)
    for k in (0, 1, -1, 2):
        opposite = at(a + k, b + 2)
        for which in (0, 1):
            arrived(which, opposite)
            forward(which, opposite, sibling)
    y_here(0, far_row)
    y_here(1, far_row)

    def from_sibling(k, carry):
        c = 2 * k + 1 - core
        pltpu.make_async_copy(block(fa, c), block(fa, c), war.at[c]).wait()
        pltpu.make_async_copy(block(fb, c), block(fb, c), wbr.at[c]).wait()
        return carry

    lax.fori_loop(0, cols // 2, from_sibling, 0)
    keep_a.wait()
    keep_b.wait()
    keep_y.wait()

    def a2a_done(d, carry):
        peer = (me + d) % cols
        pltpu.make_async_copy(piece(packed, peer), piece(packed, peer), a2a_s.at[peer]).wait()
        return carry

    lax.fori_loop(1, cols, a2a_done, 0)

    def a_done(k, carry):
        pltpu.make_async_copy(block(fa, me), block(fa, me), was.at[k]).wait()
        return carry

    lax.fori_loop(0, sent[0], a_done, 0)

    def b_done(k, carry):
        pltpu.make_async_copy(block(fb, me), block(fb, me), wbs.at[k]).wait()
        return carry

    lax.fori_loop(0, sent[1], b_done, 0)
    for k in range(6):
        h = (0, 1, 0, 1, 0, 1)[k]
        pltpu.make_async_copy(part(hid_full, h, row), part(hid_full, h, row), y_s.at[k]).wait()


def gather_all(send_from, pick, hidden, wa, wb, rows, cols, cap):
    requests, _, model = hidden.shape
    width = model // rows
    dt = hidden.dtype
    smem = pl.BlockSpec(memory_space=pltpu.SMEM)
    hbm = pl.BlockSpec(memory_space=pl.ANY)
    vmem = pl.BlockSpec(memory_space=pltpu.VMEM)
    dma = pltpu.SemaphoreType.DMA

    def body(*refs):
        gather_kernel(rows, cols, cap, *refs)

    return pl.pallas_call(
        body,
        out_shape=(
            jax.ShapeDtypeStruct(hidden.shape, dt),
            jax.ShapeDtypeStruct((wa.shape[0] * cols, wa.shape[1]), dt),
            jax.ShapeDtypeStruct((wb.shape[0] * cols, wb.shape[1]), dt),
        ),
        in_specs=[smem, smem, hbm, vmem, vmem],
        out_specs=(hbm, hbm, hbm),
        scratch_shapes=[
            pltpu.VMEM((requests, LEN, width), dt),
            pltpu.VMEM((cols * cap, LEN, width), dt),
            pltpu.VMEM((cols * cap, LEN, width), dt),
            pltpu.VMEM((requests, LEN, width), dt),
            dma((5,)), dma((cols,)), dma((cols,)),
            dma((48,)), dma((48,)), dma((cols,)), dma((cols,)),
            dma((6,)), dma((rows, 2)),
        ],
        compiler_params=pltpu.CompilerParams(
            collective_id=0, has_side_effects=True, vmem_limit_bytes=32 << 20
        ),
        name="gather_all",
    )(send_from, pick, hidden, wa, wb)


def return_kernel(
    rows, cols, cap, back_from, home_key, part, ss, mixed,
    mine, came, ss_in, scale, mix, packed, got0, got1, got2,
    loc, ss_s, ss_r, y_s, y_r, a2a_s, a2a_r,
):
    row, me = lax.axis_index("row"), lax.axis_index("col")
    barrier = greet(row, me, rows, cols)
    pieces = part.shape[0] // rows
    tokens = part.shape[1]
    keep = pltpu.make_async_copy(part.at[pl.ds(row * pieces, pieces)], mine, loc.at[0])
    keep.start()
    pl.semaphore_wait(barrier, cols - 1 + rows - 1)
    order = (1, 3, 2)
    for k, d in enumerate(order):
        peer = (row + d) % rows
        pltpu.make_async_remote_copy(
            ss, ss_in.at[row], ss_s.at[k], ss_r.at[row],
            device_id=(peer, me), device_id_type=MESH,
        ).start()
    for j in range(pieces):
        for k, d in enumerate(order):
            peer = (row + d) % rows
            pltpu.make_async_remote_copy(
                part.at[peer * pieces + j], came.at[row, j], y_s.at[j, k], y_r.at[row, j],
                device_id=(peer, me), device_id_type=MESH,
            ).start()
    total = ss[...]
    for d in order:
        peer = (row + d) % rows
        pltpu.make_async_copy(ss_in.at[peer], ss_in.at[peer], ss_r.at[peer]).wait()
        total = total + ss_in[peer]
    factor = lax.rsqrt(total / INNER + 1e-05)
    for i in range(tokens // TOK):
        line = jnp.broadcast_to(factor[i : i + 1, :], (TOK, TOK))
        scale[pl.ds(i * TOK, TOK), :] = line.T
    keep.wait()
    gots = (got0, got1, got2)

    def piece(ref, c):
        return ref.at[pl.ds(c * cap, cap)]

    for j in range(pieces):
        for d in order:
            peer = (row + d) % rows
            pltpu.make_async_copy(came.at[peer, j], came.at[peer, j], y_r.at[peer, j]).wait()

        def add(i, carry):
            at = pl.ds(pl.multiple_of(i * TOK, TOK), TOK)
            value = mine[j, at, :].astype(jnp.float32)
            for d in order:
                value = value + came[(row + d) % rows, j, at, :].astype(jnp.float32)
            value = (value * scale[at, :]).astype(mix.dtype)
            mix[pl.ds(i * GROUP, GROUP)] = value.reshape(GROUP, LEN, 128)
            return carry

        lax.fori_loop(0, tokens // TOK, add, 0)

        def pack(s, carry):
            packed[j, s] = mix[back_from[s]]
            return carry

        lax.fori_loop(0, cols * cap, pack, 0)

        def push(d, carry):
            peer = (me + d) % cols
            pltpu.make_async_remote_copy(
                piece(packed.at[j], peer), piece(gots[j], me), a2a_s.at[j, peer], a2a_r.at[j, me],
                device_id=(row, peer), device_id_type=MESH,
            ).start()
            return carry

        lax.fori_loop(1, cols, push, 0)
        pltpu.make_async_copy(piece(packed.at[j], me), piece(gots[j], me), loc.at[1 + j]).start()
    for j in range(pieces):
        got = gots[j]
        pltpu.make_async_copy(piece(packed.at[j], me), piece(got, me), loc.at[1 + j]).wait()

        def took(d, carry):
            peer = (me + d) % cols
            pltpu.make_async_copy(piece(got, peer), piece(got, peer), a2a_r.at[j, peer]).wait()
            return carry

        lax.fori_loop(1, cols, took, 0)

        def unpack(s, carry):
            mixed[s, :, j * 128 : (j + 1) * 128] = got[home_key[s]]
            return carry

        lax.fori_loop(0, mixed.shape[0], unpack, 0)
    for k in range(3):
        pltpu.make_async_copy(ss, ss, ss_s.at[k]).wait()
        for j in range(pieces):
            pltpu.make_async_copy(mine.at[j], mine.at[j], y_s.at[j, k]).wait()
    for j in range(pieces):

        def gone(d, carry):
            peer = (me + d) % cols
            pltpu.make_async_copy(
                piece(packed.at[j], peer), piece(packed.at[j], peer), a2a_s.at[j, peer]
            ).wait()
            return carry

        lax.fori_loop(1, cols, gone, 0)


def send_home(back_from, home_key, part, ss, rows, cols, cap):
    pieces = part.shape[0] // rows
    tokens = part.shape[1]
    smem = pl.BlockSpec(memory_space=pltpu.SMEM)
    hbm = pl.BlockSpec(memory_space=pl.ANY)
    vmem = pl.BlockSpec(memory_space=pltpu.VMEM)
    dma = pltpu.SemaphoreType.DMA
    slots = cols * cap
    requests = tokens // LEN
    dt = part.dtype

    def body(*refs):
        return_kernel(rows, cols, cap, *refs)

    return pl.pallas_call(
        body,
        out_shape=jax.ShapeDtypeStruct((requests, LEN, pieces * 128), dt),
        in_specs=[smem, smem, hbm, vmem],
        out_specs=vmem,
        scratch_shapes=[
            pltpu.VMEM((pieces, tokens, 128), dt),
            pltpu.VMEM((rows, pieces, tokens, 128), dt),
            pltpu.VMEM((rows,) + ss.shape, jnp.float32),
            pltpu.VMEM((tokens, 128), jnp.float32),
            pltpu.VMEM((requests, LEN, 128), dt),
            pltpu.VMEM((pieces, slots, LEN, 128), dt),
            pltpu.VMEM((slots, LEN, 128), dt),
            pltpu.VMEM((slots, LEN, 128), dt),
            pltpu.VMEM((slots, LEN, 128), dt),
            dma((1 + pieces,)), dma((3,)), dma((rows,)),
            dma((pieces, 3)), dma((rows, pieces)), dma((pieces, cols)), dma((pieces, cols)),
        ],
        compiler_params=pltpu.CompilerParams(
            collective_id=1, has_side_effects=True, vmem_limit_bytes=32 << 20
        ),
        name="send_home",
    )(back_from, home_key, part, ss)


def silu(v):
    return v / (1.0 + jnp.exp(-v))


def mixer_kernel(
    prev_slot, cont, acc, hid, fa, fb, dtb, rate, skip, cxw, cxb, cbw, cbb, gain,
    prev, pex, peb, part, ss, nst, nex, neb, zx, bc, dts, gg, cx, cb,
):
    f32, bf16 = jnp.float32, jnp.bfloat16
    inner = gain.shape[1]
    tokens = hid.shape[0]
    heads = inner // HEAD_DIM

    @pl.loop(0, 2 * inner // 256)
    def _(n):
        at = pl.ds(pl.multiple_of(n * 256, 256), 256)
        zx[:, at] = jnp.dot(hid[...], fa[:, at], preferred_element_type=f32).astype(bf16)

    bc[...] = jnp.dot(
        hid[...], fb[:, inner : inner + 2 * STATE], preferred_element_type=f32
    ).astype(bf16)
    dts[...] = jnp.dot(hid[...], fb[:, inner + 2 * STATE :], preferred_element_type=f32)

    t_ids = lax.broadcasted_iota(jnp.int32, (TOK, TOK), 0)
    s_ids = lax.broadcasted_iota(jnp.int32, (TOK, TOK), 1)
    same = (t_ids // LEN) == (s_ids // LEN)
    causal = same & (t_ids >= s_ids)
    tri = causal.astype(f32)
    spread_h = (
        lax.broadcasted_iota(jnp.int32, (TOK, inner), 1) // HEAD_DIM
        == lax.broadcasted_iota(jnp.int32, (TOK, inner), 0)
    ).astype(f32)

    @pl.loop(0, tokens // TOK)
    def _(i):
        at = pl.ds(pl.multiple_of(i * TOK, TOK), TOK)
        live, last = [], jnp.zeros((TOK, TOK), jnp.int32)
        for r in range(GROUP):
            s = i * GROUP + r
            flag = cont[s].astype(f32)
            live.append(flag)
            last = jnp.where(t_ids // LEN == r, acc[s], last)
            cx[r, 13:16, :] = pex[prev_slot[s]].astype(f32) * flag
            cb[r, 13:16, :] = peb[prev_slot[s]].astype(f32) * flag
        cx[:, 16:32, :] = zx[at, inner:].astype(f32).reshape(GROUP, LEN, inner)
        cb[:, 16:32, :] = bc[at, :].astype(f32).reshape(GROUP, LEN, 2 * STATE)
        tot_x = cxb[...].reshape(1, 1, inner) + cxw[0:1, :].reshape(1, 1, inner) * cx[:, 13:29, :]
        tot_b = cbb[...].reshape(1, 1, 2 * STATE) + cbw[0:1, :].reshape(
            1, 1, 2 * STATE
        ) * cb[:, 13:29, :]
        for k in range(1, KCONV):
            tot_x = tot_x + cxw[k : k + 1, :].reshape(1, 1, inner) * cx[:, 13 + k : 29 + k, :]
            tot_b = tot_b + cbw[k : k + 1, :].reshape(1, 1, 2 * STATE) * cb[:, 13 + k : 29 + k, :]
        xc = silu(tot_x).reshape(TOK, inner).astype(bf16)
        bcc = silu(tot_b).reshape(TOK, 2 * STATE).astype(bf16)
        for r in range(GROUP):
            s = i * GROUP + r
            nex[s] = pltpu.roll(cx[r], 19 - acc[s], 0)[0:3, :].astype(bf16)
            neb[s] = pltpu.roll(cb[r], 19 - acc[s], 0)[0:3, :].astype(bf16)
        b_in, c_in = bcc[:, :STATE], bcc[:, STATE:]
        xf = xc.astype(f32)
        raw = dts[at, :] + dtb[...]
        step = jnp.maximum(raw, 0.0) + jnp.log(1.0 + jnp.exp(-jnp.abs(raw)))
        decay = jnp.dot(tri, step * rate[...], precision=HIGHEST, preferred_element_type=f32)
        decay_t = decay.T
        step_t = step.T
        choose = (same & (s_ids % LEN == last - 1)).astype(f32)
        reach = jnp.dot(choose, decay, precision=HIGHEST, preferred_element_type=f32)
        taken = t_ids % LEN < last
        weight = jnp.where(taken, jnp.exp(jnp.minimum(reach - decay, 0.0)), 0.0) * step
        weight_x = jnp.dot(weight, spread_h, precision=HIGHEST, preferred_element_type=f32)
        grow_x = jnp.dot(jnp.exp(decay), spread_h, precision=HIGHEST, preferred_element_type=f32)
        scores = lax.dot_general(
            c_in, b_in, (((1,), (1,)), ((), ())), preferred_element_type=f32
        )
        scores = jnp.where(causal, scores, 0.0)
        half = s_ids < HEAD_DIM
        zero = jnp.zeros((TOK, 2 * HEAD_DIM), bf16)
        y = []
        for pair in range(heads // 2):
            mats = []
            for h in (2 * pair, 2 * pair + 1):
                gap = decay[:, h : h + 1] - decay_t[h : h + 1, :]
                mats.append(
                    (jnp.exp(jnp.minimum(gap, 0.0)) * scores * step_t[h : h + 1, :]).astype(bf16)
                )
            xp = xc[:, pair * 128 : (pair + 1) * 128]
            both = jnp.concatenate([jnp.where(half, xp, zero), jnp.where(half, zero, xp)], axis=0)
            y.append(
                jnp.dot(jnp.concatenate(mats, axis=1), both, preferred_element_type=f32)
            )
        y = jnp.concatenate(y, axis=1)
        carried = []
        for r in range(GROUP):
            s = i * GROUP + r
            from_state = lax.dot_general(
                c_in[r * LEN : (r + 1) * LEN, :], prev[prev_slot[s]], (((1,), (1,)), ((), ())),
                preferred_element_type=f32,
            )
            carried.append(from_state * live[r])
        y = y + grow_x * jnp.concatenate(carried, axis=0) + skip[...] * xf
        gated = y * silu(zx[at, :inner].astype(f32))
        gg[at, :] = (gated * gain[...]).astype(bf16)
        squares = jnp.sum(gated * gated, axis=1, keepdims=True)
        ss[pl.ds(i, 1), :] = jnp.broadcast_to(squares, (TOK, TOK)).T[0:1, :]

        xw = (xf * weight_x).T
        high = xw.astype(bf16)
        low = (xw - high.astype(f32)).astype(bf16)
        lhs = jnp.concatenate([high, low], axis=1)
        keep_t = jnp.exp(reach).T
        none = jnp.zeros((TOK, STATE), bf16)
        for pair in range(GROUP // 2):
            cut = jnp.concatenate(
                [
                    jnp.where(t_ids // LEN == r, b_in, none)
                    for r in (2 * pair, 2 * pair + 1)
                ],
                axis=1,
            )
            added = jnp.dot(
                lhs, jnp.concatenate([cut, cut], axis=0), preferred_element_type=f32
            )
            for k in (0, 1):
                r = 2 * pair + k
                s = i * GROUP + r
                factor = jnp.broadcast_to(keep_t[0:heads, r * LEN : r * LEN + 1], (heads, STATE))
                factor = factor * live[r]
                old = prev[prev_slot[s]].astype(f32).reshape(heads, HEAD_DIM, STATE)
                new = factor[:, None, :] * old + added[:, k * STATE : (k + 1) * STATE].reshape(
                    heads, HEAD_DIM, STATE
                )
                nst[s] = new.reshape(inner, STATE).astype(bf16)

    @pl.loop(0, part.shape[0] // 2)
    def _(q):
        at = pl.ds(pl.multiple_of(q * 256, 256), 256)
        out = lax.dot_general(
            gg[...], fb[at, :inner], (((1,), (1,)), ((), ())), preferred_element_type=f32
        ).astype(bf16)
        part[2 * q] = out[:, :128]
        part[2 * q + 1] = out[:, 128:]


def mixer(prev_slot, cont, acc, hid, fa, fb, vectors, prev, pex, peb):
    tokens, model = hid.shape
    inner = fa.shape[1] // 2
    requests = tokens // LEN
    dt = hid.dtype
    smem = pl.BlockSpec(memory_space=pltpu.SMEM)
    vmem = pl.BlockSpec(memory_space=pltpu.VMEM)
    return pl.pallas_call(
        mixer_kernel,
        out_shape=(
            jax.ShapeDtypeStruct((model // 128, tokens, 128), dt),
            jax.ShapeDtypeStruct((8, 128), jnp.float32),
            jax.ShapeDtypeStruct((requests, inner, STATE), dt),
            jax.ShapeDtypeStruct((requests, 3, inner), dt),
            jax.ShapeDtypeStruct((requests, 3, 2 * STATE), dt),
        ),
        in_specs=[smem] * 3 + [vmem] * (6 + len(vectors)),
        out_specs=(vmem,) * 5,
        scratch_shapes=[
            pltpu.VMEM((tokens, 2 * inner), dt),
            pltpu.VMEM((tokens, 2 * STATE), dt),
            pltpu.VMEM((tokens, 128), jnp.float32),
            pltpu.VMEM((tokens, inner), dt),
            pltpu.VMEM((GROUP, 32, inner), jnp.float32),
            pltpu.VMEM((GROUP, 32, 2 * STATE), jnp.float32),
        ],
        compiler_params=pltpu.CompilerParams(vmem_limit_bytes=52 << 20),
        name="mixer",
    )(prev_slot, cont, acc, hid, fa, fb, *vectors, prev, pex, peb)


def per_device(
    hidden, w_zx, w_bc, w_dt, w_out, dt_bias, a_log, d_skip, conv_x_w, conv_x_b,
    conv_bc_w, conv_bc_b, norm_gain, prev_state, prev_edge_x, prev_edge_bc,
    holder, continued, owner, accepted,
):
    rows, cols = lax.axis_size("row"), lax.axis_size("col")
    col_index = lax.axis_index("col")
    requests = hidden.shape[0] // LEN
    heads = dt_bias.shape[0]
    inner = heads * HEAD_DIM
    held = prev_state.shape[0]
    cap = 4 * ((requests // 4 + cols - 1) // cols)
    home_key, send_from, pick, acc, cont, prev_slot, back_from = routing(
        owner, accepted, continued, col_index, requests, cap
    )
    prev_slot = jnp.minimum(prev_slot, held - 1)
    depth = w_zx.shape[0]
    wa = w_zx.reshape(depth, heads, 2, HEAD_DIM).transpose(0, 2, 1, 3).reshape(depth, 2 * inner)
    pad = jnp.zeros((depth, 128 - heads), w_dt.dtype)
    wb = jnp.concatenate([w_out, w_bc, w_dt, pad], axis=1)
    tokens, model = hidden.shape
    hid, fa, fb = gather_all(
        send_from, pick, hidden.reshape(requests, LEN, model), wa, wb, rows, cols, cap
    )
    hid = hid.reshape(tokens, model)

    def line(v):
        return jnp.pad(v, (0, 128 - v.shape[0]))[None, :]

    vectors = (
        line(dt_bias), line(-jnp.exp(a_log)), jnp.repeat(d_skip, HEAD_DIM)[None, :],
        conv_x_w, conv_x_b[None, :], conv_bc_w, conv_bc_b[None, :], norm_gain[None, :],
    )
    part, ss, new_state, new_edge_x, new_edge_bc = mixer(
        prev_slot, cont, acc, hid, fa, fb, vectors,
        prev_state.reshape(held, inner, STATE), prev_edge_x, prev_edge_bc,
    )
    mixed = send_home(back_from, home_key, part, ss, rows, cols, cap)
    return (
        mixed.reshape(tokens, model // rows), new_state.reshape(requests, heads, HEAD_DIM, STATE), new_edge_x, new_edge_bc,
    )


def solution(mesh):
    return jax.shard_map(
        per_device,
        mesh=mesh,
        in_specs=(
            P("col", None),
            P("col", "row"),
            P("col", None),
            P("col", "row"),
            P("col", "row"),
            P("row"),
            P("row"),
            P("row"),
            P(None, "row"),
            P("row"),
            P(),
            P(),
            P("row"),
            P("col", "row", None, None),
            P("col", None, "row"),
            P("col", None, None),
            P(),
            P(),
            P(),
            P(),
        ),
        out_specs=(
            P("col", "row"),
            P("col", "row", None, None),
            P("col", None, "row"),
            P("col", None, None),
        ),
        check_vma=False,
    )
```

```python
import jax
import jax.numpy as jnp
from jax import lax
from jax.experimental import pallas as pl
from jax.experimental.pallas import tpu as pltpu
from jax.sharding import PartitionSpec as P

HEAD_DIM = 64
STATE = 128
KCONV = 4
LEN = 16
INNER = 2048
SIDE = 4
GROUP = 8
TOK = GROUP * LEN
MESH = pl.DeviceIdType.MESH
HIGHEST = lax.Precision.HIGHEST


def route_kernel(held, code, out):
    f32, bf16 = jnp.float32, jnp.bfloat16
    me = lax.axis_index("col")
    groups, requests = code.shape
    value = code[...]
    o, c, a = value & 63, (value >> 6) & 1, value >> 7

    def dot(x, y):
        return jnp.dot(x.astype(bf16), y.astype(bf16), preferred_element_type=f32)

    def dot0(x, y):
        return lax.dot_general(
            x.astype(bf16), y.astype(bf16), (((0,), (0,)), ((), ())), preferred_element_type=f32
        )

    def ids(shape, dim):
        return lax.broadcasted_iota(jnp.int32, shape, dim)

    below = (ids((requests, requests), 0) < ids((requests, requests), 1)).astype(f32)
    prior = (ids((groups, groups), 1) < ids((groups, groups), 0)).astype(f32)
    lane = ids((groups, 128), 1).astype(f32)
    group = ids((groups, 128), 0).astype(f32)
    spots, inside, starts = [], [], []
    for kind in (1, 0):
        mask = ((o == me) & (c == kind)).astype(f32)
        rank = dot(mask, below)
        count = jnp.broadcast_to(jnp.sum(mask, axis=1, keepdims=True), (groups, 128))
        start = dot(prior, count)
        hot = ((start <= lane) & (lane < start + count)).astype(f32)
        spots.append((jnp.where(mask > 0, rank, -1.0), hot))
        inside.append(rank)
        starts.append(start)
    rank_all, start_all = inside[0] + inside[1], starts[0] + starts[1]
    picks, places, taken = [], [], []
    for k in (0, 1):
        spot, hot = spots[k]
        order = jnp.sum(hot * (lane - starts[k]), axis=0, keepdims=True)
        any_hot = jnp.sum(hot, axis=0, keepdims=True)
        order = jnp.where(any_hot > 0, order, -5.0)
        match = (dot0(spot, hot) == order).astype(f32)
        picks.append(jnp.sum(hot * (2 * group + lane - starts[k]), axis=0, keepdims=True))
        places.append(
            jnp.sum(hot * start_all, axis=0, keepdims=True)
            + jnp.sum(match * dot0(rank_all, hot), axis=0, keepdims=True)
        )
        taken.append(jnp.sum(match * dot0(a, hot), axis=0, keepdims=True))
    lane_i, group_i = ids((groups, 128), 1), ids((groups, 128), 0)
    back = jnp.sum(
        jnp.where(lane_i // 2 == group_i, starts[0] + (lane_i % 2).astype(f32), 0.0),
        axis=0, keepdims=True,
    )
    back = jnp.minimum(back, held - 1.0)

    def my_row(x, fill):
        row = jnp.sum(
            jnp.where(ids((groups, requests), 0) == me, x, 0).astype(f32), axis=0, keepdims=True
        )
        rest = jnp.full((1, 128 - requests), fill, f32)
        return jnp.concatenate([row, rest], axis=1)

    o_row, c_row, a_row = my_row(o, 99.0), my_row(c, 2.0), my_row(a, 0.0)

    def column(row):
        return jnp.broadcast_to(row, (128, 128)).T

    o_col, c_col, a_col = column(o_row), column(c_row), column(a_row)
    ii, jj = ids((128, 128), 0), ids((128, 128), 1)
    alike = (o_col == o_row) & (c_col == c_row)
    rank_row = jnp.sum((alike & (ii < jj)).astype(f32), axis=0, keepdims=True)
    rank_col = jnp.sum((alike & (jj < ii)).astype(f32), axis=1, keepdims=True)
    nth_row = jnp.sum(((c_col == 0) & (ii < jj)).astype(f32), axis=0, keepdims=True)
    nth_col = jnp.sum(((c_row == 0) & (jj < ii)).astype(f32), axis=1, keepdims=True)
    key_row = 2 * o_row + rank_row
    key_col = 2 * o_col + rank_col
    fi, fj = ii.astype(f32), jj.astype(f32)
    goes = (c_col == 1) & (key_col == fj)
    stays = (c_col == 0) & (nth_col == fj)

    def total(mask, x):
        return jnp.sum(jnp.where(mask, x, 0.0), axis=0, keepdims=True)

    table = (
        total(goes, fi), picks[0], back,
        jnp.where(c_row == 1, key_row, 0.0), jnp.where(c_row == 0, held + nth_row, 0.0),
        (c_row == 1).astype(f32),
        total(stays, fi), total(stays, key_col), total(stays, a_col),
        taken[0], places[0], picks[1], places[1],
    )
    for k, line in enumerate(table):
        out[k : k + 1, :] = line.astype(jnp.int32)
    out[len(table) :, :] = jnp.zeros((16 - len(table), 128), jnp.int32)


SEND, PICK, BACK, FROM_MSG, FROM_MIX, MOVED, STAY, STAY_KEY, STAY_ACC, ACC, POS, PICK_O, POS_O = range(13)


def route(code, held):
    vmem = pl.BlockSpec(memory_space=pltpu.VMEM)

    def body(*refs):
        route_kernel(held, *refs)

    return pl.pallas_call(
        body, out_shape=jax.ShapeDtypeStruct((16, 128), jnp.int32),
        in_specs=[vmem], out_specs=vmem, name="route",
    )(code)


def greet(row, me, rows, cols):
    barrier = pltpu.get_barrier_semaphore()

    def along_col(d, carry):
        pl.semaphore_signal(
            barrier, inc=1, device_id=(row, (me + d) % cols), device_id_type=MESH
        )
        return carry

    lax.fori_loop(1, cols, along_col, 0)

    def along_row(d, carry):
        pl.semaphore_signal(
            barrier, inc=1, device_id=((row + d) % rows, me), device_id_type=MESH
        )
        return carry

    lax.fori_loop(1, rows, along_row, 0)
    return barrier


def gather_kernel(
    rows, cols, cap, tab, hidden, wa, w_out, w_bc, w_dt, hid_full, fa, fb,
    wb, sl, packed, got, own, loc, a2a_s, a2a_r, was, wbs, war, wbr, y_s, y_r,
):
    row, me = lax.axis_index("row"), lax.axis_index("col")
    barrier = greet(row, me, rows, cols)
    width = sl.shape[2]
    half = own.shape[0] // 2
    depth = wa.shape[0]

    def cols_of(r):
        return pl.ds(pl.multiple_of(r * width, 128), width)

    def block(ref, c):
        return ref.at[pl.ds(pl.multiple_of(c * depth, 16), depth), :]

    load = pltpu.make_async_copy(hidden.at[:, :, cols_of(row)], sl, loc.at[0])
    load.start()
    inner = w_out.shape[1]
    states = w_bc.shape[1]
    heads = w_dt.shape[0]
    wb[:, :inner] = w_out[...]
    wb[:, inner : inner + states] = w_bc[...]
    square = jnp.concatenate([w_dt[...].astype(jnp.float32), jnp.zeros((heads, 128 - depth), jnp.float32)], axis=1)
    square = jnp.concatenate([square, jnp.zeros((128 - heads, 128), jnp.float32)], axis=0).T
    wb[:, inner + states :] = square[:depth, :].astype(wb.dtype)
    keep_a = pltpu.make_async_copy(wa, block(fa, me), loc.at[1])
    keep_b = pltpu.make_async_copy(wb, block(fb, me), loc.at[2])
    keep_a.start()
    keep_b.start()
    load.wait()

    def pack(s, carry):
        packed[s] = sl[tab[SEND, s]]
        return carry

    lax.fori_loop(0, cols * cap, pack, 0)
    pl.semaphore_wait(barrier, cols - 1 + rows - 1)

    def piece(ref, c):
        return ref.at[pl.ds(c * cap, cap)]

    def push(d, carry):
        peer = (me + d) % cols
        pltpu.make_async_remote_copy(
            piece(packed, peer), piece(got, me), a2a_s.at[peer], a2a_r.at[me],
            device_id=(row, peer), device_id_type=MESH,
        ).start()
        return carry

    lax.fori_loop(1, cols, push, 0)
    keep_m = pltpu.make_async_copy(piece(packed, me), piece(got, me), loc.at[3])
    keep_m.start()

    core = me % 2
    x = (me // 2) % SIDE
    z = me // (2 * SIDE)
    a = x + core * (z - x)
    b = z + core * (x - z)

    def at(pa, pb):
        pa, pb = (pa + SIDE) % SIDE, (pb + SIDE) % SIDE
        px = pa + core * (pb - pa)
        pz = pb + core * (pa - pb)
        return (pz * SIDE + px) * 2 + core

    sibling = me + 1 - 2 * core
    sent = [0, 0]

    def send(which, src, c, dest):
        full, ss, rs = ((fa, was, war), (fb, wbs, wbr))[which]
        k = sent[which]
        sent[which] += 1
        pltpu.make_async_remote_copy(
            src, block(full, c), ss.at[k], rs.at[c],
            device_id=(row, dest), device_id_type=MESH,
        ).start()

    def forward(which, c, dest):
        send(which, block((fa, fb)[which], c), c, dest)

    def arrived(which, c):
        full, rs = ((fa, war), (fb, wbr))[which]
        pltpu.make_async_copy(block(full, c), block(full, c), rs.at[c]).wait()

    up, down = at(a + 1, b), at(a - 1, b)
    far = at(a + 2, b)
    over, under = at(a, b + 1), at(a, b - 1)
    for dest in (up, down, over, under, sibling):
        for which, src in ((0, wa), (1, wb)):
            send(which, src, me, dest)
    arrived(0, down)
    forward(0, down, up)
    arrived(1, up)
    forward(1, up, down)
    arrived(1, down)
    arrived(0, up)
    for c in (down, up):
        for which in (0, 1):
            for dest in (over, under, sibling):
                forward(which, c, dest)
    keep_m.wait()

    def took(d, carry):
        peer = (me + d) % cols
        pltpu.make_async_copy(piece(got, peer), piece(got, peer), a2a_r.at[peer]).wait()
        return carry

    lax.fori_loop(1, cols, took, 0)

    def unpack(s, carry):
        own[s] = got[tab[PICK, s]]
        return carry

    lax.fori_loop(0, own.shape[0], unpack, 0)

    def part(ref, h, r):
        return ref.at[pl.ds(h * half, half), :, cols_of(r)]

    right, left = (row + 1) % rows, (row + rows - 1) % rows
    far_row = (row + 2) % rows
    for k, dest in ((0, right), (1, left)):
        for h in (0, 1):
            pltpu.make_async_remote_copy(
                own.at[pl.ds(h * half, half)], part(hid_full, h, row),
                y_s.at[2 * k + h], y_r.at[row, h],
                device_id=(dest, me), device_id_type=MESH,
            ).start()
    keep_y = pltpu.make_async_copy(own, hid_full.at[:, :, cols_of(row)], loc.at[4])
    keep_y.start()

    for which in (0, 1):
        arrived(which, far)
        for dest in (over, under, sibling):
            forward(which, far, dest)
    for k in (0, 1, -1, 2):
        low, high = at(a + k, b - 1), at(a + k, b + 1)
        arrived(0, low)
        forward(0, low, over)
        arrived(1, high)
        forward(1, high, under)
        arrived(1, low)
        arrived(0, high)
        for which in (0, 1):
            forward(which, low, sibling)
            forward(which, high, sibling)

    def y_here(h, r):
        pltpu.make_async_copy(part(hid_full, h, r), part(hid_full, h, r), y_r.at[r, h]).wait()

    y_here(0, left)
    pltpu.make_async_remote_copy(
        part(hid_full, 0, left), part(hid_full, 0, left), y_s.at[4], y_r.at[left, 0],
        device_id=(right, me), device_id_type=MESH,
    ).start()
    y_here(1, right)
    pltpu.make_async_remote_copy(
        part(hid_full, 1, right), part(hid_full, 1, right), y_s.at[5], y_r.at[right, 1],
        device_id=(left, me), device_id_type=MESH,
    ).start()
    y_here(1, left)
    y_here(0, right)
    for k in (0, 1, -1, 2):
        opposite = at(a + k, b + 2)
        for which in (0, 1):
            arrived(which, opposite)
            forward(which, opposite, sibling)
    y_here(0, far_row)
    y_here(1, far_row)

    def from_sibling(k, carry):
        c = 2 * k + 1 - core
        pltpu.make_async_copy(block(fa, c), block(fa, c), war.at[c]).wait()
        pltpu.make_async_copy(block(fb, c), block(fb, c), wbr.at[c]).wait()
        return carry

    lax.fori_loop(0, cols // 2, from_sibling, 0)
    keep_a.wait()
    keep_b.wait()
    keep_y.wait()

    def a2a_done(d, carry):
        peer = (me + d) % cols
        pltpu.make_async_copy(piece(packed, peer), piece(packed, peer), a2a_s.at[peer]).wait()
        return carry

    lax.fori_loop(1, cols, a2a_done, 0)

    def a_done(k, carry):
        pltpu.make_async_copy(block(fa, me), block(fa, me), was.at[k]).wait()
        return carry

    lax.fori_loop(0, sent[0], a_done, 0)

    def b_done(k, carry):
        pltpu.make_async_copy(block(fb, me), block(fb, me), wbs.at[k]).wait()
        return carry

    lax.fori_loop(0, sent[1], b_done, 0)
    for k in range(6):
        h = (0, 1, 0, 1, 0, 1)[k]
        pltpu.make_async_copy(part(hid_full, h, row), part(hid_full, h, row), y_s.at[k]).wait()


def gather_all(tab, hidden, wa, w_out, w_bc, w_dt, rows, cols, cap, held):
    requests, _, model = hidden.shape
    width = model // rows
    dt = hidden.dtype
    smem = pl.BlockSpec(memory_space=pltpu.SMEM)
    hbm = pl.BlockSpec(memory_space=pltpu.HBM)
    vmem = pl.BlockSpec(memory_space=pltpu.VMEM)
    dma = pltpu.SemaphoreType.DMA
    depth = wa.shape[0]
    rest = w_out.shape[1] + w_bc.shape[1] + 128

    def body(*refs):
        gather_kernel(rows, cols, cap, *refs)

    return pl.pallas_call(
        body,
        out_shape=(
            jax.ShapeDtypeStruct((held, LEN, model), dt),
            jax.ShapeDtypeStruct((depth * cols, wa.shape[1]), dt),
            jax.ShapeDtypeStruct((depth * cols, rest), dt),
        ),
        in_specs=[smem, hbm, vmem, vmem, vmem, vmem],
        out_specs=(hbm, hbm, hbm),
        scratch_shapes=[
            pltpu.VMEM((depth, rest), dt),
            pltpu.VMEM((requests, LEN, width), dt),
            pltpu.VMEM((cols * cap, LEN, width), dt),
            pltpu.VMEM((cols * cap, LEN, width), dt),
            pltpu.VMEM((held, LEN, width), dt),
            dma((5,)), dma((cols,)), dma((cols,)),
            dma((48,)), dma((48,)), dma((cols,)), dma((cols,)),
            dma((6,)), dma((rows, 2)),
        ],
        compiler_params=pltpu.CompilerParams(
            collective_id=0, has_side_effects=True, vmem_limit_bytes=32 << 20
        ),
        name="gather_all",
    )(tab, hidden, wa, w_out, w_bc, w_dt)


def return_kernel(
    rows, cols, cap, tab, part, ss, xmsg, emsg, mixed, xgot, egot,
    mine, came, ss_in, scale, mix0, mix1, mix2, packed, got0, got1, got2,
    loc, ss_s, ss_r, y_s, y_r, a2a_s, a2a_r, x_s, x_r, e_s, e_r,
):
    row, me = lax.axis_index("row"), lax.axis_index("col")
    barrier = greet(row, me, rows, cols)
    pieces = part.shape[0] // rows
    tokens = part.shape[1]
    keep = pltpu.make_async_copy(part.at[pl.ds(row * pieces, pieces)], mine, loc.at[0])
    keep.start()
    pl.semaphore_wait(barrier, cols - 1 + rows - 1)
    order = (1, 3, 2)
    for k, d in enumerate(order):
        peer = (row + d) % rows
        pltpu.make_async_remote_copy(
            ss, ss_in.at[row], ss_s.at[k], ss_r.at[row],
            device_id=(peer, me), device_id_type=MESH,
        ).start()
    for j in range(pieces):
        for k, d in enumerate(order):
            peer = (row + d) % rows
            pltpu.make_async_remote_copy(
                part.at[peer * pieces + j], came.at[row, j], y_s.at[j, k], y_r.at[row, j],
                device_id=(peer, me), device_id_type=MESH,
            ).start()
    def piece(ref, c):
        return ref.at[pl.ds(c * cap, cap)]

    def push_factors(d, carry):
        peer = (me + d) % cols
        for src, dst, ss_, rs_ in ((xmsg, xgot, x_s, x_r), (emsg, egot, e_s, e_r)):
            pltpu.make_async_remote_copy(
                piece(src, peer), piece(dst, me), ss_.at[peer], rs_.at[me],
                device_id=(row, peer), device_id_type=MESH,
            ).start()
        return carry

    lax.fori_loop(1, cols, push_factors, 0)
    keep_x = pltpu.make_async_copy(piece(xmsg, me), piece(xgot, me), loc.at[4])
    keep_e = pltpu.make_async_copy(piece(emsg, me), piece(egot, me), loc.at[5])
    keep_x.start()
    keep_e.start()
    total = ss[...]
    for d in order:
        peer = (row + d) % rows
        pltpu.make_async_copy(ss_in.at[peer], ss_in.at[peer], ss_r.at[peer]).wait()
        total = total + ss_in[peer]
    factor = lax.rsqrt(total / INNER + 1e-05)
    for i in range(tokens // TOK):
        line = jnp.broadcast_to(factor[i : i + 1, :], (TOK, TOK))
        scale[pl.ds(i * TOK, TOK), :] = line.T
    keep.wait()
    gots = (got0, got1, got2)

    mixes = (mix0, mix1, mix2)
    for j in range(pieces):
        mix = mixes[j]
        for d in order:
            peer = (row + d) % rows
            pltpu.make_async_copy(came.at[peer, j], came.at[peer, j], y_r.at[peer, j]).wait()

        def add(i, carry):
            at = pl.ds(pl.multiple_of(i * TOK, TOK), TOK)
            value = mine[j, at, :].astype(jnp.float32)
            for d in order:
                value = value + came[(row + d) % rows, j, at, :].astype(jnp.float32)
            value = (value * scale[at, :]).astype(mix.dtype)
            mix[pl.ds(i * GROUP, GROUP)] = value.reshape(GROUP, LEN, 128)
            return carry

        lax.fori_loop(0, tokens // TOK, add, 0)

        def pack(s, carry):
            packed[j, s] = mix[tab[BACK, s]]
            return carry

        lax.fori_loop(0, cols * cap, pack, 0)

        def push(d, carry):
            peer = (me + d) % cols
            pltpu.make_async_remote_copy(
                piece(packed.at[j], peer), piece(gots[j], me), a2a_s.at[j, peer], a2a_r.at[j, me],
                device_id=(row, peer), device_id_type=MESH,
            ).start()
            return carry

        lax.fori_loop(1, cols, push, 0)
        pltpu.make_async_copy(piece(packed.at[j], me), piece(gots[j], me), loc.at[1 + j]).start()
    for j in range(pieces):
        got, mix = gots[j], mixes[j]
        pltpu.make_async_copy(piece(packed.at[j], me), piece(got, me), loc.at[1 + j]).wait()

        def took(d, carry):
            peer = (me + d) % cols
            pltpu.make_async_copy(piece(got, peer), piece(got, peer), a2a_r.at[j, peer]).wait()
            return carry

        lax.fori_loop(1, cols, took, 0)

        def unpack(s, carry):
            moved = tab[MOVED, s].astype(jnp.float32)
            away = got[tab[FROM_MSG, s]].astype(jnp.float32)
            here = mix[tab[FROM_MIX, s]].astype(jnp.float32)
            value = jnp.where(moved > 0.5, away, here)
            mixed[s, :, j * 128 : (j + 1) * 128] = value.astype(mixed.dtype)
            return carry

        lax.fori_loop(0, mixed.shape[0], unpack, 0)
    for k in range(3):
        pltpu.make_async_copy(ss, ss, ss_s.at[k]).wait()
        for j in range(pieces):
            pltpu.make_async_copy(mine.at[j], mine.at[j], y_s.at[j, k]).wait()
    for j in range(pieces):

        def gone(d, carry):
            peer = (me + d) % cols
            pltpu.make_async_copy(
                piece(packed.at[j], peer), piece(packed.at[j], peer), a2a_s.at[j, peer]
            ).wait()
            return carry

        lax.fori_loop(1, cols, gone, 0)


    keep_x.wait()
    keep_e.wait()

    def factors(d, carry):
        peer = (me + d) % cols
        for ref, ss_, rs_ in ((xgot, x_s, x_r), (egot, e_s, e_r)):
            pltpu.make_async_copy(piece(ref, peer), piece(ref, peer), rs_.at[peer]).wait()
            pltpu.make_async_copy(piece(ref, peer), piece(ref, peer), ss_.at[peer]).wait()
        return carry

    lax.fori_loop(1, cols, factors, 0)


def send_home(tab, part, ss, xmsg, emsg, rows, cols, cap):
    pieces = part.shape[0] // rows
    tokens = part.shape[1]
    smem = pl.BlockSpec(memory_space=pltpu.SMEM)
    hbm = pl.BlockSpec(memory_space=pltpu.HBM)
    vmem = pl.BlockSpec(memory_space=pltpu.VMEM)
    dma = pltpu.SemaphoreType.DMA
    slots = cols * cap
    requests = tokens // LEN
    dt = part.dtype

    def body(*refs):
        return_kernel(rows, cols, cap, *refs)

    mix = pltpu.VMEM((requests, LEN, 128), dt)
    got = pltpu.VMEM((slots, LEN, 128), dt)
    return pl.pallas_call(
        body,
        out_shape=(
            jax.ShapeDtypeStruct((requests, LEN, pieces * 128), dt),
            jax.ShapeDtypeStruct(xmsg.shape, dt),
            jax.ShapeDtypeStruct(emsg.shape, dt),
        ),
        in_specs=[smem, hbm, vmem, hbm, hbm],
        out_specs=(vmem, hbm, hbm),
        scratch_shapes=[
            pltpu.VMEM((pieces, tokens, 128), dt),
            pltpu.VMEM((rows, pieces, tokens, 128), dt),
            pltpu.VMEM((rows,) + ss.shape, jnp.float32),
            pltpu.VMEM((tokens, 128), jnp.float32),
            mix, mix, mix,
            pltpu.VMEM((pieces, slots, LEN, 128), dt),
            got, got, got,
            dma((3 + pieces,)), dma((3,)), dma((rows,)),
            dma((pieces, 3)), dma((rows, pieces)), dma((pieces, cols)), dma((pieces, cols)),
            dma((cols,)), dma((cols,)), dma((cols,)), dma((cols,)),
        ],
        compiler_params=pltpu.CompilerParams(
            collective_id=1, has_side_effects=True, vmem_limit_bytes=32 << 20
        ),
        name="send_home",
    )(tab, part, ss, xmsg, emsg)


def silu(v):
    return v / (1.0 + jnp.exp(-v))


def token_masks():
    t_ids = lax.broadcasted_iota(jnp.int32, (TOK, TOK), 0)
    s_ids = lax.broadcasted_iota(jnp.int32, (TOK, TOK), 1)
    return t_ids, s_ids


def mixer_kernel(
    held, tab, hid_c, hidden, fa, fb, dtb, alog, skip, cxw, cxb, cbw, cbb, gain, prev, pex, peb,
    part, ss, xmsg, emsg, nst, nex, neb,
    hid, wa, wb, old, gate, xin, bc, dts, gg, cx, cb, pexf, pebf, new, outs,
    h_sem, o_sem, w_sem, n_sem, p_sem,
):
    f32, bf16 = jnp.float32, jnp.bfloat16
    inner = gain.shape[1]
    requests = hid.shape[0]
    tokens = requests * LEN
    model = hid.shape[2]
    heads = inner // HEAD_DIM
    blocks = wa.shape[1] // 256

    load_h = pltpu.make_async_copy(hid_c, hid.at[pl.ds(0, held)], h_sem)
    load_h.start()

    def wa_load(n):
        at = pl.ds(n * 256, 256)
        return pltpu.make_async_copy(fa.at[:, at], wa.at[:, at], w_sem.at[n])

    wa_load(0).start()

    def home(n):
        return pltpu.make_async_copy(hidden.at[tab[STAY, n]], hid.at[held + n], o_sem.at[n])

    @pl.loop(0, requests - held)
    def _(n):
        home(n).start()

    for n in range(1, blocks):
        wa_load(n).start()
    late = pl.ds(inner, wb.shape[1] - inner)
    early = pl.ds(0, inner)
    load_bc = pltpu.make_async_copy(fb.at[:, late], wb.at[:, late], w_sem.at[blocks])
    load_out = pltpu.make_async_copy(fb.at[:, early], wb.at[:, early], w_sem.at[blocks + 1])
    load_old = pltpu.make_async_copy(prev, old, w_sem.at[blocks + 2])
    load_bc.start()
    load_old.start()
    load_out.start()
    pexf[...] = pex[...].astype(f32)
    pebf[...] = peb[...].astype(f32)

    t_ids, s_ids = token_masks()
    same = (t_ids // LEN) == (s_ids // LEN)
    causal = same & (t_ids >= s_ids)
    tri = causal.astype(f32)
    spread_h = (
        lax.broadcasted_iota(jnp.int32, (TOK, inner), 1) // HEAD_DIM
        == lax.broadcasted_iota(jnp.int32, (TOK, inner), 0)
    ).astype(f32)

    def wide(ref):
        return jnp.concatenate([ref[...], jnp.zeros((1, TOK - heads), f32)], axis=1)

    bias, rate = wide(dtb), -jnp.exp(wide(alog))
    skip_x = jnp.dot(
        jnp.broadcast_to(wide(skip), (8, TOK)), spread_h,
        precision=HIGHEST, preferred_element_type=f32,
    )[0:1, :]

    load_h.wait()

    @pl.loop(0, requests - held)
    def _(n):
        home(n).wait()

    left = lax.broadcasted_iota(jnp.int32, (tokens, 128), 1) < HEAD_DIM
    for n in range(blocks):
        wa_load(n).wait()
        z = jnp.dot(
            hid[...].reshape(tokens, model), wa[:, n * 256 : (n + 1) * 256],
            preferred_element_type=f32,
        )
        z0, z1 = z[:, :128], z[:, 128:]
        at = slice(n * 128, (n + 1) * 128)
        gate[:, at] = jnp.where(left, z0, pltpu.roll(z1, HEAD_DIM, 1)).astype(bf16)
        xin[:, at] = jnp.where(left, pltpu.roll(z0, HEAD_DIM, 1), z1).astype(bf16)
    load_bc.wait()
    z = jnp.dot(hid[...].reshape(tokens, model), wb[:, inner:], preferred_element_type=f32)
    bc[...] = z[:, : 2 * STATE].astype(bf16)
    dts[...] = z[:, 2 * STATE :]
    load_old.wait()

    def store(s):
        return pltpu.make_async_copy(new.at[s], nst.at[tab[POS, s]], n_sem.at[s])

    def group(i, live):
        at = pl.ds(pl.multiple_of(i * TOK, TOK), TOK)
        first = i * GROUP
        last = jnp.zeros((TOK, TOK), jnp.int32)
        accs = []
        for r in range(GROUP):
            acc = tab[ACC, first + r] if live else tab[STAY_ACC, first - held + r]
            accs.append(acc)
            last = jnp.where(t_ids // LEN == r, acc, last)
            if live:
                for k in range(KCONV - 1):
                    cx[r, 13 + k : 14 + k, :] = pexf[k, pl.ds(first + r, 1), :]
                    cb[r, 13 + k : 14 + k, :] = pebf[k, pl.ds(first + r, 1), :]
        if not live:
            cx[:, 8:16, :] = jnp.zeros((GROUP, 8, inner), f32)
            cb[:, 8:16, :] = jnp.zeros((GROUP, 8, 2 * STATE), f32)
        cx[:, 16:32, :] = xin[at, :].astype(f32).reshape(GROUP, LEN, inner)
        cb[:, 16:32, :] = bc[at, :].astype(f32).reshape(GROUP, LEN, 2 * STATE)
        tot_x = cxb[...].reshape(1, 1, inner) + cxw[0:1, :].reshape(1, 1, inner) * cx[:, 13:29, :]
        tot_b = cbb[...].reshape(1, 1, 2 * STATE) + cbw[0:1, :].reshape(
            1, 1, 2 * STATE
        ) * cb[:, 13:29, :]
        for k in range(1, KCONV):
            tot_x = tot_x + cxw[k : k + 1, :].reshape(1, 1, inner) * cx[:, 13 + k : 29 + k, :]
            tot_b = tot_b + cbw[k : k + 1, :].reshape(1, 1, 2 * STATE) * cb[:, 13 + k : 29 + k, :]
        xc = silu(tot_x).reshape(TOK, inner).astype(bf16)
        bcc = silu(tot_b).reshape(TOK, 2 * STATE).astype(bf16)
        for r in range(GROUP):
            ex = pltpu.roll(cx[r], 19 - accs[r], 0)
            eb = pltpu.roll(cb[r], 19 - accs[r], 0)
            if live:
                place = tab[POS, first + r]
                for k in range(KCONV - 1):
                    nex[k, pl.ds(place, 1), :] = ex[k : k + 1, :]
                    neb[k, pl.ds(place, 1), :] = eb[k : k + 1, :]
            else:
                lines = []
                for k in range(KCONV - 1):
                    lines.append(ex[k : k + 1, :384])
                    lines.append(jnp.concatenate([ex[k : k + 1, 384:], eb[k : k + 1, :]], axis=1))
                lines.append(jnp.zeros((2, 384), f32))
                emsg[tab[STAY_KEY, first - held + r]] = jnp.concatenate(lines, axis=0).astype(bf16)
        b_in, c_in = bcc[:, :STATE], bcc[:, STATE:]
        xf = xc.astype(f32)
        raw = dts[at, :] + bias
        step = jnp.maximum(raw, 0.0) + jnp.log(1.0 + jnp.exp(-jnp.abs(raw)))
        decay = jnp.dot(tri, step * rate, precision=HIGHEST, preferred_element_type=f32)
        decay_t = decay.T
        step_t = step.T
        choose = (same & (s_ids % LEN == last - 1)).astype(f32)
        reach = jnp.dot(choose, decay, precision=HIGHEST, preferred_element_type=f32)
        taken = t_ids % LEN < last
        weight = jnp.where(taken, jnp.exp(jnp.minimum(reach - decay, 0.0)), 0.0) * step
        weight_x = jnp.dot(weight, spread_h, precision=HIGHEST, preferred_element_type=f32)
        scores = lax.dot_general(
            c_in, b_in, (((1,), (1,)), ((), ())), preferred_element_type=f32
        )
        scores = jnp.where(causal, scores, 0.0)
        half = s_ids < HEAD_DIM
        zero = jnp.zeros((TOK, 2 * HEAD_DIM), bf16)
        y = []
        for pair in range(heads // 2):
            mats = []
            for h in (2 * pair, 2 * pair + 1):
                gap = decay[:, h : h + 1] - decay_t[h : h + 1, :]
                mats.append(
                    (jnp.exp(jnp.minimum(gap, 0.0)) * scores * step_t[h : h + 1, :]).astype(bf16)
                )
            xp = xc[:, pair * 128 : (pair + 1) * 128]
            both = jnp.concatenate([jnp.where(half, xp, zero), jnp.where(half, zero, xp)], axis=0)
            y.append(
                jnp.dot(jnp.concatenate(mats, axis=1), both, preferred_element_type=f32)
            )
        y = jnp.concatenate(y, axis=1)
        if live:
            grow_x = jnp.dot(jnp.exp(decay), spread_h, precision=HIGHEST, preferred_element_type=f32)
            carried = [
                lax.dot_general(
                    c_in[r * LEN : (r + 1) * LEN, :], old[first + r], (((1,), (1,)), ((), ())),
                    preferred_element_type=f32,
                )
                for r in range(GROUP)
            ]
            y = y + grow_x * jnp.concatenate(carried, axis=0)
        y = y + skip_x * xf
        gated = y * silu(gate[at, :].astype(f32))
        gg[at, :] = (gated * gain[...]).astype(bf16)
        squares = jnp.sum(gated * gated, axis=1, keepdims=True)
        ss[pl.ds(i, 1), :] = jnp.broadcast_to(squares, (TOK, TOK)).T[0:1, :]

        if not live:
            sent = (xf * weight_x).astype(bf16)
            for r in range(GROUP):
                key = tab[STAY_KEY, first - held + r]
                lines = slice(r * LEN, (r + 1) * LEN)
                xmsg[key, :, :inner] = sent[lines, :]
                xmsg[key, :, inner:] = b_in[lines, :]
            return
        xw = (xf * weight_x).T
        high = xw.astype(bf16)
        low = (xw - high.astype(f32)).astype(bf16)
        lhs = jnp.concatenate([high, low], axis=1)
        keep_t = jnp.exp(reach).T
        none = jnp.zeros((TOK, STATE), bf16)
        for pair in range(GROUP // 2):
            cut = jnp.concatenate(
                [
                    jnp.where(t_ids // LEN == r, b_in, none)
                    for r in (2 * pair, 2 * pair + 1)
                ],
                axis=1,
            )
            added = jnp.dot(
                lhs, jnp.concatenate([cut, cut], axis=0), preferred_element_type=f32
            )
            for k in (0, 1):
                r = 2 * pair + k
                s = first + r
                factor = jnp.broadcast_to(keep_t[0:heads, r * LEN : r * LEN + 1], (heads, STATE))
                was = old[s].astype(f32).reshape(heads, HEAD_DIM, STATE)
                now = factor[:, None, :] * was + added[:, k * STATE : (k + 1) * STATE].reshape(
                    heads, HEAD_DIM, STATE
                )
                new[s] = now.reshape(inner, STATE).astype(bf16)
                store(s).start()

    @pl.loop(0, held // GROUP)
    def _(i):
        group(i, True)

    @pl.loop(held // GROUP, requests // GROUP)
    def _(i):
        group(i, False)

    load_out.wait()

    def put(q):
        at = pl.ds(2 * q, 2)
        return pltpu.make_async_copy(outs.at[at], part.at[at], p_sem.at[q])

    @pl.loop(0, part.shape[0] // 2)
    def _(q):
        at = pl.ds(pl.multiple_of(q * 256, 256), 256)
        out = lax.dot_general(
            gg[...], wb[at, :inner], (((1,), (1,)), ((), ())), preferred_element_type=f32
        ).astype(bf16)
        outs[2 * q] = out[:, :128]
        outs[2 * q + 1] = out[:, 128:]
        put(q).start()

    @pl.loop(0, part.shape[0] // 2)
    def _(q):
        put(q).wait()

    @pl.loop(0, held)
    def _(s):
        store(s).wait()


def mixer(tab, hid_c, hidden, fa, fb, vectors, prev, pex, peb, slots):
    requests, _, model = hidden.shape
    held = hid_c.shape[0]
    tokens = requests * LEN
    inner = fa.shape[1] // 2
    heads = inner // HEAD_DIM
    dt = hidden.dtype
    f32 = jnp.float32
    smem = pl.BlockSpec(memory_space=pltpu.SMEM)
    vmem = pl.BlockSpec(memory_space=pltpu.VMEM)
    hbm = pl.BlockSpec(memory_space=pltpu.HBM)
    dma = pltpu.SemaphoreType.DMA

    def body(*refs):
        mixer_kernel(held, *refs)

    return pl.pallas_call(
        body,
        out_shape=(
            jax.ShapeDtypeStruct((model // 128, tokens, 128), dt),
            jax.ShapeDtypeStruct((8, 128), f32),
            jax.ShapeDtypeStruct((slots, LEN, inner + STATE), dt),
            jax.ShapeDtypeStruct((slots, 8, 384), dt),
            jax.ShapeDtypeStruct((requests, inner, STATE), dt),
            jax.ShapeDtypeStruct((3, requests, inner), f32),
            jax.ShapeDtypeStruct((3, requests, 2 * STATE), f32),
        ),
        in_specs=[smem] + [hbm] * 4 + [vmem] * len(vectors) + [hbm, vmem, vmem],
        out_specs=(hbm, vmem, vmem, vmem, hbm, vmem, vmem),
        scratch_shapes=[
            pltpu.VMEM((requests, LEN, model), dt),
            pltpu.VMEM(fa.shape, dt),
            pltpu.VMEM(fb.shape, dt),
            pltpu.VMEM((held, inner, STATE), dt),
            pltpu.VMEM((tokens, inner), dt),
            pltpu.VMEM((tokens, inner), dt),
            pltpu.VMEM((tokens, 2 * STATE), dt),
            pltpu.VMEM((tokens, 128), f32),
            pltpu.VMEM((tokens, inner), dt),
            pltpu.VMEM((GROUP, 32, inner), f32),
            pltpu.VMEM((GROUP, 32, 2 * STATE), f32),
            pltpu.VMEM((3, held, inner), f32),
            pltpu.VMEM((3, held, 2 * STATE), f32),
            pltpu.VMEM((held, inner, STATE), dt),
            pltpu.VMEM((model // 128, tokens, 128), dt),
            dma(()), dma((requests - held,)), dma((fa.shape[1] // 256 + 3,)), dma((held,)),
            dma((model // 256,)),
        ],
        compiler_params=pltpu.CompilerParams(vmem_limit_bytes=52 << 20),
        name="mixer",
    )(tab, hid_c, hidden, fa, fb, *vectors, prev, pex, peb)


def arrive_kernel(tab, xgot, egot, exf, ebf, nst_in, nst, nex, neb, xs, bs, ex, eb, new, n_sem):
    f32, bf16 = jnp.float32, jnp.bfloat16
    count, inner = new.shape[0], new.shape[1]
    t_ids, _ = token_masks()
    none = jnp.zeros((TOK, STATE), bf16)

    def store(u):
        return pltpu.make_async_copy(new.at[u], nst.at[tab[POS_O, u]], n_sem.at[u])

    @pl.loop(0, count // GROUP)
    def _(i):
        for r in range(GROUP):
            slot = tab[PICK_O, i * GROUP + r]
            xs[r] = xgot[slot, :, :inner]
            bs[r] = xgot[slot, :, inner:]
        lhs = xs[...].reshape(TOK, inner).astype(f32).T.astype(bf16)
        b_in = bs[...].reshape(TOK, STATE)
        for pair in range(GROUP // 2):
            cut = jnp.concatenate(
                [
                    jnp.where(t_ids // LEN == r, b_in, none)
                    for r in (2 * pair, 2 * pair + 1)
                ],
                axis=1,
            )
            out = jnp.dot(lhs, cut, preferred_element_type=f32).astype(bf16)
            for k in (0, 1):
                u = i * GROUP + 2 * pair + k
                new[u] = out[:, k * STATE : (k + 1) * STATE]
                store(u).start()

    ex[...] = exf[...]
    eb[...] = ebf[...]

    @pl.loop(0, count)
    def _(u):
        lines = egot[tab[PICK_O, u]].astype(f32)
        at = pl.ds(tab[POS_O, u], 1)
        for k in range(KCONV - 1):
            ex[k, at, :] = jnp.concatenate(
                [lines[2 * k : 2 * k + 1, :], lines[2 * k + 1 : 2 * k + 2, :128]], axis=1
            )
            eb[k, at, :] = lines[2 * k + 1 : 2 * k + 2, 128:]

    nex[...] = ex[...].astype(bf16)
    neb[...] = eb[...].astype(bf16)

    @pl.loop(0, count)
    def _(u):
        store(u).wait()


def arrive(tab, xgot, egot, exf, ebf, nst):
    requests, inner, _ = nst.shape
    count = requests // 2
    dt, f32 = nst.dtype, jnp.float32
    smem = pl.BlockSpec(memory_space=pltpu.SMEM)
    vmem = pl.BlockSpec(memory_space=pltpu.VMEM)
    hbm = pl.BlockSpec(memory_space=pltpu.HBM)
    return pl.pallas_call(
        arrive_kernel,
        out_shape=(
            jax.ShapeDtypeStruct(nst.shape, dt),
            jax.ShapeDtypeStruct(exf.shape, dt),
            jax.ShapeDtypeStruct(ebf.shape, dt),
        ),
        in_specs=[smem, vmem, vmem, vmem, vmem, hbm],
        out_specs=(hbm, vmem, vmem),
        scratch_shapes=[
            pltpu.VMEM((GROUP, LEN, inner), dt),
            pltpu.VMEM((GROUP, LEN, STATE), dt),
            pltpu.VMEM(exf.shape, f32),
            pltpu.VMEM(ebf.shape, f32),
            pltpu.VMEM((count, inner, STATE), dt),
            pltpu.SemaphoreType.DMA((count,)),
        ],
        input_output_aliases={5: 0},
        compiler_params=pltpu.CompilerParams(vmem_limit_bytes=40 << 20),
        name="arrive",
    )(tab, xgot, egot, exf, ebf, nst)


def per_device(
    hidden, w_zx, w_bc, w_dt, w_out, dt_bias, a_log, d_skip, conv_x_w, conv_x_b,
    conv_bc_w, conv_bc_b, norm_gain, prev_state, prev_edge_x, prev_edge_bc,
    holder, continued, owner, accepted,
):
    rows, cols = lax.axis_size("row"), lax.axis_size("col")
    tokens, model = hidden.shape
    requests = tokens // LEN
    heads = dt_bias.shape[0]
    inner = heads * HEAD_DIM
    held = prev_state.shape[0]
    cap = 2 * ((requests // 4 + cols - 1) // cols)
    code = owner + 64 * (continued == 1).astype(jnp.int32) + 128 * accepted
    tab = route(code.reshape(cols, requests), held)
    hidden = hidden.reshape(requests, LEN, model)
    hid_c, fa, fb = gather_all(tab, hidden, w_zx, w_out, w_bc, w_dt.T, rows, cols, cap, held)
    vectors = (
        dt_bias[None, :], a_log[None, :], d_skip[None, :],
        conv_x_w, conv_x_b[None, :], conv_bc_w, conv_bc_b[None, :], norm_gain[None, :],
    )
    part, ss, xmsg, emsg, states, exf, ebf = mixer(
        tab, hid_c, hidden, fa, fb, vectors, prev_state.reshape(held, inner, STATE),
        prev_edge_x.transpose(1, 0, 2), prev_edge_bc.transpose(1, 0, 2), cols * cap,
    )
    mixed, xgot, egot = send_home(tab, part, ss, xmsg, emsg, rows, cols, cap)
    states, new_x, new_bc = arrive(tab, xgot, egot, exf, ebf, states)
    return (
        mixed.reshape(tokens, model // rows),
        states.reshape(requests, heads, HEAD_DIM, STATE),
        new_x.transpose(1, 0, 2),
        new_bc.transpose(1, 0, 2),
    )


def solution(mesh):
    return jax.shard_map(
        per_device,
        mesh=mesh,
        in_specs=(
            P("col", None),
            P("col", "row"),
            P("col", None),
            P("col", "row"),
            P("col", "row"),
            P("row"),
            P("row"),
            P("row"),
            P(None, "row"),
            P("row"),
            P(),
            P(),
            P("row"),
            P("col", "row", None, None),
            P("col", None, "row"),
            P("col", None, None),
            P(),
            P(),
            P(),
            P(),
        ),
        out_specs=(
            P("col", "row"),
            P("col", "row", None, None),
            P("col", None, "row"),
            P("col", None, None),
        ),
        check_vma=False,
    )
```

```python
import jax
import jax.numpy as jnp
from jax import lax
from jax.experimental import pallas as pl
from jax.experimental.pallas import tpu as pltpu
from jax.sharding import PartitionSpec as P

HEAD_DIM = 64
STATE = 128
KCONV = 4
LEN = 16
INNER = 2048
SIDE = 4
GROUP = 8
TOK = GROUP * LEN
MESH = pl.DeviceIdType.MESH
HIGHEST = lax.Precision.HIGHEST


def route_kernel(held, code, out):
    f32, bf16 = jnp.float32, jnp.bfloat16
    me = lax.axis_index("col")
    groups, requests = code.shape
    value = code[...]
    o, c, a = value & 63, (value >> 6) & 1, value >> 7

    def dot(x, y):
        return jnp.dot(x.astype(bf16), y.astype(bf16), preferred_element_type=f32)

    def dot0(x, y):
        return lax.dot_general(
            x.astype(bf16), y.astype(bf16), (((0,), (0,)), ((), ())), preferred_element_type=f32
        )

    def ids(shape, dim):
        return lax.broadcasted_iota(jnp.int32, shape, dim)

    below = (ids((requests, requests), 0) < ids((requests, requests), 1)).astype(f32)
    prior = (ids((groups, groups), 1) < ids((groups, groups), 0)).astype(f32)
    lane = ids((groups, 128), 1).astype(f32)
    group = ids((groups, 128), 0).astype(f32)
    spots, inside, starts = [], [], []
    for kind in (1, 0):
        mask = ((o == me) & (c == kind)).astype(f32)
        rank = dot(mask, below)
        count = jnp.broadcast_to(jnp.sum(mask, axis=1, keepdims=True), (groups, 128))
        start = dot(prior, count)
        hot = ((start <= lane) & (lane < start + count)).astype(f32)
        spots.append((jnp.where(mask > 0, rank, -1.0), hot))
        inside.append(rank)
        starts.append(start)
    rank_all, start_all = inside[0] + inside[1], starts[0] + starts[1]
    picks, places, taken = [], [], []
    for k in (0, 1):
        spot, hot = spots[k]
        order = jnp.sum(hot * (lane - starts[k]), axis=0, keepdims=True)
        any_hot = jnp.sum(hot, axis=0, keepdims=True)
        order = jnp.where(any_hot > 0, order, -5.0)
        match = (dot0(spot, hot) == order).astype(f32)
        picks.append(jnp.sum(hot * (2 * group + lane - starts[k]), axis=0, keepdims=True))
        places.append(
            jnp.sum(hot * start_all, axis=0, keepdims=True)
            + jnp.sum(match * dot0(rank_all, hot), axis=0, keepdims=True)
        )
        taken.append(jnp.sum(match * dot0(a, hot), axis=0, keepdims=True))
    lane_i, group_i = ids((groups, 128), 1), ids((groups, 128), 0)
    back = jnp.sum(
        jnp.where(lane_i // 2 == group_i, starts[0] + (lane_i % 2).astype(f32), 0.0),
        axis=0, keepdims=True,
    )
    back = jnp.minimum(back, held - 1.0)

    def my_row(x, fill):
        row = jnp.sum(
            jnp.where(ids((groups, requests), 0) == me, x, 0).astype(f32), axis=0, keepdims=True
        )
        rest = jnp.full((1, 128 - requests), fill, f32)
        return jnp.concatenate([row, rest], axis=1)

    o_row, c_row, a_row = my_row(o, 99.0), my_row(c, 2.0), my_row(a, 0.0)

    def column(row):
        return jnp.broadcast_to(row, (128, 128)).T

    o_col, c_col, a_col = column(o_row), column(c_row), column(a_row)
    ii, jj = ids((128, 128), 0), ids((128, 128), 1)
    alike = (o_col == o_row) & (c_col == c_row)
    rank_row = jnp.sum((alike & (ii < jj)).astype(f32), axis=0, keepdims=True)
    rank_col = jnp.sum((alike & (jj < ii)).astype(f32), axis=1, keepdims=True)
    nth_row = jnp.sum(((c_col == 0) & (ii < jj)).astype(f32), axis=0, keepdims=True)
    nth_col = jnp.sum(((c_row == 0) & (jj < ii)).astype(f32), axis=1, keepdims=True)
    key_row = 2 * o_row + rank_row
    key_col = 2 * o_col + rank_col
    fi, fj = ii.astype(f32), jj.astype(f32)
    goes = (c_col == 1) & (key_col == fj)
    stays = (c_col == 0) & (nth_col == fj)

    def total(mask, x):
        return jnp.sum(jnp.where(mask, x, 0.0), axis=0, keepdims=True)

    table = (
        total(goes, fi), picks[0], back,
        jnp.where(c_row == 1, key_row, 0.0), jnp.where(c_row == 0, held + nth_row, 0.0),
        (c_row == 1).astype(f32),
        total(stays, fi), total(stays, key_col), total(stays, a_col),
        taken[0], places[0], picks[1], places[1],
    )
    for k, line in enumerate(table):
        out[k : k + 1, :] = line.astype(jnp.int32)
    out[len(table) :, :] = jnp.zeros((16 - len(table), 128), jnp.int32)


SEND, PICK, BACK, FROM_MSG, FROM_MIX, MOVED, STAY, STAY_KEY, STAY_ACC, ACC, POS, PICK_O, POS_O = range(13)


def route(code, held):
    vmem = pl.BlockSpec(memory_space=pltpu.VMEM)

    def body(*refs):
        route_kernel(held, *refs)

    return pl.pallas_call(
        body, out_shape=jax.ShapeDtypeStruct((16, 128), jnp.int32),
        in_specs=[vmem], out_specs=vmem, name="route",
        compiler_params=pltpu.CompilerParams(vmem_limit_bytes=60 << 20),
    )(code)


def greet(row, me, rows, cols):
    barrier = pltpu.get_barrier_semaphore()

    def along_col(d, carry):
        pl.semaphore_signal(
            barrier, inc=1, device_id=(row, (me + d) % cols), device_id_type=MESH
        )
        return carry

    lax.fori_loop(1, cols, along_col, 0)

    def along_row(d, carry):
        pl.semaphore_signal(
            barrier, inc=1, device_id=((row + d) % rows, me), device_id_type=MESH
        )
        return carry

    lax.fori_loop(1, rows, along_row, 0)
    return barrier


def gather_kernel(
    rows, cols, cap, tab_in, hidden, wa, w_out, w_bc, w_dt_in, hid_full, fa, fb,
    tab, w_dt, wb, sl, packed, got, own, loc, a2a_s, a2a_r, was, wbs, war, wbr, y_s, y_r,
):
    row, me = lax.axis_index("row"), lax.axis_index("col")
    barrier = greet(row, me, rows, cols)
    width = sl.shape[2]
    half = own.shape[0] // 2
    depth = wa.shape[0]

    def cols_of(r):
        return pl.ds(pl.multiple_of(r * width, 128), width)

    def block(ref, c):
        return ref.at[pl.ds(pl.multiple_of(c * depth, 16), depth), :]

    load = pltpu.make_async_copy(hidden.at[:, :, cols_of(row)], sl, loc.at[0])
    load.start()
    inner = w_out.shape[1]
    states = w_bc.shape[1]
    heads = w_dt_in.shape[0]
    loads = (
        pltpu.make_async_copy(tab_in, tab, loc.at[5]),
        pltpu.make_async_copy(w_dt_in, w_dt, loc.at[6]),
        pltpu.make_async_copy(w_out, wb.at[:, pl.ds(0, inner)], loc.at[7]),
        pltpu.make_async_copy(w_bc, wb.at[:, pl.ds(inner, states)], loc.at[8]),
    )
    for copy in loads:
        copy.start()
    for copy in loads:
        copy.wait()
    square = jnp.concatenate([w_dt[...].astype(jnp.float32), jnp.zeros((heads, 128 - depth), jnp.float32)], axis=1)
    square = jnp.concatenate([square, jnp.zeros((128 - heads, 128), jnp.float32)], axis=0).T
    wb[:, inner + states :] = square[:depth, :].astype(wb.dtype)
    keep_a = pltpu.make_async_copy(wa, block(fa, me), loc.at[1])
    keep_b = pltpu.make_async_copy(wb, block(fb, me), loc.at[2])
    keep_a.start()
    keep_b.start()
    load.wait()

    def pack(s, carry):
        packed[s] = sl[tab[SEND, s]]
        return carry

    lax.fori_loop(0, cols * cap, pack, 0)
    pl.semaphore_wait(barrier, cols - 1 + rows - 1)

    def piece(ref, c):
        return ref.at[pl.ds(c * cap, cap)]

    def push(d, carry):
        peer = (me + d) % cols
        pltpu.make_async_remote_copy(
            piece(packed, peer), piece(got, me), a2a_s.at[peer], a2a_r.at[me],
            device_id=(row, peer), device_id_type=MESH,
        ).start()
        return carry

    lax.fori_loop(1, cols, push, 0)
    keep_m = pltpu.make_async_copy(piece(packed, me), piece(got, me), loc.at[3])
    keep_m.start()

    core = me % 2
    x = (me // 2) % SIDE
    z = me // (2 * SIDE)
    a = x + core * (z - x)
    b = z + core * (x - z)

    def at(pa, pb):
        pa, pb = (pa + SIDE) % SIDE, (pb + SIDE) % SIDE
        px = pa + core * (pb - pa)
        pz = pb + core * (pa - pb)
        return (pz * SIDE + px) * 2 + core

    sibling = me + 1 - 2 * core
    sent = [0, 0]

    def send(which, src, c, dest):
        full, ss, rs = ((fa, was, war), (fb, wbs, wbr))[which]
        k = sent[which]
        sent[which] += 1
        pltpu.make_async_remote_copy(
            src, block(full, c), ss.at[k], rs.at[c],
            device_id=(row, dest), device_id_type=MESH,
        ).start()

    def forward(which, c, dest):
        send(which, block((fa, fb)[which], c), c, dest)

    def arrived(which, c):
        full, rs = ((fa, war), (fb, wbr))[which]
        pltpu.make_async_copy(block(full, c), block(full, c), rs.at[c]).wait()

    up, down = at(a + 1, b), at(a - 1, b)
    far = at(a + 2, b)
    over, under = at(a, b + 1), at(a, b - 1)
    for dest in (up, down, over, under, sibling):
        for which, src in ((0, wa), (1, wb)):
            send(which, src, me, dest)
    arrived(0, down)
    forward(0, down, up)
    arrived(1, up)
    forward(1, up, down)
    arrived(1, down)
    arrived(0, up)
    for c in (down, up):
        for which in (0, 1):
            for dest in (over, under, sibling):
                forward(which, c, dest)
    keep_m.wait()

    def took(d, carry):
        peer = (me + d) % cols
        pltpu.make_async_copy(piece(got, peer), piece(got, peer), a2a_r.at[peer]).wait()
        return carry

    lax.fori_loop(1, cols, took, 0)

    def unpack(s, carry):
        own[s] = got[tab[PICK, s]]
        return carry

    lax.fori_loop(0, own.shape[0], unpack, 0)

    def part(ref, h, r):
        return ref.at[pl.ds(h * half, half), :, cols_of(r)]

    right, left = (row + 1) % rows, (row + rows - 1) % rows
    far_row = (row + 2) % rows
    for k, dest in ((0, right), (1, left)):
        for h in (0, 1):
            pltpu.make_async_remote_copy(
                own.at[pl.ds(h * half, half)], part(hid_full, h, row),
                y_s.at[2 * k + h], y_r.at[row, h],
                device_id=(dest, me), device_id_type=MESH,
            ).start()
    keep_y = pltpu.make_async_copy(own, hid_full.at[:, :, cols_of(row)], loc.at[4])
    keep_y.start()

    for which in (0, 1):
        arrived(which, far)
        for dest in (over, under, sibling):
            forward(which, far, dest)
    for k in (0, 1, -1, 2):
        low, high = at(a + k, b - 1), at(a + k, b + 1)
        arrived(0, low)
        forward(0, low, over)
        arrived(1, high)
        forward(1, high, under)
        arrived(1, low)
        arrived(0, high)
        for which in (0, 1):
            forward(which, low, sibling)
            forward(which, high, sibling)

    def y_here(h, r):
        pltpu.make_async_copy(part(hid_full, h, r), part(hid_full, h, r), y_r.at[r, h]).wait()

    y_here(0, left)
    pltpu.make_async_remote_copy(
        part(hid_full, 0, left), part(hid_full, 0, left), y_s.at[4], y_r.at[left, 0],
        device_id=(right, me), device_id_type=MESH,
    ).start()
    y_here(1, right)
    pltpu.make_async_remote_copy(
        part(hid_full, 1, right), part(hid_full, 1, right), y_s.at[5], y_r.at[right, 1],
        device_id=(left, me), device_id_type=MESH,
    ).start()
    y_here(1, left)
    y_here(0, right)
    for k in (0, 1, -1, 2):
        opposite = at(a + k, b + 2)
        for which in (0, 1):
            arrived(which, opposite)
            forward(which, opposite, sibling)
    y_here(0, far_row)
    y_here(1, far_row)

    def from_sibling(k, carry):
        c = 2 * k + 1 - core
        pltpu.make_async_copy(block(fa, c), block(fa, c), war.at[c]).wait()
        pltpu.make_async_copy(block(fb, c), block(fb, c), wbr.at[c]).wait()
        return carry

    lax.fori_loop(0, cols // 2, from_sibling, 0)
    keep_a.wait()
    keep_b.wait()
    keep_y.wait()

    def a2a_done(d, carry):
        peer = (me + d) % cols
        pltpu.make_async_copy(piece(packed, peer), piece(packed, peer), a2a_s.at[peer]).wait()
        return carry

    lax.fori_loop(1, cols, a2a_done, 0)

    def a_done(k, carry):
        pltpu.make_async_copy(block(fa, me), block(fa, me), was.at[k]).wait()
        return carry

    lax.fori_loop(0, sent[0], a_done, 0)

    def b_done(k, carry):
        pltpu.make_async_copy(block(fb, me), block(fb, me), wbs.at[k]).wait()
        return carry

    lax.fori_loop(0, sent[1], b_done, 0)
    for k in range(6):
        h = (0, 1, 0, 1, 0, 1)[k]
        pltpu.make_async_copy(part(hid_full, h, row), part(hid_full, h, row), y_s.at[k]).wait()


def gather_all(tab, hidden, wa, w_out, w_bc, w_dt, rows, cols, cap, held):
    requests, _, model = hidden.shape
    width = model // rows
    dt = hidden.dtype
    hbm = pl.BlockSpec(memory_space=pltpu.HBM)
    dma = pltpu.SemaphoreType.DMA
    depth = wa.shape[0]
    rest = w_out.shape[1] + w_bc.shape[1] + 128

    def body(*refs):
        gather_kernel(rows, cols, cap, *refs)

    return pl.pallas_call(
        body,
        out_shape=(
            jax.ShapeDtypeStruct((held, LEN, model), dt),
            jax.ShapeDtypeStruct((depth * cols, wa.shape[1]), dt),
            jax.ShapeDtypeStruct((depth * cols, rest), dt),
        ),
        in_specs=[hbm] * 6,
        out_specs=(hbm, hbm, hbm),
        scratch_shapes=[
            pltpu.SMEM(tab.shape, jnp.int32),
            pltpu.VMEM(w_dt.shape, dt),
            pltpu.VMEM((depth, rest), dt),
            pltpu.VMEM((requests, LEN, width), dt),
            pltpu.VMEM((cols * cap, LEN, width), dt),
            pltpu.VMEM((cols * cap, LEN, width), dt),
            pltpu.VMEM((held, LEN, width), dt),
            dma((9,)), dma((cols,)), dma((cols,)),
            dma((48,)), dma((48,)), dma((cols,)), dma((cols,)),
            dma((6,)), dma((rows, 2)),
        ],
        compiler_params=pltpu.CompilerParams(
            collective_id=0, has_side_effects=True, vmem_limit_bytes=60 << 20
        ),
        name="gather_all",
    )(tab, hidden, wa, w_out, w_bc, w_dt)


def return_kernel(
    rows, cols, cap, tab_in, gg_in, ss_from, fb, xmsg, emsg, mixed, xgot, egot,
    tab, gg, wo, ss, part, came, ss_in, scale, mix0, mix1, mix2, packed, got0, got1, got2,
    ld, loc, ss_s, ss_r, y_s, y_r, a2a_s, a2a_r, x_s, x_r, e_s, e_r,
):
    row, me = lax.axis_index("row"), lax.axis_index("col")
    barrier = greet(row, me, rows, cols)
    pieces = part.shape[0] // rows
    tokens = part.shape[1]
    inner = gg.shape[1]
    width = pieces * 128
    loads = (
        pltpu.make_async_copy(gg_in, gg, ld.at[0]),
        pltpu.make_async_copy(fb.at[:, pl.ds(0, inner)], wo, ld.at[1]),
        pltpu.make_async_copy(ss_from, ss, ld.at[2]),
        pltpu.make_async_copy(tab_in, tab, ld.at[3]),
    )
    for copy in loads:
        copy.start()
    for copy in loads:
        copy.wait()
    order = (1, 3, 2)

    def block(peer, j, count):
        at = pl.ds(pl.multiple_of(peer * width + j * 128, 128), count * 128)
        out = lax.dot_general(
            gg[...], wo[at, :], (((1,), (1,)), ((), ())), preferred_element_type=jnp.float32
        ).astype(part.dtype)
        for k in range(count):
            part[peer * pieces + j + k] = out[:, k * 128 : (k + 1) * 128]

    def send_block(peer, j, d):
        pltpu.make_async_remote_copy(
            part.at[peer * pieces + j], came.at[row, j], y_s.at[j, d], y_r.at[row, j],
            device_id=(peer, me), device_id_type=MESH,
        ).start()

    def first(d, carry):
        peer = (row + d) % rows
        block(peer, 0, 1)
        send_block(peer, 0, d)
        return carry

    def later(d, carry):
        peer = (row + d) % rows
        block(peer, 1, pieces - 1)
        for j in range(1, pieces):
            send_block(peer, j, d)
        return carry

    def piece(ref, c):
        return ref.at[pl.ds(c * cap, cap)]

    pl.semaphore_wait(barrier, cols - 1 + rows - 1)
    for k, d in enumerate(order):
        pltpu.make_async_remote_copy(
            ss, ss_in.at[row], ss_s.at[k], ss_r.at[row],
            device_id=((row + d) % rows, me), device_id_type=MESH,
        ).start()
    lax.fori_loop(1, rows, first, 0)
    def push_factors(d, carry):
        peer = (me + d) % cols
        for src, dst, ss_, rs_ in ((xmsg, xgot, x_s, x_r), (emsg, egot, e_s, e_r)):
            pltpu.make_async_remote_copy(
                piece(src, peer), piece(dst, me), ss_.at[peer], rs_.at[me],
                device_id=(row, peer), device_id_type=MESH,
            ).start()
        return carry

    lax.fori_loop(1, cols, push_factors, 0)
    keep_x = pltpu.make_async_copy(piece(xmsg, me), piece(xgot, me), loc.at[4])
    keep_e = pltpu.make_async_copy(piece(emsg, me), piece(egot, me), loc.at[5])
    keep_x.start()
    keep_e.start()
    lax.fori_loop(1, rows, later, 0)
    block(row, 0, 1)
    block(row, 1, pieces - 1)
    total = ss[...]
    for d in order:
        peer = (row + d) % rows
        pltpu.make_async_copy(ss_in.at[peer], ss_in.at[peer], ss_r.at[peer]).wait()
        total = total + ss_in[peer]
    factor = lax.rsqrt(total / INNER + 1e-05)
    for i in range(tokens // TOK):
        line = jnp.broadcast_to(factor[i : i + 1, :], (TOK, TOK))
        scale[pl.ds(i * TOK, TOK), :] = line.T
    gots = (got0, got1, got2)

    mixes = (mix0, mix1, mix2)
    for j in range(pieces):
        mix = mixes[j]
        for d in order:
            peer = (row + d) % rows
            pltpu.make_async_copy(came.at[peer, j], came.at[peer, j], y_r.at[peer, j]).wait()

        def add(i, carry):
            at = pl.ds(pl.multiple_of(i * TOK, TOK), TOK)
            value = part[row * pieces + j, at, :].astype(jnp.float32)
            for d in order:
                value = value + came[(row + d) % rows, j, at, :].astype(jnp.float32)
            value = (value * scale[at, :]).astype(mix.dtype)
            mix[pl.ds(i * GROUP, GROUP)] = value.reshape(GROUP, LEN, 128)
            return carry

        lax.fori_loop(0, tokens // TOK, add, 0)

        def pack(s, carry):
            packed[j, s] = mix[tab[BACK, s]]
            return carry

        lax.fori_loop(0, cols * cap, pack, 0)

        def push(d, carry):
            peer = (me + d) % cols
            pltpu.make_async_remote_copy(
                piece(packed.at[j], peer), piece(gots[j], me), a2a_s.at[j, peer], a2a_r.at[j, me],
                device_id=(row, peer), device_id_type=MESH,
            ).start()
            return carry

        lax.fori_loop(1, cols, push, 0)
        pltpu.make_async_copy(piece(packed.at[j], me), piece(gots[j], me), loc.at[1 + j]).start()
    for j in range(pieces):
        got, mix = gots[j], mixes[j]
        pltpu.make_async_copy(piece(packed.at[j], me), piece(got, me), loc.at[1 + j]).wait()

        def took(d, carry):
            peer = (me + d) % cols
            pltpu.make_async_copy(piece(got, peer), piece(got, peer), a2a_r.at[j, peer]).wait()
            return carry

        lax.fori_loop(1, cols, took, 0)

        def unpack(s, carry):
            moved = tab[MOVED, s].astype(jnp.float32)
            away = got[tab[FROM_MSG, s]].astype(jnp.float32)
            here = mix[tab[FROM_MIX, s]].astype(jnp.float32)
            value = jnp.where(moved > 0.5, away, here)
            mixed[s, :, j * 128 : (j + 1) * 128] = value.astype(mixed.dtype)
            return carry

        lax.fori_loop(0, mixed.shape[0], unpack, 0)
    for k in range(3):
        pltpu.make_async_copy(ss, ss, ss_s.at[k]).wait()
        for j in range(pieces):
            pltpu.make_async_copy(part.at[j], part.at[j], y_s.at[j, k + 1]).wait()
    for j in range(pieces):

        def gone(d, carry):
            peer = (me + d) % cols
            pltpu.make_async_copy(
                piece(packed.at[j], peer), piece(packed.at[j], peer), a2a_s.at[j, peer]
            ).wait()
            return carry

        lax.fori_loop(1, cols, gone, 0)


    keep_x.wait()
    keep_e.wait()

    def factors(d, carry):
        peer = (me + d) % cols
        for ref, ss_, rs_ in ((xgot, x_s, x_r), (egot, e_s, e_r)):
            pltpu.make_async_copy(piece(ref, peer), piece(ref, peer), rs_.at[peer]).wait()
            pltpu.make_async_copy(piece(ref, peer), piece(ref, peer), ss_.at[peer]).wait()
        return carry

    lax.fori_loop(1, cols, factors, 0)


def send_home(tab, gg, ss, fb, xmsg, emsg, rows, cols, cap):
    blocks = fb.shape[0] // 128
    pieces = blocks // rows
    tokens, inner = gg.shape
    hbm = pl.BlockSpec(memory_space=pltpu.HBM)
    vmem = pl.BlockSpec(memory_space=pltpu.VMEM)
    dma = pltpu.SemaphoreType.DMA
    slots = cols * cap
    requests = tokens // LEN
    dt = gg.dtype

    def body(*refs):
        return_kernel(rows, cols, cap, *refs)

    mix = pltpu.VMEM((requests, LEN, 128), dt)
    got = pltpu.VMEM((slots, LEN, 128), dt)
    return pl.pallas_call(
        body,
        out_shape=(
            jax.ShapeDtypeStruct((requests, LEN, pieces * 128), dt),
            jax.ShapeDtypeStruct(xmsg.shape, dt),
            jax.ShapeDtypeStruct(emsg.shape, dt),
        ),
        in_specs=[hbm] * 6,
        out_specs=(vmem, hbm, hbm),
        scratch_shapes=[
            pltpu.SMEM(tab.shape, jnp.int32),
            pltpu.VMEM((tokens, inner), dt),
            pltpu.VMEM((fb.shape[0], inner), dt),
            pltpu.VMEM(ss.shape, jnp.float32),
            pltpu.VMEM((blocks, tokens, 128), dt),
            pltpu.VMEM((rows, pieces, tokens, 128), dt),
            pltpu.VMEM((rows,) + ss.shape, jnp.float32),
            pltpu.VMEM((tokens, 128), jnp.float32),
            mix, mix, mix,
            pltpu.VMEM((pieces, slots, LEN, 128), dt),
            got, got, got,
            dma((4,)), dma((3 + pieces,)), dma((3,)), dma((rows,)),
            dma((pieces, rows)), dma((rows, pieces)), dma((pieces, cols)), dma((pieces, cols)),
            dma((cols,)), dma((cols,)), dma((cols,)), dma((cols,)),
        ],
        compiler_params=pltpu.CompilerParams(
            collective_id=1, has_side_effects=True, vmem_limit_bytes=60 << 20
        ),
        name="send_home",
    )(tab, gg, ss, fb, xmsg, emsg)


def silu(v):
    return v / (1.0 + jnp.exp(-v))


def token_masks():
    t_ids = lax.broadcasted_iota(jnp.int32, (TOK, TOK), 0)
    s_ids = lax.broadcasted_iota(jnp.int32, (TOK, TOK), 1)
    return t_ids, s_ids


def mixer_kernel(
    held, tab_in, hid_c, hidden, fa, fb, *refs,
):
    sources, refs = refs[:8], refs[8:]
    prev, pex_in, peb_in, gg, ss, xmsg, emsg, nst, nex, neb, tab, *refs = refs
    params, refs = refs[:8], refs[8:]
    dtb, alog, skip, cxw, cxb, cbw, cbb, gain = params
    (
        pex, peb, hid, wa, wb, old, gate, xin, bc, dts, cx, cb, pexf, pebf, new,
        h_sem, o_sem, w_sem, n_sem, v_sem,
    ) = refs
    f32, bf16 = jnp.float32, jnp.bfloat16
    inner = gain.shape[1]
    requests = hid.shape[0]
    tokens = requests * LEN
    model = hid.shape[2]
    heads = inner // HEAD_DIM
    blocks = wa.shape[1] // 256

    load_h = pltpu.make_async_copy(hid_c, hid.at[pl.ds(0, held)], h_sem)
    load_h.start()
    small = list(zip(sources + (pex_in, peb_in, tab_in), list(params) + [pex, peb, tab]))
    small = [pltpu.make_async_copy(a, b, v_sem.at[k]) for k, (a, b) in enumerate(small)]
    small[-1].start()
    for copy in small[:-1]:
        copy.start()
    small[-1].wait()

    def wa_load(n):
        at = pl.ds(n * 256, 256)
        return pltpu.make_async_copy(fa.at[:, at], wa.at[:, at], w_sem.at[n])

    wa_load(0).start()

    def home(n):
        return pltpu.make_async_copy(hidden.at[tab[STAY, n]], hid.at[held + n], o_sem.at[n])

    @pl.loop(0, requests - held)
    def _(n):
        home(n).start()

    for n in range(1, blocks):
        wa_load(n).start()
    late = pl.ds(inner, wb.shape[1])
    load_bc = pltpu.make_async_copy(fb.at[:, late], wb, w_sem.at[blocks])
    load_old = pltpu.make_async_copy(prev, old, w_sem.at[blocks + 1])
    load_bc.start()
    load_old.start()
    for copy in small[:-1]:
        copy.wait()
    pexf[...] = pex[...].astype(f32)
    pebf[...] = peb[...].astype(f32)

    t_ids, s_ids = token_masks()
    same = (t_ids // LEN) == (s_ids // LEN)
    causal = same & (t_ids >= s_ids)
    tri = causal.astype(f32)
    spread_h = (
        lax.broadcasted_iota(jnp.int32, (TOK, inner), 1) // HEAD_DIM
        == lax.broadcasted_iota(jnp.int32, (TOK, inner), 0)
    ).astype(f32)

    def wide(ref):
        return jnp.concatenate([ref[...], jnp.zeros((1, TOK - heads), f32)], axis=1)

    bias, rate = wide(dtb), -jnp.exp(wide(alog))
    skip_x = jnp.dot(
        jnp.broadcast_to(wide(skip), (8, TOK)), spread_h,
        precision=HIGHEST, preferred_element_type=f32,
    )[0:1, :]

    load_h.wait()

    @pl.loop(0, requests - held)
    def _(n):
        home(n).wait()

    left = lax.broadcasted_iota(jnp.int32, (tokens, 128), 1) < HEAD_DIM
    for n in range(blocks):
        wa_load(n).wait()
        z = jnp.dot(
            hid[...].reshape(tokens, model), wa[:, n * 256 : (n + 1) * 256],
            preferred_element_type=f32,
        )
        z0, z1 = z[:, :128], z[:, 128:]
        at = slice(n * 128, (n + 1) * 128)
        gate[:, at] = jnp.where(left, z0, pltpu.roll(z1, HEAD_DIM, 1)).astype(bf16)
        xin[:, at] = jnp.where(left, pltpu.roll(z0, HEAD_DIM, 1), z1).astype(bf16)
    load_bc.wait()
    z = jnp.dot(hid[...].reshape(tokens, model), wb[...], preferred_element_type=f32)
    bc[...] = z[:, : 2 * STATE].astype(bf16)
    dts[...] = z[:, 2 * STATE :]
    load_old.wait()

    def store(s):
        return pltpu.make_async_copy(new.at[s], nst.at[tab[POS, s]], n_sem.at[s])

    def group(i, live):
        at = pl.ds(pl.multiple_of(i * TOK, TOK), TOK)
        first = i * GROUP
        last = jnp.zeros((TOK, TOK), jnp.int32)
        accs = []
        for r in range(GROUP):
            acc = tab[ACC, first + r] if live else tab[STAY_ACC, first - held + r]
            accs.append(acc)
            last = jnp.where(t_ids // LEN == r, acc, last)
            if live:
                for k in range(KCONV - 1):
                    cx[r, 13 + k : 14 + k, :] = pexf[k, pl.ds(first + r, 1), :]
                    cb[r, 13 + k : 14 + k, :] = pebf[k, pl.ds(first + r, 1), :]
        if not live:
            cx[:, 8:16, :] = jnp.zeros((GROUP, 8, inner), f32)
            cb[:, 8:16, :] = jnp.zeros((GROUP, 8, 2 * STATE), f32)
        cx[:, 16:32, :] = xin[at, :].astype(f32).reshape(GROUP, LEN, inner)
        cb[:, 16:32, :] = bc[at, :].astype(f32).reshape(GROUP, LEN, 2 * STATE)
        tot_x = cxb[...].reshape(1, 1, inner) + cxw[0:1, :].reshape(1, 1, inner) * cx[:, 13:29, :]
        tot_b = cbb[...].reshape(1, 1, 2 * STATE) + cbw[0:1, :].reshape(
            1, 1, 2 * STATE
        ) * cb[:, 13:29, :]
        for k in range(1, KCONV):
            tot_x = tot_x + cxw[k : k + 1, :].reshape(1, 1, inner) * cx[:, 13 + k : 29 + k, :]
            tot_b = tot_b + cbw[k : k + 1, :].reshape(1, 1, 2 * STATE) * cb[:, 13 + k : 29 + k, :]
        xc = silu(tot_x).reshape(TOK, inner).astype(bf16)
        bcc = silu(tot_b).reshape(TOK, 2 * STATE).astype(bf16)
        for r in range(GROUP):
            ex = pltpu.roll(cx[r], 19 - accs[r], 0)
            eb = pltpu.roll(cb[r], 19 - accs[r], 0)
            if live:
                place = tab[POS, first + r]
                for k in range(KCONV - 1):
                    nex[k, pl.ds(place, 1), :] = ex[k : k + 1, :]
                    neb[k, pl.ds(place, 1), :] = eb[k : k + 1, :]
            else:
                lines = []
                for k in range(KCONV - 1):
                    lines.append(ex[k : k + 1, :384])
                    lines.append(jnp.concatenate([ex[k : k + 1, 384:], eb[k : k + 1, :]], axis=1))
                lines.append(jnp.zeros((2, 384), f32))
                emsg[tab[STAY_KEY, first - held + r]] = jnp.concatenate(lines, axis=0).astype(bf16)
        b_in, c_in = bcc[:, :STATE], bcc[:, STATE:]
        xf = xc.astype(f32)
        raw = dts[at, :] + bias
        step = jnp.maximum(raw, 0.0) + jnp.log(1.0 + jnp.exp(-jnp.abs(raw)))
        decay = jnp.dot(tri, step * rate, precision=HIGHEST, preferred_element_type=f32)
        decay_t = decay.T
        step_t = step.T
        choose = (same & (s_ids % LEN == last - 1)).astype(f32)
        reach = jnp.dot(choose, decay, precision=HIGHEST, preferred_element_type=f32)
        taken = t_ids % LEN < last
        weight = jnp.where(taken, jnp.exp(jnp.minimum(reach - decay, 0.0)), 0.0) * step
        weight_x = jnp.dot(weight, spread_h, precision=HIGHEST, preferred_element_type=f32)
        scores = lax.dot_general(
            c_in, b_in, (((1,), (1,)), ((), ())), preferred_element_type=f32
        )
        scores = jnp.where(causal, scores, 0.0)
        half = s_ids < HEAD_DIM
        zero = jnp.zeros((TOK, 2 * HEAD_DIM), bf16)
        y = []
        for pair in range(heads // 2):
            mats = []
            for h in (2 * pair, 2 * pair + 1):
                gap = decay[:, h : h + 1] - decay_t[h : h + 1, :]
                mats.append(
                    (jnp.exp(jnp.minimum(gap, 0.0)) * scores * step_t[h : h + 1, :]).astype(bf16)
                )
            xp = xc[:, pair * 128 : (pair + 1) * 128]
            both = jnp.concatenate([jnp.where(half, xp, zero), jnp.where(half, zero, xp)], axis=0)
            y.append(
                jnp.dot(jnp.concatenate(mats, axis=1), both, preferred_element_type=f32)
            )
        y = jnp.concatenate(y, axis=1)
        if live:
            grow_x = jnp.dot(jnp.exp(decay), spread_h, precision=HIGHEST, preferred_element_type=f32)
            carried = [
                lax.dot_general(
                    c_in[r * LEN : (r + 1) * LEN, :], old[first + r], (((1,), (1,)), ((), ())),
                    preferred_element_type=f32,
                )
                for r in range(GROUP)
            ]
            y = y + grow_x * jnp.concatenate(carried, axis=0)
        y = y + skip_x * xf
        gated = y * silu(gate[at, :].astype(f32))
        gg[at, :] = (gated * gain[...]).astype(bf16)
        squares = jnp.sum(gated * gated, axis=1, keepdims=True)
        ss[pl.ds(i, 1), :] = jnp.broadcast_to(squares, (TOK, TOK)).T[0:1, :]

        if not live:
            sent = (xf * weight_x).astype(bf16)
            for r in range(GROUP):
                key = tab[STAY_KEY, first - held + r]
                lines = slice(r * LEN, (r + 1) * LEN)
                xmsg[key, :, :inner] = sent[lines, :]
                xmsg[key, :, inner:] = b_in[lines, :]
            return
        xw = (xf * weight_x).T
        high = xw.astype(bf16)
        low = (xw - high.astype(f32)).astype(bf16)
        lhs = jnp.concatenate([high, low], axis=1)
        keep_t = jnp.exp(reach).T
        none = jnp.zeros((TOK, STATE), bf16)
        for pair in range(GROUP // 2):
            cut = jnp.concatenate(
                [
                    jnp.where(t_ids // LEN == r, b_in, none)
                    for r in (2 * pair, 2 * pair + 1)
                ],
                axis=1,
            )
            added = jnp.dot(
                lhs, jnp.concatenate([cut, cut], axis=0), preferred_element_type=f32
            )
            for k in (0, 1):
                r = 2 * pair + k
                s = first + r
                factor = jnp.broadcast_to(keep_t[0:heads, r * LEN : r * LEN + 1], (heads, STATE))
                was = old[s].astype(f32).reshape(heads, HEAD_DIM, STATE)
                now = factor[:, None, :] * was + added[:, k * STATE : (k + 1) * STATE].reshape(
                    heads, HEAD_DIM, STATE
                )
                new[s] = now.reshape(inner, STATE).astype(bf16)
                store(s).start()

    @pl.loop(0, held // GROUP)
    def _(i):
        group(i, True)

    @pl.loop(held // GROUP, requests // GROUP)
    def _(i):
        group(i, False)

    @pl.loop(0, held)
    def _(s):
        store(s).wait()


def mixer(tab, hid_c, hidden, fa, fb, vectors, prev, pex, peb, slots):
    requests, _, model = hidden.shape
    held = hid_c.shape[0]
    tokens = requests * LEN
    inner = fa.shape[1] // 2
    heads = inner // HEAD_DIM
    dt = hidden.dtype
    f32 = jnp.float32
    vmem = pl.BlockSpec(memory_space=pltpu.VMEM)
    hbm = pl.BlockSpec(memory_space=pltpu.HBM)
    dma = pltpu.SemaphoreType.DMA

    def body(*refs):
        mixer_kernel(held, *refs)

    return pl.pallas_call(
        body,
        out_shape=(
            jax.ShapeDtypeStruct((tokens, inner), dt),
            jax.ShapeDtypeStruct((8, 128), f32),
            jax.ShapeDtypeStruct((slots, LEN, inner + STATE), dt),
            jax.ShapeDtypeStruct((slots, 8, 384), dt),
            jax.ShapeDtypeStruct((requests, inner, STATE), dt),
            jax.ShapeDtypeStruct((3, requests, inner), f32),
            jax.ShapeDtypeStruct((3, requests, 2 * STATE), f32),
        ),
        in_specs=[hbm] * (8 + len(vectors)),
        out_specs=(vmem, vmem, vmem, vmem, hbm, vmem, vmem),
        scratch_shapes=[
            pltpu.SMEM(tab.shape, jnp.int32),
            *[pltpu.VMEM(v.shape, v.dtype) for v in vectors],
            pltpu.VMEM(pex.shape, dt),
            pltpu.VMEM(peb.shape, dt),
            pltpu.VMEM((requests, LEN, model), dt),
            pltpu.VMEM(fa.shape, dt),
            pltpu.VMEM((fb.shape[0], fb.shape[1] - inner), dt),
            pltpu.VMEM((held, inner, STATE), dt),
            pltpu.VMEM((tokens, inner), dt),
            pltpu.VMEM((tokens, inner), dt),
            pltpu.VMEM((tokens, 2 * STATE), dt),
            pltpu.VMEM((tokens, 128), f32),
            pltpu.VMEM((GROUP, 32, inner), f32),
            pltpu.VMEM((GROUP, 32, 2 * STATE), f32),
            pltpu.VMEM((3, held, inner), f32),
            pltpu.VMEM((3, held, 2 * STATE), f32),
            pltpu.VMEM((held, inner, STATE), dt),
            dma(()), dma((requests - held,)), dma((fa.shape[1] // 256 + 2,)), dma((held,)),
            dma((len(vectors) + 3,)),
        ],
        compiler_params=pltpu.CompilerParams(vmem_limit_bytes=60 << 20),
        name="mixer",
    )(tab, hid_c, hidden, fa, fb, *vectors, prev, pex, peb)


def arrive_kernel(
    tab_in, xgot_in, egot_in, exf, ebf, nst_in, nst, nex, neb,
    tab, xgot, egot, xs, bs, ex, eb, new, n_sem, l_sem,
):
    f32, bf16 = jnp.float32, jnp.bfloat16
    count, inner = new.shape[0], new.shape[1]
    loads = [
        pltpu.make_async_copy(a, b, l_sem.at[k])
        for k, (a, b) in enumerate(
            ((tab_in, tab), (xgot_in, xgot), (egot_in, egot), (exf, ex), (ebf, eb))
        )
    ]
    for copy in loads:
        copy.start()
    loads[0].wait()
    loads[1].wait()
    t_ids, _ = token_masks()
    none = jnp.zeros((TOK, STATE), bf16)

    def store(u):
        return pltpu.make_async_copy(new.at[u], nst.at[tab[POS_O, u]], n_sem.at[u])

    @pl.loop(0, count // GROUP)
    def _(i):
        for r in range(GROUP):
            slot = tab[PICK_O, i * GROUP + r]
            xs[r] = xgot[slot, :, :inner]
            bs[r] = xgot[slot, :, inner:]
        lhs = xs[...].reshape(TOK, inner).astype(f32).T.astype(bf16)
        b_in = bs[...].reshape(TOK, STATE)
        for pair in range(GROUP // 2):
            cut = jnp.concatenate(
                [
                    jnp.where(t_ids // LEN == r, b_in, none)
                    for r in (2 * pair, 2 * pair + 1)
                ],
                axis=1,
            )
            out = jnp.dot(lhs, cut, preferred_element_type=f32).astype(bf16)
            for k in (0, 1):
                u = i * GROUP + 2 * pair + k
                new[u] = out[:, k * STATE : (k + 1) * STATE]
                store(u).start()

    for copy in loads[2:]:
        copy.wait()

    @pl.loop(0, count)
    def _(u):
        lines = egot[tab[PICK_O, u]].astype(f32)
        at = pl.ds(tab[POS_O, u], 1)
        for k in range(KCONV - 1):
            ex[k, at, :] = jnp.concatenate(
                [lines[2 * k : 2 * k + 1, :], lines[2 * k + 1 : 2 * k + 2, :128]], axis=1
            )
            eb[k, at, :] = lines[2 * k + 1 : 2 * k + 2, 128:]

    nex[...] = ex[...].astype(bf16)
    neb[...] = eb[...].astype(bf16)

    @pl.loop(0, count)
    def _(u):
        store(u).wait()


def arrive(tab, xgot, egot, exf, ebf, nst):
    requests, inner, _ = nst.shape
    count = requests // 2
    dt, f32 = nst.dtype, jnp.float32
    vmem = pl.BlockSpec(memory_space=pltpu.VMEM)
    hbm = pl.BlockSpec(memory_space=pltpu.HBM)
    return pl.pallas_call(
        arrive_kernel,
        out_shape=(
            jax.ShapeDtypeStruct(nst.shape, dt),
            jax.ShapeDtypeStruct(exf.shape, dt),
            jax.ShapeDtypeStruct(ebf.shape, dt),
        ),
        in_specs=[hbm] * 6,
        out_specs=(hbm, vmem, vmem),
        scratch_shapes=[
            pltpu.SMEM(tab.shape, jnp.int32),
            pltpu.VMEM(xgot.shape, dt),
            pltpu.VMEM(egot.shape, dt),
            pltpu.VMEM((GROUP, LEN, inner), dt),
            pltpu.VMEM((GROUP, LEN, STATE), dt),
            pltpu.VMEM(exf.shape, f32),
            pltpu.VMEM(ebf.shape, f32),
            pltpu.VMEM((count, inner, STATE), dt),
            pltpu.SemaphoreType.DMA((count,)),
            pltpu.SemaphoreType.DMA((5,)),
        ],
        input_output_aliases={5: 0},
        compiler_params=pltpu.CompilerParams(vmem_limit_bytes=60 << 20),
        name="arrive",
    )(tab, xgot, egot, exf, ebf, nst)


def per_device(
    hidden, w_zx, w_bc, w_dt, w_out, dt_bias, a_log, d_skip, conv_x_w, conv_x_b,
    conv_bc_w, conv_bc_b, norm_gain, prev_state, prev_edge_x, prev_edge_bc,
    holder, continued, owner, accepted,
):
    rows, cols = lax.axis_size("row"), lax.axis_size("col")
    tokens, model = hidden.shape
    requests = tokens // LEN
    heads = dt_bias.shape[0]
    inner = heads * HEAD_DIM
    held = prev_state.shape[0]
    cap = 2 * ((requests // 4 + cols - 1) // cols)
    code = owner + 64 * (continued == 1).astype(jnp.int32) + 128 * accepted
    tab = route(code.reshape(cols, requests), held)
    hidden = hidden.reshape(requests, LEN, model)
    hid_c, fa, fb = gather_all(tab, hidden, w_zx, w_out, w_bc, w_dt.T, rows, cols, cap, held)
    vectors = (
        dt_bias[None, :], a_log[None, :], d_skip[None, :],
        conv_x_w, conv_x_b[None, :], conv_bc_w, conv_bc_b[None, :], norm_gain[None, :],
    )
    gg, ss, xmsg, emsg, states, exf, ebf = mixer(
        tab, hid_c, hidden, fa, fb, vectors, prev_state.reshape(held, inner, STATE),
        prev_edge_x.transpose(1, 0, 2), prev_edge_bc.transpose(1, 0, 2), cols * cap,
    )
    mixed, xgot, egot = send_home(tab, gg, ss, fb, xmsg, emsg, rows, cols, cap)
    states, new_x, new_bc = arrive(tab, xgot, egot, exf, ebf, states)
    return (
        mixed.reshape(tokens, model // rows),
        states.reshape(requests, heads, HEAD_DIM, STATE),
        new_x.transpose(1, 0, 2),
        new_bc.transpose(1, 0, 2),
    )


def solution(mesh):
    return jax.shard_map(
        per_device,
        mesh=mesh,
        in_specs=(
            P("col", None),
            P("col", "row"),
            P("col", None),
            P("col", "row"),
            P("col", "row"),
            P("row"),
            P("row"),
            P("row"),
            P(None, "row"),
            P("row"),
            P(),
            P(),
            P("row"),
            P("col", "row", None, None),
            P("col", None, "row"),
            P("col", None, None),
            P(),
            P(),
            P(),
            P(),
        ),
        out_specs=(
            P("col", "row"),
            P("col", "row", None, None),
            P("col", None, "row"),
            P("col", None, None),
        ),
        check_vma=False,
    )
```

```python
import jax
import jax.numpy as jnp
from jax import lax
from jax.experimental import pallas as pl
from jax.experimental.pallas import tpu as pltpu
from jax.sharding import PartitionSpec as P

HEAD_DIM = 64
STATE = 128
KCONV = 4
LEN = 16
INNER = 2048
SIDE = 4
GROUP = 8
TOK = GROUP * LEN
MESH = pl.DeviceIdType.MESH
HIGHEST = lax.Precision.HIGHEST


def route_kernel(held, code, out):
    f32, bf16 = jnp.float32, jnp.bfloat16
    me = lax.axis_index("col")
    groups, requests = code.shape
    value = code[...]
    o, c, a = value & 63, (value >> 6) & 1, value >> 7

    def dot(x, y):
        return jnp.dot(x.astype(bf16), y.astype(bf16), preferred_element_type=f32)

    def dot0(x, y):
        return lax.dot_general(
            x.astype(bf16), y.astype(bf16), (((0,), (0,)), ((), ())), preferred_element_type=f32
        )

    def ids(shape, dim):
        return lax.broadcasted_iota(jnp.int32, shape, dim)

    below = (ids((requests, requests), 0) < ids((requests, requests), 1)).astype(f32)
    prior = (ids((groups, groups), 1) < ids((groups, groups), 0)).astype(f32)
    lane = ids((groups, 128), 1).astype(f32)
    group = ids((groups, 128), 0).astype(f32)
    spots, inside, starts = [], [], []
    for kind in (1, 0):
        mask = ((o == me) & (c == kind)).astype(f32)
        rank = dot(mask, below)
        count = jnp.broadcast_to(jnp.sum(mask, axis=1, keepdims=True), (groups, 128))
        start = dot(prior, count)
        hot = ((start <= lane) & (lane < start + count)).astype(f32)
        spots.append((jnp.where(mask > 0, rank, -1.0), hot))
        inside.append(rank)
        starts.append(start)
    rank_all, start_all = inside[0] + inside[1], starts[0] + starts[1]
    picks, places, taken = [], [], []
    for k in (0, 1):
        spot, hot = spots[k]
        order = jnp.sum(hot * (lane - starts[k]), axis=0, keepdims=True)
        any_hot = jnp.sum(hot, axis=0, keepdims=True)
        order = jnp.where(any_hot > 0, order, -5.0)
        match = (dot0(spot, hot) == order).astype(f32)
        picks.append(jnp.sum(hot * (2 * group + lane - starts[k]), axis=0, keepdims=True))
        places.append(
            jnp.sum(hot * start_all, axis=0, keepdims=True)
            + jnp.sum(match * dot0(rank_all, hot), axis=0, keepdims=True)
        )
        taken.append(jnp.sum(match * dot0(a, hot), axis=0, keepdims=True))
    lane_i, group_i = ids((groups, 128), 1), ids((groups, 128), 0)
    back = jnp.sum(
        jnp.where(lane_i // 2 == group_i, starts[0] + (lane_i % 2).astype(f32), 0.0),
        axis=0, keepdims=True,
    )
    back = jnp.minimum(back, held - 1.0)

    def my_row(x, fill):
        row = jnp.sum(
            jnp.where(ids((groups, requests), 0) == me, x, 0).astype(f32), axis=0, keepdims=True
        )
        rest = jnp.full((1, 128 - requests), fill, f32)
        return jnp.concatenate([row, rest], axis=1)

    o_row, c_row, a_row = my_row(o, 99.0), my_row(c, 2.0), my_row(a, 0.0)

    def column(row):
        return jnp.broadcast_to(row, (128, 128)).T

    o_col, c_col, a_col = column(o_row), column(c_row), column(a_row)
    ii, jj = ids((128, 128), 0), ids((128, 128), 1)
    alike = (o_col == o_row) & (c_col == c_row)
    rank_row = jnp.sum((alike & (ii < jj)).astype(f32), axis=0, keepdims=True)
    rank_col = jnp.sum((alike & (jj < ii)).astype(f32), axis=1, keepdims=True)
    nth_row = jnp.sum(((c_col == 0) & (ii < jj)).astype(f32), axis=0, keepdims=True)
    nth_col = jnp.sum(((c_row == 0) & (jj < ii)).astype(f32), axis=1, keepdims=True)
    key_row = 2 * o_row + rank_row
    key_col = 2 * o_col + rank_col
    fi, fj = ii.astype(f32), jj.astype(f32)
    goes = (c_col == 1) & (key_col == fj)
    leaves = (c_col == 0) & (key_col == fj)
    stays = (c_col == 0) & (nth_col == fj)

    def total(mask, x):
        return jnp.sum(jnp.where(mask, x, 0.0), axis=0, keepdims=True)

    table = (
        total(goes, fi), picks[0], back,
        jnp.where(c_row == 1, key_row, 0.0), jnp.where(c_row == 0, nth_row, 0.0),
        (c_row == 1).astype(f32),
        total(stays, fi), total(stays, key_col), total(stays, a_col),
        taken[0], places[0], picks[1], places[1], total(leaves, nth_col),
    )
    for k, line in enumerate(table):
        out[k : k + 1, :] = line.astype(jnp.int32)
    out[len(table) :, :] = jnp.zeros((16 - len(table), 128), jnp.int32)


SEND, PICK, BACK, FROM_MSG, FROM_MIX, MOVED, STAY, STAY_KEY, STAY_ACC, ACC, POS, PICK_O, POS_O, LEAVE = range(14)


def route(code, held):
    vmem = pl.BlockSpec(memory_space=pltpu.VMEM)

    def body(*refs):
        route_kernel(held, *refs)

    return pl.pallas_call(
        body, out_shape=jax.ShapeDtypeStruct((16, 128), jnp.int32),
        in_specs=[vmem], out_specs=vmem, name="route",
        compiler_params=pltpu.CompilerParams(vmem_limit_bytes=60 << 20),
    )(code)


def greet(row, me, rows, cols):
    barrier = pltpu.get_barrier_semaphore()

    def along_col(d, carry):
        pl.semaphore_signal(
            barrier, inc=1, device_id=(row, (me + d) % cols), device_id_type=MESH
        )
        return carry

    lax.fori_loop(1, cols, along_col, 0)

    def along_row(d, carry):
        pl.semaphore_signal(
            barrier, inc=1, device_id=((row + d) % rows, me), device_id_type=MESH
        )
        return carry

    lax.fori_loop(1, rows, along_row, 0)
    return barrier


def gather_kernel(
    rows, cols, cap, tab_in, hidden, wa, w_out, w_bc, w_dt_in, hid_full, fa, fb,
    tab, w_dt, wb, sl, packed, got, own, loc, a2a_s, a2a_r, was, wbs, war, wbr, y_s, y_r,
):
    row, me = lax.axis_index("row"), lax.axis_index("col")
    barrier = greet(row, me, rows, cols)
    width = sl.shape[2]
    half = own.shape[0] // 2
    depth = wa.shape[0]

    def cols_of(r):
        return pl.ds(pl.multiple_of(r * width, 128), width)

    def block(ref, c):
        return ref.at[pl.ds(pl.multiple_of(c * depth, 16), depth), :]

    load = pltpu.make_async_copy(hidden.at[:, :, cols_of(row)], sl, loc.at[0])
    load.start()
    inner = w_out.shape[1]
    states = w_bc.shape[1]
    heads = w_dt_in.shape[0]
    loads = (
        pltpu.make_async_copy(tab_in, tab, loc.at[5]),
        pltpu.make_async_copy(w_dt_in, w_dt, loc.at[6]),
        pltpu.make_async_copy(w_out, wb.at[:, pl.ds(0, inner)], loc.at[7]),
        pltpu.make_async_copy(w_bc, wb.at[:, pl.ds(inner, states)], loc.at[8]),
    )
    for copy in loads:
        copy.start()
    for copy in loads:
        copy.wait()
    square = jnp.concatenate([w_dt[...].astype(jnp.float32), jnp.zeros((heads, 128 - depth), jnp.float32)], axis=1)
    square = jnp.concatenate([square, jnp.zeros((128 - heads, 128), jnp.float32)], axis=0).T
    wb[:, inner + states :] = square[:depth, :].astype(wb.dtype)
    keep_a = pltpu.make_async_copy(wa, block(fa, me), loc.at[1])
    keep_b = pltpu.make_async_copy(wb, block(fb, me), loc.at[2])
    keep_a.start()
    keep_b.start()
    load.wait()

    def pack(s, carry):
        packed[s] = sl[tab[SEND, s]]
        return carry

    lax.fori_loop(0, cols * cap, pack, 0)
    pl.semaphore_wait(barrier, cols - 1 + rows - 1)

    def piece(ref, c):
        return ref.at[pl.ds(c * cap, cap)]

    def push(d, carry):
        peer = (me + d) % cols
        pltpu.make_async_remote_copy(
            piece(packed, peer), piece(got, me), a2a_s.at[peer], a2a_r.at[me],
            device_id=(row, peer), device_id_type=MESH,
        ).start()
        return carry

    lax.fori_loop(1, cols, push, 0)
    keep_m = pltpu.make_async_copy(piece(packed, me), piece(got, me), loc.at[3])
    keep_m.start()

    core = me % 2
    x = (me // 2) % SIDE
    z = me // (2 * SIDE)
    a = x + core * (z - x)
    b = z + core * (x - z)

    def at(pa, pb):
        pa, pb = (pa + SIDE) % SIDE, (pb + SIDE) % SIDE
        px = pa + core * (pb - pa)
        pz = pb + core * (pa - pb)
        return (pz * SIDE + px) * 2 + core

    sibling = me + 1 - 2 * core
    sent = [0, 0]

    def send(which, src, c, dest):
        full, ss, rs = ((fa, was, war), (fb, wbs, wbr))[which]
        k = sent[which]
        sent[which] += 1
        pltpu.make_async_remote_copy(
            src, block(full, c), ss.at[k], rs.at[c],
            device_id=(row, dest), device_id_type=MESH,
        ).start()

    def forward(which, c, dest):
        send(which, block((fa, fb)[which], c), c, dest)

    def arrived(which, c):
        full, rs = ((fa, war), (fb, wbr))[which]
        pltpu.make_async_copy(block(full, c), block(full, c), rs.at[c]).wait()

    up, down = at(a + 1, b), at(a - 1, b)
    far = at(a + 2, b)
    over, under = at(a, b + 1), at(a, b - 1)
    for dest in (up, down, over, under, sibling):
        for which, src in ((0, wa), (1, wb)):
            send(which, src, me, dest)
    arrived(0, down)
    forward(0, down, up)
    arrived(1, up)
    forward(1, up, down)
    arrived(1, down)
    arrived(0, up)
    for c in (down, up):
        for which in (0, 1):
            for dest in (over, under, sibling):
                forward(which, c, dest)
    keep_m.wait()

    def took(d, carry):
        peer = (me + d) % cols
        pltpu.make_async_copy(piece(got, peer), piece(got, peer), a2a_r.at[peer]).wait()
        return carry

    lax.fori_loop(1, cols, took, 0)

    def unpack(s, carry):
        own[s] = got[tab[PICK, s]]
        return carry

    lax.fori_loop(0, own.shape[0], unpack, 0)

    def part(ref, h, r):
        return ref.at[pl.ds(h * half, half), :, cols_of(r)]

    right, left = (row + 1) % rows, (row + rows - 1) % rows
    far_row = (row + 2) % rows
    for k, dest in ((0, right), (1, left)):
        for h in (0, 1):
            pltpu.make_async_remote_copy(
                own.at[pl.ds(h * half, half)], part(hid_full, h, row),
                y_s.at[2 * k + h], y_r.at[row, h],
                device_id=(dest, me), device_id_type=MESH,
            ).start()
    keep_y = pltpu.make_async_copy(own, hid_full.at[:, :, cols_of(row)], loc.at[4])
    keep_y.start()

    for which in (0, 1):
        arrived(which, far)
        for dest in (over, under, sibling):
            forward(which, far, dest)
    for k in (0, 1, -1, 2):
        low, high = at(a + k, b - 1), at(a + k, b + 1)
        arrived(0, low)
        forward(0, low, over)
        arrived(1, high)
        forward(1, high, under)
        arrived(1, low)
        arrived(0, high)
        for which in (0, 1):
            forward(which, low, sibling)
            forward(which, high, sibling)

    def y_here(h, r):
        pltpu.make_async_copy(part(hid_full, h, r), part(hid_full, h, r), y_r.at[r, h]).wait()

    y_here(0, left)
    pltpu.make_async_remote_copy(
        part(hid_full, 0, left), part(hid_full, 0, left), y_s.at[4], y_r.at[left, 0],
        device_id=(right, me), device_id_type=MESH,
    ).start()
    y_here(1, right)
    pltpu.make_async_remote_copy(
        part(hid_full, 1, right), part(hid_full, 1, right), y_s.at[5], y_r.at[right, 1],
        device_id=(left, me), device_id_type=MESH,
    ).start()
    y_here(1, left)
    y_here(0, right)
    for k in (0, 1, -1, 2):
        opposite = at(a + k, b + 2)
        for which in (0, 1):
            arrived(which, opposite)
            forward(which, opposite, sibling)
    y_here(0, far_row)
    y_here(1, far_row)

    def from_sibling(k, carry):
        c = 2 * k + 1 - core
        pltpu.make_async_copy(block(fa, c), block(fa, c), war.at[c]).wait()
        pltpu.make_async_copy(block(fb, c), block(fb, c), wbr.at[c]).wait()
        return carry

    lax.fori_loop(0, cols // 2, from_sibling, 0)
    keep_a.wait()
    keep_b.wait()
    keep_y.wait()

    def a2a_done(d, carry):
        peer = (me + d) % cols
        pltpu.make_async_copy(piece(packed, peer), piece(packed, peer), a2a_s.at[peer]).wait()
        return carry

    lax.fori_loop(1, cols, a2a_done, 0)

    def a_done(k, carry):
        pltpu.make_async_copy(block(fa, me), block(fa, me), was.at[k]).wait()
        return carry

    lax.fori_loop(0, sent[0], a_done, 0)

    def b_done(k, carry):
        pltpu.make_async_copy(block(fb, me), block(fb, me), wbs.at[k]).wait()
        return carry

    lax.fori_loop(0, sent[1], b_done, 0)
    for k in range(6):
        h = (0, 1, 0, 1, 0, 1)[k]
        pltpu.make_async_copy(part(hid_full, h, row), part(hid_full, h, row), y_s.at[k]).wait()


def gather_all(tab, hidden, wa, w_out, w_bc, w_dt, rows, cols, cap, held):
    requests, _, model = hidden.shape
    width = model // rows
    dt = hidden.dtype
    hbm = pl.BlockSpec(memory_space=pltpu.HBM)
    dma = pltpu.SemaphoreType.DMA
    depth = wa.shape[0]
    rest = w_out.shape[1] + w_bc.shape[1] + 128

    def body(*refs):
        gather_kernel(rows, cols, cap, *refs)

    return pl.pallas_call(
        body,
        out_shape=(
            jax.ShapeDtypeStruct((held, LEN, model), dt),
            jax.ShapeDtypeStruct((depth * cols, wa.shape[1]), dt),
            jax.ShapeDtypeStruct((depth * cols, rest), dt),
        ),
        in_specs=[hbm] * 6,
        out_specs=(hbm, hbm, hbm),
        scratch_shapes=[
            pltpu.SMEM(tab.shape, jnp.int32),
            pltpu.VMEM(w_dt.shape, dt),
            pltpu.VMEM((depth, rest), dt),
            pltpu.VMEM((requests, LEN, width), dt),
            pltpu.VMEM((cols * cap, LEN, width), dt),
            pltpu.VMEM((cols * cap, LEN, width), dt),
            pltpu.VMEM((held, LEN, width), dt),
            dma((9,)), dma((cols,)), dma((cols,)),
            dma((48,)), dma((48,)), dma((cols,)), dma((cols,)),
            dma((6,)), dma((rows, 2)),
        ],
        compiler_params=pltpu.CompilerParams(
            collective_id=0, has_side_effects=True, vmem_limit_bytes=60 << 20
        ),
        name="gather_all",
    )(tab, hidden, wa, w_out, w_bc, w_dt)


def silu(v):
    return v / (1.0 + jnp.exp(-v))


def token_masks():
    t_ids = lax.broadcasted_iota(jnp.int32, (TOK, TOK), 0)
    s_ids = lax.broadcasted_iota(jnp.int32, (TOK, TOK), 1)
    return t_ids, s_ids


def mixer_kernel(
    rows, cols, cap, held, tab_in, hid_c, hidden, fa, fb, *refs,
):
    sources, refs = refs[:8], refs[8:]
    prev, pex_in, peb_in, mixed, nst, edge_c, xgot, egot, tab, *refs = refs
    params, refs = refs[:8], refs[8:]
    dtb, alog, skip, cxw, cxb, cbw, cbb, gain = params
    (
        pex, peb, hid, home, wa, wb, wo, old, gate, xin, bc, dts, gg, ss, cx, cb, pexf, pebf, es,
        new, sent, edge_o, xmsg, emsg, part_o, part_c, came_o, came_c, ss_in, scale, mix_o,
        mix0, mix1, mix2, packed, got0, got1, got2,
        h_sem, o_sem, w_sem, n_sem, v_sem, loc, ss_s, ss_r, yo_s, yo_r, yc_s, yc_r,
        a2a_s, a2a_r, x_s, x_r, e_s, e_r,
    ) = refs
    row, me = lax.axis_index("row"), lax.axis_index("col")
    barrier = greet(row, me, rows, cols)
    f32, bf16 = jnp.float32, jnp.bfloat16
    inner = gain.shape[1]
    requests = hid.shape[0]
    tokens = requests * LEN
    model = hid.shape[2]
    heads = inner // HEAD_DIM
    blocks = wa.shape[1] // 256

    load_h = pltpu.make_async_copy(hid_c, hid.at[pl.ds(0, held)], h_sem)
    load_h.start()
    small = list(zip(sources + (pex_in, peb_in, tab_in), list(params) + [pex, peb, tab]))
    small = [pltpu.make_async_copy(a, b, v_sem.at[k]) for k, (a, b) in enumerate(small)]
    small[-1].start()
    for copy in small[:-1]:
        copy.start()
    small[-1].wait()

    def wa_load(n):
        at = pl.ds(n * 256, 256)
        return pltpu.make_async_copy(fa.at[:, at], wa.at[:, at], w_sem.at[n])

    wa_load(0).start()

    load_home = pltpu.make_async_copy(hidden, home, o_sem)
    load_home.start()
    for n in range(1, blocks):
        wa_load(n).start()
    late = pl.ds(inner, wb.shape[1])
    load_bc = pltpu.make_async_copy(fb.at[:, late], wb, w_sem.at[blocks])
    load_out = pltpu.make_async_copy(fb.at[:, pl.ds(0, inner)], wo, w_sem.at[blocks + 2])
    load_old = pltpu.make_async_copy(prev, old, w_sem.at[blocks + 1])
    load_bc.start()
    load_out.start()
    load_old.start()
    for copy in small[:-1]:
        copy.wait()
    pexf[...] = pex[...].astype(f32)
    pebf[...] = peb[...].astype(f32)

    t_ids, s_ids = token_masks()
    row_ids = lax.broadcasted_iota(jnp.int32, (4 * GROUP, TOK), 0)
    k_ids = lax.broadcasted_iota(jnp.int32, (4 * GROUP, TOK), 1)
    r_ids, q_ids = row_ids // 4, row_ids % 4
    es[...] = jnp.zeros(es.shape, f32)
    same = (t_ids // LEN) == (s_ids // LEN)
    causal = same & (t_ids >= s_ids)
    tri = causal.astype(f32)
    spread_h = (
        lax.broadcasted_iota(jnp.int32, (TOK, inner), 1) // HEAD_DIM
        == lax.broadcasted_iota(jnp.int32, (TOK, inner), 0)
    ).astype(f32)

    def wide(ref):
        return jnp.concatenate([ref[...], jnp.zeros((1, TOK - heads), f32)], axis=1)

    bias, rate = wide(dtb), -jnp.exp(wide(alog))
    skip_x = jnp.dot(
        jnp.broadcast_to(wide(skip), (8, TOK)), spread_h,
        precision=HIGHEST, preferred_element_type=f32,
    )[0:1, :]

    load_h.wait()
    load_home.wait()

    def stay(n, carry):
        hid[held + n] = home[tab[STAY, n]]
        return carry

    lax.fori_loop(0, requests - held, stay, 0)
    left = lax.broadcasted_iota(jnp.int32, (tokens, 128), 1) < HEAD_DIM
    for n in range(blocks):
        wa_load(n).wait()
        z = jnp.dot(
            hid[...].reshape(tokens, model), wa[:, n * 256 : (n + 1) * 256],
            preferred_element_type=f32,
        )
        z0, z1 = z[:, :128], z[:, 128:]
        at = slice(n * 128, (n + 1) * 128)
        gate[:, at] = jnp.where(left, z0, pltpu.roll(z1, HEAD_DIM, 1)).astype(bf16)
        xin[:, at] = jnp.where(left, pltpu.roll(z0, HEAD_DIM, 1), z1).astype(bf16)
    load_bc.wait()
    z = jnp.dot(hid[...].reshape(tokens, model), wb[...], preferred_element_type=f32)
    bc[...] = z[:, : 2 * STATE].astype(bf16)
    dts[...] = z[:, 2 * STATE :]
    load_old.wait()

    def store(s):
        return pltpu.make_async_copy(new.at[s], nst.at[s], n_sem.at[s])

    def group(i, live):
        at = pl.ds(pl.multiple_of(i * TOK, TOK), TOK)
        first = i * GROUP
        last = jnp.zeros((TOK, TOK), jnp.int32)
        row_acc = jnp.zeros((4 * GROUP, TOK), jnp.int32)
        for r in range(GROUP):
            acc = tab[ACC, first + r] if live else tab[STAY_ACC, first - held + r]
            row_acc = jnp.where(r_ids == r, acc, row_acc)
            last = jnp.where(t_ids // LEN == r, acc, last)
            if live:
                for k in range(KCONV - 1):
                    cx[r, 13 + k : 14 + k, :] = pexf[k, pl.ds(first + r, 1), :]
                    cb[r, 13 + k : 14 + k, :] = pebf[k, pl.ds(first + r, 1), :]
        if not live:
            cx[:, 8:16, :] = jnp.zeros((GROUP, 8, inner), f32)
            cb[:, 8:16, :] = jnp.zeros((GROUP, 8, 2 * STATE), f32)
        cx[:, 16:32, :] = xin[at, :].astype(f32).reshape(GROUP, LEN, inner)
        cb[:, 16:32, :] = bc[at, :].astype(f32).reshape(GROUP, LEN, 2 * STATE)
        tot_x = cxb[...].reshape(1, 1, inner) + cxw[0:1, :].reshape(1, 1, inner) * cx[:, 13:29, :]
        tot_b = cbb[...].reshape(1, 1, 2 * STATE) + cbw[0:1, :].reshape(
            1, 1, 2 * STATE
        ) * cb[:, 13:29, :]
        for k in range(1, KCONV):
            tot_x = tot_x + cxw[k : k + 1, :].reshape(1, 1, inner) * cx[:, 13 + k : 29 + k, :]
            tot_b = tot_b + cbw[k : k + 1, :].reshape(1, 1, 2 * STATE) * cb[:, 13 + k : 29 + k, :]
        xc = silu(tot_x).reshape(TOK, inner).astype(bf16)
        bcc = silu(tot_b).reshape(TOK, 2 * STATE).astype(bf16)
        near = jnp.concatenate([xin[at, :], bc[at, :]], axis=1)
        want = q_ids + row_acc
        pick = (k_ids == LEN * r_ids + want - 3) & (want >= 3) & (q_ids < 3)
        edge = jnp.dot(pick.astype(bf16), near, preferred_element_type=f32)
        if live:
            for k in range(KCONV - 1):
                rows8 = pl.ds(pl.multiple_of(first, GROUP), GROUP)
                es[k * GROUP : (k + 1) * GROUP, :inner] = pexf[k, rows8, :]
                es[k * GROUP : (k + 1) * GROUP, inner:] = pebf[k, rows8, :]
            pick = (k_ids == GROUP * want + r_ids) & (want < 3) & (q_ids < 3)
            edge = edge + jnp.dot(
                pick.astype(bf16), es[...].astype(bf16), preferred_element_type=f32
            )
        for r in range(GROUP):
            lines = edge[4 * r : 4 * r + 4, :].astype(bf16)
            if live:
                edge_c[first + r] = lines
            else:
                edge_o[first - held + r] = lines
        b_in, c_in = bcc[:, :STATE], bcc[:, STATE:]
        xf = xc.astype(f32)
        raw = dts[at, :] + bias
        step = jnp.maximum(raw, 0.0) + jnp.log(1.0 + jnp.exp(-jnp.abs(raw)))
        decay = jnp.dot(tri, step * rate, precision=HIGHEST, preferred_element_type=f32)
        decay_t = decay.T
        step_t = step.T
        choose = (same & (s_ids % LEN == last - 1)).astype(f32)
        reach = jnp.dot(choose, decay, precision=HIGHEST, preferred_element_type=f32)
        taken = t_ids % LEN < last
        weight = jnp.where(taken, jnp.exp(jnp.minimum(reach - decay, 0.0)), 0.0) * step
        weight_x = jnp.dot(weight, spread_h, precision=HIGHEST, preferred_element_type=f32)
        scores = lax.dot_general(
            c_in, b_in, (((1,), (1,)), ((), ())), preferred_element_type=f32
        )
        scores = jnp.where(causal, scores, 0.0)
        half = s_ids < HEAD_DIM
        zero = jnp.zeros((TOK, 2 * HEAD_DIM), bf16)
        y = []
        for pair in range(heads // 2):
            mats = []
            for h in (2 * pair, 2 * pair + 1):
                gap = decay[:, h : h + 1] - decay_t[h : h + 1, :]
                mats.append(
                    (jnp.exp(jnp.minimum(gap, 0.0)) * scores * step_t[h : h + 1, :]).astype(bf16)
                )
            xp = xc[:, pair * 128 : (pair + 1) * 128]
            both = jnp.concatenate([jnp.where(half, xp, zero), jnp.where(half, zero, xp)], axis=0)
            y.append(
                jnp.dot(jnp.concatenate(mats, axis=1), both, preferred_element_type=f32)
            )
        y = jnp.concatenate(y, axis=1)
        if live:
            grow_x = jnp.dot(jnp.exp(decay), spread_h, precision=HIGHEST, preferred_element_type=f32)
            carried = [
                lax.dot_general(
                    c_in[r * LEN : (r + 1) * LEN, :], old[first + r], (((1,), (1,)), ((), ())),
                    preferred_element_type=f32,
                )
                for r in range(GROUP)
            ]
            y = y + grow_x * jnp.concatenate(carried, axis=0)
        y = y + skip_x * xf
        gated = y * silu(gate[at, :].astype(f32))
        gg[at, :] = (gated * gain[...]).astype(bf16)
        squares = jnp.sum(gated * gated, axis=1, keepdims=True)
        ss[pl.ds(i, 1), :] = jnp.broadcast_to(squares, (TOK, TOK)).T[0:1, :]

        if not live:
            out = (xf * weight_x).astype(bf16)
            for r in range(GROUP):
                lines = slice(r * LEN, (r + 1) * LEN)
                sent[first - held + r, :, :inner] = out[lines, :]
                sent[first - held + r, :, inner:] = b_in[lines, :]
            return
        xw = (xf * weight_x).T
        high = xw.astype(bf16)
        low = (xw - high.astype(f32)).astype(bf16)
        lhs = jnp.concatenate([high, low], axis=1)
        keep_t = jnp.exp(reach).T
        none = jnp.zeros((TOK, STATE), bf16)
        for pair in range(GROUP // 2):
            cut = jnp.concatenate(
                [
                    jnp.where(t_ids // LEN == r, b_in, none)
                    for r in (2 * pair, 2 * pair + 1)
                ],
                axis=1,
            )
            added = jnp.dot(
                lhs, jnp.concatenate([cut, cut], axis=0), preferred_element_type=f32
            )
            for k in (0, 1):
                r = 2 * pair + k
                s = first + r
                factor = jnp.broadcast_to(keep_t[0:heads, r * LEN : r * LEN + 1], (heads, STATE))
                was = old[s].astype(f32).reshape(heads, HEAD_DIM, STATE)
                now = factor[:, None, :] * was + added[:, k * STATE : (k + 1) * STATE].reshape(
                    heads, HEAD_DIM, STATE
                )
                new[s] = now.reshape(inner, STATE).astype(bf16)
                store(s).start()

    @pl.loop(held // GROUP, requests // GROUP)
    def _(i):
        group(i, False)

    load_out.wait()
    moving = held * LEN
    resting = tokens - moving
    pieces = part_c.shape[1]
    width = pieces * 128
    order = (1, 3, 2)

    def project(lines, peer, j, count):
        at = pl.ds(pl.multiple_of(peer * width + j * 128, 128), count * 128)
        return lax.dot_general(
            gg[lines, :], wo[at, :], (((1,), (1,)), ((), ())), preferred_element_type=f32
        ).astype(bf16)

    def rest_block(peer):
        part_o[peer] = project(slice(moving, tokens), peer, 0, pieces)

    def move_block(peer, j, count):
        out = project(slice(0, moving), peer, j, count)
        for k in range(count):
            part_c[peer, j + k] = out[:, k * 128 : (k + 1) * 128]

    def piece(ref, c):
        return ref.at[pl.ds(c * cap, cap)]

    def to_slots(q, carry):
        n = tab[LEAVE, q]
        xmsg[q] = sent[n]
        emsg[q] = edge_o[n]
        return carry

    lax.fori_loop(0, cols * cap, to_slots, 0)
    pl.semaphore_wait(barrier, cols - 1 + rows - 1)

    def push_factors(d, carry):
        peer = (me + d) % cols
        for a, b, s_, r_ in ((xmsg, xgot, x_s, x_r), (emsg, egot, e_s, e_r)):
            pltpu.make_async_remote_copy(
                piece(a, peer), piece(b, me), s_.at[peer], r_.at[me],
                device_id=(row, peer), device_id_type=MESH,
            ).start()
        return carry

    lax.fori_loop(1, cols, push_factors, 0)
    keep_x = pltpu.make_async_copy(piece(xmsg, me), piece(xgot, me), loc.at[0])
    keep_e = pltpu.make_async_copy(piece(emsg, me), piece(egot, me), loc.at[1])
    keep_x.start()
    keep_e.start()

    def send_rest(d, carry):
        peer = (row + d) % rows
        rest_block(peer)
        pltpu.make_async_remote_copy(
            part_o.at[peer], came_o.at[row], yo_s.at[d], yo_r.at[row],
            device_id=(peer, me), device_id_type=MESH,
        ).start()
        return carry

    lax.fori_loop(1, rows, send_rest, 0)

    @pl.loop(0, held // GROUP)
    def _(i):
        group(i, True)

    for k, d in enumerate(order):
        pltpu.make_async_remote_copy(
            ss, ss_in.at[row], ss_s.at[k], ss_r.at[row],
            device_id=((row + d) % rows, me), device_id_type=MESH,
        ).start()

    def send_block(peer, j, d):
        pltpu.make_async_remote_copy(
            part_c.at[peer, j], came_c.at[row, j], yc_s.at[j, d], yc_r.at[row, j],
            device_id=(peer, me), device_id_type=MESH,
        ).start()

    def first_block(d, carry):
        peer = (row + d) % rows
        move_block(peer, 0, 1)
        send_block(peer, 0, d)
        return carry

    def later_blocks(d, carry):
        peer = (row + d) % rows
        move_block(peer, 1, pieces - 1)
        for j in range(1, pieces):
            send_block(peer, j, d)
        return carry

    lax.fori_loop(1, rows, first_block, 0)
    lax.fori_loop(1, rows, later_blocks, 0)
    move_block(row, 0, 1)
    move_block(row, 1, pieces - 1)
    rest_block(row)
    total = ss[...]
    for d in order:
        peer = (row + d) % rows
        pltpu.make_async_copy(ss_in.at[peer], ss_in.at[peer], ss_r.at[peer]).wait()
        total = total + ss_in[peer]
    factor = lax.rsqrt(total / INNER + 1e-05)
    for i in range(tokens // TOK):
        line = jnp.broadcast_to(factor[i : i + 1, :], (TOK, TOK))
        scale[pl.ds(i * TOK, TOK), :] = line.T
    for d in order:
        peer = (row + d) % rows
        pltpu.make_async_copy(came_o.at[peer], came_o.at[peer], yo_r.at[peer]).wait()

    def add_rest(i, carry):
        at = pl.ds(pl.multiple_of(i * TOK, TOK), TOK)
        by = scale[pl.ds(pl.multiple_of(moving + i * TOK, TOK), TOK), :]
        for j in range(pieces):
            lanes = slice(j * 128, (j + 1) * 128)
            value = part_o[row, at, lanes].astype(f32)
            for d in order:
                value = value + came_o[(row + d) % rows, at, lanes].astype(f32)
            mix_o[j, pl.ds(i * GROUP, GROUP)] = (value * by).astype(bf16).reshape(GROUP, LEN, 128)
        return carry

    lax.fori_loop(0, resting // TOK, add_rest, 0)
    gots, mixes = (got0, got1, got2), (mix0, mix1, mix2)
    for j in range(pieces):
        mix = mixes[j]
        for d in order:
            peer = (row + d) % rows
            pltpu.make_async_copy(came_c.at[peer, j], came_c.at[peer, j], yc_r.at[peer, j]).wait()

        def add(i, carry):
            at = pl.ds(pl.multiple_of(i * TOK, TOK), TOK)
            value = part_c[row, j, at, :].astype(f32)
            for d in order:
                value = value + came_c[(row + d) % rows, j, at, :].astype(f32)
            value = (value * scale[at, :]).astype(bf16)
            mix[pl.ds(i * GROUP, GROUP)] = value.reshape(GROUP, LEN, 128)
            return carry

        lax.fori_loop(0, moving // TOK, add, 0)

        def pack(q, carry):
            packed[j, q] = mix[tab[BACK, q]]
            return carry

        lax.fori_loop(0, cols * cap, pack, 0)

        def push(d, carry):
            peer = (me + d) % cols
            pltpu.make_async_remote_copy(
                piece(packed.at[j], peer), piece(gots[j], me), a2a_s.at[j, peer], a2a_r.at[j, me],
                device_id=(row, peer), device_id_type=MESH,
            ).start()
            return carry

        lax.fori_loop(1, cols, push, 0)
        pltpu.make_async_copy(piece(packed.at[j], me), piece(gots[j], me), loc.at[2 + j]).start()
    for j in range(pieces):
        got = gots[j]
        pltpu.make_async_copy(piece(packed.at[j], me), piece(got, me), loc.at[2 + j]).wait()

        def took(d, carry):
            peer = (me + d) % cols
            pltpu.make_async_copy(piece(got, peer), piece(got, peer), a2a_r.at[j, peer]).wait()
            return carry

        lax.fori_loop(1, cols, took, 0)

        def unpack(s, carry):
            moved = tab[MOVED, s].astype(f32)
            away = got[tab[FROM_MSG, s]].astype(f32)
            here = mix_o[j, tab[FROM_MIX, s]].astype(f32)
            value = jnp.where(moved > 0.5, away, here)
            mixed[s, :, j * 128 : (j + 1) * 128] = value.astype(bf16)
            return carry

        lax.fori_loop(0, requests, unpack, 0)
    for k in range(rows - 1):
        pltpu.make_async_copy(ss, ss, ss_s.at[k]).wait()
        pltpu.make_async_copy(part_o.at[0], part_o.at[0], yo_s.at[k + 1]).wait()
        for j in range(pieces):
            pltpu.make_async_copy(part_c.at[0, j], part_c.at[0, j], yc_s.at[j, k + 1]).wait()
    for j in range(pieces):

        def gone(d, carry):
            peer = (me + d) % cols
            pltpu.make_async_copy(
                piece(packed.at[j], peer), piece(packed.at[j], peer), a2a_s.at[j, peer]
            ).wait()
            return carry

        lax.fori_loop(1, cols, gone, 0)
    keep_x.wait()
    keep_e.wait()

    def factors(d, carry):
        peer = (me + d) % cols
        for ref, s_, r_ in ((xgot, x_s, x_r), (egot, e_s, e_r)):
            pltpu.make_async_copy(piece(ref, peer), piece(ref, peer), r_.at[peer]).wait()
            pltpu.make_async_copy(piece(ref, peer), piece(ref, peer), s_.at[peer]).wait()
        return carry

    lax.fori_loop(1, cols, factors, 0)

    @pl.loop(0, held)
    def _(s):
        store(s).wait()


def mixer(tab, hid_c, hidden, fa, fb, vectors, prev, pex, peb, rows, cols, cap):
    requests, _, model = hidden.shape
    held = hid_c.shape[0]
    tokens = requests * LEN
    inner = fa.shape[1] // 2
    width = model // rows
    pieces = width // 128
    slots = cols * cap
    rest = requests - held
    dt = hidden.dtype
    f32 = jnp.float32
    vmem = pl.BlockSpec(memory_space=pltpu.VMEM)
    hbm = pl.BlockSpec(memory_space=pltpu.HBM)
    dma = pltpu.SemaphoreType.DMA

    def body(*refs):
        mixer_kernel(rows, cols, cap, held, *refs)

    wide = inner + 2 * STATE
    mix = pltpu.VMEM((held, LEN, 128), dt)
    got = pltpu.VMEM((slots, LEN, 128), dt)
    return pl.pallas_call(
        body,
        out_shape=(
            jax.ShapeDtypeStruct((requests, LEN, width), dt),
            jax.ShapeDtypeStruct((held, inner, STATE), dt),
            jax.ShapeDtypeStruct((held, 4, wide), dt),
            jax.ShapeDtypeStruct((slots, LEN, inner + STATE), dt),
            jax.ShapeDtypeStruct((slots, 4, wide), dt),
        ),
        in_specs=[hbm] * (8 + len(vectors)),
        out_specs=(vmem, hbm, vmem, hbm, hbm),
        scratch_shapes=[
            pltpu.SMEM(tab.shape, jnp.int32),
            *[pltpu.VMEM(v.shape, v.dtype) for v in vectors],
            pltpu.VMEM(pex.shape, dt),
            pltpu.VMEM(peb.shape, dt),
            pltpu.VMEM((requests, LEN, model), dt),
            pltpu.VMEM((requests, LEN, model), dt),
            pltpu.VMEM(fa.shape, dt),
            pltpu.VMEM((fb.shape[0], fb.shape[1] - inner), dt),
            pltpu.VMEM((fb.shape[0], inner), dt),
            pltpu.VMEM((held, inner, STATE), dt),
            pltpu.VMEM((tokens, inner), dt),
            pltpu.VMEM((tokens, inner), dt),
            pltpu.VMEM((tokens, 2 * STATE), dt),
            pltpu.VMEM((tokens, 128), f32),
            pltpu.VMEM((tokens, inner), dt),
            pltpu.VMEM((8, 128), f32),
            pltpu.VMEM((GROUP, 32, inner), f32),
            pltpu.VMEM((GROUP, 32, 2 * STATE), f32),
            pltpu.VMEM((3, held, inner), f32),
            pltpu.VMEM((3, held, 2 * STATE), f32),
            pltpu.VMEM((TOK, wide), f32),
            pltpu.VMEM((held, inner, STATE), dt),
            pltpu.VMEM((rest, LEN, inner + STATE), dt),
            pltpu.VMEM((rest, 4, wide), dt),
            pltpu.VMEM((slots, LEN, inner + STATE), dt),
            pltpu.VMEM((slots, 4, wide), dt),
            pltpu.VMEM((rows, rest * LEN, width), dt),
            pltpu.VMEM((rows, pieces, held * LEN, 128), dt),
            pltpu.VMEM((rows, rest * LEN, width), dt),
            pltpu.VMEM((rows, pieces, held * LEN, 128), dt),
            pltpu.VMEM((rows, 8, 128), f32),
            pltpu.VMEM((tokens, 128), f32),
            pltpu.VMEM((pieces, rest, LEN, 128), dt),
            mix, mix, mix,
            pltpu.VMEM((pieces, slots, LEN, 128), dt),
            got, got, got,
            dma(()), dma(()), dma((fa.shape[1] // 256 + 3,)), dma((held,)),
            dma((len(vectors) + 3,)), dma((2 + pieces,)), dma((3,)), dma((rows,)),
            dma((rows,)), dma((rows,)), dma((pieces, rows)), dma((rows, pieces)),
            dma((pieces, cols)), dma((pieces, cols)),
            dma((cols,)), dma((cols,)), dma((cols,)), dma((cols,)),
        ],
        compiler_params=pltpu.CompilerParams(
            collective_id=1, has_side_effects=True, vmem_limit_bytes=60 << 20
        ),
        name="mixer",
    )(tab, hid_c, hidden, fa, fb, *vectors, prev, pex, peb)


def arrive_kernel(
    tab_in, xgot_in, egot_in, edge_in, nst_in, nst, nex, neb,
    tab, xgot, egot, edge, xs, bs, ex, eb, new, n_sem, m_sem, l_sem,
):
    f32, bf16 = jnp.float32, jnp.bfloat16
    count, inner = new.shape[0], new.shape[1]
    loads = [
        pltpu.make_async_copy(a, b, l_sem.at[k])
        for k, (a, b) in enumerate(
            ((tab_in, tab), (xgot_in, xgot), (egot_in, egot), (edge_in, edge))
        )
    ]
    for copy in loads:
        copy.start()
    loads[0].wait()

    def place(s):
        return pltpu.make_async_copy(nst_in.at[s], nst.at[tab[POS, s]], m_sem.at[s])

    @pl.loop(0, count)
    def _(s):
        place(s).start()

    loads[1].wait()
    t_ids, _ = token_masks()
    none = jnp.zeros((TOK, STATE), bf16)

    def store(u):
        return pltpu.make_async_copy(new.at[u], nst.at[tab[POS_O, u]], n_sem.at[u])

    @pl.loop(0, count // GROUP)
    def _(i):
        for r in range(GROUP):
            slot = tab[PICK_O, i * GROUP + r]
            xs[r] = xgot[slot, :, :inner]
            bs[r] = xgot[slot, :, inner:]
        lhs = xs[...].reshape(TOK, inner).astype(f32).T.astype(bf16)
        b_in = bs[...].reshape(TOK, STATE)
        for pair in range(GROUP // 2):
            cut = jnp.concatenate(
                [
                    jnp.where(t_ids // LEN == r, b_in, none)
                    for r in (2 * pair, 2 * pair + 1)
                ],
                axis=1,
            )
            out = jnp.dot(lhs, cut, preferred_element_type=f32).astype(bf16)
            for k in (0, 1):
                u = i * GROUP + 2 * pair + k
                new[u] = out[:, k * STATE : (k + 1) * STATE]
                store(u).start()

    for copy in loads[2:]:
        copy.wait()

    @pl.loop(0, count)
    def _(u):
        for source, k, spot in (
            (egot, tab[PICK_O, u], tab[POS_O, u]), (edge, u, tab[POS, u])
        ):
            lines = source[k].astype(f32)
            at = pl.ds(spot, 1)
            for q in range(KCONV - 1):
                ex[q, at, :] = lines[q : q + 1, :inner]
                eb[q, at, :] = lines[q : q + 1, inner:]

    nex[...] = ex[...].astype(bf16)
    neb[...] = eb[...].astype(bf16)

    @pl.loop(0, count)
    def _(u):
        store(u).wait()
        place(u).wait()


def arrive(tab, xgot, egot, edge, nst):
    count, inner, _ = nst.shape
    requests = 2 * count
    dt, f32 = nst.dtype, jnp.float32
    vmem = pl.BlockSpec(memory_space=pltpu.VMEM)
    hbm = pl.BlockSpec(memory_space=pltpu.HBM)
    return pl.pallas_call(
        arrive_kernel,
        out_shape=(
            jax.ShapeDtypeStruct((requests, inner, STATE), dt),
            jax.ShapeDtypeStruct((3, requests, inner), dt),
            jax.ShapeDtypeStruct((3, requests, 2 * STATE), dt),
        ),
        in_specs=[hbm] * 5,
        out_specs=(hbm, vmem, vmem),
        scratch_shapes=[
            pltpu.SMEM(tab.shape, jnp.int32),
            pltpu.VMEM(xgot.shape, dt),
            pltpu.VMEM(egot.shape, dt),
            pltpu.VMEM(edge.shape, dt),
            pltpu.VMEM((GROUP, LEN, inner), dt),
            pltpu.VMEM((GROUP, LEN, STATE), dt),
            pltpu.VMEM((3, requests, inner), f32),
            pltpu.VMEM((3, requests, 2 * STATE), f32),
            pltpu.VMEM((count, inner, STATE), dt),
            pltpu.SemaphoreType.DMA((count,)),
            pltpu.SemaphoreType.DMA((count,)),
            pltpu.SemaphoreType.DMA((4,)),
        ],
        compiler_params=pltpu.CompilerParams(vmem_limit_bytes=60 << 20),
        name="arrive",
    )(tab, xgot, egot, edge, nst)


def per_device(
    hidden, w_zx, w_bc, w_dt, w_out, dt_bias, a_log, d_skip, conv_x_w, conv_x_b,
    conv_bc_w, conv_bc_b, norm_gain, prev_state, prev_edge_x, prev_edge_bc,
    holder, continued, owner, accepted,
):
    rows, cols = lax.axis_size("row"), lax.axis_size("col")
    tokens, model = hidden.shape
    requests = tokens // LEN
    heads = dt_bias.shape[0]
    inner = heads * HEAD_DIM
    held = prev_state.shape[0]
    cap = 2 * ((requests // 4 + cols - 1) // cols)
    code = owner + 64 * (continued == 1).astype(jnp.int32) + 128 * accepted
    tab = route(code.reshape(cols, requests), held)
    hidden = hidden.reshape(requests, LEN, model)
    hid_c, fa, fb = gather_all(tab, hidden, w_zx, w_out, w_bc, w_dt.T, rows, cols, cap, held)
    vectors = (
        dt_bias[None, :], a_log[None, :], d_skip[None, :],
        conv_x_w, conv_x_b[None, :], conv_bc_w, conv_bc_b[None, :], norm_gain[None, :],
    )
    mixed, moved, edge, xgot, egot = mixer(
        tab, hid_c, hidden, fa, fb, vectors, prev_state.reshape(held, inner, STATE),
        prev_edge_x.transpose(1, 0, 2), prev_edge_bc.transpose(1, 0, 2),
        rows, cols, cap,
    )
    states, new_x, new_bc = arrive(tab, xgot, egot, edge, moved)
    return (
        mixed.reshape(tokens, model // rows),
        states.reshape(requests, heads, HEAD_DIM, STATE),
        new_x.transpose(1, 0, 2),
        new_bc.transpose(1, 0, 2),
    )


def solution(mesh):
    return jax.shard_map(
        per_device,
        mesh=mesh,
        in_specs=(
            P("col", None),
            P("col", "row"),
            P("col", None),
            P("col", "row"),
            P("col", "row"),
            P("row"),
            P("row"),
            P("row"),
            P(None, "row"),
            P("row"),
            P(),
            P(),
            P("row"),
            P("col", "row", None, None),
            P("col", None, "row"),
            P("col", None, None),
            P(),
            P(),
            P(),
            P(),
        ),
        out_specs=(
            P("col", "row"),
            P("col", "row", None, None),
            P("col", None, "row"),
            P("col", None, None),
        ),
        check_vma=False,
    )
```

```python
import jax
import jax.numpy as jnp
from jax import lax
from jax.experimental import pallas as pl
from jax.experimental.pallas import tpu as pltpu
from jax.sharding import PartitionSpec as P

HEAD_DIM = 64
STATE = 128
KCONV = 4
LEN = 16
INNER = 2048
SIDE = 4
GROUP = 8
TOK = GROUP * LEN
MESH = pl.DeviceIdType.MESH
HIGHEST = lax.Precision.HIGHEST


def route_kernel(held, code, out):
    f32, bf16 = jnp.float32, jnp.bfloat16
    me = lax.axis_index("col")
    groups, requests = code.shape
    value = code[...]
    o, c, a = value & 63, (value >> 6) & 1, value >> 7

    def dot(x, y):
        return jnp.dot(x.astype(bf16), y.astype(bf16), preferred_element_type=f32)

    def dot0(x, y):
        return lax.dot_general(
            x.astype(bf16), y.astype(bf16), (((0,), (0,)), ((), ())), preferred_element_type=f32
        )

    def ids(shape, dim):
        return lax.broadcasted_iota(jnp.int32, shape, dim)

    below = (ids((requests, requests), 0) < ids((requests, requests), 1)).astype(f32)
    prior = (ids((groups, groups), 1) < ids((groups, groups), 0)).astype(f32)
    lane = ids((groups, 128), 1).astype(f32)
    group = ids((groups, 128), 0).astype(f32)
    spots, inside, starts = [], [], []
    for kind in (1, 0):
        mask = ((o == me) & (c == kind)).astype(f32)
        rank = dot(mask, below)
        count = jnp.broadcast_to(jnp.sum(mask, axis=1, keepdims=True), (groups, 128))
        start = dot(prior, count)
        hot = ((start <= lane) & (lane < start + count)).astype(f32)
        spots.append((jnp.where(mask > 0, rank, -1.0), hot))
        inside.append(rank)
        starts.append(start)
    rank_all, start_all = inside[0] + inside[1], starts[0] + starts[1]
    picks, places, taken = [], [], []
    for k in (0, 1):
        spot, hot = spots[k]
        order = jnp.sum(hot * (lane - starts[k]), axis=0, keepdims=True)
        any_hot = jnp.sum(hot, axis=0, keepdims=True)
        order = jnp.where(any_hot > 0, order, -5.0)
        match = (dot0(spot, hot) == order).astype(f32)
        picks.append(jnp.sum(hot * (2 * group + lane - starts[k]), axis=0, keepdims=True))
        places.append(
            jnp.sum(hot * start_all, axis=0, keepdims=True)
            + jnp.sum(match * dot0(rank_all, hot), axis=0, keepdims=True)
        )
        taken.append(jnp.sum(match * dot0(a, hot), axis=0, keepdims=True))
    lane_i, group_i = ids((groups, 128), 1), ids((groups, 128), 0)
    back = jnp.sum(
        jnp.where(lane_i // 2 == group_i, starts[0] + (lane_i % 2).astype(f32), 0.0),
        axis=0, keepdims=True,
    )
    back = jnp.minimum(back, held - 1.0)

    def my_row(x, fill):
        row = jnp.sum(
            jnp.where(ids((groups, requests), 0) == me, x, 0).astype(f32), axis=0, keepdims=True
        )
        rest = jnp.full((1, 128 - requests), fill, f32)
        return jnp.concatenate([row, rest], axis=1)

    o_row, c_row, a_row = my_row(o, 99.0), my_row(c, 2.0), my_row(a, 0.0)

    def column(row):
        return jnp.broadcast_to(row, (128, 128)).T

    o_col, c_col, a_col = column(o_row), column(c_row), column(a_row)
    ii, jj = ids((128, 128), 0), ids((128, 128), 1)
    alike = (o_col == o_row) & (c_col == c_row)
    rank_row = jnp.sum((alike & (ii < jj)).astype(f32), axis=0, keepdims=True)
    rank_col = jnp.sum((alike & (jj < ii)).astype(f32), axis=1, keepdims=True)
    nth_row = jnp.sum(((c_col == 0) & (ii < jj)).astype(f32), axis=0, keepdims=True)
    nth_col = jnp.sum(((c_row == 0) & (jj < ii)).astype(f32), axis=1, keepdims=True)
    key_row = 2 * o_row + rank_row
    key_col = 2 * o_col + rank_col
    fi, fj = ii.astype(f32), jj.astype(f32)
    goes = (c_col == 1) & (key_col == fj)
    leaves = (c_col == 0) & (key_col == fj)
    stays = (c_col == 0) & (nth_col == fj)

    def total(mask, x):
        return jnp.sum(jnp.where(mask, x, 0.0), axis=0, keepdims=True)

    table = (
        total(goes, fi), picks[0], back,
        jnp.where(c_row == 1, key_row, 0.0), jnp.where(c_row == 0, nth_row, 0.0),
        (c_row == 1).astype(f32),
        total(stays, fi), total(stays, key_col), total(stays, a_col),
        taken[0], places[0], picks[1], places[1], total(leaves, nth_col),
    )
    for k, line in enumerate(table):
        out[k : k + 1, :] = line.astype(jnp.int32)
    out[len(table) :, :] = jnp.zeros((16 - len(table), 128), jnp.int32)


SEND, PICK, BACK, FROM_MSG, FROM_MIX, MOVED, STAY, STAY_KEY, STAY_ACC, ACC, POS, PICK_O, POS_O, LEAVE = range(14)


def route(code, held):
    vmem = pl.BlockSpec(memory_space=pltpu.VMEM)

    def body(*refs):
        route_kernel(held, *refs)

    return pl.pallas_call(
        body, out_shape=jax.ShapeDtypeStruct((16, 128), jnp.int32),
        in_specs=[vmem], out_specs=vmem, name="route",
        compiler_params=pltpu.CompilerParams(vmem_limit_bytes=60 << 20),
    )(code)


def unrolled(count, step, body):
    def some(i, carry):
        for k in range(step):
            body(i * step + k)
        return carry

    lax.fori_loop(0, count // step, some, 0)


def greet(row, me, rows, cols):
    barrier = pltpu.get_barrier_semaphore()

    def along_col(d, carry):
        pl.semaphore_signal(
            barrier, inc=1, device_id=(row, (me + d) % cols), device_id_type=MESH
        )
        return carry

    lax.fori_loop(1, cols, along_col, 0)

    def along_row(d, carry):
        pl.semaphore_signal(
            barrier, inc=1, device_id=((row + d) % rows, me), device_id_type=MESH
        )
        return carry

    lax.fori_loop(1, rows, along_row, 0)
    return barrier


def gather_kernel(
    rows, cols, cap, tab_in, hidden, wa, w_out, w_bc, w_dt_in, hid_full, fa, fb,
    tab, w_dt, wb, sl, packed, got, own, loc, a2a_s, a2a_r, gone, twin, war, wbr, y_s, y_r,
):
    row, me = lax.axis_index("row"), lax.axis_index("col")
    barrier = greet(row, me, rows, cols)
    width = sl.shape[2]
    half = own.shape[0] // 2
    depth = wa.shape[0]

    def cols_of(r):
        return pl.ds(pl.multiple_of(r * width, 128), width)

    def block(ref, c):
        return ref.at[pl.ds(pl.multiple_of(c * depth, 16), depth), :]

    load = pltpu.make_async_copy(hidden.at[:, :, cols_of(row)], sl, loc.at[0])
    load.start()
    inner = w_out.shape[1]
    states = w_bc.shape[1]
    heads = w_dt_in.shape[0]
    loads = (
        pltpu.make_async_copy(tab_in, tab, loc.at[5]),
        pltpu.make_async_copy(w_dt_in, w_dt, loc.at[6]),
        pltpu.make_async_copy(w_out, wb.at[:, pl.ds(0, inner)], loc.at[7]),
        pltpu.make_async_copy(w_bc, wb.at[:, pl.ds(inner, states)], loc.at[8]),
    )
    for copy in loads:
        copy.start()
    for copy in loads:
        copy.wait()
    square = jnp.concatenate([w_dt[...].astype(jnp.float32), jnp.zeros((heads, 128 - depth), jnp.float32)], axis=1)
    square = jnp.concatenate([square, jnp.zeros((128 - heads, 128), jnp.float32)], axis=0).T
    wb[:, inner + states :] = square[:depth, :].astype(wb.dtype)
    keep_a = pltpu.make_async_copy(wa, block(fa, me), loc.at[1])
    keep_b = pltpu.make_async_copy(wb, block(fb, me), loc.at[2])
    keep_a.start()
    keep_b.start()
    load.wait()

    def pack(s):
        packed[s] = sl[tab[SEND, s]]

    unrolled(cols * cap, 8, pack)
    pl.semaphore_wait(barrier, cols - 1 + rows - 1)

    def piece(ref, c):
        return ref.at[pl.ds(c * cap, cap)]

    def push(d, carry):
        peer = (me + d) % cols
        pltpu.make_async_remote_copy(
            piece(packed, peer), piece(got, me), a2a_s, a2a_r,
            device_id=(row, peer), device_id_type=MESH,
        ).start()
        return carry

    lax.fori_loop(1, cols, push, 0)
    keep_m = pltpu.make_async_copy(piece(packed, me), piece(got, me), loc.at[3])
    keep_m.start()

    core = me % 2
    x = (me // 2) % SIDE
    z = me // (2 * SIDE)
    a = x + core * (z - x)
    b = z + core * (x - z)

    def at(pa, pb):
        pa, pb = (pa + SIDE) % SIDE, (pb + SIDE) % SIDE
        px = pa + core * (pb - pa)
        pz = pb + core * (pa - pb)
        return (pz * SIDE + px) * 2 + core

    sibling = me + 1 - 2 * core
    sent = [0, 0]

    def send(which, src, c, dest):
        full, rs = ((fa, war), (fb, wbr))[which]
        sent[which] += 1
        rs = twin.at[which] if dest is sibling else rs.at[c]
        pltpu.make_async_remote_copy(
            src, block(full, c), gone.at[which], rs,
            device_id=(row, dest), device_id_type=MESH,
        ).start()

    def forward(which, c, dest):
        send(which, block((fa, fb)[which], c), c, dest)

    def arrived(which, c):
        full, rs = ((fa, war), (fb, wbr))[which]
        pltpu.make_async_copy(block(full, c), block(full, c), rs.at[c]).wait()

    up, down = at(a + 1, b), at(a - 1, b)
    far = at(a + 2, b)
    over, under = at(a, b + 1), at(a, b - 1)
    for dest in (up, down, over, under, sibling):
        for which, src in ((0, wa), (1, wb)):
            send(which, src, me, dest)
    arrived(0, down)
    forward(0, down, up)
    arrived(1, up)
    forward(1, up, down)
    arrived(1, down)
    arrived(0, up)
    for c in (down, up):
        for which in (0, 1):
            for dest in (over, under, sibling):
                forward(which, c, dest)
    keep_m.wait()

    others = pl.ds(0, (cols - 1) * cap)
    pltpu.make_async_copy(got.at[others], got.at[others], a2a_r).wait()

    def unpack(s):
        own[s] = got[tab[PICK, s]]

    unrolled(own.shape[0], 8, unpack)

    def part(ref, h, r):
        return ref.at[pl.ds(h * half, half), :, cols_of(r)]

    right, left = (row + 1) % rows, (row + rows - 1) % rows
    far_row = (row + 2) % rows
    for k, dest in ((0, right), (1, left)):
        for h in (0, 1):
            pltpu.make_async_remote_copy(
                own.at[pl.ds(h * half, half)], part(hid_full, h, row),
                y_s.at[2 * k + h], y_r.at[row, h],
                device_id=(dest, me), device_id_type=MESH,
            ).start()
    keep_y = pltpu.make_async_copy(own, hid_full.at[:, :, cols_of(row)], loc.at[4])
    keep_y.start()

    for which in (0, 1):
        arrived(which, far)
        for dest in (over, under, sibling):
            forward(which, far, dest)
    for k in (0, 1, -1, 2):
        low, high = at(a + k, b - 1), at(a + k, b + 1)
        arrived(0, low)
        forward(0, low, over)
        arrived(1, high)
        forward(1, high, under)
        arrived(1, low)
        arrived(0, high)
        for which in (0, 1):
            forward(which, low, sibling)
            forward(which, high, sibling)

    def y_here(h, r):
        pltpu.make_async_copy(part(hid_full, h, r), part(hid_full, h, r), y_r.at[r, h]).wait()

    y_here(0, left)
    pltpu.make_async_remote_copy(
        part(hid_full, 0, left), part(hid_full, 0, left), y_s.at[4], y_r.at[left, 0],
        device_id=(right, me), device_id_type=MESH,
    ).start()
    y_here(1, right)
    pltpu.make_async_remote_copy(
        part(hid_full, 1, right), part(hid_full, 1, right), y_s.at[5], y_r.at[right, 1],
        device_id=(left, me), device_id_type=MESH,
    ).start()
    y_here(1, left)
    y_here(0, right)
    for k in (0, 1, -1, 2):
        opposite = at(a + k, b + 2)
        for which in (0, 1):
            arrived(which, opposite)
            forward(which, opposite, sibling)
    y_here(0, far_row)
    y_here(1, far_row)

    for which, ref in ((0, fa), (1, fb)):
        lines = pl.ds(0, (cols // 2) * depth)
        pltpu.make_async_copy(ref.at[lines, :], ref.at[lines, :], twin.at[which]).wait()
    keep_a.wait()
    keep_b.wait()
    keep_y.wait()

    pltpu.make_async_copy(packed.at[others], packed.at[others], a2a_s).wait()

    for which, ref in ((0, fa), (1, fb)):
        lines = pl.ds(0, sent[which] * depth)
        pltpu.make_async_copy(ref.at[lines, :], ref.at[lines, :], gone.at[which]).wait()
    for k in range(6):
        h = (0, 1, 0, 1, 0, 1)[k]
        pltpu.make_async_copy(part(hid_full, h, row), part(hid_full, h, row), y_s.at[k]).wait()


def gather_all(tab, hidden, wa, w_out, w_bc, w_dt, rows, cols, cap, held):
    requests, _, model = hidden.shape
    width = model // rows
    dt = hidden.dtype
    hbm = pl.BlockSpec(memory_space=pltpu.HBM)
    dma = pltpu.SemaphoreType.DMA
    depth = wa.shape[0]
    rest = w_out.shape[1] + w_bc.shape[1] + 128

    def body(*refs):
        gather_kernel(rows, cols, cap, *refs)

    return pl.pallas_call(
        body,
        out_shape=(
            jax.ShapeDtypeStruct((held, LEN, model), dt),
            jax.ShapeDtypeStruct((depth * cols, wa.shape[1]), dt),
            jax.ShapeDtypeStruct((depth * cols, rest), dt),
        ),
        in_specs=[hbm] * 6,
        out_specs=(hbm, hbm, hbm),
        scratch_shapes=[
            pltpu.SMEM(tab.shape, jnp.int32),
            pltpu.VMEM(w_dt.shape, dt),
            pltpu.VMEM((depth, rest), dt),
            pltpu.VMEM((requests, LEN, width), dt),
            pltpu.VMEM((cols * cap, LEN, width), dt),
            pltpu.VMEM((cols * cap, LEN, width), dt),
            pltpu.VMEM((held, LEN, width), dt),
            dma((9,)), dma(()), dma(()),
            dma((2,)), dma((2,)), dma((cols,)), dma((cols,)),
            dma((6,)), dma((rows, 2)),
        ],
        compiler_params=pltpu.CompilerParams(
            collective_id=0, has_side_effects=True, vmem_limit_bytes=60 << 20
        ),
        name="gather_all",
    )(tab, hidden, wa, w_out, w_bc, w_dt)


def silu(v):
    return v / (1.0 + jnp.exp(-v))


def token_masks():
    t_ids = lax.broadcasted_iota(jnp.int32, (TOK, TOK), 0)
    s_ids = lax.broadcasted_iota(jnp.int32, (TOK, TOK), 1)
    return t_ids, s_ids


def mixer_kernel(
    rows, cols, cap, held, tab_in, hid_c, hidden, fa, fb, *refs,
):
    sources, refs = refs[:8], refs[8:]
    prev, pex_in, peb_in, mixed, nst, edge_c, xgot, egot, tab, *refs = refs
    params, refs = refs[:8], refs[8:]
    dtb, alog, skip, cxw, cxb, cbw, cbb, gain = params
    (
        pex, peb, hid, home, wa, wb, wo, old, gate, xin, bc, dts, gg, ss, cx, cb, pexf, pebf, es,
        new, sent, edge_o, xmsg, emsg, part_o, part_c, came_o, came_c, ss_in, scale, mix_o,
        mix0, mix1, mix2, packed, got0, got1, got2,
        h_sem, o_sem, w_sem, n_sem, v_sem, loc, ss_s, ss_r, yo_s, yo_r, yc_s, yc_r,
        a2a_s, a2a_r, x_s, x_r, e_s, e_r,
    ) = refs
    row, me = lax.axis_index("row"), lax.axis_index("col")
    barrier = greet(row, me, rows, cols)
    f32, bf16 = jnp.float32, jnp.bfloat16
    inner = gain.shape[1]
    requests = hid.shape[0]
    tokens = requests * LEN
    model = hid.shape[2]
    heads = inner // HEAD_DIM
    blocks = wa.shape[1] // 256

    load_h = pltpu.make_async_copy(hid_c, hid.at[pl.ds(0, held)], h_sem)
    load_h.start()
    small = list(zip(sources + (pex_in, peb_in, tab_in), list(params) + [pex, peb, tab]))
    small = [pltpu.make_async_copy(a, b, v_sem.at[k]) for k, (a, b) in enumerate(small)]
    small[-1].start()
    for copy in small[:-1]:
        copy.start()
    small[-1].wait()

    def wa_load(n):
        at = pl.ds(n * 256, 256)
        return pltpu.make_async_copy(fa.at[:, at], wa.at[:, at], w_sem.at[n])

    wa_load(0).start()

    load_home = pltpu.make_async_copy(hidden, home, o_sem)
    load_home.start()
    for n in range(1, blocks):
        wa_load(n).start()
    late = pl.ds(inner, wb.shape[1])
    load_bc = pltpu.make_async_copy(fb.at[:, late], wb, w_sem.at[blocks])
    load_out = pltpu.make_async_copy(fb.at[:, pl.ds(0, inner)], wo, w_sem.at[blocks + 2])
    load_old = pltpu.make_async_copy(prev, old, w_sem.at[blocks + 1])
    load_bc.start()
    load_out.start()
    load_old.start()
    for copy in small[:-1]:
        copy.wait()
    pexf[...] = pex[...].astype(f32)
    pebf[...] = peb[...].astype(f32)

    t_ids, s_ids = token_masks()
    row_ids = lax.broadcasted_iota(jnp.int32, (4 * GROUP, TOK), 0)
    k_ids = lax.broadcasted_iota(jnp.int32, (4 * GROUP, TOK), 1)
    r_ids, q_ids = row_ids // 4, row_ids % 4
    es[...] = jnp.zeros(es.shape, f32)
    same = (t_ids // LEN) == (s_ids // LEN)
    causal = same & (t_ids >= s_ids)
    tri = causal.astype(f32)
    spread_h = (
        lax.broadcasted_iota(jnp.int32, (TOK, inner), 1) // HEAD_DIM
        == lax.broadcasted_iota(jnp.int32, (TOK, inner), 0)
    ).astype(f32)

    def wide(ref):
        return jnp.concatenate([ref[...], jnp.zeros((1, TOK - heads), f32)], axis=1)

    bias, rate = wide(dtb), -jnp.exp(wide(alog))
    skip_x = jnp.dot(
        jnp.broadcast_to(wide(skip), (8, TOK)), spread_h,
        precision=HIGHEST, preferred_element_type=f32,
    )[0:1, :]

    load_h.wait()
    load_home.wait()

    def stay(n):
        hid[held + n] = home[tab[STAY, n]]

    unrolled(requests - held, 4, stay)
    left = lax.broadcasted_iota(jnp.int32, (tokens, 128), 1) < HEAD_DIM
    for n in range(blocks):
        wa_load(n).wait()
        z = jnp.dot(
            hid[...].reshape(tokens, model), wa[:, n * 256 : (n + 1) * 256],
            preferred_element_type=f32,
        )
        z0, z1 = z[:, :128], z[:, 128:]
        at = slice(n * 128, (n + 1) * 128)
        gate[:, at] = jnp.where(left, z0, pltpu.roll(z1, HEAD_DIM, 1)).astype(bf16)
        xin[:, at] = jnp.where(left, pltpu.roll(z0, HEAD_DIM, 1), z1).astype(bf16)
    load_bc.wait()
    z = jnp.dot(hid[...].reshape(tokens, model), wb[...], preferred_element_type=f32)
    bc[...] = z[:, : 2 * STATE].astype(bf16)
    dts[...] = z[:, 2 * STATE :]
    load_old.wait()

    def store(s):
        return pltpu.make_async_copy(new.at[s], nst.at[s], n_sem.at[s])

    def group(i, live):
        at = pl.ds(pl.multiple_of(i * TOK, TOK), TOK)
        first = i * GROUP
        last = jnp.zeros((TOK, TOK), jnp.int32)
        row_acc = jnp.zeros((4 * GROUP, TOK), jnp.int32)
        for r in range(GROUP):
            acc = tab[ACC, first + r] if live else tab[STAY_ACC, first - held + r]
            row_acc = jnp.where(r_ids == r, acc, row_acc)
            last = jnp.where(t_ids // LEN == r, acc, last)
            if live:
                for k in range(KCONV - 1):
                    cx[r, 13 + k : 14 + k, :] = pexf[k, pl.ds(first + r, 1), :]
                    cb[r, 13 + k : 14 + k, :] = pebf[k, pl.ds(first + r, 1), :]
        if not live:
            cx[:, 8:16, :] = jnp.zeros((GROUP, 8, inner), f32)
            cb[:, 8:16, :] = jnp.zeros((GROUP, 8, 2 * STATE), f32)
        cx[:, 16:32, :] = xin[at, :].astype(f32).reshape(GROUP, LEN, inner)
        cb[:, 16:32, :] = bc[at, :].astype(f32).reshape(GROUP, LEN, 2 * STATE)
        tot_x = cxb[...].reshape(1, 1, inner) + cxw[0:1, :].reshape(1, 1, inner) * cx[:, 13:29, :]
        tot_b = cbb[...].reshape(1, 1, 2 * STATE) + cbw[0:1, :].reshape(
            1, 1, 2 * STATE
        ) * cb[:, 13:29, :]
        for k in range(1, KCONV):
            tot_x = tot_x + cxw[k : k + 1, :].reshape(1, 1, inner) * cx[:, 13 + k : 29 + k, :]
            tot_b = tot_b + cbw[k : k + 1, :].reshape(1, 1, 2 * STATE) * cb[:, 13 + k : 29 + k, :]
        xc = silu(tot_x).reshape(TOK, inner).astype(bf16)
        bcc = silu(tot_b).reshape(TOK, 2 * STATE).astype(bf16)
        near = jnp.concatenate([xin[at, :], bc[at, :]], axis=1)
        want = q_ids + row_acc
        pick = (k_ids == LEN * r_ids + want - 3) & (want >= 3) & (q_ids < 3)
        edge = jnp.dot(pick.astype(bf16), near, preferred_element_type=f32)
        if live:
            for k in range(KCONV - 1):
                rows8 = pl.ds(pl.multiple_of(first, GROUP), GROUP)
                es[k * GROUP : (k + 1) * GROUP, :inner] = pexf[k, rows8, :]
                es[k * GROUP : (k + 1) * GROUP, inner:] = pebf[k, rows8, :]
            pick = (k_ids == GROUP * want + r_ids) & (want < 3) & (q_ids < 3)
            edge = edge + jnp.dot(
                pick.astype(bf16), es[...].astype(bf16), preferred_element_type=f32
            )
        for r in range(GROUP):
            lines = edge[4 * r : 4 * r + 4, :].astype(bf16)
            if live:
                edge_c[first + r] = lines
            else:
                edge_o[first - held + r] = lines
        b_in, c_in = bcc[:, :STATE], bcc[:, STATE:]
        xf = xc.astype(f32)
        raw = dts[at, :] + bias
        step = jnp.maximum(raw, 0.0) + jnp.log(1.0 + jnp.exp(-jnp.abs(raw)))
        decay = jnp.dot(tri, step * rate, precision=HIGHEST, preferred_element_type=f32)
        decay_t = decay.T
        step_t = step.T
        choose = (same & (s_ids % LEN == last - 1)).astype(f32)
        reach = jnp.dot(choose, decay, precision=HIGHEST, preferred_element_type=f32)
        taken = t_ids % LEN < last
        weight = jnp.where(taken, jnp.exp(jnp.minimum(reach - decay, 0.0)), 0.0) * step
        weight_x = jnp.dot(weight, spread_h, precision=HIGHEST, preferred_element_type=f32)
        scores = lax.dot_general(
            c_in, b_in, (((1,), (1,)), ((), ())), preferred_element_type=f32
        )
        scores = jnp.where(causal, scores, 0.0)
        half = s_ids < HEAD_DIM
        zero = jnp.zeros((TOK, 2 * HEAD_DIM), bf16)
        y = []
        for pair in range(heads // 2):
            mats = []
            for h in (2 * pair, 2 * pair + 1):
                gap = decay[:, h : h + 1] - decay_t[h : h + 1, :]
                mats.append(
                    (jnp.exp(jnp.minimum(gap, 0.0)) * scores * step_t[h : h + 1, :]).astype(bf16)
                )
            xp = xc[:, pair * 128 : (pair + 1) * 128]
            both = jnp.concatenate([jnp.where(half, xp, zero), jnp.where(half, zero, xp)], axis=0)
            y.append(
                jnp.dot(jnp.concatenate(mats, axis=1), both, preferred_element_type=f32)
            )
        y = jnp.concatenate(y, axis=1)
        if live:
            grow_x = jnp.dot(jnp.exp(decay), spread_h, precision=HIGHEST, preferred_element_type=f32)
            carried = [
                lax.dot_general(
                    c_in[r * LEN : (r + 1) * LEN, :], old[first + r], (((1,), (1,)), ((), ())),
                    preferred_element_type=f32,
                )
                for r in range(GROUP)
            ]
            y = y + grow_x * jnp.concatenate(carried, axis=0)
        y = y + skip_x * xf
        gated = y * silu(gate[at, :].astype(f32))
        gg[at, :] = (gated * gain[...]).astype(bf16)
        squares = jnp.sum(gated * gated, axis=1, keepdims=True)
        ss[pl.ds(i, 1), :] = jnp.broadcast_to(squares, (TOK, TOK)).T[0:1, :]

        if not live:
            out = (xf * weight_x).astype(bf16)
            for r in range(GROUP):
                lines = slice(r * LEN, (r + 1) * LEN)
                sent[first - held + r, :, :inner] = out[lines, :]
                sent[first - held + r, :, inner:] = b_in[lines, :]
            return
        xw = (xf * weight_x).T
        high = xw.astype(bf16)
        low = (xw - high.astype(f32)).astype(bf16)
        lhs = jnp.concatenate([high, low], axis=1)
        keep_t = jnp.exp(reach).T
        none = jnp.zeros((TOK, STATE), bf16)
        for pair in range(GROUP // 2):
            cut = jnp.concatenate(
                [
                    jnp.where(t_ids // LEN == r, b_in, none)
                    for r in (2 * pair, 2 * pair + 1)
                ],
                axis=1,
            )
            added = jnp.dot(
                lhs, jnp.concatenate([cut, cut], axis=0), preferred_element_type=f32
            )
            for k in (0, 1):
                r = 2 * pair + k
                s = first + r
                factor = jnp.broadcast_to(keep_t[0:heads, r * LEN : r * LEN + 1], (heads, STATE))
                was = old[s].astype(f32).reshape(heads, HEAD_DIM, STATE)
                now = factor[:, None, :] * was + added[:, k * STATE : (k + 1) * STATE].reshape(
                    heads, HEAD_DIM, STATE
                )
                new[s] = now.reshape(inner, STATE).astype(bf16)
                store(s).start()

    @pl.loop(held // GROUP, requests // GROUP)
    def _(i):
        group(i, False)

    load_out.wait()
    moving = held * LEN
    resting = tokens - moving
    pieces = part_c.shape[1]
    width = pieces * 128
    order = (1, 3, 2)

    def project(lines, peer, j, count):
        at = pl.ds(pl.multiple_of(peer * width + j * 128, 128), count * 128)
        return lax.dot_general(
            gg[lines, :], wo[at, :], (((1,), (1,)), ((), ())), preferred_element_type=f32
        ).astype(bf16)

    def rest_block(peer):
        part_o[peer] = project(slice(moving, tokens), peer, 0, pieces)

    def move_block(peer, j, count):
        out = project(slice(0, moving), peer, j, count)
        for k in range(count):
            part_c[peer, j + k] = out[:, k * 128 : (k + 1) * 128]

    def piece(ref, c):
        return ref.at[pl.ds(c * cap, cap)]

    def to_slots(q):
        n = tab[LEAVE, q]
        xmsg[q] = sent[n]
        emsg[q] = edge_o[n]

    unrolled(cols * cap, 8, to_slots)
    others = pl.ds(0, (cols - 1) * cap)
    pl.semaphore_wait(barrier, cols - 1 + rows - 1)

    def push_factors(d, carry):
        peer = (me + d) % cols
        for a, b, s_, r_ in ((xmsg, xgot, x_s, x_r), (emsg, egot, e_s, e_r)):
            pltpu.make_async_remote_copy(
                piece(a, peer), piece(b, me), s_, r_,
                device_id=(row, peer), device_id_type=MESH,
            ).start()
        return carry

    lax.fori_loop(1, cols, push_factors, 0)
    keep_x = pltpu.make_async_copy(piece(xmsg, me), piece(xgot, me), loc.at[0])
    keep_e = pltpu.make_async_copy(piece(emsg, me), piece(egot, me), loc.at[1])
    keep_x.start()
    keep_e.start()

    def send_rest(d, carry):
        peer = (row + d) % rows
        rest_block(peer)
        pltpu.make_async_remote_copy(
            part_o.at[peer], came_o.at[row], yo_s.at[d], yo_r.at[row],
            device_id=(peer, me), device_id_type=MESH,
        ).start()
        return carry

    lax.fori_loop(1, rows, send_rest, 0)

    @pl.loop(0, held // GROUP)
    def _(i):
        group(i, True)

    for k, d in enumerate(order):
        pltpu.make_async_remote_copy(
            ss, ss_in.at[row], ss_s.at[k], ss_r.at[row],
            device_id=((row + d) % rows, me), device_id_type=MESH,
        ).start()

    def send_block(peer, j, d):
        pltpu.make_async_remote_copy(
            part_c.at[peer, j], came_c.at[row, j], yc_s.at[j, d], yc_r.at[row, j],
            device_id=(peer, me), device_id_type=MESH,
        ).start()

    def first_block(d, carry):
        peer = (row + d) % rows
        move_block(peer, 0, 1)
        send_block(peer, 0, d)
        return carry

    def later_blocks(d, carry):
        peer = (row + d) % rows
        move_block(peer, 1, pieces - 1)
        for j in range(1, pieces):
            send_block(peer, j, d)
        return carry

    lax.fori_loop(1, rows, first_block, 0)
    lax.fori_loop(1, rows, later_blocks, 0)
    move_block(row, 0, 1)
    move_block(row, 1, pieces - 1)
    rest_block(row)
    total = ss[...]
    for d in order:
        peer = (row + d) % rows
        pltpu.make_async_copy(ss_in.at[peer], ss_in.at[peer], ss_r.at[peer]).wait()
        total = total + ss_in[peer]
    factor = lax.rsqrt(total / INNER + 1e-05)
    for i in range(tokens // TOK):
        line = jnp.broadcast_to(factor[i : i + 1, :], (TOK, TOK))
        scale[pl.ds(i * TOK, TOK), :] = line.T
    for d in order:
        peer = (row + d) % rows
        pltpu.make_async_copy(came_o.at[peer], came_o.at[peer], yo_r.at[peer]).wait()

    def add_rest(i, carry):
        at = pl.ds(pl.multiple_of(i * TOK, TOK), TOK)
        by = scale[pl.ds(pl.multiple_of(moving + i * TOK, TOK), TOK), :]
        for j in range(pieces):
            lanes = slice(j * 128, (j + 1) * 128)
            value = part_o[row, at, lanes].astype(f32)
            for d in order:
                value = value + came_o[(row + d) % rows, at, lanes].astype(f32)
            mix_o[j, pl.ds(i * GROUP, GROUP)] = (value * by).astype(bf16).reshape(GROUP, LEN, 128)
        return carry

    lax.fori_loop(0, resting // TOK, add_rest, 0)
    gots, mixes = (got0, got1, got2), (mix0, mix1, mix2)
    for j in range(pieces):
        mix = mixes[j]
        for d in order:
            peer = (row + d) % rows
            pltpu.make_async_copy(came_c.at[peer, j], came_c.at[peer, j], yc_r.at[peer, j]).wait()

        def add(i, carry):
            at = pl.ds(pl.multiple_of(i * TOK, TOK), TOK)
            value = part_c[row, j, at, :].astype(f32)
            for d in order:
                value = value + came_c[(row + d) % rows, j, at, :].astype(f32)
            value = (value * scale[at, :]).astype(bf16)
            mix[pl.ds(i * GROUP, GROUP)] = value.reshape(GROUP, LEN, 128)
            return carry

        lax.fori_loop(0, moving // TOK, add, 0)

        def pack(q):
            packed[j, q] = mix[tab[BACK, q]]

        unrolled(cols * cap, 16, pack)

        def push(d, carry):
            peer = (me + d) % cols
            pltpu.make_async_remote_copy(
                piece(packed.at[j], peer), piece(gots[j], me), a2a_s.at[j], a2a_r.at[j],
                device_id=(row, peer), device_id_type=MESH,
            ).start()
            return carry

        lax.fori_loop(1, cols, push, 0)
        pltpu.make_async_copy(piece(packed.at[j], me), piece(gots[j], me), loc.at[2 + j]).start()
    for j in range(pieces):
        got = gots[j]
        pltpu.make_async_copy(piece(packed.at[j], me), piece(got, me), loc.at[2 + j]).wait()

        pltpu.make_async_copy(got.at[others], got.at[others], a2a_r.at[j]).wait()

        def unpack(s):
            moved = tab[MOVED, s].astype(f32)
            away = got[tab[FROM_MSG, s]].astype(f32)
            here = mix_o[j, tab[FROM_MIX, s]].astype(f32)
            value = jnp.where(moved > 0.5, away, here)
            mixed[s, :, j * 128 : (j + 1) * 128] = value.astype(bf16)

        unrolled(requests, 8, unpack)
    for k in range(rows - 1):
        pltpu.make_async_copy(ss, ss, ss_s.at[k]).wait()
        pltpu.make_async_copy(part_o.at[0], part_o.at[0], yo_s.at[k + 1]).wait()
        for j in range(pieces):
            pltpu.make_async_copy(part_c.at[0, j], part_c.at[0, j], yc_s.at[j, k + 1]).wait()
    for j in range(pieces):
        pltpu.make_async_copy(gots[j].at[others], gots[j].at[others], a2a_s.at[j]).wait()
    keep_x.wait()
    keep_e.wait()

    for ref, s_, r_ in ((xgot, x_s, x_r), (egot, e_s, e_r)):
        pltpu.make_async_copy(ref.at[others], ref.at[others], r_).wait()
        pltpu.make_async_copy(ref.at[others], ref.at[others], s_).wait()

    @pl.loop(0, held)
    def _(s):
        store(s).wait()


def mixer(tab, hid_c, hidden, fa, fb, vectors, prev, pex, peb, rows, cols, cap):
    requests, _, model = hidden.shape
    held = hid_c.shape[0]
    tokens = requests * LEN
    inner = fa.shape[1] // 2
    width = model // rows
    pieces = width // 128
    slots = cols * cap
    rest = requests - held
    dt = hidden.dtype
    f32 = jnp.float32
    vmem = pl.BlockSpec(memory_space=pltpu.VMEM)
    hbm = pl.BlockSpec(memory_space=pltpu.HBM)
    dma = pltpu.SemaphoreType.DMA

    def body(*refs):
        mixer_kernel(rows, cols, cap, held, *refs)

    wide = inner + 2 * STATE
    mix = pltpu.VMEM((held, LEN, 128), dt)
    got = pltpu.VMEM((slots, LEN, 128), dt)
    return pl.pallas_call(
        body,
        out_shape=(
            jax.ShapeDtypeStruct((requests, LEN, width), dt),
            jax.ShapeDtypeStruct((held, inner, STATE), dt),
            jax.ShapeDtypeStruct((held, 4, wide), dt),
            jax.ShapeDtypeStruct((slots, LEN, inner + STATE), dt),
            jax.ShapeDtypeStruct((slots, 4, wide), dt),
        ),
        in_specs=[hbm] * (8 + len(vectors)),
        out_specs=(vmem, hbm, vmem, hbm, hbm),
        scratch_shapes=[
            pltpu.SMEM(tab.shape, jnp.int32),
            *[pltpu.VMEM(v.shape, v.dtype) for v in vectors],
            pltpu.VMEM(pex.shape, dt),
            pltpu.VMEM(peb.shape, dt),
            pltpu.VMEM((requests, LEN, model), dt),
            pltpu.VMEM((requests, LEN, model), dt),
            pltpu.VMEM(fa.shape, dt),
            pltpu.VMEM((fb.shape[0], fb.shape[1] - inner), dt),
            pltpu.VMEM((fb.shape[0], inner), dt),
            pltpu.VMEM((held, inner, STATE), dt),
            pltpu.VMEM((tokens, inner), dt),
            pltpu.VMEM((tokens, inner), dt),
            pltpu.VMEM((tokens, 2 * STATE), dt),
            pltpu.VMEM((tokens, 128), f32),
            pltpu.VMEM((tokens, inner), dt),
            pltpu.VMEM((8, 128), f32),
            pltpu.VMEM((GROUP, 32, inner), f32),
            pltpu.VMEM((GROUP, 32, 2 * STATE), f32),
            pltpu.VMEM((3, held, inner), f32),
            pltpu.VMEM((3, held, 2 * STATE), f32),
            pltpu.VMEM((TOK, wide), f32),
            pltpu.VMEM((held, inner, STATE), dt),
            pltpu.VMEM((rest, LEN, inner + STATE), dt),
            pltpu.VMEM((rest, 4, wide), dt),
            pltpu.VMEM((slots, LEN, inner + STATE), dt),
            pltpu.VMEM((slots, 4, wide), dt),
            pltpu.VMEM((rows, rest * LEN, width), dt),
            pltpu.VMEM((rows, pieces, held * LEN, 128), dt),
            pltpu.VMEM((rows, rest * LEN, width), dt),
            pltpu.VMEM((rows, pieces, held * LEN, 128), dt),
            pltpu.VMEM((rows, 8, 128), f32),
            pltpu.VMEM((tokens, 128), f32),
            pltpu.VMEM((pieces, rest, LEN, 128), dt),
            mix, mix, mix,
            pltpu.VMEM((pieces, slots, LEN, 128), dt),
            got, got, got,
            dma(()), dma(()), dma((fa.shape[1] // 256 + 3,)), dma((held,)),
            dma((len(vectors) + 3,)), dma((2 + pieces,)), dma((3,)), dma((rows,)),
            dma((rows,)), dma((rows,)), dma((pieces, rows)), dma((rows, pieces)),
            dma((pieces,)), dma((pieces,)),
            dma(()), dma(()), dma(()), dma(()),
        ],
        compiler_params=pltpu.CompilerParams(
            collective_id=1, has_side_effects=True, vmem_limit_bytes=60 << 20
        ),
        name="mixer",
    )(tab, hid_c, hidden, fa, fb, *vectors, prev, pex, peb)


def arrive_kernel(
    tab_in, xgot_in, egot_in, edge_in, nst_in, nst, nex, neb,
    tab, xgot, egot, edge, was, xs, bs, ex, eb, new, n_sem, m_sem, l_sem,
):
    f32, bf16 = jnp.float32, jnp.bfloat16
    count, inner = new.shape[0], new.shape[1]
    loads = [
        pltpu.make_async_copy(a, b, l_sem.at[k])
        for k, (a, b) in enumerate(
            ((tab_in, tab), (xgot_in, xgot), (nst_in, was), (egot_in, egot), (edge_in, edge))
        )
    ]
    for copy in loads:
        copy.start()
    loads[0].wait()

    def place(s):
        return pltpu.make_async_copy(was.at[s], nst.at[tab[POS, s]], m_sem.at[s])

    loads[1].wait()
    loads[2].wait()

    @pl.loop(0, count)
    def _(s):
        place(s).start()

    t_ids, _ = token_masks()
    none = jnp.zeros((TOK, STATE), bf16)

    def store(u):
        return pltpu.make_async_copy(new.at[u], nst.at[tab[POS_O, u]], n_sem.at[u])

    @pl.loop(0, count // GROUP)
    def _(i):
        for r in range(GROUP):
            slot = tab[PICK_O, i * GROUP + r]
            xs[r] = xgot[slot, :, :inner]
            bs[r] = xgot[slot, :, inner:]
        lhs = xs[...].reshape(TOK, inner).astype(f32).T.astype(bf16)
        b_in = bs[...].reshape(TOK, STATE)
        for pair in range(GROUP // 2):
            cut = jnp.concatenate(
                [
                    jnp.where(t_ids // LEN == r, b_in, none)
                    for r in (2 * pair, 2 * pair + 1)
                ],
                axis=1,
            )
            out = jnp.dot(lhs, cut, preferred_element_type=f32).astype(bf16)
            for k in (0, 1):
                u = i * GROUP + 2 * pair + k
                new[u] = out[:, k * STATE : (k + 1) * STATE]
                store(u).start()

    for copy in loads[3:]:
        copy.wait()

    @pl.loop(0, count)
    def _(u):
        for source, k, spot in (
            (egot, tab[PICK_O, u], tab[POS_O, u]), (edge, u, tab[POS, u])
        ):
            lines = source[k].astype(f32)
            at = pl.ds(spot, 1)
            for q in range(KCONV - 1):
                ex[q, at, :] = lines[q : q + 1, :inner]
                eb[q, at, :] = lines[q : q + 1, inner:]

    nex[...] = ex[...].astype(bf16)
    neb[...] = eb[...].astype(bf16)

    @pl.loop(0, count)
    def _(u):
        store(u).wait()
        place(u).wait()


def arrive(tab, xgot, egot, edge, nst):
    count, inner, _ = nst.shape
    requests = 2 * count
    dt, f32 = nst.dtype, jnp.float32
    vmem = pl.BlockSpec(memory_space=pltpu.VMEM)
    hbm = pl.BlockSpec(memory_space=pltpu.HBM)
    return pl.pallas_call(
        arrive_kernel,
        out_shape=(
            jax.ShapeDtypeStruct((requests, inner, STATE), dt),
            jax.ShapeDtypeStruct((3, requests, inner), dt),
            jax.ShapeDtypeStruct((3, requests, 2 * STATE), dt),
        ),
        in_specs=[hbm] * 5,
        out_specs=(hbm, vmem, vmem),
        scratch_shapes=[
            pltpu.SMEM(tab.shape, jnp.int32),
            pltpu.VMEM(xgot.shape, dt),
            pltpu.VMEM(egot.shape, dt),
            pltpu.VMEM(edge.shape, dt),
            pltpu.VMEM(nst.shape, dt),
            pltpu.VMEM((GROUP, LEN, inner), dt),
            pltpu.VMEM((GROUP, LEN, STATE), dt),
            pltpu.VMEM((3, requests, inner), f32),
            pltpu.VMEM((3, requests, 2 * STATE), f32),
            pltpu.VMEM((count, inner, STATE), dt),
            pltpu.SemaphoreType.DMA((count,)),
            pltpu.SemaphoreType.DMA((count,)),
            pltpu.SemaphoreType.DMA((5,)),
        ],
        compiler_params=pltpu.CompilerParams(vmem_limit_bytes=60 << 20),
        name="arrive",
    )(tab, xgot, egot, edge, nst)


def per_device(
    hidden, w_zx, w_bc, w_dt, w_out, dt_bias, a_log, d_skip, conv_x_w, conv_x_b,
    conv_bc_w, conv_bc_b, norm_gain, prev_state, prev_edge_x, prev_edge_bc,
    holder, continued, owner, accepted,
):
    rows, cols = lax.axis_size("row"), lax.axis_size("col")
    tokens, model = hidden.shape
    requests = tokens // LEN
    heads = dt_bias.shape[0]
    inner = heads * HEAD_DIM
    held = prev_state.shape[0]
    cap = 2 * ((requests // 4 + cols - 1) // cols)
    code = owner + 64 * (continued == 1).astype(jnp.int32) + 128 * accepted
    tab = route(code.reshape(cols, requests), held)
    hidden = hidden.reshape(requests, LEN, model)
    hid_c, fa, fb = gather_all(tab, hidden, w_zx, w_out, w_bc, w_dt.T, rows, cols, cap, held)
    vectors = (
        dt_bias[None, :], a_log[None, :], d_skip[None, :],
        conv_x_w, conv_x_b[None, :], conv_bc_w, conv_bc_b[None, :], norm_gain[None, :],
    )
    mixed, moved, edge, xgot, egot = mixer(
        tab, hid_c, hidden, fa, fb, vectors, prev_state.reshape(held, inner, STATE),
        prev_edge_x.transpose(1, 0, 2), prev_edge_bc.transpose(1, 0, 2),
        rows, cols, cap,
    )
    states, new_x, new_bc = arrive(tab, xgot, egot, edge, moved)
    return (
        mixed.reshape(tokens, model // rows),
        states.reshape(requests, heads, HEAD_DIM, STATE),
        new_x.transpose(1, 0, 2),
        new_bc.transpose(1, 0, 2),
    )


def solution(mesh):
    return jax.shard_map(
        per_device,
        mesh=mesh,
        in_specs=(
            P("col", None),
            P("col", "row"),
            P("col", None),
            P("col", "row"),
            P("col", "row"),
            P("row"),
            P("row"),
            P("row"),
            P(None, "row"),
            P("row"),
            P(),
            P(),
            P("row"),
            P("col", "row", None, None),
            P("col", None, "row"),
            P("col", None, None),
            P(),
            P(),
            P(),
            P(),
        ),
        out_specs=(
            P("col", "row"),
            P("col", "row", None, None),
            P("col", None, "row"),
            P("col", None, None),
        ),
        check_vma=False,
    )
```

```python
import jax
import jax.numpy as jnp
from jax import lax
from jax.experimental import pallas as pl
from jax.experimental.pallas import tpu as pltpu
from jax.sharding import PartitionSpec as P

HEAD_DIM = 64
STATE = 128
KCONV = 4
LEN = 16
INNER = 2048
SIDE = 4
GROUP = 8
TOK = GROUP * LEN
MESH = pl.DeviceIdType.MESH
HIGHEST = lax.Precision.HIGHEST


def route_kernel(held, code, out):
    f32, bf16 = jnp.float32, jnp.bfloat16
    me = lax.axis_index("col")
    groups, requests = code.shape
    value = code[...]
    o, c, a = value & 63, (value >> 6) & 1, value >> 7

    def dot(x, y):
        return jnp.dot(x.astype(bf16), y.astype(bf16), preferred_element_type=f32)

    def dot0(x, y):
        return lax.dot_general(
            x.astype(bf16), y.astype(bf16), (((0,), (0,)), ((), ())), preferred_element_type=f32
        )

    def ids(shape, dim):
        return lax.broadcasted_iota(jnp.int32, shape, dim)

    below = (ids((requests, requests), 0) < ids((requests, requests), 1)).astype(f32)
    prior = (ids((groups, groups), 1) < ids((groups, groups), 0)).astype(f32)
    lane = ids((groups, 128), 1).astype(f32)
    group = ids((groups, 128), 0).astype(f32)
    spots, inside, starts = [], [], []
    for kind in (1, 0):
        mask = ((o == me) & (c == kind)).astype(f32)
        rank = dot(mask, below)
        count = jnp.broadcast_to(jnp.sum(mask, axis=1, keepdims=True), (groups, 128))
        start = dot(prior, count)
        hot = ((start <= lane) & (lane < start + count)).astype(f32)
        spots.append((jnp.where(mask > 0, rank, -1.0), hot))
        inside.append(rank)
        starts.append(start)
    rank_all, start_all = inside[0] + inside[1], starts[0] + starts[1]
    picks, places, taken = [], [], []
    for k in (0, 1):
        spot, hot = spots[k]
        order = jnp.sum(hot * (lane - starts[k]), axis=0, keepdims=True)
        any_hot = jnp.sum(hot, axis=0, keepdims=True)
        order = jnp.where(any_hot > 0, order, -5.0)
        match = (dot0(spot, hot) == order).astype(f32)
        picks.append(jnp.sum(hot * (2 * group + lane - starts[k]), axis=0, keepdims=True))
        places.append(
            jnp.sum(hot * start_all, axis=0, keepdims=True)
            + jnp.sum(match * dot0(rank_all, hot), axis=0, keepdims=True)
        )
        taken.append(jnp.sum(match * dot0(a, hot), axis=0, keepdims=True))
    lane_i, group_i = ids((groups, 128), 1), ids((groups, 128), 0)
    back = jnp.sum(
        jnp.where(lane_i // 2 == group_i, starts[0] + (lane_i % 2).astype(f32), 0.0),
        axis=0, keepdims=True,
    )
    back = jnp.minimum(back, held - 1.0)

    def my_row(x, fill):
        row = jnp.sum(
            jnp.where(ids((groups, requests), 0) == me, x, 0).astype(f32), axis=0, keepdims=True
        )
        rest = jnp.full((1, 128 - requests), fill, f32)
        return jnp.concatenate([row, rest], axis=1)

    o_row, c_row, a_row = my_row(o, 99.0), my_row(c, 2.0), my_row(a, 0.0)

    def column(row):
        return jnp.broadcast_to(row, (128, 128)).T

    o_col, c_col, a_col = column(o_row), column(c_row), column(a_row)
    ii, jj = ids((128, 128), 0), ids((128, 128), 1)
    alike = (o_col == o_row) & (c_col == c_row)
    rank_row = jnp.sum((alike & (ii < jj)).astype(f32), axis=0, keepdims=True)
    rank_col = jnp.sum((alike & (jj < ii)).astype(f32), axis=1, keepdims=True)
    nth_row = jnp.sum(((c_col == 0) & (ii < jj)).astype(f32), axis=0, keepdims=True)
    nth_col = jnp.sum(((c_row == 0) & (jj < ii)).astype(f32), axis=1, keepdims=True)
    key_row = 2 * o_row + rank_row
    key_col = 2 * o_col + rank_col
    fi, fj = ii.astype(f32), jj.astype(f32)
    goes = (c_col == 1) & (key_col == fj)
    leaves = (c_col == 0) & (key_col == fj)
    stays = (c_col == 0) & (nth_col == fj)

    def total(mask, x):
        return jnp.sum(jnp.where(mask, x, 0.0), axis=0, keepdims=True)

    table = (
        total(goes, fi), picks[0], back,
        jnp.where(c_row == 1, key_row, 0.0), jnp.where(c_row == 0, nth_row, 0.0),
        (c_row == 1).astype(f32),
        total(stays, fi), total(stays, key_col), total(stays, a_col),
        taken[0], places[0], picks[1], places[1], total(leaves, nth_col),
    )
    for k, line in enumerate(table):
        out[k : k + 1, :] = line.astype(jnp.int32)
    out[len(table) :, :] = jnp.zeros((16 - len(table), 128), jnp.int32)


SEND, PICK, BACK, FROM_MSG, FROM_MIX, MOVED, STAY, STAY_KEY, STAY_ACC, ACC, POS, PICK_O, POS_O, LEAVE = range(14)


def route(code, held):
    vmem = pl.BlockSpec(memory_space=pltpu.VMEM)

    def body(*refs):
        route_kernel(held, *refs)

    return pl.pallas_call(
        body, out_shape=jax.ShapeDtypeStruct((16, 128), jnp.int32),
        in_specs=[vmem], out_specs=vmem, name="route",
        compiler_params=pltpu.CompilerParams(vmem_limit_bytes=60 << 20),
    )(code)


def unrolled(count, step, body):
    def some(i, carry):
        for k in range(step):
            body(i * step + k)
        return carry

    lax.fori_loop(0, count // step, some, 0)


def greet(row, me, rows, cols):
    barrier = pltpu.get_barrier_semaphore()

    def along_col(d, carry):
        pl.semaphore_signal(
            barrier, inc=1, device_id=(row, (me + d) % cols), device_id_type=MESH
        )
        return carry

    lax.fori_loop(1, cols, along_col, 0)

    def along_row(d, carry):
        pl.semaphore_signal(
            barrier, inc=1, device_id=((row + d) % rows, me), device_id_type=MESH
        )
        return carry

    lax.fori_loop(1, rows, along_row, 0)
    return barrier


def gather_kernel(
    rows, cols, cap, tab_in, hidden, wa, w_out, w_bc, w_dt_in, hid_full, fa, fb,
    tab, w_dt, wb, sl, packed, got, own, loc, a2a_s, a2a_r, gone, twin, war, wbr, y_s, y_r,
):
    row, me = lax.axis_index("row"), lax.axis_index("col")
    barrier = greet(row, me, rows, cols)
    width = sl.shape[2]
    half = own.shape[0] // 2
    depth = wa.shape[0]

    def cols_of(r):
        return pl.ds(pl.multiple_of(r * width, 128), width)

    def block(ref, c):
        return ref.at[pl.ds(pl.multiple_of(c * depth, 16), depth), :]

    load = pltpu.make_async_copy(hidden.at[:, :, cols_of(row)], sl, loc.at[0])
    load.start()
    inner = w_out.shape[1]
    states = w_bc.shape[1]
    heads = w_dt_in.shape[0]
    loads = (
        pltpu.make_async_copy(tab_in, tab, loc.at[5]),
        pltpu.make_async_copy(w_dt_in, w_dt, loc.at[6]),
        pltpu.make_async_copy(w_out, wb.at[:, pl.ds(0, inner)], loc.at[7]),
        pltpu.make_async_copy(w_bc, wb.at[:, pl.ds(inner, states)], loc.at[8]),
    )
    for copy in loads:
        copy.start()
    for copy in loads:
        copy.wait()
    square = jnp.concatenate([w_dt[...].astype(jnp.float32), jnp.zeros((heads, 128 - depth), jnp.float32)], axis=1)
    square = jnp.concatenate([square, jnp.zeros((128 - heads, 128), jnp.float32)], axis=0).T
    wb[:, inner + states :] = square[:depth, :].astype(wb.dtype)
    keep_a = pltpu.make_async_copy(wa, block(fa, me), loc.at[1])
    keep_b = pltpu.make_async_copy(wb, block(fb, me), loc.at[2])
    keep_a.start()
    keep_b.start()
    load.wait()

    def pack(s):
        packed[s] = sl[tab[SEND, s]]

    unrolled(cols * cap, 8, pack)
    pl.semaphore_wait(barrier, cols - 1 + rows - 1)

    def piece(ref, c):
        return ref.at[pl.ds(c * cap, cap)]

    def push(d, carry):
        peer = (me + d) % cols
        pltpu.make_async_remote_copy(
            piece(packed, peer), piece(got, me), a2a_s, a2a_r,
            device_id=(row, peer), device_id_type=MESH,
        ).start()
        return carry

    lax.fori_loop(1, cols, push, 0)
    keep_m = pltpu.make_async_copy(piece(packed, me), piece(got, me), loc.at[3])
    keep_m.start()

    core = me % 2
    x = (me // 2) % SIDE
    z = me // (2 * SIDE)
    a = x + core * (z - x)
    b = z + core * (x - z)

    def at(pa, pb):
        pa, pb = (pa + SIDE) % SIDE, (pb + SIDE) % SIDE
        px = pa + core * (pb - pa)
        pz = pb + core * (pa - pb)
        return (pz * SIDE + px) * 2 + core

    sibling = me + 1 - 2 * core
    sent = [0, 0]

    def send(which, src, c, dest):
        full, rs = ((fa, war), (fb, wbr))[which]
        sent[which] += 1
        rs = twin.at[which] if dest is sibling else rs.at[c]
        pltpu.make_async_remote_copy(
            src, block(full, c), gone.at[which], rs,
            device_id=(row, dest), device_id_type=MESH,
        ).start()

    def forward(which, c, dest):
        send(which, block((fa, fb)[which], c), c, dest)

    def arrived(which, c):
        full, rs = ((fa, war), (fb, wbr))[which]
        pltpu.make_async_copy(block(full, c), block(full, c), rs.at[c]).wait()

    up, down = at(a + 1, b), at(a - 1, b)
    far = at(a + 2, b)
    over, under = at(a, b + 1), at(a, b - 1)
    for dest in (up, down, over, under, sibling):
        for which, src in ((0, wa), (1, wb)):
            send(which, src, me, dest)
    arrived(0, down)
    forward(0, down, up)
    arrived(1, up)
    forward(1, up, down)
    arrived(1, down)
    arrived(0, up)
    for c in (down, up):
        for which in (0, 1):
            for dest in (over, under, sibling):
                forward(which, c, dest)
    keep_m.wait()

    others = pl.ds(0, (cols - 1) * cap)
    pltpu.make_async_copy(got.at[others], got.at[others], a2a_r).wait()

    def unpack(s):
        own[s] = got[tab[PICK, s]]

    unrolled(own.shape[0], 8, unpack)

    def part(ref, h, r):
        return ref.at[pl.ds(h * half, half), :, cols_of(r)]

    right, left = (row + 1) % rows, (row + rows - 1) % rows
    far_row = (row + 2) % rows
    for k, dest in ((0, right), (1, left)):
        for h in (0, 1):
            pltpu.make_async_remote_copy(
                own.at[pl.ds(h * half, half)], part(hid_full, h, row),
                y_s.at[2 * k + h], y_r.at[row, h],
                device_id=(dest, me), device_id_type=MESH,
            ).start()
    keep_y = pltpu.make_async_copy(own, hid_full.at[:, :, cols_of(row)], loc.at[4])
    keep_y.start()

    for which in (0, 1):
        arrived(which, far)
        for dest in (over, under, sibling):
            forward(which, far, dest)
    for k in (0, 1, -1, 2):
        low, high = at(a + k, b - 1), at(a + k, b + 1)
        arrived(0, low)
        forward(0, low, over)
        arrived(1, high)
        forward(1, high, under)
        arrived(1, low)
        arrived(0, high)
        for which in (0, 1):
            forward(which, low, sibling)
            forward(which, high, sibling)

    def y_here(h, r):
        pltpu.make_async_copy(part(hid_full, h, r), part(hid_full, h, r), y_r.at[r, h]).wait()

    y_here(0, left)
    pltpu.make_async_remote_copy(
        part(hid_full, 0, left), part(hid_full, 0, left), y_s.at[4], y_r.at[left, 0],
        device_id=(right, me), device_id_type=MESH,
    ).start()
    y_here(1, right)
    pltpu.make_async_remote_copy(
        part(hid_full, 1, right), part(hid_full, 1, right), y_s.at[5], y_r.at[right, 1],
        device_id=(left, me), device_id_type=MESH,
    ).start()
    y_here(1, left)
    y_here(0, right)
    for k in (0, 1, -1, 2):
        opposite = at(a + k, b + 2)
        for which in (0, 1):
            arrived(which, opposite)
            forward(which, opposite, sibling)
    y_here(0, far_row)
    y_here(1, far_row)

    for which, ref in ((0, fa), (1, fb)):
        lines = pl.ds(0, (cols // 2) * depth)
        pltpu.make_async_copy(ref.at[lines, :], ref.at[lines, :], twin.at[which]).wait()
    keep_a.wait()
    keep_b.wait()
    keep_y.wait()

    pltpu.make_async_copy(packed.at[others], packed.at[others], a2a_s).wait()

    for which, ref in ((0, fa), (1, fb)):
        lines = pl.ds(0, sent[which] * depth)
        pltpu.make_async_copy(ref.at[lines, :], ref.at[lines, :], gone.at[which]).wait()
    for k in range(6):
        h = (0, 1, 0, 1, 0, 1)[k]
        pltpu.make_async_copy(part(hid_full, h, row), part(hid_full, h, row), y_s.at[k]).wait()


def gather_all(tab, hidden, wa, w_out, w_bc, w_dt, rows, cols, cap, held):
    requests, _, model = hidden.shape
    width = model // rows
    dt = hidden.dtype
    hbm = pl.BlockSpec(memory_space=pltpu.HBM)
    dma = pltpu.SemaphoreType.DMA
    depth = wa.shape[0]
    rest = w_out.shape[1] + w_bc.shape[1] + 128

    def body(*refs):
        gather_kernel(rows, cols, cap, *refs)

    return pl.pallas_call(
        body,
        out_shape=(
            jax.ShapeDtypeStruct((held, LEN, model), dt),
            jax.ShapeDtypeStruct((depth * cols, wa.shape[1]), dt),
            jax.ShapeDtypeStruct((depth * cols, rest), dt),
        ),
        in_specs=[hbm] * 6,
        out_specs=(hbm, hbm, hbm),
        scratch_shapes=[
            pltpu.SMEM(tab.shape, jnp.int32),
            pltpu.VMEM(w_dt.shape, dt),
            pltpu.VMEM((depth, rest), dt),
            pltpu.VMEM((requests, LEN, width), dt),
            pltpu.VMEM((cols * cap, LEN, width), dt),
            pltpu.VMEM((cols * cap, LEN, width), dt),
            pltpu.VMEM((held, LEN, width), dt),
            dma((9,)), dma(()), dma(()),
            dma((2,)), dma((2,)), dma((cols,)), dma((cols,)),
            dma((6,)), dma((rows, 2)),
        ],
        compiler_params=pltpu.CompilerParams(
            collective_id=0, has_side_effects=True, vmem_limit_bytes=60 << 20
        ),
        name="gather_all",
    )(tab, hidden, wa, w_out, w_bc, w_dt)


def silu(v):
    return v / (1.0 + jnp.exp(-v))


def token_masks():
    t_ids = lax.broadcasted_iota(jnp.int32, (TOK, TOK), 0)
    s_ids = lax.broadcasted_iota(jnp.int32, (TOK, TOK), 1)
    return t_ids, s_ids


def mixer_kernel(
    rows, cols, cap, held, tab_in, hid_c, hidden, fa, fb, *refs,
):
    sources, refs = refs[:8], refs[8:]
    prev, pex_in, peb_in, mixed, nst, edge_c, xgot, egot, tab, *refs = refs
    params, refs = refs[:8], refs[8:]
    dtb, alog, skip, cxw, cxb, cbw, cbb, gain = params
    (
        pex, peb, hid, home, wa, wb, wo, old, gate, xin, bc, dts, gg, ss, cx, cb, pexf, pebf, es,
        new, sent, edge_o, xmsg, emsg, part_o, part_c, came_o, came_c, ss_in, scale, mix_o,
        mix, packed, got,
        h_sem, o_sem, w_sem, n_sem, v_sem, loc, ss_s, ss_r, yo_s, yo_r, yc_s, yc_r,
        a2a_s, a2a_r, x_s, x_r, e_s, e_r,
    ) = refs
    row, me = lax.axis_index("row"), lax.axis_index("col")
    barrier = greet(row, me, rows, cols)
    f32, bf16 = jnp.float32, jnp.bfloat16
    inner = gain.shape[1]
    requests = hid.shape[0]
    tokens = requests * LEN
    model = hid.shape[2]
    heads = inner // HEAD_DIM
    blocks = wa.shape[1] // 256

    load_h = pltpu.make_async_copy(hid_c, hid.at[pl.ds(0, held)], h_sem)
    load_h.start()
    small = list(zip(sources + (pex_in, peb_in, tab_in), list(params) + [pex, peb, tab]))
    small = [pltpu.make_async_copy(a, b, v_sem.at[k]) for k, (a, b) in enumerate(small)]
    small[-1].start()
    for copy in small[:-1]:
        copy.start()
    small[-1].wait()

    def wa_load(n):
        at = pl.ds(n * 256, 256)
        return pltpu.make_async_copy(fa.at[:, at], wa.at[:, at], w_sem.at[n])

    wa_load(0).start()

    load_home = pltpu.make_async_copy(hidden, home, o_sem)
    load_home.start()
    for n in range(1, blocks):
        wa_load(n).start()
    late = pl.ds(inner, wb.shape[1])
    load_bc = pltpu.make_async_copy(fb.at[:, late], wb, w_sem.at[blocks])
    load_out = pltpu.make_async_copy(fb.at[:, pl.ds(0, inner)], wo, w_sem.at[blocks + 2])
    load_old = pltpu.make_async_copy(prev, old, w_sem.at[blocks + 1])
    load_bc.start()
    load_out.start()
    load_old.start()
    for copy in small[:-1]:
        copy.wait()
    pexf[...] = pex[...].astype(f32)
    pebf[...] = peb[...].astype(f32)

    t_ids, s_ids = token_masks()
    row_ids = lax.broadcasted_iota(jnp.int32, (4 * GROUP, TOK), 0)
    k_ids = lax.broadcasted_iota(jnp.int32, (4 * GROUP, TOK), 1)
    r_ids, q_ids = row_ids // 4, row_ids % 4
    es[...] = jnp.zeros(es.shape, f32)
    same = (t_ids // LEN) == (s_ids // LEN)
    causal = same & (t_ids >= s_ids)
    tri = causal.astype(f32)
    spread_h = (
        lax.broadcasted_iota(jnp.int32, (TOK, inner), 1) // HEAD_DIM
        == lax.broadcasted_iota(jnp.int32, (TOK, inner), 0)
    ).astype(f32)

    def wide(ref):
        return jnp.concatenate([ref[...], jnp.zeros((1, TOK - heads), f32)], axis=1)

    bias, rate = wide(dtb), -jnp.exp(wide(alog))
    skip_x = jnp.dot(
        jnp.broadcast_to(wide(skip), (8, TOK)), spread_h,
        precision=HIGHEST, preferred_element_type=f32,
    )[0:1, :]

    load_h.wait()
    load_home.wait()

    def stay(n):
        hid[held + n] = home[tab[STAY, n]]

    unrolled(requests - held, 4, stay)
    left = lax.broadcasted_iota(jnp.int32, (tokens, 128), 1) < HEAD_DIM
    for n in range(blocks):
        wa_load(n).wait()
        z = jnp.dot(
            hid[...].reshape(tokens, model), wa[:, n * 256 : (n + 1) * 256],
            preferred_element_type=f32,
        )
        z0, z1 = z[:, :128], z[:, 128:]
        at = slice(n * 128, (n + 1) * 128)
        gate[:, at] = jnp.where(left, z0, pltpu.roll(z1, HEAD_DIM, 1)).astype(bf16)
        xin[:, at] = jnp.where(left, pltpu.roll(z0, HEAD_DIM, 1), z1).astype(bf16)
    load_bc.wait()
    z = jnp.dot(hid[...].reshape(tokens, model), wb[...], preferred_element_type=f32)
    bc[...] = z[:, : 2 * STATE].astype(bf16)
    dts[...] = z[:, 2 * STATE :]
    load_old.wait()

    def store(s):
        return pltpu.make_async_copy(new.at[s], nst.at[s], n_sem.at[s])

    def group(i, live):
        at = pl.ds(pl.multiple_of(i * TOK, TOK), TOK)
        first = i * GROUP
        last = jnp.zeros((TOK, TOK), jnp.int32)
        row_acc = jnp.zeros((4 * GROUP, TOK), jnp.int32)
        for r in range(GROUP):
            acc = tab[ACC, first + r] if live else tab[STAY_ACC, first - held + r]
            row_acc = jnp.where(r_ids == r, acc, row_acc)
            last = jnp.where(t_ids // LEN == r, acc, last)
            if live:
                for k in range(KCONV - 1):
                    cx[r, 13 + k : 14 + k, :] = pexf[k, pl.ds(first + r, 1), :]
                    cb[r, 13 + k : 14 + k, :] = pebf[k, pl.ds(first + r, 1), :]
        if not live:
            cx[:, 8:16, :] = jnp.zeros((GROUP, 8, inner), f32)
            cb[:, 8:16, :] = jnp.zeros((GROUP, 8, 2 * STATE), f32)
        cx[:, 16:32, :] = xin[at, :].astype(f32).reshape(GROUP, LEN, inner)
        cb[:, 16:32, :] = bc[at, :].astype(f32).reshape(GROUP, LEN, 2 * STATE)
        tot_x = cxb[...].reshape(1, 1, inner) + cxw[0:1, :].reshape(1, 1, inner) * cx[:, 13:29, :]
        tot_b = cbb[...].reshape(1, 1, 2 * STATE) + cbw[0:1, :].reshape(
            1, 1, 2 * STATE
        ) * cb[:, 13:29, :]
        for k in range(1, KCONV):
            tot_x = tot_x + cxw[k : k + 1, :].reshape(1, 1, inner) * cx[:, 13 + k : 29 + k, :]
            tot_b = tot_b + cbw[k : k + 1, :].reshape(1, 1, 2 * STATE) * cb[:, 13 + k : 29 + k, :]
        xc = silu(tot_x).reshape(TOK, inner).astype(bf16)
        bcc = silu(tot_b).reshape(TOK, 2 * STATE).astype(bf16)
        near = jnp.concatenate([xin[at, :], bc[at, :]], axis=1)
        want = q_ids + row_acc
        pick = (k_ids == LEN * r_ids + want - 3) & (want >= 3) & (q_ids < 3)
        edge = jnp.dot(pick.astype(bf16), near, preferred_element_type=f32)
        if live:
            for k in range(KCONV - 1):
                rows8 = pl.ds(pl.multiple_of(first, GROUP), GROUP)
                es[k * GROUP : (k + 1) * GROUP, :inner] = pexf[k, rows8, :]
                es[k * GROUP : (k + 1) * GROUP, inner:] = pebf[k, rows8, :]
            pick = (k_ids == GROUP * want + r_ids) & (want < 3) & (q_ids < 3)
            edge = edge + jnp.dot(
                pick.astype(bf16), es[...].astype(bf16), preferred_element_type=f32
            )
        for r in range(GROUP):
            lines = edge[4 * r : 4 * r + 4, :].astype(bf16)
            if live:
                edge_c[first + r] = lines
            else:
                edge_o[first - held + r] = lines
        b_in, c_in = bcc[:, :STATE], bcc[:, STATE:]
        xf = xc.astype(f32)
        raw = dts[at, :] + bias
        step = jnp.maximum(raw, 0.0) + jnp.log(1.0 + jnp.exp(-jnp.abs(raw)))
        decay = jnp.dot(tri, step * rate, precision=HIGHEST, preferred_element_type=f32)
        decay_t = decay.T
        step_t = step.T
        choose = (same & (s_ids % LEN == last - 1)).astype(f32)
        reach = jnp.dot(choose, decay, precision=HIGHEST, preferred_element_type=f32)
        taken = t_ids % LEN < last
        weight = jnp.where(taken, jnp.exp(jnp.minimum(reach - decay, 0.0)), 0.0) * step
        weight_x = jnp.dot(weight, spread_h, precision=HIGHEST, preferred_element_type=f32)
        scores = lax.dot_general(
            c_in, b_in, (((1,), (1,)), ((), ())), preferred_element_type=f32
        )
        scores = jnp.where(causal, scores, 0.0)
        half = s_ids < HEAD_DIM
        zero = jnp.zeros((TOK, 2 * HEAD_DIM), bf16)
        y = []
        for pair in range(heads // 2):
            mats = []
            for h in (2 * pair, 2 * pair + 1):
                gap = decay[:, h : h + 1] - decay_t[h : h + 1, :]
                mats.append(
                    (jnp.exp(jnp.minimum(gap, 0.0)) * scores * step_t[h : h + 1, :]).astype(bf16)
                )
            xp = xc[:, pair * 128 : (pair + 1) * 128]
            both = jnp.concatenate([jnp.where(half, xp, zero), jnp.where(half, zero, xp)], axis=0)
            y.append(
                jnp.dot(jnp.concatenate(mats, axis=1), both, preferred_element_type=f32)
            )
        y = jnp.concatenate(y, axis=1)
        if live:
            grow_x = jnp.dot(jnp.exp(decay), spread_h, precision=HIGHEST, preferred_element_type=f32)
            carried = [
                lax.dot_general(
                    c_in[r * LEN : (r + 1) * LEN, :], old[first + r], (((1,), (1,)), ((), ())),
                    preferred_element_type=f32,
                )
                for r in range(GROUP)
            ]
            y = y + grow_x * jnp.concatenate(carried, axis=0)
        y = y + skip_x * xf
        gated = y * silu(gate[at, :].astype(f32))
        gg[at, :] = (gated * gain[...]).astype(bf16)
        squares = jnp.sum(gated * gated, axis=1, keepdims=True)
        ss[pl.ds(i, 1), :] = jnp.broadcast_to(squares, (TOK, TOK)).T[0:1, :]

        if not live:
            out = (xf * weight_x).astype(bf16)
            for r in range(GROUP):
                lines = slice(r * LEN, (r + 1) * LEN)
                sent[first - held + r, :, :inner] = out[lines, :]
                sent[first - held + r, :, inner:] = b_in[lines, :]
            return
        xw = (xf * weight_x).T
        high = xw.astype(bf16)
        low = (xw - high.astype(f32)).astype(bf16)
        lhs = jnp.concatenate([high, low], axis=1)
        keep_t = jnp.exp(reach).T
        none = jnp.zeros((TOK, STATE), bf16)
        for pair in range(GROUP // 2):
            cut = jnp.concatenate(
                [
                    jnp.where(t_ids // LEN == r, b_in, none)
                    for r in (2 * pair, 2 * pair + 1)
                ],
                axis=1,
            )
            added = jnp.dot(
                lhs, jnp.concatenate([cut, cut], axis=0), preferred_element_type=f32
            )
            for k in (0, 1):
                r = 2 * pair + k
                s = first + r
                factor = jnp.broadcast_to(keep_t[0:heads, r * LEN : r * LEN + 1], (heads, STATE))
                was = old[s].astype(f32).reshape(heads, HEAD_DIM, STATE)
                now = factor[:, None, :] * was + added[:, k * STATE : (k + 1) * STATE].reshape(
                    heads, HEAD_DIM, STATE
                )
                new[s] = now.reshape(inner, STATE).astype(bf16)
                store(s).start()

    @pl.loop(held // GROUP, requests // GROUP)
    def _(i):
        group(i, False)

    load_out.wait()
    moving = held * LEN
    resting = tokens - moving
    width = part_c.shape[2]
    pieces = width // 128
    order = (1, 3, 2)

    def project(lines, peer, j, count):
        at = pl.ds(pl.multiple_of(peer * width + j * 128, 128), count * 128)
        return lax.dot_general(
            gg[lines, :], wo[at, :], (((1,), (1,)), ((), ())), preferred_element_type=f32
        ).astype(bf16)

    def rest_block(peer):
        part_o[peer] = project(slice(moving, tokens), peer, 0, pieces)

    def move_block(i, peer):
        lines = pl.ds(pl.multiple_of(i * TOK, TOK), TOK)
        part_c[peer, lines, :] = project(lines, peer, 0, pieces)

    def piece(ref, c):
        return ref.at[pl.ds(c * cap, cap)]

    def to_slots(q):
        n = tab[LEAVE, q]
        xmsg[q] = sent[n]
        emsg[q] = edge_o[n]

    unrolled(cols * cap, 8, to_slots)
    others = pl.ds(0, (cols - 1) * cap)
    pl.semaphore_wait(barrier, cols - 1 + rows - 1)

    def push_factors(d, carry):
        peer = (me + d) % cols
        for a, b, s_, r_ in ((xmsg, xgot, x_s, x_r), (emsg, egot, e_s, e_r)):
            pltpu.make_async_remote_copy(
                piece(a, peer), piece(b, me), s_, r_,
                device_id=(row, peer), device_id_type=MESH,
            ).start()
        return carry

    lax.fori_loop(1, cols, push_factors, 0)
    keep_x = pltpu.make_async_copy(piece(xmsg, me), piece(xgot, me), loc.at[0])
    keep_e = pltpu.make_async_copy(piece(emsg, me), piece(egot, me), loc.at[1])
    keep_x.start()
    keep_e.start()

    @pl.loop(0, held // GROUP)
    def _(i):
        group(i, True)

        def send_moved(d, carry):
            peer = (row + d) % rows
            move_block(i, peer)
            at = pl.ds(pl.multiple_of(i * TOK, TOK), TOK)
            pltpu.make_async_remote_copy(
                part_c.at[peer, at], came_c.at[row, at], yc_s.at[d, i], yc_r.at[row, i],
                device_id=(peer, me), device_id_type=MESH,
            ).start()
            return carry

        lax.fori_loop(1, rows, send_moved, 0)

    for k, d in enumerate(order):
        pltpu.make_async_remote_copy(
            ss, ss_in.at[row], ss_s.at[k], ss_r.at[row],
            device_id=((row + d) % rows, me), device_id_type=MESH,
        ).start()

    def send_rest(d, carry):
        peer = (row + d) % rows
        rest_block(peer)
        pltpu.make_async_remote_copy(
            part_o.at[peer], came_o.at[row], yo_s.at[d], yo_r.at[row],
            device_id=(peer, me), device_id_type=MESH,
        ).start()
        return carry

    lax.fori_loop(1, rows, send_rest, 0)

    for i in range(held // GROUP):
        move_block(i, row)
    rest_block(row)
    total = ss[...]
    for d in order:
        peer = (row + d) % rows
        pltpu.make_async_copy(ss_in.at[peer], ss_in.at[peer], ss_r.at[peer]).wait()
        total = total + ss_in[peer]
    factor = lax.rsqrt(total / INNER + 1e-05)
    for i in range(tokens // TOK):
        line = jnp.broadcast_to(factor[i : i + 1, :], (TOK, TOK))
        scale[pl.ds(i * TOK, TOK), :] = line.T

    def add(part, came, into, start, count):
        def some(i, carry):
            at = pl.ds(pl.multiple_of(i * TOK, TOK), TOK)
            by = scale[pl.ds(pl.multiple_of(start + i * TOK, TOK), TOK), :]
            for j in range(pieces):
                lanes = slice(j * 128, (j + 1) * 128)
                value = part[row, at, lanes].astype(f32)
                for d in order:
                    value = value + came[(row + d) % rows, at, lanes].astype(f32)
                value = (value * by).astype(bf16)
                into[pl.ds(i * GROUP, GROUP), :, lanes] = value.reshape(GROUP, LEN, 128)
            return carry

        lax.fori_loop(0, count // TOK, some, 0)

    for i in range(held // GROUP):
        at = pl.ds(i * TOK, TOK)
        for d in order:
            spot = came_c.at[(row + d) % rows, at]
            pltpu.make_async_copy(spot, spot, yc_r.at[(row + d) % rows, i]).wait()
    add(part_c, came_c, mix, 0, moving)

    def pack(q):
        packed[q] = mix[tab[BACK, q]]

    unrolled(cols * cap, 8, pack)

    def push(d, carry):
        peer = (me + d) % cols
        pltpu.make_async_remote_copy(
            piece(packed, peer), piece(got, me), a2a_s, a2a_r,
            device_id=(row, peer), device_id_type=MESH,
        ).start()
        return carry

    lax.fori_loop(1, cols, push, 0)
    keep_m = pltpu.make_async_copy(piece(packed, me), piece(got, me), loc.at[2])
    keep_m.start()
    for d in order:
        spot = came_o.at[(row + d) % rows]
        pltpu.make_async_copy(spot, spot, yo_r.at[(row + d) % rows]).wait()
    add(part_o, came_o, mix_o, moving, resting)
    keep_m.wait()
    pltpu.make_async_copy(got.at[others], got.at[others], a2a_r).wait()

    def unpack(s):
        moved = tab[MOVED, s].astype(f32)
        away = got[tab[FROM_MSG, s]].astype(f32)
        here = mix_o[tab[FROM_MIX, s]].astype(f32)
        mixed[s] = jnp.where(moved > 0.5, away, here).astype(bf16)

    unrolled(requests, 8, unpack)
    for k in range(rows - 1):
        pltpu.make_async_copy(ss, ss, ss_s.at[k]).wait()
        pltpu.make_async_copy(part_o.at[0], part_o.at[0], yo_s.at[k + 1]).wait()
        for i in range(held // GROUP):
            spot = part_c.at[0, pl.ds(i * TOK, TOK)]
            pltpu.make_async_copy(spot, spot, yc_s.at[k + 1, i]).wait()
    pltpu.make_async_copy(got.at[others], got.at[others], a2a_s).wait()
    keep_x.wait()
    keep_e.wait()

    for ref, s_, r_ in ((xgot, x_s, x_r), (egot, e_s, e_r)):
        pltpu.make_async_copy(ref.at[others], ref.at[others], r_).wait()
        pltpu.make_async_copy(ref.at[others], ref.at[others], s_).wait()

    @pl.loop(0, held)
    def _(s):
        store(s).wait()


def mixer(tab, hid_c, hidden, fa, fb, vectors, prev, pex, peb, rows, cols, cap):
    requests, _, model = hidden.shape
    held = hid_c.shape[0]
    tokens = requests * LEN
    inner = fa.shape[1] // 2
    width = model // rows
    slots = cols * cap
    rest = requests - held
    dt = hidden.dtype
    f32 = jnp.float32
    vmem = pl.BlockSpec(memory_space=pltpu.VMEM)
    hbm = pl.BlockSpec(memory_space=pltpu.HBM)
    dma = pltpu.SemaphoreType.DMA

    def body(*refs):
        mixer_kernel(rows, cols, cap, held, *refs)

    wide = inner + 2 * STATE
    return pl.pallas_call(
        body,
        out_shape=(
            jax.ShapeDtypeStruct((requests, LEN, width), dt),
            jax.ShapeDtypeStruct((held, inner, STATE), dt),
            jax.ShapeDtypeStruct((held, 4, wide), dt),
            jax.ShapeDtypeStruct((slots, LEN, inner + STATE), dt),
            jax.ShapeDtypeStruct((slots, 4, wide), dt),
        ),
        in_specs=[hbm] * (8 + len(vectors)),
        out_specs=(vmem, hbm, vmem, hbm, hbm),
        scratch_shapes=[
            pltpu.SMEM(tab.shape, jnp.int32),
            *[pltpu.VMEM(v.shape, v.dtype) for v in vectors],
            pltpu.VMEM(pex.shape, dt),
            pltpu.VMEM(peb.shape, dt),
            pltpu.VMEM((requests, LEN, model), dt),
            pltpu.VMEM((requests, LEN, model), dt),
            pltpu.VMEM(fa.shape, dt),
            pltpu.VMEM((fb.shape[0], fb.shape[1] - inner), dt),
            pltpu.VMEM((fb.shape[0], inner), dt),
            pltpu.VMEM((held, inner, STATE), dt),
            pltpu.VMEM((tokens, inner), dt),
            pltpu.VMEM((tokens, inner), dt),
            pltpu.VMEM((tokens, 2 * STATE), dt),
            pltpu.VMEM((tokens, 128), f32),
            pltpu.VMEM((tokens, inner), dt),
            pltpu.VMEM((8, 128), f32),
            pltpu.VMEM((GROUP, 32, inner), f32),
            pltpu.VMEM((GROUP, 32, 2 * STATE), f32),
            pltpu.VMEM((3, held, inner), f32),
            pltpu.VMEM((3, held, 2 * STATE), f32),
            pltpu.VMEM((TOK, wide), f32),
            pltpu.VMEM((held, inner, STATE), dt),
            pltpu.VMEM((rest, LEN, inner + STATE), dt),
            pltpu.VMEM((rest, 4, wide), dt),
            pltpu.VMEM((slots, LEN, inner + STATE), dt),
            pltpu.VMEM((slots, 4, wide), dt),
            pltpu.VMEM((rows, rest * LEN, width), dt),
            pltpu.VMEM((rows, held * LEN, width), dt),
            pltpu.VMEM((rows, rest * LEN, width), dt),
            pltpu.VMEM((rows, held * LEN, width), dt),
            pltpu.VMEM((rows, 8, 128), f32),
            pltpu.VMEM((tokens, 128), f32),
            pltpu.VMEM((rest, LEN, width), dt),
            pltpu.VMEM((held, LEN, width), dt),
            pltpu.VMEM((slots, LEN, width), dt),
            pltpu.VMEM((slots, LEN, width), dt),
            dma(()), dma(()), dma((fa.shape[1] // 256 + 3,)), dma((held,)),
            dma((len(vectors) + 3,)), dma((3,)), dma((3,)), dma((rows,)),
            dma((rows,)), dma((rows,)), dma((rows, held // GROUP)), dma((rows, held // GROUP)),
            dma(()), dma(()),
            dma(()), dma(()), dma(()), dma(()),
        ],
        compiler_params=pltpu.CompilerParams(
            collective_id=1, has_side_effects=True, vmem_limit_bytes=60 << 20
        ),
        name="mixer",
    )(tab, hid_c, hidden, fa, fb, *vectors, prev, pex, peb)


def arrive_kernel(
    tab_in, xgot_in, egot_in, edge_in, nst_in, nst, nex, neb,
    tab, xgot, egot, edge, was, xs, bs, ex, eb, new, n_sem, m_sem, l_sem,
):
    f32, bf16 = jnp.float32, jnp.bfloat16
    count, inner = new.shape[0], new.shape[1]
    loads = [
        pltpu.make_async_copy(a, b, l_sem.at[k])
        for k, (a, b) in enumerate(
            ((tab_in, tab), (xgot_in, xgot), (nst_in, was), (egot_in, egot), (edge_in, edge))
        )
    ]
    for copy in loads:
        copy.start()
    loads[0].wait()

    def place(s):
        return pltpu.make_async_copy(was.at[s], nst.at[tab[POS, s]], m_sem.at[s])

    loads[1].wait()
    loads[2].wait()

    @pl.loop(0, count)
    def _(s):
        place(s).start()

    t_ids, _ = token_masks()
    none = jnp.zeros((TOK, STATE), bf16)

    def store(u):
        return pltpu.make_async_copy(new.at[u], nst.at[tab[POS_O, u]], n_sem.at[u])

    @pl.loop(0, count // GROUP)
    def _(i):
        for r in range(GROUP):
            slot = tab[PICK_O, i * GROUP + r]
            xs[r] = xgot[slot, :, :inner]
            bs[r] = xgot[slot, :, inner:]
        lhs = xs[...].reshape(TOK, inner).astype(f32).T.astype(bf16)
        b_in = bs[...].reshape(TOK, STATE)
        for pair in range(GROUP // 2):
            cut = jnp.concatenate(
                [
                    jnp.where(t_ids // LEN == r, b_in, none)
                    for r in (2 * pair, 2 * pair + 1)
                ],
                axis=1,
            )
            out = jnp.dot(lhs, cut, preferred_element_type=f32).astype(bf16)
            for k in (0, 1):
                u = i * GROUP + 2 * pair + k
                new[u] = out[:, k * STATE : (k + 1) * STATE]
                store(u).start()

    for copy in loads[3:]:
        copy.wait()

    @pl.loop(0, count)
    def _(u):
        for source, k, spot in (
            (egot, tab[PICK_O, u], tab[POS_O, u]), (edge, u, tab[POS, u])
        ):
            lines = source[k].astype(f32)
            at = pl.ds(spot, 1)
            for q in range(KCONV - 1):
                ex[q, at, :] = lines[q : q + 1, :inner]
                eb[q, at, :] = lines[q : q + 1, inner:]

    nex[...] = ex[...].astype(bf16)
    neb[...] = eb[...].astype(bf16)

    @pl.loop(0, count)
    def _(u):
        store(u).wait()
        place(u).wait()


def arrive(tab, xgot, egot, edge, nst):
    count, inner, _ = nst.shape
    requests = 2 * count
    dt, f32 = nst.dtype, jnp.float32
    vmem = pl.BlockSpec(memory_space=pltpu.VMEM)
    hbm = pl.BlockSpec(memory_space=pltpu.HBM)
    return pl.pallas_call(
        arrive_kernel,
        out_shape=(
            jax.ShapeDtypeStruct((requests, inner, STATE), dt),
            jax.ShapeDtypeStruct((3, requests, inner), dt),
            jax.ShapeDtypeStruct((3, requests, 2 * STATE), dt),
        ),
        in_specs=[hbm] * 5,
        out_specs=(hbm, vmem, vmem),
        scratch_shapes=[
            pltpu.SMEM(tab.shape, jnp.int32),
            pltpu.VMEM(xgot.shape, dt),
            pltpu.VMEM(egot.shape, dt),
            pltpu.VMEM(edge.shape, dt),
            pltpu.VMEM(nst.shape, dt),
            pltpu.VMEM((GROUP, LEN, inner), dt),
            pltpu.VMEM((GROUP, LEN, STATE), dt),
            pltpu.VMEM((3, requests, inner), f32),
            pltpu.VMEM((3, requests, 2 * STATE), f32),
            pltpu.VMEM((count, inner, STATE), dt),
            pltpu.SemaphoreType.DMA((count,)),
            pltpu.SemaphoreType.DMA((count,)),
            pltpu.SemaphoreType.DMA((5,)),
        ],
        compiler_params=pltpu.CompilerParams(vmem_limit_bytes=60 << 20),
        name="arrive",
    )(tab, xgot, egot, edge, nst)


def per_device(
    hidden, w_zx, w_bc, w_dt, w_out, dt_bias, a_log, d_skip, conv_x_w, conv_x_b,
    conv_bc_w, conv_bc_b, norm_gain, prev_state, prev_edge_x, prev_edge_bc,
    holder, continued, owner, accepted,
):
    rows, cols = lax.axis_size("row"), lax.axis_size("col")
    tokens, model = hidden.shape
    requests = tokens // LEN
    heads = dt_bias.shape[0]
    inner = heads * HEAD_DIM
    held = prev_state.shape[0]
    cap = 2 * ((requests // 4 + cols - 1) // cols)
    code = owner + 64 * (continued == 1).astype(jnp.int32) + 128 * accepted
    tab = route(code.reshape(cols, requests), held)
    hidden = hidden.reshape(requests, LEN, model)
    hid_c, fa, fb = gather_all(tab, hidden, w_zx, w_out, w_bc, w_dt.T, rows, cols, cap, held)
    vectors = (
        dt_bias[None, :], a_log[None, :], d_skip[None, :],
        conv_x_w, conv_x_b[None, :], conv_bc_w, conv_bc_b[None, :], norm_gain[None, :],
    )
    mixed, moved, edge, xgot, egot = mixer(
        tab, hid_c, hidden, fa, fb, vectors, prev_state.reshape(held, inner, STATE),
        prev_edge_x.transpose(1, 0, 2), prev_edge_bc.transpose(1, 0, 2),
        rows, cols, cap,
    )
    states, new_x, new_bc = arrive(tab, xgot, egot, edge, moved)
    return (
        mixed.reshape(tokens, model // rows),
        states.reshape(requests, heads, HEAD_DIM, STATE),
        new_x.transpose(1, 0, 2),
        new_bc.transpose(1, 0, 2),
    )


def solution(mesh):
    return jax.shard_map(
        per_device,
        mesh=mesh,
        in_specs=(
            P("col", None),
            P("col", "row"),
            P("col", None),
            P("col", "row"),
            P("col", "row"),
            P("row"),
            P("row"),
            P("row"),
            P(None, "row"),
            P("row"),
            P(),
            P(),
            P("row"),
            P("col", "row", None, None),
            P("col", None, "row"),
            P("col", None, None),
            P(),
            P(),
            P(),
            P(),
        ),
        out_specs=(
            P("col", "row"),
            P("col", "row", None, None),
            P("col", None, "row"),
            P("col", None, None),
        ),
        check_vma=False,
    )
```

```python
import jax
import jax.numpy as jnp
from jax import lax
from jax.experimental import pallas as pl
from jax.experimental.pallas import tpu as pltpu
from jax.sharding import PartitionSpec as P

HEAD_DIM = 64
STATE = 128
KCONV = 4
LEN = 16
INNER = 2048
SIDE = 4
GROUP = 8
TOK = GROUP * LEN
MESH = pl.DeviceIdType.MESH
HIGHEST = lax.Precision.HIGHEST


def route_kernel(held, code, out):
    f32, bf16 = jnp.float32, jnp.bfloat16
    me = lax.axis_index("col")
    groups, requests = code.shape
    value = code[...]
    o, c, a = value & 63, (value >> 6) & 1, value >> 7

    def dot(x, y):
        return jnp.dot(x.astype(bf16), y.astype(bf16), preferred_element_type=f32)

    def dot0(x, y):
        return lax.dot_general(
            x.astype(bf16), y.astype(bf16), (((0,), (0,)), ((), ())), preferred_element_type=f32
        )

    def ids(shape, dim):
        return lax.broadcasted_iota(jnp.int32, shape, dim)

    below = (ids((requests, requests), 0) < ids((requests, requests), 1)).astype(f32)
    prior = (ids((groups, groups), 1) < ids((groups, groups), 0)).astype(f32)
    lane = ids((groups, 128), 1).astype(f32)
    group = ids((groups, 128), 0).astype(f32)
    spots, inside, starts = [], [], []
    for kind in (1, 0):
        mask = ((o == me) & (c == kind)).astype(f32)
        rank = dot(mask, below)
        count = jnp.broadcast_to(jnp.sum(mask, axis=1, keepdims=True), (groups, 128))
        start = dot(prior, count)
        hot = ((start <= lane) & (lane < start + count)).astype(f32)
        spots.append((jnp.where(mask > 0, rank, -1.0), hot))
        inside.append(rank)
        starts.append(start)
    rank_all, start_all = inside[0] + inside[1], starts[0] + starts[1]
    picks, places, taken = [], [], []
    for k in (0, 1):
        spot, hot = spots[k]
        order = jnp.sum(hot * (lane - starts[k]), axis=0, keepdims=True)
        any_hot = jnp.sum(hot, axis=0, keepdims=True)
        order = jnp.where(any_hot > 0, order, -5.0)
        match = (dot0(spot, hot) == order).astype(f32)
        picks.append(jnp.sum(hot * (2 * group + lane - starts[k]), axis=0, keepdims=True))
        places.append(
            jnp.sum(hot * start_all, axis=0, keepdims=True)
            + jnp.sum(match * dot0(rank_all, hot), axis=0, keepdims=True)
        )
        taken.append(jnp.sum(match * dot0(a, hot), axis=0, keepdims=True))
    lane_i, group_i = ids((groups, 128), 1), ids((groups, 128), 0)
    back = jnp.sum(
        jnp.where(lane_i // 2 == group_i, starts[0] + (lane_i % 2).astype(f32), 0.0),
        axis=0, keepdims=True,
    )
    back = jnp.minimum(back, held - 1.0)

    def my_row(x, fill):
        row = jnp.sum(
            jnp.where(ids((groups, requests), 0) == me, x, 0).astype(f32), axis=0, keepdims=True
        )
        rest = jnp.full((1, 128 - requests), fill, f32)
        return jnp.concatenate([row, rest], axis=1)

    o_row, c_row, a_row = my_row(o, 99.0), my_row(c, 2.0), my_row(a, 0.0)

    def column(row):
        return jnp.broadcast_to(row, (128, 128)).T

    o_col, c_col, a_col = column(o_row), column(c_row), column(a_row)
    ii, jj = ids((128, 128), 0), ids((128, 128), 1)
    alike = (o_col == o_row) & (c_col == c_row)
    rank_row = jnp.sum((alike & (ii < jj)).astype(f32), axis=0, keepdims=True)
    rank_col = jnp.sum((alike & (jj < ii)).astype(f32), axis=1, keepdims=True)
    nth_row = jnp.sum(((c_col == 0) & (ii < jj)).astype(f32), axis=0, keepdims=True)
    nth_col = jnp.sum(((c_row == 0) & (jj < ii)).astype(f32), axis=1, keepdims=True)
    key_row = 2 * o_row + rank_row
    key_col = 2 * o_col + rank_col
    fi, fj = ii.astype(f32), jj.astype(f32)
    goes = (c_col == 1) & (key_col == fj)
    leaves = (c_col == 0) & (key_col == fj)
    stays = (c_col == 0) & (nth_col == fj)

    def total(mask, x):
        return jnp.sum(jnp.where(mask, x, 0.0), axis=0, keepdims=True)

    table = (
        total(goes, fi), picks[0], back,
        jnp.where(c_row == 1, key_row, 0.0), jnp.where(c_row == 0, nth_row, 0.0),
        (c_row == 1).astype(f32),
        total(stays, fi), total(stays, key_col), total(stays, a_col),
        taken[0], places[0], picks[1], places[1], total(leaves, nth_col),
    )
    for k, line in enumerate(table):
        out[k : k + 1, :] = line.astype(jnp.int32)
    out[len(table) :, :] = jnp.zeros((16 - len(table), 128), jnp.int32)


SEND, PICK, BACK, FROM_MSG, FROM_MIX, MOVED, STAY, STAY_KEY, STAY_ACC, ACC, POS, PICK_O, POS_O, LEAVE = range(14)


def route(code, held):
    vmem = pl.BlockSpec(memory_space=pltpu.VMEM)

    def body(*refs):
        route_kernel(held, *refs)

    return pl.pallas_call(
        body, out_shape=jax.ShapeDtypeStruct((16, 128), jnp.int32),
        in_specs=[vmem], out_specs=vmem, name="route",
        compiler_params=pltpu.CompilerParams(vmem_limit_bytes=60 << 20),
    )(code)


def unrolled(count, step, body):
    def some(i, carry):
        for k in range(step):
            body(i * step + k)
        return carry

    lax.fori_loop(0, count // step, some, 0)


def greet(row, me, rows, cols):
    barrier = pltpu.get_barrier_semaphore()

    def along_col(d, carry):
        pl.semaphore_signal(
            barrier, inc=1, device_id=(row, (me + d) % cols), device_id_type=MESH
        )
        return carry

    lax.fori_loop(1, cols, along_col, 0)

    def along_row(d, carry):
        pl.semaphore_signal(
            barrier, inc=1, device_id=((row + d) % rows, me), device_id_type=MESH
        )
        return carry

    lax.fori_loop(1, rows, along_row, 0)
    return barrier


def torus_ring(row, me, depth, block, own, span, gone, twin, came):
    core = me % 2
    x = (me // 2) % SIDE
    z = me // (2 * SIDE)
    a = x + core * (z - x)
    b = z + core * (x - z)

    def at(pa, pb):
        pa, pb = (pa + SIDE) % SIDE, (pb + SIDE) % SIDE
        px = pa + core * (pb - pa)
        pz = pb + core * (pa - pb)
        return (pz * SIDE + px) * 2 + core

    sibling = me + 1 - 2 * core
    sent = [0, 0]

    def send(h, source, c, dest):
        sent[h] += 1
        arrival = twin.at[h] if dest is sibling else came.at[h, c]
        pltpu.make_async_remote_copy(
            source, block(h, c), gone.at[h], arrival,
            device_id=(row, dest), device_id_type=MESH,
        ).start()

    def forward(h, c, dest):
        send(h, block(h, c), c, dest)

    def arrived(h, c):
        pltpu.make_async_copy(block(h, c), block(h, c), came.at[h, c]).wait()

    up, down, far = at(a + 1, b), at(a - 1, b), at(a + 2, b)
    over, under = at(a, b + 1), at(a, b - 1)

    def begin():
        for dest in (up, down, over, under, sibling):
            for h in (0, 1):
                send(h, own(h), me, dest)

    def near():
        arrived(0, down)
        forward(0, down, up)
        arrived(1, up)
        forward(1, up, down)
        arrived(1, down)
        arrived(0, up)
        for c in (down, up):
            for h in (0, 1):
                for dest in (over, under, sibling):
                    forward(h, c, dest)

    def beyond():
        for h in (0, 1):
            arrived(h, far)
            for dest in (over, under, sibling):
                forward(h, far, dest)

    def beside():
        for k in (0, 1, -1, 2):
            low, high = at(a + k, b - 1), at(a + k, b + 1)
            arrived(0, low)
            forward(0, low, over)
            arrived(1, high)
            forward(1, high, under)
            arrived(1, low)
            arrived(0, high)
            for h in (0, 1):
                forward(h, low, sibling)
                forward(h, high, sibling)

    def opposite():
        for k in (0, 1, -1, 2):
            c = at(a + k, b + 2)
            for h in (0, 1):
                arrived(h, c)
                forward(h, c, sibling)

    def finish():
        for h in (0, 1):
            half = span(h, 16 * depth)
            pltpu.make_async_copy(half, half, twin.at[h]).wait()
        for h in (0, 1):
            part = span(h, sent[h] * depth)
            pltpu.make_async_copy(part, part, gone.at[h]).wait()

    return begin, near, beyond, beside, opposite, finish


def gather_kernel(
    rows, cols, cap, tab_in, hidden, w_zx, w_bc, w_dt_in, hid_full, fw,
    tab, w_dt, ws, sl, packed0, packed1, got0, got1, own0, own1, loc, a2a_s, a2a_r, gone, twin, arr, y_s, y_r,
):
    row, me = lax.axis_index("row"), lax.axis_index("col")
    barrier = greet(row, me, rows, cols)
    width = sl.shape[2]
    half = own0.shape[0] // 2
    packs, gots, owns = (packed0, packed1), (got0, got1), (own0, own1)
    lows = (0, packed0.shape[2])
    depth = w_zx.shape[0]

    def cols_of(r):
        return pl.ds(pl.multiple_of(r * width, 128), width)

    cut = 128 * (ws.shape[1] // 256)
    lanes_of = (pl.ds(0, cut), pl.ds(cut, ws.shape[1] - cut))

    def lines(c):
        return pl.ds(pl.multiple_of(c * depth, 16), depth)

    ring = torus_ring(
        row, me, depth,
        lambda h, c: fw.at[lines(c), lanes_of[h]],
        lambda h: ws.at[:, lanes_of[h]],
        lambda h, count: fw.at[pl.ds(0, count), lanes_of[h]],
        gone, twin, arr,
    )
    begin, near, beyond, beside, opposite, finish = ring

    load = pltpu.make_async_copy(hidden.at[:, :, cols_of(row)], sl, loc.at[0])
    load.start()
    inner = w_zx.shape[1]
    states = w_bc.shape[1]
    heads = w_dt_in.shape[0]
    loads = (
        pltpu.make_async_copy(tab_in, tab, loc.at[5]),
        pltpu.make_async_copy(w_dt_in, w_dt, loc.at[6]),
        pltpu.make_async_copy(w_zx, ws.at[:, pl.ds(0, inner)], loc.at[7]),
        pltpu.make_async_copy(w_bc, ws.at[:, pl.ds(inner, states)], loc.at[8]),
    )
    for copy in loads:
        copy.start()
    for copy in loads:
        copy.wait()
    square = jnp.concatenate(
        [w_dt[...].astype(jnp.float32), jnp.zeros((heads, 128 - depth), jnp.float32)], axis=1
    )
    square = jnp.concatenate([square, jnp.zeros((128 - heads, 128), jnp.float32)], axis=0).T
    ws[:, inner + states :] = square[:depth, :].astype(ws.dtype)
    keep_w = pltpu.make_async_copy(ws, fw.at[lines(me), :], loc.at[1])
    keep_w.start()
    load.wait()

    def piece(ref, c):
        return ref.at[pl.ds(c * cap, cap)]

    keeps = []
    for k in (0, 1):
        packed, got, low = packs[k], gots[k], lows[k]

        def pack(s):
            packed[s] = sl[tab[SEND, s], :, low : low + packed.shape[2]]

        unrolled(cols * cap, 8, pack)
        if k == 0:
            pl.semaphore_wait(barrier, cols - 1 + rows - 1)

        def push(d, carry):
            peer = (me + d) % cols
            pltpu.make_async_remote_copy(
                piece(packed, peer), piece(got, me), a2a_s.at[k], a2a_r.at[k],
                device_id=(row, peer), device_id_type=MESH,
            ).start()
            return carry

        lax.fori_loop(1, cols, push, 0)
        keeps.append(pltpu.make_async_copy(piece(packed, me), piece(got, me), loc.at[3 + 6 * k]))
        keeps[k].start()

    begin()
    near()
    others = pl.ds(0, (cols - 1) * cap)
    right, left = (row + 1) % rows, (row + rows - 1) % rows
    far_row = (row + 2) % rows

    def part(ref, k, h, r):
        low, size = lows[k], owns[k].shape[2]
        lanes = pl.ds(pl.multiple_of(r * width + low, 128), size)
        return ref.at[pl.ds(h * half, half), :, lanes]

    def y_here(k, h, r):
        spot = part(hid_full, k, h, r)
        pltpu.make_async_copy(spot, spot, y_r.at[k, r, h]).wait()

    def pass_on(k, h, source, dest):
        spot = part(hid_full, k, h, source)
        pltpu.make_async_remote_copy(
            spot, spot, y_s.at[k, 4 + h], y_r.at[k, source, h],
            device_id=(dest, me), device_id_type=MESH,
        ).start()

    for k in (0, 1):
        got, own = gots[k], owns[k]
        keeps[k].wait()
        pltpu.make_async_copy(got.at[others], got.at[others], a2a_r.at[k]).wait()

        def unpack(s):
            own[s] = got[tab[PICK, s]]

        unrolled(own.shape[0], 8, unpack)
        for n, dest in ((0, right), (1, left)):
            for h in (n, 1 - n):
                pltpu.make_async_remote_copy(
                    own.at[pl.ds(h * half, half)], part(hid_full, k, h, row),
                    y_s.at[k, 2 * n + h], y_r.at[k, row, h],
                    device_id=(dest, me), device_id_type=MESH,
                ).start()
        lanes = pl.ds(pl.multiple_of(row * width + lows[k], 128), own.shape[2])
        keeps.append(pltpu.make_async_copy(own, hid_full.at[:, :, lanes], loc.at[4 + 6 * k]))
        keeps[2 + k].start()

    beyond()
    y_here(0, 0, left)
    pass_on(0, 0, left, right)
    y_here(0, 1, right)
    pass_on(0, 1, right, left)
    beside()
    y_here(1, 0, left)
    pass_on(1, 0, left, right)
    y_here(1, 1, right)
    pass_on(1, 1, right, left)
    opposite()
    for k in (0, 1):
        y_here(k, 1, left)
        y_here(k, 0, right)
        y_here(k, 0, far_row)
        y_here(k, 1, far_row)

    finish()
    keep_w.wait()
    keeps[2].wait()
    keeps[3].wait()

    for k in (0, 1):
        pltpu.make_async_copy(packs[k].at[others], packs[k].at[others], a2a_s.at[k]).wait()

    for k in (0, 1):
        for n in range(6):
            spot = part(hid_full, k, n % 2, row)
            pltpu.make_async_copy(spot, spot, y_s.at[k, n]).wait()


def gather_all(tab, hidden, w_zx, w_bc, w_dt, rows, cols, cap, held):
    requests, _, model = hidden.shape
    width = model // rows
    dt = hidden.dtype
    hbm = pl.BlockSpec(memory_space=pltpu.HBM)
    dma = pltpu.SemaphoreType.DMA
    depth = w_zx.shape[0]
    wide = w_zx.shape[1] + w_bc.shape[1] + 128

    def body(*refs):
        gather_kernel(rows, cols, cap, *refs)

    return pl.pallas_call(
        body,
        out_shape=(
            jax.ShapeDtypeStruct((held, LEN, model), dt),
            jax.ShapeDtypeStruct((depth * cols, wide), dt),
        ),
        in_specs=[hbm] * 5,
        out_specs=(hbm, hbm),
        scratch_shapes=[
            pltpu.SMEM(tab.shape, jnp.int32),
            pltpu.VMEM(w_dt.shape, dt),
            pltpu.VMEM((depth, wide), dt),
            pltpu.VMEM((requests, LEN, width), dt),
            pltpu.VMEM((cols * cap, LEN, 128), dt),
            pltpu.VMEM((cols * cap, LEN, width - 128), dt),
            pltpu.VMEM((cols * cap, LEN, 128), dt),
            pltpu.VMEM((cols * cap, LEN, width - 128), dt),
            pltpu.VMEM((held, LEN, 128), dt),
            pltpu.VMEM((held, LEN, width - 128), dt),
            dma((11,)), dma((2,)), dma((2,)),
            dma((2,)), dma((2,)), dma((2, cols)),
            dma((2, 6)), dma((2, rows, 2)),
        ],
        compiler_params=pltpu.CompilerParams(
            collective_id=0, has_side_effects=True, vmem_limit_bytes=60 << 20
        ),
        name="gather_all",
    )(tab, hidden, w_zx, w_bc, w_dt)


def silu(v):
    return v / (1.0 + jnp.exp(-v))


def token_masks():
    t_ids = lax.broadcasted_iota(jnp.int32, (TOK, TOK), 0)
    s_ids = lax.broadcasted_iota(jnp.int32, (TOK, TOK), 1)
    return t_ids, s_ids


def mixer_kernel(
    rows, cols, cap, held, tab_in, hid_c, hidden, fw, w_out, *refs,
):
    sources, refs = refs[:8], refs[8:]
    prev, pex_in, peb_in, mixed, nst, edge_c, xgot, egot, tab, *refs = refs
    params, refs = refs[:8], refs[8:]
    dtb, alog, skip, cxw, cxb, cbw, cbb, gain = params
    (
        pex, peb, hid, home, wa, wb, wo, old, gate, xin, bc, dts, gg, ss, cx, cb, pexf, pebf, es,
        new, sent, edge_o, xmsg, emsg, part_o, part_c, came_o, came_c, ss_in, scale, mix_o,
        mix, packed, got,
        h_sem, o_sem, w_sem, n_sem, v_sem, loc, ss_s, ss_r, yo_s, yo_r, yc_s, yc_r,
        a2a_s, a2a_r, x_s, x_r, e_s, e_r, mine, gone, twin, arr,
    ) = refs
    row, me = lax.axis_index("row"), lax.axis_index("col")
    barrier = greet(row, me, rows, cols)
    depth = w_out.shape[0]
    load_mine = pltpu.make_async_copy(w_out, mine, loc.at[3])
    load_mine.start()
    f32, bf16 = jnp.float32, jnp.bfloat16
    inner = gain.shape[1]
    requests = hid.shape[0]
    tokens = requests * LEN
    model = hid.shape[2]
    heads = inner // HEAD_DIM
    blocks = wa.shape[1] // 256
    assert blocks == 4

    load_h = pltpu.make_async_copy(hid_c, hid.at[pl.ds(0, held)], h_sem)
    load_h.start()
    small = list(zip(sources + (pex_in, peb_in, tab_in), list(params) + [pex, peb, tab]))
    small = [pltpu.make_async_copy(a, b, v_sem.at[k]) for k, (a, b) in enumerate(small)]
    small[-1].start()
    for copy in small[:-1]:
        copy.start()
    small[-1].wait()

    def wa_load(n):
        at = pl.ds(n * 256, 256)
        return pltpu.make_async_copy(fw.at[:, at], wa.at[:, at], w_sem.at[n])

    wa_load(0).start()

    load_home = pltpu.make_async_copy(hidden, home, o_sem)
    load_home.start()
    for n in range(1, blocks):
        wa_load(n).start()
    late = pl.ds(2 * inner, wb.shape[1])
    load_bc = pltpu.make_async_copy(fw.at[:, late], wb, w_sem.at[blocks])
    load_old = pltpu.make_async_copy(prev, old, w_sem.at[blocks + 1])
    load_bc.start()
    load_old.start()
    load_mine.wait()
    cut = inner // 2

    def lines_of(c):
        return pl.ds(pl.multiple_of(c * depth, 16), depth)

    begin, near, beyond, beside, opposite, finish = torus_ring(
        row, me, depth,
        lambda h, c: wo.at[lines_of(c), pl.ds(h * cut, cut)],
        lambda h: mine.at[:, pl.ds(h * cut, cut)],
        lambda h, count: wo.at[pl.ds(0, count), pl.ds(h * cut, cut)],
        gone, twin, arr,
    )
    keep_mine = pltpu.make_async_copy(mine, wo.at[lines_of(me), :], loc.at[4])
    keep_mine.start()
    for copy in small[:-1]:
        copy.wait()
    pexf[...] = pex[...].astype(f32)
    pebf[...] = peb[...].astype(f32)

    t_ids, s_ids = token_masks()
    row_ids = lax.broadcasted_iota(jnp.int32, (4 * GROUP, TOK), 0)
    k_ids = lax.broadcasted_iota(jnp.int32, (4 * GROUP, TOK), 1)
    r_ids, q_ids = row_ids // 4, row_ids % 4
    es[...] = jnp.zeros(es.shape, f32)
    same = (t_ids // LEN) == (s_ids // LEN)
    causal = same & (t_ids >= s_ids)
    tri = causal.astype(f32)
    spread_h = (
        lax.broadcasted_iota(jnp.int32, (TOK, inner), 1) // HEAD_DIM
        == lax.broadcasted_iota(jnp.int32, (TOK, inner), 0)
    ).astype(f32)

    def wide(ref):
        return jnp.concatenate([ref[...], jnp.zeros((1, TOK - heads), f32)], axis=1)

    bias, rate = wide(dtb), -jnp.exp(wide(alog))
    skip_x = jnp.dot(
        jnp.broadcast_to(wide(skip), (8, TOK)), spread_h,
        precision=HIGHEST, preferred_element_type=f32,
    )[0:1, :]

    load_h.wait()
    load_home.wait()

    def stay(n):
        hid[held + n] = home[tab[STAY, n]]

    unrolled(requests - held, 4, stay)
    left = lax.broadcasted_iota(jnp.int32, (tokens, 128), 1) < HEAD_DIM
    for n in range(blocks):
        wa_load(n).wait()
        z = jnp.dot(
            hid[...].reshape(tokens, model), wa[:, n * 256 : (n + 1) * 256],
            preferred_element_type=f32,
        )
        z0, z1 = z[:, :128], z[:, 128:]
        at = slice(n * 128, (n + 1) * 128)
        gate[:, at] = jnp.where(left, z0, pltpu.roll(z1, HEAD_DIM, 1)).astype(bf16)
        xin[:, at] = jnp.where(left, pltpu.roll(z0, HEAD_DIM, 1), z1).astype(bf16)
        if n == 0:
            pl.semaphore_wait(barrier, cols - 1 + rows - 1)
            begin()
        if n == 2:
            near()
    load_bc.wait()
    z = jnp.dot(hid[...].reshape(tokens, model), wb[...], preferred_element_type=f32)
    bc[...] = z[:, : 2 * STATE].astype(bf16)
    dts[...] = z[:, 2 * STATE :]
    beyond()
    load_old.wait()

    def store(s):
        return pltpu.make_async_copy(new.at[s], nst.at[s], n_sem.at[s])

    def group(i, live):
        at = pl.ds(pl.multiple_of(i * TOK, TOK), TOK)
        first = i * GROUP
        last = jnp.zeros((TOK, TOK), jnp.int32)
        row_acc = jnp.zeros((4 * GROUP, TOK), jnp.int32)
        for r in range(GROUP):
            acc = tab[ACC, first + r] if live else tab[STAY_ACC, first - held + r]
            row_acc = jnp.where(r_ids == r, acc, row_acc)
            last = jnp.where(t_ids // LEN == r, acc, last)
            if live:
                for k in range(KCONV - 1):
                    cx[r, 13 + k : 14 + k, :] = pexf[k, pl.ds(first + r, 1), :]
                    cb[r, 13 + k : 14 + k, :] = pebf[k, pl.ds(first + r, 1), :]
        if not live:
            cx[:, 8:16, :] = jnp.zeros((GROUP, 8, inner), f32)
            cb[:, 8:16, :] = jnp.zeros((GROUP, 8, 2 * STATE), f32)
        cx[:, 16:32, :] = xin[at, :].astype(f32).reshape(GROUP, LEN, inner)
        cb[:, 16:32, :] = bc[at, :].astype(f32).reshape(GROUP, LEN, 2 * STATE)
        tot_x = cxb[...].reshape(1, 1, inner) + cxw[0:1, :].reshape(1, 1, inner) * cx[:, 13:29, :]
        tot_b = cbb[...].reshape(1, 1, 2 * STATE) + cbw[0:1, :].reshape(
            1, 1, 2 * STATE
        ) * cb[:, 13:29, :]
        for k in range(1, KCONV):
            tot_x = tot_x + cxw[k : k + 1, :].reshape(1, 1, inner) * cx[:, 13 + k : 29 + k, :]
            tot_b = tot_b + cbw[k : k + 1, :].reshape(1, 1, 2 * STATE) * cb[:, 13 + k : 29 + k, :]
        xc = silu(tot_x).reshape(TOK, inner).astype(bf16)
        bcc = silu(tot_b).reshape(TOK, 2 * STATE).astype(bf16)
        near = jnp.concatenate([xin[at, :], bc[at, :]], axis=1)
        want = q_ids + row_acc
        pick = (k_ids == LEN * r_ids + want - 3) & (want >= 3) & (q_ids < 3)
        edge = jnp.dot(pick.astype(bf16), near, preferred_element_type=f32)
        if live:
            for k in range(KCONV - 1):
                rows8 = pl.ds(pl.multiple_of(first, GROUP), GROUP)
                es[k * GROUP : (k + 1) * GROUP, :inner] = pexf[k, rows8, :]
                es[k * GROUP : (k + 1) * GROUP, inner:] = pebf[k, rows8, :]
            pick = (k_ids == GROUP * want + r_ids) & (want < 3) & (q_ids < 3)
            edge = edge + jnp.dot(
                pick.astype(bf16), es[...].astype(bf16), preferred_element_type=f32
            )
        for r in range(GROUP):
            lines = edge[4 * r : 4 * r + 4, :].astype(bf16)
            if live:
                edge_c[first + r] = lines
            else:
                edge_o[first - held + r] = lines
        b_in, c_in = bcc[:, :STATE], bcc[:, STATE:]
        xf = xc.astype(f32)
        raw = dts[at, :] + bias
        step = jnp.maximum(raw, 0.0) + jnp.log(1.0 + jnp.exp(-jnp.abs(raw)))
        decay = jnp.dot(tri, step * rate, precision=HIGHEST, preferred_element_type=f32)
        decay_t = decay.T
        step_t = step.T
        choose = (same & (s_ids % LEN == last - 1)).astype(f32)
        reach = jnp.dot(choose, decay, precision=HIGHEST, preferred_element_type=f32)
        taken = t_ids % LEN < last
        weight = jnp.where(taken, jnp.exp(jnp.minimum(reach - decay, 0.0)), 0.0) * step
        weight_x = jnp.dot(weight, spread_h, precision=HIGHEST, preferred_element_type=f32)
        scores = lax.dot_general(
            c_in, b_in, (((1,), (1,)), ((), ())), preferred_element_type=f32
        )
        scores = jnp.where(causal, scores, 0.0)
        half = s_ids < HEAD_DIM
        zero = jnp.zeros((TOK, 2 * HEAD_DIM), bf16)
        y = []
        for pair in range(heads // 2):
            mats = []
            for h in (2 * pair, 2 * pair + 1):
                gap = decay[:, h : h + 1] - decay_t[h : h + 1, :]
                mats.append(
                    (jnp.exp(jnp.minimum(gap, 0.0)) * scores * step_t[h : h + 1, :]).astype(bf16)
                )
            xp = xc[:, pair * 128 : (pair + 1) * 128]
            both = jnp.concatenate([jnp.where(half, xp, zero), jnp.where(half, zero, xp)], axis=0)
            y.append(
                jnp.dot(jnp.concatenate(mats, axis=1), both, preferred_element_type=f32)
            )
        y = jnp.concatenate(y, axis=1)
        if live:
            grow_x = jnp.dot(jnp.exp(decay), spread_h, precision=HIGHEST, preferred_element_type=f32)
            carried = [
                lax.dot_general(
                    c_in[r * LEN : (r + 1) * LEN, :], old[first + r], (((1,), (1,)), ((), ())),
                    preferred_element_type=f32,
                )
                for r in range(GROUP)
            ]
            y = y + grow_x * jnp.concatenate(carried, axis=0)
        y = y + skip_x * xf
        gated = y * silu(gate[at, :].astype(f32))
        gg[at, :] = (gated * gain[...]).astype(bf16)
        squares = jnp.sum(gated * gated, axis=1, keepdims=True)
        ss[pl.ds(i, 1), :] = jnp.broadcast_to(squares, (TOK, TOK)).T[0:1, :]

        if not live:
            out = (xf * weight_x).astype(bf16)
            for r in range(GROUP):
                lines = slice(r * LEN, (r + 1) * LEN)
                sent[first - held + r, :, :inner] = out[lines, :]
                sent[first - held + r, :, inner:] = b_in[lines, :]
            return
        xw = (xf * weight_x).T
        high = xw.astype(bf16)
        low = (xw - high.astype(f32)).astype(bf16)
        lhs = jnp.concatenate([high, low], axis=1)
        keep_t = jnp.exp(reach).T
        none = jnp.zeros((TOK, STATE), bf16)
        for pair in range(GROUP // 2):
            cut = jnp.concatenate(
                [
                    jnp.where(t_ids // LEN == r, b_in, none)
                    for r in (2 * pair, 2 * pair + 1)
                ],
                axis=1,
            )
            added = jnp.dot(
                lhs, jnp.concatenate([cut, cut], axis=0), preferred_element_type=f32
            )
            for k in (0, 1):
                r = 2 * pair + k
                s = first + r
                factor = jnp.broadcast_to(keep_t[0:heads, r * LEN : r * LEN + 1], (heads, STATE))
                was = old[s].astype(f32).reshape(heads, HEAD_DIM, STATE)
                now = factor[:, None, :] * was + added[:, k * STATE : (k + 1) * STATE].reshape(
                    heads, HEAD_DIM, STATE
                )
                new[s] = now.reshape(inner, STATE).astype(bf16)
                store(s).start()

    group(held // GROUP, False)
    beside()

    @pl.loop(held // GROUP + 1, requests // GROUP)
    def _(i):
        group(i, False)

    opposite()

    moving = held * LEN
    resting = tokens - moving
    width = part_c.shape[2]
    pieces = width // 128
    order = (1, 3, 2)

    def project(lines, peer, j, count):
        at = pl.ds(pl.multiple_of(peer * width + j * 128, 128), count * 128)
        return lax.dot_general(
            gg[lines, :], wo[at, :], (((1,), (1,)), ((), ())), preferred_element_type=f32
        ).astype(bf16)

    def rest_block(peer):
        part_o[peer] = project(slice(moving, tokens), peer, 0, pieces)

    def move_block(i, peer):
        lines = pl.ds(pl.multiple_of(i * TOK, TOK), TOK)
        part_c[peer, lines, :] = project(lines, peer, 0, pieces)

    def piece(ref, c):
        return ref.at[pl.ds(c * cap, cap)]

    def to_slots(q):
        n = tab[LEAVE, q]
        xmsg[q] = sent[n]
        emsg[q] = edge_o[n]

    unrolled(cols * cap, 8, to_slots)
    others = pl.ds(0, (cols - 1) * cap)

    def push_factors(d, carry):
        peer = (me + d) % cols
        for a, b, s_, r_ in ((xmsg, xgot, x_s, x_r), (emsg, egot, e_s, e_r)):
            pltpu.make_async_remote_copy(
                piece(a, peer), piece(b, me), s_, r_,
                device_id=(row, peer), device_id_type=MESH,
            ).start()
        return carry

    lax.fori_loop(1, cols, push_factors, 0)
    keep_x = pltpu.make_async_copy(piece(xmsg, me), piece(xgot, me), loc.at[0])
    keep_e = pltpu.make_async_copy(piece(emsg, me), piece(egot, me), loc.at[1])
    keep_x.start()
    keep_e.start()

    finish()
    keep_mine.wait()

    @pl.loop(0, held // GROUP)
    def _(i):
        group(i, True)

        def send_moved(d, carry):
            peer = (row + d) % rows
            move_block(i, peer)
            at = pl.ds(pl.multiple_of(i * TOK, TOK), TOK)
            pltpu.make_async_remote_copy(
                part_c.at[peer, at], came_c.at[row, at], yc_s.at[d, i], yc_r.at[row, i],
                device_id=(peer, me), device_id_type=MESH,
            ).start()
            return carry

        lax.fori_loop(1, rows, send_moved, 0)

    for k, d in enumerate(order):
        pltpu.make_async_remote_copy(
            ss, ss_in.at[row], ss_s.at[k], ss_r.at[row],
            device_id=((row + d) % rows, me), device_id_type=MESH,
        ).start()

    def send_rest(d, carry):
        peer = (row + d) % rows
        rest_block(peer)
        pltpu.make_async_remote_copy(
            part_o.at[peer], came_o.at[row], yo_s.at[d], yo_r.at[row],
            device_id=(peer, me), device_id_type=MESH,
        ).start()
        return carry

    lax.fori_loop(1, rows, send_rest, 0)

    for i in range(held // GROUP):
        move_block(i, row)
    rest_block(row)
    total = ss[...]
    for d in order:
        peer = (row + d) % rows
        pltpu.make_async_copy(ss_in.at[peer], ss_in.at[peer], ss_r.at[peer]).wait()
        total = total + ss_in[peer]
    factor = lax.rsqrt(total / INNER + 1e-05)
    for i in range(tokens // TOK):
        line = jnp.broadcast_to(factor[i : i + 1, :], (TOK, TOK))
        scale[pl.ds(i * TOK, TOK), :] = line.T

    def add(part, came, into, start, count):
        def some(i, carry):
            at = pl.ds(pl.multiple_of(i * TOK, TOK), TOK)
            by = scale[pl.ds(pl.multiple_of(start + i * TOK, TOK), TOK), :]
            for j in range(pieces):
                lanes = slice(j * 128, (j + 1) * 128)
                value = part[row, at, lanes].astype(f32)
                for d in order:
                    value = value + came[(row + d) % rows, at, lanes].astype(f32)
                value = (value * by).astype(bf16)
                into[pl.ds(i * GROUP, GROUP), :, lanes] = value.reshape(GROUP, LEN, 128)
            return carry

        lax.fori_loop(0, count // TOK, some, 0)

    for i in range(held // GROUP):
        at = pl.ds(i * TOK, TOK)
        for d in order:
            spot = came_c.at[(row + d) % rows, at]
            pltpu.make_async_copy(spot, spot, yc_r.at[(row + d) % rows, i]).wait()
    add(part_c, came_c, mix, 0, moving)

    def pack(q):
        packed[q] = mix[tab[BACK, q]]

    unrolled(cols * cap, 8, pack)

    def push(d, carry):
        peer = (me + d) % cols
        pltpu.make_async_remote_copy(
            piece(packed, peer), piece(got, me), a2a_s, a2a_r,
            device_id=(row, peer), device_id_type=MESH,
        ).start()
        return carry

    lax.fori_loop(1, cols, push, 0)
    keep_m = pltpu.make_async_copy(piece(packed, me), piece(got, me), loc.at[2])
    keep_m.start()
    for d in order:
        spot = came_o.at[(row + d) % rows]
        pltpu.make_async_copy(spot, spot, yo_r.at[(row + d) % rows]).wait()
    add(part_o, came_o, mix_o, moving, resting)
    keep_m.wait()
    pltpu.make_async_copy(got.at[others], got.at[others], a2a_r).wait()

    def unpack(s):
        moved = tab[MOVED, s].astype(f32)
        away = got[tab[FROM_MSG, s]].astype(f32)
        here = mix_o[tab[FROM_MIX, s]].astype(f32)
        mixed[s] = jnp.where(moved > 0.5, away, here).astype(bf16)

    unrolled(requests, 8, unpack)
    for k in range(rows - 1):
        pltpu.make_async_copy(ss, ss, ss_s.at[k]).wait()
        pltpu.make_async_copy(part_o.at[0], part_o.at[0], yo_s.at[k + 1]).wait()
        for i in range(held // GROUP):
            spot = part_c.at[0, pl.ds(i * TOK, TOK)]
            pltpu.make_async_copy(spot, spot, yc_s.at[k + 1, i]).wait()
    pltpu.make_async_copy(got.at[others], got.at[others], a2a_s).wait()
    keep_x.wait()
    keep_e.wait()

    for ref, s_, r_ in ((xgot, x_s, x_r), (egot, e_s, e_r)):
        pltpu.make_async_copy(ref.at[others], ref.at[others], r_).wait()
        pltpu.make_async_copy(ref.at[others], ref.at[others], s_).wait()

    @pl.loop(0, held)
    def _(s):
        store(s).wait()


def mixer(tab, hid_c, hidden, fw, w_out, vectors, prev, pex, peb, rows, cols, cap):
    requests, _, model = hidden.shape
    held = hid_c.shape[0]
    tokens = requests * LEN
    depth, inner = w_out.shape
    width = model // rows
    slots = cols * cap
    rest = requests - held
    dt = hidden.dtype
    f32 = jnp.float32
    vmem = pl.BlockSpec(memory_space=pltpu.VMEM)
    hbm = pl.BlockSpec(memory_space=pltpu.HBM)
    dma = pltpu.SemaphoreType.DMA

    def body(*refs):
        mixer_kernel(rows, cols, cap, held, *refs)

    wide = inner + 2 * STATE
    return pl.pallas_call(
        body,
        out_shape=(
            jax.ShapeDtypeStruct((requests, LEN, width), dt),
            jax.ShapeDtypeStruct((held, inner, STATE), dt),
            jax.ShapeDtypeStruct((held, 4, wide), dt),
            jax.ShapeDtypeStruct((slots, LEN, inner + STATE), dt),
            jax.ShapeDtypeStruct((slots, 4, wide), dt),
        ),
        in_specs=[hbm] * (8 + len(vectors)),
        out_specs=(vmem, hbm, vmem, hbm, hbm),
        scratch_shapes=[
            pltpu.SMEM(tab.shape, jnp.int32),
            *[pltpu.VMEM(v.shape, v.dtype) for v in vectors],
            pltpu.VMEM(pex.shape, dt),
            pltpu.VMEM(peb.shape, dt),
            pltpu.VMEM((requests, LEN, model), dt),
            pltpu.VMEM((requests, LEN, model), dt),
            pltpu.VMEM((model, 2 * inner), dt),
            pltpu.VMEM((model, fw.shape[1] - 2 * inner), dt),
            pltpu.VMEM((model, inner), dt),
            pltpu.VMEM((held, inner, STATE), dt),
            pltpu.VMEM((tokens, inner), dt),
            pltpu.VMEM((tokens, inner), dt),
            pltpu.VMEM((tokens, 2 * STATE), dt),
            pltpu.VMEM((tokens, 128), f32),
            pltpu.VMEM((tokens, inner), dt),
            pltpu.VMEM((8, 128), f32),
            pltpu.VMEM((GROUP, 32, inner), f32),
            pltpu.VMEM((GROUP, 32, 2 * STATE), f32),
            pltpu.VMEM((3, held, inner), f32),
            pltpu.VMEM((3, held, 2 * STATE), f32),
            pltpu.VMEM((TOK, wide), f32),
            pltpu.VMEM((held, inner, STATE), dt),
            pltpu.VMEM((rest, LEN, inner + STATE), dt),
            pltpu.VMEM((rest, 4, wide), dt),
            pltpu.VMEM((slots, LEN, inner + STATE), dt),
            pltpu.VMEM((slots, 4, wide), dt),
            pltpu.VMEM((rows, rest * LEN, width), dt),
            pltpu.VMEM((rows, held * LEN, width), dt),
            pltpu.VMEM((rows, rest * LEN, width), dt),
            pltpu.VMEM((rows, held * LEN, width), dt),
            pltpu.VMEM((rows, 8, 128), f32),
            pltpu.VMEM((tokens, 128), f32),
            pltpu.VMEM((rest, LEN, width), dt),
            pltpu.VMEM((held, LEN, width), dt),
            pltpu.VMEM((slots, LEN, width), dt),
            pltpu.VMEM((slots, LEN, width), dt),
            dma(()), dma(()), dma((2 * inner // 256 + 2,)), dma((held,)),
            dma((len(vectors) + 3,)), dma((5,)), dma((3,)), dma((rows,)),
            dma((rows,)), dma((rows,)), dma((rows, held // GROUP)), dma((rows, held // GROUP)),
            dma(()), dma(()),
            dma(()), dma(()), dma(()), dma(()),
            pltpu.VMEM(w_out.shape, dt), dma((2,)), dma((2,)), dma((2, cols)),
        ],
        compiler_params=pltpu.CompilerParams(
            collective_id=1, has_side_effects=True, vmem_limit_bytes=60 << 20
        ),
        name="mixer",
    )(tab, hid_c, hidden, fw, w_out, *vectors, prev, pex, peb)


def arrive_kernel(
    tab_in, xgot_in, egot_in, edge_in, nst_in, nst, nex, neb,
    tab, xgot, egot, edge, was, xs, bs, ex, eb, new, n_sem, m_sem, l_sem,
):
    f32, bf16 = jnp.float32, jnp.bfloat16
    count, inner = new.shape[0], new.shape[1]
    loads = [
        pltpu.make_async_copy(a, b, l_sem.at[k])
        for k, (a, b) in enumerate(
            ((tab_in, tab), (xgot_in, xgot), (nst_in, was), (egot_in, egot), (edge_in, edge))
        )
    ]
    for copy in loads:
        copy.start()
    loads[0].wait()

    def place(s):
        return pltpu.make_async_copy(was.at[s], nst.at[tab[POS, s]], m_sem.at[s])

    loads[1].wait()
    loads[2].wait()

    @pl.loop(0, count)
    def _(s):
        place(s).start()

    t_ids, _ = token_masks()
    none = jnp.zeros((TOK, STATE), bf16)

    def store(u):
        return pltpu.make_async_copy(new.at[u], nst.at[tab[POS_O, u]], n_sem.at[u])

    @pl.loop(0, count // GROUP)
    def _(i):
        for r in range(GROUP):
            slot = tab[PICK_O, i * GROUP + r]
            xs[r] = xgot[slot, :, :inner]
            bs[r] = xgot[slot, :, inner:]
        lhs = xs[...].reshape(TOK, inner).astype(f32).T.astype(bf16)
        b_in = bs[...].reshape(TOK, STATE)
        for pair in range(GROUP // 2):
            cut = jnp.concatenate(
                [
                    jnp.where(t_ids // LEN == r, b_in, none)
                    for r in (2 * pair, 2 * pair + 1)
                ],
                axis=1,
            )
            out = jnp.dot(lhs, cut, preferred_element_type=f32).astype(bf16)
            for k in (0, 1):
                u = i * GROUP + 2 * pair + k
                new[u] = out[:, k * STATE : (k + 1) * STATE]
                store(u).start()

    for copy in loads[3:]:
        copy.wait()

    @pl.loop(0, count)
    def _(u):
        for source, k, spot in (
            (egot, tab[PICK_O, u], tab[POS_O, u]), (edge, u, tab[POS, u])
        ):
            lines = source[k].astype(f32)
            at = pl.ds(spot, 1)
            for q in range(KCONV - 1):
                ex[q, at, :] = lines[q : q + 1, :inner]
                eb[q, at, :] = lines[q : q + 1, inner:]

    nex[...] = ex[...].astype(bf16)
    neb[...] = eb[...].astype(bf16)

    @pl.loop(0, count)
    def _(u):
        store(u).wait()
        place(u).wait()


def arrive(tab, xgot, egot, edge, nst):
    count, inner, _ = nst.shape
    requests = 2 * count
    dt, f32 = nst.dtype, jnp.float32
    vmem = pl.BlockSpec(memory_space=pltpu.VMEM)
    hbm = pl.BlockSpec(memory_space=pltpu.HBM)
    return pl.pallas_call(
        arrive_kernel,
        out_shape=(
            jax.ShapeDtypeStruct((requests, inner, STATE), dt),
            jax.ShapeDtypeStruct((3, requests, inner), dt),
            jax.ShapeDtypeStruct((3, requests, 2 * STATE), dt),
        ),
        in_specs=[hbm] * 5,
        out_specs=(hbm, vmem, vmem),
        scratch_shapes=[
            pltpu.SMEM(tab.shape, jnp.int32),
            pltpu.VMEM(xgot.shape, dt),
            pltpu.VMEM(egot.shape, dt),
            pltpu.VMEM(edge.shape, dt),
            pltpu.VMEM(nst.shape, dt),
            pltpu.VMEM((GROUP, LEN, inner), dt),
            pltpu.VMEM((GROUP, LEN, STATE), dt),
            pltpu.VMEM((3, requests, inner), f32),
            pltpu.VMEM((3, requests, 2 * STATE), f32),
            pltpu.VMEM((count, inner, STATE), dt),
            pltpu.SemaphoreType.DMA((count,)),
            pltpu.SemaphoreType.DMA((count,)),
            pltpu.SemaphoreType.DMA((5,)),
        ],
        compiler_params=pltpu.CompilerParams(vmem_limit_bytes=60 << 20),
        name="arrive",
    )(tab, xgot, egot, edge, nst)


def per_device(
    hidden, w_zx, w_bc, w_dt, w_out, dt_bias, a_log, d_skip, conv_x_w, conv_x_b,
    conv_bc_w, conv_bc_b, norm_gain, prev_state, prev_edge_x, prev_edge_bc,
    holder, continued, owner, accepted,
):
    rows, cols = lax.axis_size("row"), lax.axis_size("col")
    tokens, model = hidden.shape
    requests = tokens // LEN
    heads = dt_bias.shape[0]
    inner = heads * HEAD_DIM
    held = prev_state.shape[0]
    cap = 2 * ((requests // 4 + cols - 1) // cols)
    code = owner + 64 * (continued == 1).astype(jnp.int32) + 128 * accepted
    tab = route(code.reshape(cols, requests), held)
    hidden = hidden.reshape(requests, LEN, model)
    hid_c, fw = gather_all(tab, hidden, w_zx, w_bc, w_dt.T, rows, cols, cap, held)
    vectors = (
        dt_bias[None, :], a_log[None, :], d_skip[None, :],
        conv_x_w, conv_x_b[None, :], conv_bc_w, conv_bc_b[None, :], norm_gain[None, :],
    )
    mixed, moved, edge, xgot, egot = mixer(
        tab, hid_c, hidden, fw, w_out, vectors, prev_state.reshape(held, inner, STATE),
        prev_edge_x.transpose(1, 0, 2), prev_edge_bc.transpose(1, 0, 2),
        rows, cols, cap,
    )
    states, new_x, new_bc = arrive(tab, xgot, egot, edge, moved)
    return (
        mixed.reshape(tokens, model // rows),
        states.reshape(requests, heads, HEAD_DIM, STATE),
        new_x.transpose(1, 0, 2),
        new_bc.transpose(1, 0, 2),
    )


def solution(mesh):
    return jax.shard_map(
        per_device,
        mesh=mesh,
        in_specs=(
            P("col", None),
            P("col", "row"),
            P("col", None),
            P("col", "row"),
            P("col", "row"),
            P("row"),
            P("row"),
            P("row"),
            P(None, "row"),
            P("row"),
            P(),
            P(),
            P("row"),
            P("col", "row", None, None),
            P("col", None, "row"),
            P("col", None, None),
            P(),
            P(),
            P(),
            P(),
        ),
        out_specs=(
            P("col", "row"),
            P("col", "row", None, None),
            P("col", None, "row"),
            P("col", None, None),
        ),
        check_vma=False,
    )
```

```python
import jax
import jax.numpy as jnp
from jax import lax
from jax.experimental import pallas as pl
from jax.experimental.pallas import tpu as pltpu
from jax.sharding import PartitionSpec as P

HEAD_DIM = 64
STATE = 128
KCONV = 4
LEN = 16
INNER = 2048
SIDE = 4
GROUP = 8
TOK = GROUP * LEN
MESH = pl.DeviceIdType.MESH
HIGHEST = lax.Precision.HIGHEST


def route_kernel(held, code, out):
    f32, bf16 = jnp.float32, jnp.bfloat16
    me = lax.axis_index("col")
    groups, requests = code.shape
    value = code[...]
    o, c, a = value & 63, (value >> 6) & 1, value >> 7

    def dot(x, y):
        return jnp.dot(x.astype(bf16), y.astype(bf16), preferred_element_type=f32)

    def dot0(x, y):
        return lax.dot_general(
            x.astype(bf16), y.astype(bf16), (((0,), (0,)), ((), ())), preferred_element_type=f32
        )

    def ids(shape, dim):
        return lax.broadcasted_iota(jnp.int32, shape, dim)

    below = (ids((requests, requests), 0) < ids((requests, requests), 1)).astype(f32)
    prior = (ids((groups, groups), 1) < ids((groups, groups), 0)).astype(f32)
    lane = ids((groups, 128), 1).astype(f32)
    group = ids((groups, 128), 0).astype(f32)
    spots, inside, starts = [], [], []
    for kind in (1, 0):
        mask = ((o == me) & (c == kind)).astype(f32)
        rank = dot(mask, below)
        count = jnp.broadcast_to(jnp.sum(mask, axis=1, keepdims=True), (groups, 128))
        start = dot(prior, count)
        hot = ((start <= lane) & (lane < start + count)).astype(f32)
        spots.append((jnp.where(mask > 0, rank, -1.0), hot))
        inside.append(rank)
        starts.append(start)
    rank_all, start_all = inside[0] + inside[1], starts[0] + starts[1]
    picks, places, taken = [], [], []
    for k in (0, 1):
        spot, hot = spots[k]
        order = jnp.sum(hot * (lane - starts[k]), axis=0, keepdims=True)
        any_hot = jnp.sum(hot, axis=0, keepdims=True)
        order = jnp.where(any_hot > 0, order, -5.0)
        match = (dot0(spot, hot) == order).astype(f32)
        picks.append(jnp.sum(hot * (2 * group + lane - starts[k]), axis=0, keepdims=True))
        places.append(
            jnp.sum(hot * start_all, axis=0, keepdims=True)
            + jnp.sum(match * dot0(rank_all, hot), axis=0, keepdims=True)
        )
        taken.append(jnp.sum(match * dot0(a, hot), axis=0, keepdims=True))
    lane_i, group_i = ids((groups, 128), 1), ids((groups, 128), 0)
    back = jnp.sum(
        jnp.where(lane_i // 2 == group_i, starts[0] + (lane_i % 2).astype(f32), 0.0),
        axis=0, keepdims=True,
    )
    back = jnp.minimum(back, held - 1.0)

    def my_row(x, fill):
        row = jnp.sum(
            jnp.where(ids((groups, requests), 0) == me, x, 0).astype(f32), axis=0, keepdims=True
        )
        rest = jnp.full((1, 128 - requests), fill, f32)
        return jnp.concatenate([row, rest], axis=1)

    o_row, c_row, a_row = my_row(o, 99.0), my_row(c, 2.0), my_row(a, 0.0)

    def column(row):
        return jnp.broadcast_to(row, (128, 128)).T

    o_col, c_col, a_col = column(o_row), column(c_row), column(a_row)
    ii, jj = ids((128, 128), 0), ids((128, 128), 1)
    alike = (o_col == o_row) & (c_col == c_row)
    rank_row = jnp.sum((alike & (ii < jj)).astype(f32), axis=0, keepdims=True)
    rank_col = jnp.sum((alike & (jj < ii)).astype(f32), axis=1, keepdims=True)
    nth_row = jnp.sum(((c_col == 0) & (ii < jj)).astype(f32), axis=0, keepdims=True)
    nth_col = jnp.sum(((c_row == 0) & (jj < ii)).astype(f32), axis=1, keepdims=True)
    key_row = 2 * o_row + rank_row
    key_col = 2 * o_col + rank_col
    fi, fj = ii.astype(f32), jj.astype(f32)
    goes = (c_col == 1) & (key_col == fj)
    leaves = (c_col == 0) & (key_col == fj)
    stays = (c_col == 0) & (nth_col == fj)

    def total(mask, x):
        return jnp.sum(jnp.where(mask, x, 0.0), axis=0, keepdims=True)

    table = (
        total(goes, fi), picks[0], back,
        jnp.where(c_row == 1, key_row, 0.0), jnp.where(c_row == 0, nth_row, 0.0),
        (c_row == 1).astype(f32),
        total(stays, fi), total(stays, key_col), total(stays, a_col),
        taken[0], places[0], picks[1], places[1], total(leaves, nth_col),
    )
    for k, line in enumerate(table):
        out[k : k + 1, :] = line.astype(jnp.int32)
    out[len(table) :, :] = jnp.zeros((16 - len(table), 128), jnp.int32)


SEND, PICK, BACK, FROM_MSG, FROM_MIX, MOVED, STAY, STAY_KEY, STAY_ACC, ACC, POS, PICK_O, POS_O, LEAVE = range(14)


def unrolled(count, step, body):
    def some(i, carry):
        for k in range(step):
            body(i * step + k)
        return carry

    lax.fori_loop(0, count // step, some, 0)


def greet(row, me, rows, cols):
    barrier = pltpu.get_barrier_semaphore()

    def along_col(d, carry):
        pl.semaphore_signal(
            barrier, inc=1, device_id=(row, (me + d) % cols), device_id_type=MESH
        )
        return carry

    lax.fori_loop(1, cols, along_col, 0)

    def along_row(d, carry):
        pl.semaphore_signal(
            barrier, inc=1, device_id=((row + d) % rows, me), device_id_type=MESH
        )
        return carry

    lax.fori_loop(1, rows, along_row, 0)
    return barrier


def torus_ring(row, me, depth, block, own, span, gone, twin, came):
    core = me % 2
    x = (me // 2) % SIDE
    z = me // (2 * SIDE)
    a = x + core * (z - x)
    b = z + core * (x - z)

    def at(pa, pb):
        pa, pb = (pa + SIDE) % SIDE, (pb + SIDE) % SIDE
        px = pa + core * (pb - pa)
        pz = pb + core * (pa - pb)
        return (pz * SIDE + px) * 2 + core

    sibling = me + 1 - 2 * core
    sent = [0, 0]

    def send(h, source, c, dest):
        sent[h] += 1
        arrival = twin.at[h] if dest is sibling else came.at[h, c]
        pltpu.make_async_remote_copy(
            source, block(h, c), gone.at[h], arrival,
            device_id=(row, dest), device_id_type=MESH,
        ).start()

    def forward(h, c, dest):
        send(h, block(h, c), c, dest)

    def arrived(h, c):
        pltpu.make_async_copy(block(h, c), block(h, c), came.at[h, c]).wait()

    up, down, far = at(a + 1, b), at(a - 1, b), at(a + 2, b)
    over, under = at(a, b + 1), at(a, b - 1)

    def begin():
        for dest in (up, down, over, under, sibling):
            for h in (0, 1):
                send(h, own(h), me, dest)

    def near():
        arrived(0, down)
        forward(0, down, up)
        arrived(1, up)
        forward(1, up, down)
        arrived(1, down)
        arrived(0, up)
        for c in (down, up):
            for h in (0, 1):
                for dest in (over, under, sibling):
                    forward(h, c, dest)

    def beyond():
        for h in (0, 1):
            arrived(h, far)
            for dest in (over, under, sibling):
                forward(h, far, dest)

    def beside():
        for k in (0, 1, -1, 2):
            low, high = at(a + k, b - 1), at(a + k, b + 1)
            arrived(0, low)
            forward(0, low, over)
            arrived(1, high)
            forward(1, high, under)
            arrived(1, low)
            arrived(0, high)
            for h in (0, 1):
                forward(h, low, sibling)
                forward(h, high, sibling)

    def opposite():
        for k in (0, 1, -1, 2):
            c = at(a + k, b + 2)
            for h in (0, 1):
                arrived(h, c)
                forward(h, c, sibling)

    def finish():
        for h in (0, 1):
            half = span(h, 16 * depth)
            pltpu.make_async_copy(half, half, twin.at[h]).wait()
        for h in (0, 1):
            part = span(h, sent[h] * depth)
            pltpu.make_async_copy(part, part, gone.at[h]).wait()

    return begin, near, beyond, beside, opposite, finish


def gather_kernel(
    rows, cols, cap, code, hidden, w_zx, w_bc, w_dt_in, hid_full, fw, tab_out,
    table, tab, w_dt, ws, sl, packed0, packed1, got0, got1, own0, own1, loc, a2a_s, a2a_r, gone, twin, arr, y_s, y_r,
):
    row, me = lax.axis_index("row"), lax.axis_index("col")
    barrier = greet(row, me, rows, cols)
    width = sl.shape[2]
    half = own0.shape[0] // 2
    packs, gots, owns = (packed0, packed1), (got0, got1), (own0, own1)
    lows = (0, packed0.shape[2])
    depth = w_zx.shape[0]

    def cols_of(r):
        return pl.ds(pl.multiple_of(r * width, 128), width)

    cut = 128 * (ws.shape[1] // 256)
    lanes_of = (pl.ds(0, cut), pl.ds(cut, ws.shape[1] - cut))

    def lines(c):
        return pl.ds(pl.multiple_of(c * depth, 16), depth)

    ring = torus_ring(
        row, me, depth,
        lambda h, c: fw.at[lines(c), lanes_of[h]],
        lambda h: ws.at[:, lanes_of[h]],
        lambda h, count: fw.at[pl.ds(0, count), lanes_of[h]],
        gone, twin, arr,
    )
    begin, near, beyond, beside, opposite, finish = ring

    load = pltpu.make_async_copy(hidden.at[:, :, cols_of(row)], sl, loc.at[0])
    load.start()
    inner = w_zx.shape[1]
    states = w_bc.shape[1]
    heads = w_dt_in.shape[0]
    loads = (
        pltpu.make_async_copy(w_dt_in, w_dt, loc.at[6]),
        pltpu.make_async_copy(w_zx, ws.at[:, pl.ds(0, inner)], loc.at[7]),
        pltpu.make_async_copy(w_bc, ws.at[:, pl.ds(inner, states)], loc.at[8]),
    )
    for copy in loads:
        copy.start()
    route_kernel(own0.shape[0], code, table)
    to_scalars = pltpu.make_async_copy(table, tab, loc.at[5])
    to_scalars.start()
    keep_t = pltpu.make_async_copy(table, tab_out, loc.at[2])
    keep_t.start()
    for copy in loads:
        copy.wait()
    square = jnp.concatenate(
        [w_dt[...].astype(jnp.float32), jnp.zeros((heads, 128 - depth), jnp.float32)], axis=1
    )
    square = jnp.concatenate([square, jnp.zeros((128 - heads, 128), jnp.float32)], axis=0).T
    ws[:, inner + states :] = square[:depth, :].astype(ws.dtype)
    keep_w = pltpu.make_async_copy(ws, fw.at[lines(me), :], loc.at[1])
    keep_w.start()
    load.wait()
    to_scalars.wait()

    def piece(ref, c):
        return ref.at[pl.ds(c * cap, cap)]

    keeps = []
    for k in (0, 1):
        packed, got, low = packs[k], gots[k], lows[k]

        def pack(s):
            j = jnp.clip(tab[SEND, s], 0, sl.shape[0] - 1)
            packed[s] = sl[j, :, low : low + packed.shape[2]]

        unrolled(cols * cap, 8, pack)
        if k == 0:
            pl.semaphore_wait(barrier, cols - 1 + rows - 1)

        def push(d, carry):
            peer = (me + d) % cols
            pltpu.make_async_remote_copy(
                piece(packed, peer), piece(got, me), a2a_s.at[k], a2a_r.at[k],
                device_id=(row, peer), device_id_type=MESH,
            ).start()
            return carry

        lax.fori_loop(1, cols, push, 0)
        keeps.append(pltpu.make_async_copy(piece(packed, me), piece(got, me), loc.at[3 + 6 * k]))
        keeps[k].start()

    begin()
    near()
    others = pl.ds(0, (cols - 1) * cap)
    right, left = (row + 1) % rows, (row + rows - 1) % rows
    far_row = (row + 2) % rows

    def part(ref, k, h, r):
        low, size = lows[k], owns[k].shape[2]
        lanes = pl.ds(pl.multiple_of(r * width + low, 128), size)
        return ref.at[pl.ds(h * half, half), :, lanes]

    def y_here(k, h, r):
        spot = part(hid_full, k, h, r)
        pltpu.make_async_copy(spot, spot, y_r.at[k, r, h]).wait()

    def pass_on(k, h, source, dest):
        spot = part(hid_full, k, h, source)
        pltpu.make_async_remote_copy(
            spot, spot, y_s.at[k, 4 + h], y_r.at[k, source, h],
            device_id=(dest, me), device_id_type=MESH,
        ).start()

    for k in (0, 1):
        got, own = gots[k], owns[k]
        keeps[k].wait()
        pltpu.make_async_copy(got.at[others], got.at[others], a2a_r.at[k]).wait()

        def unpack(s):
            own[s] = got[jnp.clip(tab[PICK, s], 0, got.shape[0] - 1)]

        unrolled(own.shape[0], 8, unpack)
        for n, dest in ((0, right), (1, left)):
            for h in (n, 1 - n):
                pltpu.make_async_remote_copy(
                    own.at[pl.ds(h * half, half)], part(hid_full, k, h, row),
                    y_s.at[k, 2 * n + h], y_r.at[k, row, h],
                    device_id=(dest, me), device_id_type=MESH,
                ).start()
        lanes = pl.ds(pl.multiple_of(row * width + lows[k], 128), own.shape[2])
        keeps.append(pltpu.make_async_copy(own, hid_full.at[:, :, lanes], loc.at[4 + 6 * k]))
        keeps[2 + k].start()

    beyond()
    y_here(0, 0, left)
    pass_on(0, 0, left, right)
    y_here(0, 1, right)
    pass_on(0, 1, right, left)
    beside()
    y_here(1, 0, left)
    pass_on(1, 0, left, right)
    y_here(1, 1, right)
    pass_on(1, 1, right, left)
    opposite()
    for k in (0, 1):
        y_here(k, 1, left)
        y_here(k, 0, right)
        y_here(k, 0, far_row)
        y_here(k, 1, far_row)

    finish()
    keep_w.wait()
    keep_t.wait()
    keeps[2].wait()
    keeps[3].wait()

    for k in (0, 1):
        pltpu.make_async_copy(packs[k].at[others], packs[k].at[others], a2a_s.at[k]).wait()

    for k in (0, 1):
        for n in range(6):
            spot = part(hid_full, k, n % 2, row)
            pltpu.make_async_copy(spot, spot, y_s.at[k, n]).wait()


def gather_all(code, hidden, w_zx, w_bc, w_dt, rows, cols, cap, held):
    requests, _, model = hidden.shape
    width = model // rows
    dt = hidden.dtype
    hbm = pl.BlockSpec(memory_space=pltpu.HBM)
    dma = pltpu.SemaphoreType.DMA
    depth = w_zx.shape[0]
    wide = w_zx.shape[1] + w_bc.shape[1] + 128

    def body(*refs):
        gather_kernel(rows, cols, cap, *refs)

    return pl.pallas_call(
        body,
        out_shape=(
            jax.ShapeDtypeStruct((held, LEN, model), dt),
            jax.ShapeDtypeStruct((depth * cols, wide), dt),
            jax.ShapeDtypeStruct((16, 128), jnp.int32),
        ),
        in_specs=[pl.BlockSpec(memory_space=pltpu.VMEM)] + [hbm] * 4,
        out_specs=(hbm, hbm, hbm),
        scratch_shapes=[
            pltpu.VMEM((16, 128), jnp.int32),
            pltpu.SMEM((16, 128), jnp.int32),
            pltpu.VMEM(w_dt.shape, dt),
            pltpu.VMEM((depth, wide), dt),
            pltpu.VMEM((requests, LEN, width), dt),
            pltpu.VMEM((cols * cap, LEN, 128), dt),
            pltpu.VMEM((cols * cap, LEN, width - 128), dt),
            pltpu.VMEM((cols * cap, LEN, 128), dt),
            pltpu.VMEM((cols * cap, LEN, width - 128), dt),
            pltpu.VMEM((held, LEN, 128), dt),
            pltpu.VMEM((held, LEN, width - 128), dt),
            dma((11,)), dma((2,)), dma((2,)),
            dma((2,)), dma((2,)), dma((2, cols)),
            dma((2, 6)), dma((2, rows, 2)),
        ],
        compiler_params=pltpu.CompilerParams(
            collective_id=0, has_side_effects=True, vmem_limit_bytes=60 << 20
        ),
        name="gather_all",
    )(code, hidden, w_zx, w_bc, w_dt)


def silu(v):
    return v / (1.0 + jnp.exp(-v))


def token_masks():
    t_ids = lax.broadcasted_iota(jnp.int32, (TOK, TOK), 0)
    s_ids = lax.broadcasted_iota(jnp.int32, (TOK, TOK), 1)
    return t_ids, s_ids


def mixer_kernel(
    rows, cols, cap, held, tab_in, hid_c, hidden, fw, w_out, *refs,
):
    sources, refs = refs[:8], refs[8:]
    prev, pex_in, peb_in, mixed, nst, edge_c, xgot, egot, tab, *refs = refs
    params, refs = refs[:8], refs[8:]
    dtb, alog, skip, cxw, cxb, cbw, cbb, gain = params
    (
        pex, peb, hid, home, wa, wb, wo, old, gate, xin, bc, dts, gg, ss, cx, cb, pexf, pebf, es,
        new, sent, edge_o, xmsg, emsg, part_o, part_c, came_o, came_c, ss_in, scale, mix_o,
        mix, packed, got,
        h_sem, o_sem, w_sem, n_sem, v_sem, loc, ss_s, ss_r, yo_s, yo_r, yc_s, yc_r,
        a2a_s, a2a_r, x_s, x_r, e_s, e_r, mine, gone, twin, arr,
    ) = refs
    row, me = lax.axis_index("row"), lax.axis_index("col")
    barrier = greet(row, me, rows, cols)
    depth = w_out.shape[0]
    load_mine = pltpu.make_async_copy(w_out, mine, loc.at[3])
    load_mine.start()
    f32, bf16 = jnp.float32, jnp.bfloat16
    inner = gain.shape[1]
    requests = hid.shape[0]
    tokens = requests * LEN
    model = hid.shape[2]
    heads = inner // HEAD_DIM
    blocks = wa.shape[1] // 256
    assert blocks == 4

    load_h = pltpu.make_async_copy(hid_c, hid.at[pl.ds(0, held)], h_sem)
    load_h.start()
    small = list(zip(sources + (pex_in, peb_in, tab_in), list(params) + [pex, peb, tab]))
    small = [pltpu.make_async_copy(a, b, v_sem.at[k]) for k, (a, b) in enumerate(small)]
    small[-1].start()
    for copy in small[:-1]:
        copy.start()
    small[-1].wait()

    def wa_load(n):
        at = pl.ds(n * 256, 256)
        return pltpu.make_async_copy(fw.at[:, at], wa.at[:, at], w_sem.at[n])

    wa_load(0).start()

    load_home = pltpu.make_async_copy(hidden, home, o_sem)
    load_home.start()
    for n in range(1, blocks):
        wa_load(n).start()
    late = pl.ds(2 * inner, wb.shape[1])
    load_bc = pltpu.make_async_copy(fw.at[:, late], wb, w_sem.at[blocks])
    load_old = pltpu.make_async_copy(prev, old, w_sem.at[blocks + 1])
    load_bc.start()
    load_old.start()
    load_mine.wait()
    cut = inner // 2

    def lines_of(c):
        return pl.ds(pl.multiple_of(c * depth, 16), depth)

    begin, near, beyond, beside, opposite, finish = torus_ring(
        row, me, depth,
        lambda h, c: wo.at[lines_of(c), pl.ds(h * cut, cut)],
        lambda h: mine.at[:, pl.ds(h * cut, cut)],
        lambda h, count: wo.at[pl.ds(0, count), pl.ds(h * cut, cut)],
        gone, twin, arr,
    )
    keep_mine = pltpu.make_async_copy(mine, wo.at[lines_of(me), :], loc.at[4])
    keep_mine.start()
    for copy in small[:-1]:
        copy.wait()
    pexf[...] = pex[...].astype(f32)
    pebf[...] = peb[...].astype(f32)

    t_ids, s_ids = token_masks()
    row_ids = lax.broadcasted_iota(jnp.int32, (4 * GROUP, TOK), 0)
    k_ids = lax.broadcasted_iota(jnp.int32, (4 * GROUP, TOK), 1)
    r_ids, q_ids = row_ids // 4, row_ids % 4
    es[...] = jnp.zeros(es.shape, f32)
    same = (t_ids // LEN) == (s_ids // LEN)
    causal = same & (t_ids >= s_ids)
    tri = causal.astype(f32)
    spread_h = (
        lax.broadcasted_iota(jnp.int32, (TOK, inner), 1) // HEAD_DIM
        == lax.broadcasted_iota(jnp.int32, (TOK, inner), 0)
    ).astype(f32)

    def wide(ref):
        return jnp.concatenate([ref[...], jnp.zeros((1, TOK - heads), f32)], axis=1)

    bias, rate = wide(dtb), -jnp.exp(wide(alog))
    skip_x = jnp.dot(
        jnp.broadcast_to(wide(skip), (8, TOK)), spread_h,
        precision=HIGHEST, preferred_element_type=f32,
    )[0:1, :]

    load_h.wait()
    load_home.wait()

    def stay(n):
        hid[held + n] = home[tab[STAY, n]]

    unrolled(requests - held, 4, stay)
    left = lax.broadcasted_iota(jnp.int32, (tokens, 128), 1) < HEAD_DIM
    for n in range(blocks):
        wa_load(n).wait()
        z = jnp.dot(
            hid[...].reshape(tokens, model), wa[:, n * 256 : (n + 1) * 256],
            preferred_element_type=f32,
        )
        z0, z1 = z[:, :128], z[:, 128:]
        at = slice(n * 128, (n + 1) * 128)
        gate[:, at] = jnp.where(left, z0, pltpu.roll(z1, HEAD_DIM, 1)).astype(bf16)
        xin[:, at] = jnp.where(left, pltpu.roll(z0, HEAD_DIM, 1), z1).astype(bf16)
        if n == 0:
            pl.semaphore_wait(barrier, cols - 1 + rows - 1)
            begin()
        if n == 2:
            near()
    load_bc.wait()
    z = jnp.dot(hid[...].reshape(tokens, model), wb[...], preferred_element_type=f32)
    bc[...] = z[:, : 2 * STATE].astype(bf16)
    dts[...] = z[:, 2 * STATE :]
    beyond()
    load_old.wait()

    def store(s):
        return pltpu.make_async_copy(new.at[s], nst.at[s], n_sem.at[s])

    def group(i, live):
        at = pl.ds(pl.multiple_of(i * TOK, TOK), TOK)
        first = i * GROUP
        last = jnp.zeros((TOK, TOK), jnp.int32)
        row_acc = jnp.zeros((4 * GROUP, TOK), jnp.int32)
        for r in range(GROUP):
            acc = tab[ACC, first + r] if live else tab[STAY_ACC, first - held + r]
            row_acc = jnp.where(r_ids == r, acc, row_acc)
            last = jnp.where(t_ids // LEN == r, acc, last)
            if live:
                for k in range(KCONV - 1):
                    cx[r, 13 + k : 14 + k, :] = pexf[k, pl.ds(first + r, 1), :]
                    cb[r, 13 + k : 14 + k, :] = pebf[k, pl.ds(first + r, 1), :]
        if not live:
            cx[:, 8:16, :] = jnp.zeros((GROUP, 8, inner), f32)
            cb[:, 8:16, :] = jnp.zeros((GROUP, 8, 2 * STATE), f32)
        cx[:, 16:32, :] = xin[at, :].astype(f32).reshape(GROUP, LEN, inner)
        cb[:, 16:32, :] = bc[at, :].astype(f32).reshape(GROUP, LEN, 2 * STATE)
        tot_x = cxb[...].reshape(1, 1, inner) + cxw[0:1, :].reshape(1, 1, inner) * cx[:, 13:29, :]
        tot_b = cbb[...].reshape(1, 1, 2 * STATE) + cbw[0:1, :].reshape(
            1, 1, 2 * STATE
        ) * cb[:, 13:29, :]
        for k in range(1, KCONV):
            tot_x = tot_x + cxw[k : k + 1, :].reshape(1, 1, inner) * cx[:, 13 + k : 29 + k, :]
            tot_b = tot_b + cbw[k : k + 1, :].reshape(1, 1, 2 * STATE) * cb[:, 13 + k : 29 + k, :]
        xc = silu(tot_x).reshape(TOK, inner).astype(bf16)
        bcc = silu(tot_b).reshape(TOK, 2 * STATE).astype(bf16)
        near = jnp.concatenate([xin[at, :], bc[at, :]], axis=1)
        want = q_ids + row_acc
        pick = (k_ids == LEN * r_ids + want - 3) & (want >= 3) & (q_ids < 3)
        edge = jnp.dot(pick.astype(bf16), near, preferred_element_type=f32)
        if live:
            for k in range(KCONV - 1):
                rows8 = pl.ds(pl.multiple_of(first, GROUP), GROUP)
                es[k * GROUP : (k + 1) * GROUP, :inner] = pexf[k, rows8, :]
                es[k * GROUP : (k + 1) * GROUP, inner:] = pebf[k, rows8, :]
            pick = (k_ids == GROUP * want + r_ids) & (want < 3) & (q_ids < 3)
            edge = edge + jnp.dot(
                pick.astype(bf16), es[...].astype(bf16), preferred_element_type=f32
            )
        for r in range(GROUP):
            lines = edge[4 * r : 4 * r + 4, :].astype(bf16)
            if live:
                edge_c[first + r] = lines
            else:
                edge_o[first - held + r] = lines
        b_in, c_in = bcc[:, :STATE], bcc[:, STATE:]
        xf = xc.astype(f32)
        raw = dts[at, :] + bias
        step = jnp.maximum(raw, 0.0) + jnp.log(1.0 + jnp.exp(-jnp.abs(raw)))
        decay = jnp.dot(tri, step * rate, precision=HIGHEST, preferred_element_type=f32)
        decay_t = decay.T
        step_t = step.T
        choose = (same & (s_ids % LEN == last - 1)).astype(f32)
        reach = jnp.dot(choose, decay, precision=HIGHEST, preferred_element_type=f32)
        taken = t_ids % LEN < last
        weight = jnp.where(taken, jnp.exp(jnp.minimum(reach - decay, 0.0)), 0.0) * step
        weight_x = jnp.dot(weight, spread_h, precision=HIGHEST, preferred_element_type=f32)
        scores = lax.dot_general(
            c_in, b_in, (((1,), (1,)), ((), ())), preferred_element_type=f32
        )
        scores = jnp.where(causal, scores, 0.0)
        half = s_ids < HEAD_DIM
        zero = jnp.zeros((TOK, 2 * HEAD_DIM), bf16)
        y = []
        for pair in range(heads // 2):
            mats = []
            for h in (2 * pair, 2 * pair + 1):
                gap = decay[:, h : h + 1] - decay_t[h : h + 1, :]
                mats.append(
                    (jnp.exp(jnp.minimum(gap, 0.0)) * scores * step_t[h : h + 1, :]).astype(bf16)
                )
            xp = xc[:, pair * 128 : (pair + 1) * 128]
            both = jnp.concatenate([jnp.where(half, xp, zero), jnp.where(half, zero, xp)], axis=0)
            y.append(
                jnp.dot(jnp.concatenate(mats, axis=1), both, preferred_element_type=f32)
            )
        y = jnp.concatenate(y, axis=1)
        if live:
            grow_x = jnp.dot(jnp.exp(decay), spread_h, precision=HIGHEST, preferred_element_type=f32)
            carried = [
                lax.dot_general(
                    c_in[r * LEN : (r + 1) * LEN, :], old[first + r], (((1,), (1,)), ((), ())),
                    preferred_element_type=f32,
                )
                for r in range(GROUP)
            ]
            y = y + grow_x * jnp.concatenate(carried, axis=0)
        y = y + skip_x * xf
        gated = y * silu(gate[at, :].astype(f32))
        gg[at, :] = (gated * gain[...]).astype(bf16)
        squares = jnp.sum(gated * gated, axis=1, keepdims=True)
        ss[pl.ds(i, 1), :] = jnp.broadcast_to(squares, (TOK, TOK)).T[0:1, :]

        if not live:
            out = (xf * weight_x).astype(bf16)
            for r in range(GROUP):
                lines = slice(r * LEN, (r + 1) * LEN)
                sent[first - held + r, :, :inner] = out[lines, :]
                sent[first - held + r, :, inner:] = b_in[lines, :]
            return
        xw = (xf * weight_x).T
        high = xw.astype(bf16)
        low = (xw - high.astype(f32)).astype(bf16)
        lhs = jnp.concatenate([high, low], axis=1)
        keep_t = jnp.exp(reach).T
        none = jnp.zeros((TOK, STATE), bf16)
        for pair in range(GROUP // 2):
            cut = jnp.concatenate(
                [
                    jnp.where(t_ids // LEN == r, b_in, none)
                    for r in (2 * pair, 2 * pair + 1)
                ],
                axis=1,
            )
            added = jnp.dot(
                lhs, jnp.concatenate([cut, cut], axis=0), preferred_element_type=f32
            )
            for k in (0, 1):
                r = 2 * pair + k
                s = first + r
                factor = jnp.broadcast_to(keep_t[0:heads, r * LEN : r * LEN + 1], (heads, STATE))
                was = old[s].astype(f32).reshape(heads, HEAD_DIM, STATE)
                now = factor[:, None, :] * was + added[:, k * STATE : (k + 1) * STATE].reshape(
                    heads, HEAD_DIM, STATE
                )
                new[s] = now.reshape(inner, STATE).astype(bf16)
                store(s).start()

    group(held // GROUP, False)
    beside()

    @pl.loop(held // GROUP + 1, requests // GROUP)
    def _(i):
        group(i, False)

    opposite()

    moving = held * LEN
    resting = tokens - moving
    width = part_c.shape[2]
    pieces = width // 128
    order = (1, 3, 2)

    def project(lines, peer, j, count):
        at = pl.ds(pl.multiple_of(peer * width + j * 128, 128), count * 128)
        return lax.dot_general(
            gg[lines, :], wo[at, :], (((1,), (1,)), ((), ())), preferred_element_type=f32
        ).astype(bf16)

    def rest_block(peer):
        part_o[peer] = project(slice(moving, tokens), peer, 0, pieces)

    def move_block(i, peer):
        lines = pl.ds(pl.multiple_of(i * TOK, TOK), TOK)
        part_c[peer, lines, :] = project(lines, peer, 0, pieces)

    def piece(ref, c):
        return ref.at[pl.ds(c * cap, cap)]

    def to_slots(q):
        n = tab[LEAVE, q]
        xmsg[q] = sent[n]
        emsg[q] = edge_o[n]

    unrolled(cols * cap, 8, to_slots)
    others = pl.ds(0, (cols - 1) * cap)

    def push_factors(d, carry):
        peer = (me + d) % cols
        for a, b, s_, r_ in ((xmsg, xgot, x_s, x_r), (emsg, egot, e_s, e_r)):
            pltpu.make_async_remote_copy(
                piece(a, peer), piece(b, me), s_, r_,
                device_id=(row, peer), device_id_type=MESH,
            ).start()
        return carry

    lax.fori_loop(1, cols, push_factors, 0)
    keep_x = pltpu.make_async_copy(piece(xmsg, me), piece(xgot, me), loc.at[0])
    keep_e = pltpu.make_async_copy(piece(emsg, me), piece(egot, me), loc.at[1])
    keep_x.start()
    keep_e.start()

    finish()
    keep_mine.wait()

    @pl.loop(0, held // GROUP)
    def _(i):
        group(i, True)

        def send_moved(d, carry):
            peer = (row + d) % rows
            move_block(i, peer)
            at = pl.ds(pl.multiple_of(i * TOK, TOK), TOK)
            pltpu.make_async_remote_copy(
                part_c.at[peer, at], came_c.at[row, at], yc_s.at[d, i], yc_r.at[row, i],
                device_id=(peer, me), device_id_type=MESH,
            ).start()
            return carry

        lax.fori_loop(1, rows, send_moved, 0)

    for k, d in enumerate(order):
        pltpu.make_async_remote_copy(
            ss, ss_in.at[row], ss_s.at[k], ss_r.at[row],
            device_id=((row + d) % rows, me), device_id_type=MESH,
        ).start()

    def send_rest(d, carry):
        peer = (row + d) % rows
        rest_block(peer)
        pltpu.make_async_remote_copy(
            part_o.at[peer], came_o.at[row], yo_s.at[d], yo_r.at[row],
            device_id=(peer, me), device_id_type=MESH,
        ).start()
        return carry

    lax.fori_loop(1, rows, send_rest, 0)

    for i in range(held // GROUP):
        move_block(i, row)
    rest_block(row)
    total = ss[...]
    for d in order:
        peer = (row + d) % rows
        pltpu.make_async_copy(ss_in.at[peer], ss_in.at[peer], ss_r.at[peer]).wait()
        total = total + ss_in[peer]
    factor = lax.rsqrt(total / INNER + 1e-05)
    for i in range(tokens // TOK):
        line = jnp.broadcast_to(factor[i : i + 1, :], (TOK, TOK))
        scale[pl.ds(i * TOK, TOK), :] = line.T

    def add(part, came, into, start, count):
        def some(i, carry):
            at = pl.ds(pl.multiple_of(i * TOK, TOK), TOK)
            by = scale[pl.ds(pl.multiple_of(start + i * TOK, TOK), TOK), :]
            for j in range(pieces):
                lanes = slice(j * 128, (j + 1) * 128)
                value = part[row, at, lanes].astype(f32)
                for d in order:
                    value = value + came[(row + d) % rows, at, lanes].astype(f32)
                value = (value * by).astype(bf16)
                into[pl.ds(i * GROUP, GROUP), :, lanes] = value.reshape(GROUP, LEN, 128)
            return carry

        lax.fori_loop(0, count // TOK, some, 0)

    for i in range(held // GROUP):
        at = pl.ds(i * TOK, TOK)
        for d in order:
            spot = came_c.at[(row + d) % rows, at]
            pltpu.make_async_copy(spot, spot, yc_r.at[(row + d) % rows, i]).wait()
    add(part_c, came_c, mix, 0, moving)

    def pack(q):
        packed[q] = mix[tab[BACK, q]]

    unrolled(cols * cap, 8, pack)

    def push(d, carry):
        peer = (me + d) % cols
        pltpu.make_async_remote_copy(
            piece(packed, peer), piece(got, me), a2a_s, a2a_r,
            device_id=(row, peer), device_id_type=MESH,
        ).start()
        return carry

    lax.fori_loop(1, cols, push, 0)
    keep_m = pltpu.make_async_copy(piece(packed, me), piece(got, me), loc.at[2])
    keep_m.start()
    for d in order:
        spot = came_o.at[(row + d) % rows]
        pltpu.make_async_copy(spot, spot, yo_r.at[(row + d) % rows]).wait()
    add(part_o, came_o, mix_o, moving, resting)
    keep_m.wait()
    pltpu.make_async_copy(got.at[others], got.at[others], a2a_r).wait()

    def unpack(s):
        moved = tab[MOVED, s].astype(f32)
        away = got[tab[FROM_MSG, s]].astype(f32)
        here = mix_o[tab[FROM_MIX, s]].astype(f32)
        mixed[s] = jnp.where(moved > 0.5, away, here).astype(bf16)

    unrolled(requests, 8, unpack)
    for k in range(rows - 1):
        pltpu.make_async_copy(ss, ss, ss_s.at[k]).wait()
        pltpu.make_async_copy(part_o.at[0], part_o.at[0], yo_s.at[k + 1]).wait()
        for i in range(held // GROUP):
            spot = part_c.at[0, pl.ds(i * TOK, TOK)]
            pltpu.make_async_copy(spot, spot, yc_s.at[k + 1, i]).wait()
    pltpu.make_async_copy(got.at[others], got.at[others], a2a_s).wait()
    keep_x.wait()
    keep_e.wait()

    for ref, s_, r_ in ((xgot, x_s, x_r), (egot, e_s, e_r)):
        pltpu.make_async_copy(ref.at[others], ref.at[others], r_).wait()
        pltpu.make_async_copy(ref.at[others], ref.at[others], s_).wait()

    @pl.loop(0, held)
    def _(s):
        store(s).wait()


def mixer(tab, hid_c, hidden, fw, w_out, vectors, prev, pex, peb, rows, cols, cap):
    requests, _, model = hidden.shape
    held = hid_c.shape[0]
    tokens = requests * LEN
    depth, inner = w_out.shape
    width = model // rows
    slots = cols * cap
    rest = requests - held
    dt = hidden.dtype
    f32 = jnp.float32
    vmem = pl.BlockSpec(memory_space=pltpu.VMEM)
    hbm = pl.BlockSpec(memory_space=pltpu.HBM)
    dma = pltpu.SemaphoreType.DMA

    def body(*refs):
        mixer_kernel(rows, cols, cap, held, *refs)

    wide = inner + 2 * STATE
    return pl.pallas_call(
        body,
        out_shape=(
            jax.ShapeDtypeStruct((requests, LEN, width), dt),
            jax.ShapeDtypeStruct((held, inner, STATE), dt),
            jax.ShapeDtypeStruct((held, 4, wide), dt),
            jax.ShapeDtypeStruct((slots, LEN, inner + STATE), dt),
            jax.ShapeDtypeStruct((slots, 4, wide), dt),
        ),
        in_specs=[hbm] * (8 + len(vectors)),
        out_specs=(vmem, hbm, vmem, hbm, hbm),
        scratch_shapes=[
            pltpu.SMEM(tab.shape, jnp.int32),
            *[pltpu.VMEM(v.shape, v.dtype) for v in vectors],
            pltpu.VMEM(pex.shape, dt),
            pltpu.VMEM(peb.shape, dt),
            pltpu.VMEM((requests, LEN, model), dt),
            pltpu.VMEM((requests, LEN, model), dt),
            pltpu.VMEM((model, 2 * inner), dt),
            pltpu.VMEM((model, fw.shape[1] - 2 * inner), dt),
            pltpu.VMEM((model, inner), dt),
            pltpu.VMEM((held, inner, STATE), dt),
            pltpu.VMEM((tokens, inner), dt),
            pltpu.VMEM((tokens, inner), dt),
            pltpu.VMEM((tokens, 2 * STATE), dt),
            pltpu.VMEM((tokens, 128), f32),
            pltpu.VMEM((tokens, inner), dt),
            pltpu.VMEM((8, 128), f32),
            pltpu.VMEM((GROUP, 32, inner), f32),
            pltpu.VMEM((GROUP, 32, 2 * STATE), f32),
            pltpu.VMEM((3, held, inner), f32),
            pltpu.VMEM((3, held, 2 * STATE), f32),
            pltpu.VMEM((TOK, wide), f32),
            pltpu.VMEM((held, inner, STATE), dt),
            pltpu.VMEM((rest, LEN, inner + STATE), dt),
            pltpu.VMEM((rest, 4, wide), dt),
            pltpu.VMEM((slots, LEN, inner + STATE), dt),
            pltpu.VMEM((slots, 4, wide), dt),
            pltpu.VMEM((rows, rest * LEN, width), dt),
            pltpu.VMEM((rows, held * LEN, width), dt),
            pltpu.VMEM((rows, rest * LEN, width), dt),
            pltpu.VMEM((rows, held * LEN, width), dt),
            pltpu.VMEM((rows, 8, 128), f32),
            pltpu.VMEM((tokens, 128), f32),
            pltpu.VMEM((rest, LEN, width), dt),
            pltpu.VMEM((held, LEN, width), dt),
            pltpu.VMEM((slots, LEN, width), dt),
            pltpu.VMEM((slots, LEN, width), dt),
            dma(()), dma(()), dma((2 * inner // 256 + 2,)), dma((held,)),
            dma((len(vectors) + 3,)), dma((5,)), dma((3,)), dma((rows,)),
            dma((rows,)), dma((rows,)), dma((rows, held // GROUP)), dma((rows, held // GROUP)),
            dma(()), dma(()),
            dma(()), dma(()), dma(()), dma(()),
            pltpu.VMEM(w_out.shape, dt), dma((2,)), dma((2,)), dma((2, cols)),
        ],
        compiler_params=pltpu.CompilerParams(
            collective_id=1, has_side_effects=True, vmem_limit_bytes=60 << 20
        ),
        name="mixer",
    )(tab, hid_c, hidden, fw, w_out, *vectors, prev, pex, peb)


def arrive_kernel(
    tab_in, xgot_in, egot_in, edge_in, nst_in, nst, nex, neb,
    tab, xgot, egot, edge, was, xs, bs, ex, eb, new, n_sem, m_sem, l_sem,
):
    f32, bf16 = jnp.float32, jnp.bfloat16
    count, inner = new.shape[0], new.shape[1]
    loads = [
        pltpu.make_async_copy(a, b, l_sem.at[k])
        for k, (a, b) in enumerate(
            ((tab_in, tab), (xgot_in, xgot), (nst_in, was), (egot_in, egot), (edge_in, edge))
        )
    ]
    for copy in loads:
        copy.start()
    loads[0].wait()

    def place(s):
        return pltpu.make_async_copy(was.at[s], nst.at[tab[POS, s]], m_sem.at[s])

    loads[1].wait()
    t_ids, _ = token_masks()
    none = jnp.zeros((TOK, STATE), bf16)

    def store(u):
        return pltpu.make_async_copy(new.at[u], nst.at[tab[POS_O, u]], n_sem.at[u])

    @pl.loop(0, count // GROUP)
    def _(i):
        for r in range(GROUP):
            slot = tab[PICK_O, i * GROUP + r]
            xs[r] = xgot[slot, :, :inner]
            bs[r] = xgot[slot, :, inner:]
        lhs = xs[...].reshape(TOK, inner).astype(f32).T.astype(bf16)
        b_in = bs[...].reshape(TOK, STATE)
        for pair in range(GROUP // 2):
            cut = jnp.concatenate(
                [
                    jnp.where(t_ids // LEN == r, b_in, none)
                    for r in (2 * pair, 2 * pair + 1)
                ],
                axis=1,
            )
            out = jnp.dot(lhs, cut, preferred_element_type=f32).astype(bf16)
            for k in (0, 1):
                u = i * GROUP + 2 * pair + k
                new[u] = out[:, k * STATE : (k + 1) * STATE]
                store(u).start()

    loads[2].wait()

    @pl.loop(0, count)
    def _(s):
        place(s).start()

    for copy in loads[3:]:
        copy.wait()

    @pl.loop(0, count)
    def _(u):
        for source, k, spot in (
            (egot, tab[PICK_O, u], tab[POS_O, u]), (edge, u, tab[POS, u])
        ):
            lines = source[k].astype(f32)
            at = pl.ds(spot, 1)
            for q in range(KCONV - 1):
                ex[q, at, :] = lines[q : q + 1, :inner]
                eb[q, at, :] = lines[q : q + 1, inner:]

    nex[...] = ex[...].astype(bf16)
    neb[...] = eb[...].astype(bf16)

    @pl.loop(0, count)
    def _(u):
        store(u).wait()
        place(u).wait()


def arrive(tab, xgot, egot, edge, nst):
    count, inner, _ = nst.shape
    requests = 2 * count
    dt, f32 = nst.dtype, jnp.float32
    vmem = pl.BlockSpec(memory_space=pltpu.VMEM)
    hbm = pl.BlockSpec(memory_space=pltpu.HBM)
    return pl.pallas_call(
        arrive_kernel,
        out_shape=(
            jax.ShapeDtypeStruct((requests, inner, STATE), dt),
            jax.ShapeDtypeStruct((3, requests, inner), dt),
            jax.ShapeDtypeStruct((3, requests, 2 * STATE), dt),
        ),
        in_specs=[hbm] * 5,
        out_specs=(hbm, vmem, vmem),
        scratch_shapes=[
            pltpu.SMEM(tab.shape, jnp.int32),
            pltpu.VMEM(xgot.shape, dt),
            pltpu.VMEM(egot.shape, dt),
            pltpu.VMEM(edge.shape, dt),
            pltpu.VMEM(nst.shape, dt),
            pltpu.VMEM((GROUP, LEN, inner), dt),
            pltpu.VMEM((GROUP, LEN, STATE), dt),
            pltpu.VMEM((3, requests, inner), f32),
            pltpu.VMEM((3, requests, 2 * STATE), f32),
            pltpu.VMEM((count, inner, STATE), dt),
            pltpu.SemaphoreType.DMA((count,)),
            pltpu.SemaphoreType.DMA((count,)),
            pltpu.SemaphoreType.DMA((5,)),
        ],
        compiler_params=pltpu.CompilerParams(vmem_limit_bytes=60 << 20),
        name="arrive",
    )(tab, xgot, egot, edge, nst)


def per_device(
    hidden, w_zx, w_bc, w_dt, w_out, dt_bias, a_log, d_skip, conv_x_w, conv_x_b,
    conv_bc_w, conv_bc_b, norm_gain, prev_state, prev_edge_x, prev_edge_bc,
    holder, continued, owner, accepted,
):
    rows, cols = lax.axis_size("row"), lax.axis_size("col")
    tokens, model = hidden.shape
    requests = tokens // LEN
    heads = dt_bias.shape[0]
    inner = heads * HEAD_DIM
    held = prev_state.shape[0]
    cap = 2 * ((requests // 4 + cols - 1) // cols)
    code = owner + 64 * (continued == 1).astype(jnp.int32) + 128 * accepted
    code = code.reshape(cols, requests)
    hidden = hidden.reshape(requests, LEN, model)
    hid_c, fw, tab = gather_all(code, hidden, w_zx, w_bc, w_dt.T, rows, cols, cap, held)
    vectors = (
        dt_bias[None, :], a_log[None, :], d_skip[None, :],
        conv_x_w, conv_x_b[None, :], conv_bc_w, conv_bc_b[None, :], norm_gain[None, :],
    )
    mixed, moved, edge, xgot, egot = mixer(
        tab, hid_c, hidden, fw, w_out, vectors, prev_state.reshape(held, inner, STATE),
        prev_edge_x.transpose(1, 0, 2), prev_edge_bc.transpose(1, 0, 2),
        rows, cols, cap,
    )
    states, new_x, new_bc = arrive(tab, xgot, egot, edge, moved)
    return (
        mixed.reshape(tokens, model // rows),
        states.reshape(requests, heads, HEAD_DIM, STATE),
        new_x.transpose(1, 0, 2),
        new_bc.transpose(1, 0, 2),
    )


def solution(mesh):
    return jax.shard_map(
        per_device,
        mesh=mesh,
        in_specs=(
            P("col", None),
            P("col", "row"),
            P("col", None),
            P("col", "row"),
            P("col", "row"),
            P("row"),
            P("row"),
            P("row"),
            P(None, "row"),
            P("row"),
            P(),
            P(),
            P("row"),
            P("col", "row", None, None),
            P("col", None, "row"),
            P("col", None, None),
            P(),
            P(),
            P(),
            P(),
        ),
        out_specs=(
            P("col", "row"),
            P("col", "row", None, None),
            P("col", None, "row"),
            P("col", None, None),
        ),
        check_vma=False,
    )
```

```python
import jax
import jax.numpy as jnp
from jax import lax
from jax.experimental import pallas as pl
from jax.experimental.pallas import tpu as pltpu
from jax.sharding import PartitionSpec as P

HEAD_DIM = 64
STATE = 128
KCONV = 4
LEN = 16
INNER = 2048
SIDE = 4
GROUP = 8
TOK = GROUP * LEN
MESH = pl.DeviceIdType.MESH
HIGHEST = lax.Precision.HIGHEST


def route_kernel(held, code, out):
    f32, bf16 = jnp.float32, jnp.bfloat16
    me = lax.axis_index("col")
    groups, requests = code.shape
    value = code[...]
    o, c, a = value & 63, (value >> 6) & 1, value >> 7

    def dot(x, y):
        return jnp.dot(x.astype(bf16), y.astype(bf16), preferred_element_type=f32)

    def dot0(x, y):
        return lax.dot_general(
            x.astype(bf16), y.astype(bf16), (((0,), (0,)), ((), ())), preferred_element_type=f32
        )

    def ids(shape, dim):
        return lax.broadcasted_iota(jnp.int32, shape, dim)

    below = (ids((requests, requests), 0) < ids((requests, requests), 1)).astype(f32)
    prior = (ids((groups, groups), 1) < ids((groups, groups), 0)).astype(f32)
    lane = ids((groups, 128), 1).astype(f32)
    group = ids((groups, 128), 0).astype(f32)
    spots, inside, starts = [], [], []
    for kind in (1, 0):
        mask = ((o == me) & (c == kind)).astype(f32)
        rank = dot(mask, below)
        count = jnp.broadcast_to(jnp.sum(mask, axis=1, keepdims=True), (groups, 128))
        start = dot(prior, count)
        hot = ((start <= lane) & (lane < start + count)).astype(f32)
        spots.append((jnp.where(mask > 0, rank, -1.0), hot))
        inside.append(rank)
        starts.append(start)
    rank_all, start_all = inside[0] + inside[1], starts[0] + starts[1]
    picks, places, taken = [], [], []
    for k in (0, 1):
        spot, hot = spots[k]
        order = jnp.sum(hot * (lane - starts[k]), axis=0, keepdims=True)
        any_hot = jnp.sum(hot, axis=0, keepdims=True)
        order = jnp.where(any_hot > 0, order, -5.0)
        match = (dot0(spot, hot) == order).astype(f32)
        picks.append(jnp.sum(hot * (2 * group + lane - starts[k]), axis=0, keepdims=True))
        places.append(
            jnp.sum(hot * start_all, axis=0, keepdims=True)
            + jnp.sum(match * dot0(rank_all, hot), axis=0, keepdims=True)
        )
        taken.append(jnp.sum(match * dot0(a, hot), axis=0, keepdims=True))
    lane_i, group_i = ids((groups, 128), 1), ids((groups, 128), 0)
    back = jnp.sum(
        jnp.where(lane_i // 2 == group_i, starts[0] + (lane_i % 2).astype(f32), 0.0),
        axis=0, keepdims=True,
    )
    back = jnp.minimum(back, held - 1.0)

    def my_row(x, fill):
        row = jnp.sum(
            jnp.where(ids((groups, requests), 0) == me, x, 0).astype(f32), axis=0, keepdims=True
        )
        rest = jnp.full((1, 128 - requests), fill, f32)
        return jnp.concatenate([row, rest], axis=1)

    o_row, c_row, a_row = my_row(o, 99.0), my_row(c, 2.0), my_row(a, 0.0)

    def column(row):
        return jnp.broadcast_to(row, (128, 128)).T

    o_col, c_col, a_col = column(o_row), column(c_row), column(a_row)
    ii, jj = ids((128, 128), 0), ids((128, 128), 1)
    alike = (o_col == o_row) & (c_col == c_row)
    rank_row = jnp.sum((alike & (ii < jj)).astype(f32), axis=0, keepdims=True)
    rank_col = jnp.sum((alike & (jj < ii)).astype(f32), axis=1, keepdims=True)
    nth_row = jnp.sum(((c_col == 0) & (ii < jj)).astype(f32), axis=0, keepdims=True)
    nth_col = jnp.sum(((c_row == 0) & (jj < ii)).astype(f32), axis=1, keepdims=True)
    key_row = 2 * o_row + rank_row
    key_col = 2 * o_col + rank_col
    fi, fj = ii.astype(f32), jj.astype(f32)
    goes = (c_col == 1) & (key_col == fj)
    leaves = (c_col == 0) & (key_col == fj)
    stays = (c_col == 0) & (nth_col == fj)

    def total(mask, x):
        return jnp.sum(jnp.where(mask, x, 0.0), axis=0, keepdims=True)

    table = (
        total(goes, fi), picks[0], back,
        jnp.where(c_row == 1, key_row, 0.0), jnp.where(c_row == 0, nth_row, 0.0),
        (c_row == 1).astype(f32),
        total(stays, fi), total(stays, key_col), total(stays, a_col),
        taken[0], places[0], picks[1], places[1], total(leaves, nth_col),
    )
    for k, line in enumerate(table):
        out[k : k + 1, :] = line.astype(jnp.int32)
    out[len(table) :, :] = jnp.zeros((16 - len(table), 128), jnp.int32)


SEND, PICK, BACK, FROM_MSG, FROM_MIX, MOVED, STAY, STAY_KEY, STAY_ACC, ACC, POS, PICK_O, POS_O, LEAVE = range(14)


def unrolled(count, step, body):
    def some(i, carry):
        for k in range(step):
            body(i * step + k)
        return carry

    lax.fori_loop(0, count // step, some, 0)


def greet(row, me, rows, cols):
    barrier = pltpu.get_barrier_semaphore()

    def along_col(d, carry):
        pl.semaphore_signal(
            barrier, inc=1, device_id=(row, (me + d) % cols), device_id_type=MESH
        )
        return carry

    lax.fori_loop(1, cols, along_col, 0)

    def along_row(d, carry):
        pl.semaphore_signal(
            barrier, inc=1, device_id=((row + d) % rows, me), device_id_type=MESH
        )
        return carry

    lax.fori_loop(1, rows, along_row, 0)
    return barrier


def torus_ring(row, me, depth, block, own, span, gone, twin, came):
    core = me % 2
    x = (me // 2) % SIDE
    z = me // (2 * SIDE)
    a = x + core * (z - x)
    b = z + core * (x - z)

    def at(pa, pb):
        pa, pb = (pa + SIDE) % SIDE, (pb + SIDE) % SIDE
        px = pa + core * (pb - pa)
        pz = pb + core * (pa - pb)
        return (pz * SIDE + px) * 2 + core

    sibling = me + 1 - 2 * core
    sent = [0, 0]

    def send(h, source, c, dest):
        sent[h] += 1
        arrival = twin.at[h] if dest is sibling else came.at[h, c]
        pltpu.make_async_remote_copy(
            source, block(h, c), gone.at[h], arrival,
            device_id=(row, dest), device_id_type=MESH,
        ).start()

    def forward(h, c, dest):
        send(h, block(h, c), c, dest)

    def arrived(h, c):
        pltpu.make_async_copy(block(h, c), block(h, c), came.at[h, c]).wait()

    up, down, far = at(a + 1, b), at(a - 1, b), at(a + 2, b)
    over, under = at(a, b + 1), at(a, b - 1)

    def begin():
        for dest in (up, down, over, under, sibling):
            for h in (0, 1):
                send(h, own(h), me, dest)

    def near():
        arrived(0, down)
        forward(0, down, up)
        arrived(1, up)
        forward(1, up, down)
        arrived(1, down)
        arrived(0, up)
        for c in (down, up):
            for h in (0, 1):
                for dest in (over, under, sibling):
                    forward(h, c, dest)

    def beyond():
        for h in (0, 1):
            arrived(h, far)
            for dest in (over, under, sibling):
                forward(h, far, dest)

    def beside():
        for k in (0, 1, -1, 2):
            low, high = at(a + k, b - 1), at(a + k, b + 1)
            arrived(0, low)
            forward(0, low, over)
            arrived(1, high)
            forward(1, high, under)
            arrived(1, low)
            arrived(0, high)
            for h in (0, 1):
                forward(h, low, sibling)
                forward(h, high, sibling)

    def opposite():
        for k in (0, 1, -1, 2):
            c = at(a + k, b + 2)
            for h in (0, 1):
                arrived(h, c)
                forward(h, c, sibling)

    def finish():
        for h in (0, 1):
            half = span(h, 16 * depth)
            pltpu.make_async_copy(half, half, twin.at[h]).wait()
        for h in (0, 1):
            part = span(h, sent[h] * depth)
            pltpu.make_async_copy(part, part, gone.at[h]).wait()

    return begin, near, beyond, beside, opposite, finish


def gather_kernel(
    rows, cols, cap, code, hidden, w_zx, w_bc, w_dt_in, hid_full, fw, tab_out,
    table, tab, w_dt, ws, sl, packed0, packed1, got0, got1, own0, own1, loc, a2a_s, a2a_r, gone, twin, arr, y_s, y_r,
):
    row, me = lax.axis_index("row"), lax.axis_index("col")
    barrier = greet(row, me, rows, cols)
    width = sl.shape[2]
    half = own0.shape[0] // 2
    packs, gots, owns = (packed0, packed1), (got0, got1), (own0, own1)
    lows = (0, packed0.shape[2])
    depth = w_zx.shape[0]

    def cols_of(r):
        return pl.ds(pl.multiple_of(r * width, 128), width)

    cut = 128 * (ws.shape[1] // 256)
    lanes_of = (pl.ds(0, cut), pl.ds(cut, ws.shape[1] - cut))

    def lines(c):
        return pl.ds(pl.multiple_of(c * depth, 16), depth)

    ring = torus_ring(
        row, me, depth,
        lambda h, c: fw.at[lines(c), lanes_of[h]],
        lambda h: ws.at[:, lanes_of[h]],
        lambda h, count: fw.at[pl.ds(0, count), lanes_of[h]],
        gone, twin, arr,
    )
    begin, near, beyond, beside, opposite, finish = ring

    load = pltpu.make_async_copy(hidden.at[:, :, cols_of(row)], sl, loc.at[0])
    load.start()
    inner = w_zx.shape[1]
    states = w_bc.shape[1]
    heads = w_dt_in.shape[0]
    loads = (
        pltpu.make_async_copy(w_dt_in, w_dt, loc.at[6]),
        pltpu.make_async_copy(w_zx, ws.at[:, pl.ds(0, inner)], loc.at[7]),
        pltpu.make_async_copy(w_bc, ws.at[:, pl.ds(inner, states)], loc.at[8]),
    )
    for copy in loads:
        copy.start()
    route_kernel(own0.shape[0], code, table)
    to_scalars = pltpu.make_async_copy(table, tab, loc.at[5])
    to_scalars.start()
    keep_t = pltpu.make_async_copy(table, tab_out, loc.at[2])
    keep_t.start()
    for copy in loads:
        copy.wait()
    square = jnp.concatenate(
        [w_dt[...].astype(jnp.float32), jnp.zeros((heads, 128 - depth), jnp.float32)], axis=1
    )
    square = jnp.concatenate([square, jnp.zeros((128 - heads, 128), jnp.float32)], axis=0).T
    ws[:, inner + states :] = square[:depth, :].astype(ws.dtype)
    keep_w = pltpu.make_async_copy(ws, fw.at[lines(me), :], loc.at[1])
    keep_w.start()
    load.wait()
    to_scalars.wait()

    def piece(ref, c):
        return ref.at[pl.ds(c * cap, cap)]

    keeps = []
    for k in (0, 1):
        packed, got, low = packs[k], gots[k], lows[k]

        def pack(s):
            j = jnp.clip(tab[SEND, s], 0, sl.shape[0] - 1)
            packed[s] = sl[j, :, low : low + packed.shape[2]]

        unrolled(cols * cap, 8, pack)
        if k == 0:
            pl.semaphore_wait(barrier, cols - 1 + rows - 1)

        def push(d, carry):
            peer = (me + d) % cols
            pltpu.make_async_remote_copy(
                piece(packed, peer), piece(got, me), a2a_s.at[k], a2a_r.at[k],
                device_id=(row, peer), device_id_type=MESH,
            ).start()
            return carry

        lax.fori_loop(1, cols, push, 0)
        keeps.append(pltpu.make_async_copy(piece(packed, me), piece(got, me), loc.at[3 + 6 * k]))
        keeps[k].start()

    begin()
    near()
    others = pl.ds(0, (cols - 1) * cap)
    right, left = (row + 1) % rows, (row + rows - 1) % rows
    far_row = (row + 2) % rows

    def part(ref, k, h, r):
        low, size = lows[k], owns[k].shape[2]
        lanes = pl.ds(pl.multiple_of(r * width + low, 128), size)
        return ref.at[pl.ds(h * half, half), :, lanes]

    def y_here(k, h, r):
        spot = part(hid_full, k, h, r)
        pltpu.make_async_copy(spot, spot, y_r.at[k, r, h]).wait()

    def pass_on(k, h, source, dest):
        spot = part(hid_full, k, h, source)
        pltpu.make_async_remote_copy(
            spot, spot, y_s.at[k, 4 + h], y_r.at[k, source, h],
            device_id=(dest, me), device_id_type=MESH,
        ).start()

    for k in (0, 1):
        got, own = gots[k], owns[k]
        keeps[k].wait()
        pltpu.make_async_copy(got.at[others], got.at[others], a2a_r.at[k]).wait()

        def unpack(s):
            own[s] = got[jnp.clip(tab[PICK, s], 0, got.shape[0] - 1)]

        unrolled(own.shape[0], 8, unpack)
        for n, dest in ((0, right), (1, left)):
            for h in (n, 1 - n):
                pltpu.make_async_remote_copy(
                    own.at[pl.ds(h * half, half)], part(hid_full, k, h, row),
                    y_s.at[k, 2 * n + h], y_r.at[k, row, h],
                    device_id=(dest, me), device_id_type=MESH,
                ).start()
        lanes = pl.ds(pl.multiple_of(row * width + lows[k], 128), own.shape[2])
        keeps.append(pltpu.make_async_copy(own, hid_full.at[:, :, lanes], loc.at[4 + 6 * k]))
        keeps[2 + k].start()

    beyond()
    y_here(0, 0, left)
    pass_on(0, 0, left, right)
    y_here(0, 1, right)
    pass_on(0, 1, right, left)
    beside()
    y_here(1, 0, left)
    pass_on(1, 0, left, right)
    y_here(1, 1, right)
    pass_on(1, 1, right, left)
    opposite()
    for k in (0, 1):
        y_here(k, 1, left)
        y_here(k, 0, right)
        y_here(k, 0, far_row)
        y_here(k, 1, far_row)

    finish()
    keep_w.wait()
    keep_t.wait()
    keeps[2].wait()
    keeps[3].wait()

    for k in (0, 1):
        pltpu.make_async_copy(packs[k].at[others], packs[k].at[others], a2a_s.at[k]).wait()

    for k in (0, 1):
        for n in range(6):
            spot = part(hid_full, k, n % 2, row)
            pltpu.make_async_copy(spot, spot, y_s.at[k, n]).wait()


def gather_all(code, hidden, w_zx, w_bc, w_dt, rows, cols, cap, held):
    requests, _, model = hidden.shape
    width = model // rows
    dt = hidden.dtype
    hbm = pl.BlockSpec(memory_space=pltpu.HBM)
    dma = pltpu.SemaphoreType.DMA
    depth = w_zx.shape[0]
    wide = w_zx.shape[1] + w_bc.shape[1] + 128

    def body(*refs):
        gather_kernel(rows, cols, cap, *refs)

    return pl.pallas_call(
        body,
        out_shape=(
            jax.ShapeDtypeStruct((held, LEN, model), dt),
            jax.ShapeDtypeStruct((depth * cols, wide), dt),
            jax.ShapeDtypeStruct((16, 128), jnp.int32),
        ),
        in_specs=[pl.BlockSpec(memory_space=pltpu.VMEM)] + [hbm] * 4,
        out_specs=(hbm, hbm, hbm),
        scratch_shapes=[
            pltpu.VMEM((16, 128), jnp.int32),
            pltpu.SMEM((16, 128), jnp.int32),
            pltpu.VMEM(w_dt.shape, dt),
            pltpu.VMEM((depth, wide), dt),
            pltpu.VMEM((requests, LEN, width), dt),
            pltpu.VMEM((cols * cap, LEN, 128), dt),
            pltpu.VMEM((cols * cap, LEN, width - 128), dt),
            pltpu.VMEM((cols * cap, LEN, 128), dt),
            pltpu.VMEM((cols * cap, LEN, width - 128), dt),
            pltpu.VMEM((held, LEN, 128), dt),
            pltpu.VMEM((held, LEN, width - 128), dt),
            dma((11,)), dma((2,)), dma((2,)),
            dma((2,)), dma((2,)), dma((2, cols)),
            dma((2, 6)), dma((2, rows, 2)),
        ],
        compiler_params=pltpu.CompilerParams(
            collective_id=0, has_side_effects=True, vmem_limit_bytes=60 << 20
        ),
        name="gather_all",
    )(code, hidden, w_zx, w_bc, w_dt)


def silu(v):
    return v / (1.0 + jnp.exp(-v))


def token_masks():
    t_ids = lax.broadcasted_iota(jnp.int32, (TOK, TOK), 0)
    s_ids = lax.broadcasted_iota(jnp.int32, (TOK, TOK), 1)
    return t_ids, s_ids


def mixer_kernel(
    rows, cols, cap, held, tab_in, hid_c, hidden, fw, w_out, *refs,
):
    sources, refs = refs[:8], refs[8:]
    prev, pex_in, peb_in, mixed, nst, edge_c, xgot, egot, tab, *refs = refs
    params, refs = refs[:8], refs[8:]
    dtb, alog, skip, cxw, cxb, cbw, cbb, gain = params
    (
        pex, peb, hid, home, wa, wb, wo, old, gate, xin, bc, dts, gg, ss, cx, cb, pexf, pebf, es,
        new, sent, edge_o, xmsg, emsg, part_o, part_c, came_o, came_c, ss_in, scale, mix_o,
        mix, packed, got,
        h_sem, o_sem, w_sem, n_sem, v_sem, loc, ss_s, ss_r, yo_s, yo_r, yc_s, yc_r,
        a2a_s, a2a_r, x_s, x_r, e_s, e_r, mine, gone, twin, arr,
    ) = refs
    row, me = lax.axis_index("row"), lax.axis_index("col")
    barrier = greet(row, me, rows, cols)
    depth = w_out.shape[0]
    load_mine = pltpu.make_async_copy(w_out, mine, loc.at[3])
    load_mine.start()
    f32, bf16 = jnp.float32, jnp.bfloat16
    inner = gain.shape[1]
    requests = hid.shape[0]
    tokens = requests * LEN
    model = hid.shape[2]
    heads = inner // HEAD_DIM
    blocks = wa.shape[1] // 256
    assert blocks == 4

    load_h = pltpu.make_async_copy(hid_c, hid.at[pl.ds(0, held)], h_sem)
    load_h.start()
    small = list(zip(sources + (pex_in, peb_in, tab_in), list(params) + [pex, peb, tab]))
    small = [pltpu.make_async_copy(a, b, v_sem.at[k]) for k, (a, b) in enumerate(small)]
    small[-1].start()
    for copy in small[:-1]:
        copy.start()
    small[-1].wait()

    def wa_load(n):
        at = pl.ds(n * 256, 256)
        return pltpu.make_async_copy(fw.at[:, at], wa.at[:, at], w_sem.at[n])

    wa_load(0).start()

    load_home = pltpu.make_async_copy(hidden, home, o_sem)
    load_home.start()
    for n in range(1, blocks):
        wa_load(n).start()
    late = pl.ds(2 * inner, wb.shape[1])
    load_bc = pltpu.make_async_copy(fw.at[:, late], wb, w_sem.at[blocks])
    load_old = pltpu.make_async_copy(prev, old, w_sem.at[blocks + 1])
    load_bc.start()
    load_old.start()
    load_mine.wait()
    cut = inner // 2

    def lines_of(c):
        return pl.ds(pl.multiple_of(c * depth, 16), depth)

    begin, near, beyond, beside, opposite, finish = torus_ring(
        row, me, depth,
        lambda h, c: wo.at[lines_of(c), pl.ds(h * cut, cut)],
        lambda h: mine.at[:, pl.ds(h * cut, cut)],
        lambda h, count: wo.at[pl.ds(0, count), pl.ds(h * cut, cut)],
        gone, twin, arr,
    )
    keep_mine = pltpu.make_async_copy(mine, wo.at[lines_of(me), :], loc.at[4])
    keep_mine.start()
    for copy in small[:-1]:
        copy.wait()
    pexf[...] = pex[...].astype(f32)
    pebf[...] = peb[...].astype(f32)

    t_ids, s_ids = token_masks()
    row_ids = lax.broadcasted_iota(jnp.int32, (4 * GROUP, TOK), 0)
    k_ids = lax.broadcasted_iota(jnp.int32, (4 * GROUP, TOK), 1)
    r_ids, q_ids = row_ids // 4, row_ids % 4
    es[...] = jnp.zeros(es.shape, f32)
    same = (t_ids // LEN) == (s_ids // LEN)
    causal = same & (t_ids >= s_ids)
    tri = causal.astype(f32)
    spread_h = (
        lax.broadcasted_iota(jnp.int32, (TOK, inner), 1) // HEAD_DIM
        == lax.broadcasted_iota(jnp.int32, (TOK, inner), 0)
    ).astype(f32)

    def wide(ref):
        return jnp.concatenate([ref[...], jnp.zeros((1, TOK - heads), f32)], axis=1)

    bias, rate = wide(dtb), -jnp.exp(wide(alog))
    skip_x = jnp.dot(
        jnp.broadcast_to(wide(skip), (8, TOK)), spread_h,
        precision=HIGHEST, preferred_element_type=f32,
    )[0:1, :]

    load_h.wait()
    load_home.wait()

    def stay(n):
        hid[held + n] = home[tab[STAY, n]]

    unrolled(requests - held, 4, stay)
    left = lax.broadcasted_iota(jnp.int32, (tokens, 128), 1) < HEAD_DIM
    for n in range(blocks):
        wa_load(n).wait()
        z = jnp.dot(
            hid[...].reshape(tokens, model), wa[:, n * 256 : (n + 1) * 256],
            preferred_element_type=f32,
        )
        z0, z1 = z[:, :128], z[:, 128:]
        at = slice(n * 128, (n + 1) * 128)
        gate[:, at] = jnp.where(left, z0, pltpu.roll(z1, HEAD_DIM, 1)).astype(bf16)
        xin[:, at] = jnp.where(left, pltpu.roll(z0, HEAD_DIM, 1), z1).astype(bf16)
        if n == 0:
            pl.semaphore_wait(barrier, cols - 1 + rows - 1)
            begin()
        if n == 2:
            near()
    load_bc.wait()
    z = jnp.dot(hid[...].reshape(tokens, model), wb[...], preferred_element_type=f32)
    bc[...] = z[:, : 2 * STATE].astype(bf16)
    dts[...] = z[:, 2 * STATE :]
    beyond()
    load_old.wait()

    def store(s):
        return pltpu.make_async_copy(new.at[s], nst.at[s], n_sem.at[s])

    def group(i, live):
        at = pl.ds(pl.multiple_of(i * TOK, TOK), TOK)
        first = i * GROUP
        last = jnp.zeros((TOK, TOK), jnp.int32)
        row_acc = jnp.zeros((4 * GROUP, TOK), jnp.int32)
        for r in range(GROUP):
            acc = tab[ACC, first + r] if live else tab[STAY_ACC, first - held + r]
            row_acc = jnp.where(r_ids == r, acc, row_acc)
            last = jnp.where(t_ids // LEN == r, acc, last)
            if live:
                for k in range(KCONV - 1):
                    cx[r, 13 + k : 14 + k, :] = pexf[k, pl.ds(first + r, 1), :]
                    cb[r, 13 + k : 14 + k, :] = pebf[k, pl.ds(first + r, 1), :]
        if not live:
            cx[:, 8:16, :] = jnp.zeros((GROUP, 8, inner), f32)
            cb[:, 8:16, :] = jnp.zeros((GROUP, 8, 2 * STATE), f32)
        cx[:, 16:32, :] = xin[at, :].astype(f32).reshape(GROUP, LEN, inner)
        cb[:, 16:32, :] = bc[at, :].astype(f32).reshape(GROUP, LEN, 2 * STATE)
        tot_x = cxb[...].reshape(1, 1, inner) + cxw[0:1, :].reshape(1, 1, inner) * cx[:, 13:29, :]
        tot_b = cbb[...].reshape(1, 1, 2 * STATE) + cbw[0:1, :].reshape(
            1, 1, 2 * STATE
        ) * cb[:, 13:29, :]
        for k in range(1, KCONV):
            tot_x = tot_x + cxw[k : k + 1, :].reshape(1, 1, inner) * cx[:, 13 + k : 29 + k, :]
            tot_b = tot_b + cbw[k : k + 1, :].reshape(1, 1, 2 * STATE) * cb[:, 13 + k : 29 + k, :]
        xc = silu(tot_x).reshape(TOK, inner).astype(bf16)
        bcc = silu(tot_b).reshape(TOK, 2 * STATE).astype(bf16)
        near = jnp.concatenate([xin[at, :], bc[at, :]], axis=1)
        want = q_ids + row_acc
        pick = (k_ids == LEN * r_ids + want - 3) & (want >= 3) & (q_ids < 3)
        edge = jnp.dot(pick.astype(bf16), near, preferred_element_type=f32)
        if live:
            for k in range(KCONV - 1):
                rows8 = pl.ds(pl.multiple_of(first, GROUP), GROUP)
                es[k * GROUP : (k + 1) * GROUP, :inner] = pexf[k, rows8, :]
                es[k * GROUP : (k + 1) * GROUP, inner:] = pebf[k, rows8, :]
            pick = (k_ids == GROUP * want + r_ids) & (want < 3) & (q_ids < 3)
            edge = edge + jnp.dot(
                pick.astype(bf16), es[...].astype(bf16), preferred_element_type=f32
            )
        for r in range(GROUP):
            lines = edge[4 * r : 4 * r + 4, :].astype(bf16)
            if live:
                edge_c[first + r] = lines
            else:
                edge_o[first - held + r] = lines
        b_in, c_in = bcc[:, :STATE], bcc[:, STATE:]
        xf = xc.astype(f32)
        raw = dts[at, :] + bias
        step = jnp.maximum(raw, 0.0) + jnp.log(1.0 + jnp.exp(-jnp.abs(raw)))
        decay = jnp.dot(tri, step * rate, precision=HIGHEST, preferred_element_type=f32)
        decay_t = decay.T
        step_t = step.T
        choose = (same & (s_ids % LEN == last - 1)).astype(f32)
        reach = jnp.dot(choose, decay, precision=HIGHEST, preferred_element_type=f32)
        taken = t_ids % LEN < last
        weight = jnp.where(taken, jnp.exp(jnp.minimum(reach - decay, 0.0)), 0.0) * step
        weight_x = jnp.dot(weight, spread_h, precision=HIGHEST, preferred_element_type=f32)
        scores = lax.dot_general(
            c_in, b_in, (((1,), (1,)), ((), ())), preferred_element_type=f32
        )
        scores = jnp.where(causal, scores, 0.0)
        half = s_ids < HEAD_DIM
        zero = jnp.zeros((TOK, 2 * HEAD_DIM), bf16)
        y = []
        for pair in range(heads // 2):
            mats = []
            for h in (2 * pair, 2 * pair + 1):
                gap = decay[:, h : h + 1] - decay_t[h : h + 1, :]
                mats.append(
                    (jnp.exp(jnp.minimum(gap, 0.0)) * scores * step_t[h : h + 1, :]).astype(bf16)
                )
            xp = xc[:, pair * 128 : (pair + 1) * 128]
            both = jnp.concatenate([jnp.where(half, xp, zero), jnp.where(half, zero, xp)], axis=0)
            y.append(
                jnp.dot(jnp.concatenate(mats, axis=1), both, preferred_element_type=f32)
            )
        y = jnp.concatenate(y, axis=1)
        if live:
            grow_x = jnp.dot(jnp.exp(decay), spread_h, precision=HIGHEST, preferred_element_type=f32)
            carried = [
                lax.dot_general(
                    c_in[r * LEN : (r + 1) * LEN, :], old[first + r], (((1,), (1,)), ((), ())),
                    preferred_element_type=f32,
                )
                for r in range(GROUP)
            ]
            y = y + grow_x * jnp.concatenate(carried, axis=0)
        y = y + skip_x * xf
        gated = y * silu(gate[at, :].astype(f32))
        gg[at, :] = (gated * gain[...]).astype(bf16)
        squares = jnp.sum(gated * gated, axis=1, keepdims=True)
        ss[pl.ds(i, 1), :] = jnp.broadcast_to(squares, (TOK, TOK)).T[0:1, :]

        if not live:
            out = (xf * weight_x).astype(bf16)
            for r in range(GROUP):
                lines = slice(r * LEN, (r + 1) * LEN)
                sent[first - held + r, :, :inner] = out[lines, :]
                sent[first - held + r, :, inner:] = b_in[lines, :]
            return
        xw = (xf * weight_x).T
        high = xw.astype(bf16)
        low = (xw - high.astype(f32)).astype(bf16)
        lhs = jnp.concatenate([high, low], axis=1)
        keep_t = jnp.exp(reach).T
        none = jnp.zeros((TOK, STATE), bf16)
        for pair in range(GROUP // 2):
            cut = jnp.concatenate(
                [
                    jnp.where(t_ids // LEN == r, b_in, none)
                    for r in (2 * pair, 2 * pair + 1)
                ],
                axis=1,
            )
            added = jnp.dot(
                lhs, jnp.concatenate([cut, cut], axis=0), preferred_element_type=f32
            )
            for k in (0, 1):
                r = 2 * pair + k
                s = first + r
                factor = jnp.broadcast_to(keep_t[0:heads, r * LEN : r * LEN + 1], (heads, STATE))
                was = old[s].astype(f32).reshape(heads, HEAD_DIM, STATE)
                now = factor[:, None, :] * was + added[:, k * STATE : (k + 1) * STATE].reshape(
                    heads, HEAD_DIM, STATE
                )
                new[s] = now.reshape(inner, STATE).astype(bf16)
                store(s).start()

    group(held // GROUP, False)
    beside()

    @pl.loop(held // GROUP + 1, requests // GROUP)
    def _(i):
        group(i, False)

    opposite()

    moving = held * LEN
    resting = tokens - moving
    width = part_c.shape[2]
    pieces = width // 128
    order = (1, 3, 2)

    def project(lines, peer, j, count):
        at = pl.ds(pl.multiple_of(peer * width + j * 128, 128), count * 128)
        return lax.dot_general(
            gg[lines, :], wo[at, :], (((1,), (1,)), ((), ())), preferred_element_type=f32
        ).astype(bf16)

    def rest_block(peer):
        part_o[peer] = project(slice(moving, tokens), peer, 0, pieces)

    def move_block(i, peer):
        lines = pl.ds(pl.multiple_of(i * TOK, TOK), TOK)
        part_c[peer, lines, :] = project(lines, peer, 0, pieces)

    def piece(ref, c):
        return ref.at[pl.ds(c * cap, cap)]

    def to_slots(q):
        n = tab[LEAVE, q]
        xmsg[q] = sent[n]
        emsg[q] = edge_o[n]

    unrolled(cols * cap, 16, to_slots)
    others = pl.ds(0, (cols - 1) * cap)

    def push_factors(d, carry):
        peer = (me + d) % cols
        for a, b, s_, r_ in ((xmsg, xgot, x_s, x_r), (emsg, egot, e_s, e_r)):
            pltpu.make_async_remote_copy(
                piece(a, peer), piece(b, me), s_, r_,
                device_id=(row, peer), device_id_type=MESH,
            ).start()
        return carry

    lax.fori_loop(1, cols, push_factors, 0)
    keep_x = pltpu.make_async_copy(piece(xmsg, me), piece(xgot, me), loc.at[0])
    keep_e = pltpu.make_async_copy(piece(emsg, me), piece(egot, me), loc.at[1])
    keep_x.start()
    keep_e.start()

    finish()
    keep_mine.wait()

    @pl.loop(0, held // GROUP)
    def _(i):
        group(i, True)

        def send_moved(d, carry):
            peer = (row + d) % rows
            move_block(i, peer)
            at = pl.ds(pl.multiple_of(i * TOK, TOK), TOK)
            pltpu.make_async_remote_copy(
                part_c.at[peer, at], came_c.at[row, at], yc_s.at[d, i], yc_r.at[row, i],
                device_id=(peer, me), device_id_type=MESH,
            ).start()
            return carry

        lax.fori_loop(1, rows, send_moved, 0)

    for k, d in enumerate(order):
        pltpu.make_async_remote_copy(
            ss, ss_in.at[row], ss_s.at[k], ss_r.at[row],
            device_id=((row + d) % rows, me), device_id_type=MESH,
        ).start()

    def send_rest(d, carry):
        peer = (row + d) % rows
        rest_block(peer)
        pltpu.make_async_remote_copy(
            part_o.at[peer], came_o.at[row], yo_s.at[d], yo_r.at[row],
            device_id=(peer, me), device_id_type=MESH,
        ).start()
        return carry

    lax.fori_loop(1, rows, send_rest, 0)

    for i in range(held // GROUP):
        move_block(i, row)
    rest_block(row)
    total = ss[...]
    for d in order:
        peer = (row + d) % rows
        pltpu.make_async_copy(ss_in.at[peer], ss_in.at[peer], ss_r.at[peer]).wait()
        total = total + ss_in[peer]
    factor = lax.rsqrt(total / INNER + 1e-05)
    for i in range(tokens // TOK):
        line = jnp.broadcast_to(factor[i : i + 1, :], (TOK, TOK))
        scale[pl.ds(i * TOK, TOK), :] = line.T

    def add(part, came, into, start, count):
        def some(i, carry):
            at = pl.ds(pl.multiple_of(i * TOK, TOK), TOK)
            by = scale[pl.ds(pl.multiple_of(start + i * TOK, TOK), TOK), :]
            for j in range(pieces):
                lanes = slice(j * 128, (j + 1) * 128)
                value = part[row, at, lanes].astype(f32)
                for d in order:
                    value = value + came[(row + d) % rows, at, lanes].astype(f32)
                value = (value * by).astype(bf16)
                into[pl.ds(i * GROUP, GROUP), :, lanes] = value.reshape(GROUP, LEN, 128)
            return carry

        lax.fori_loop(0, count // TOK, some, 0)

    for i in range(held // GROUP):
        at = pl.ds(i * TOK, TOK)
        for d in order:
            spot = came_c.at[(row + d) % rows, at]
            pltpu.make_async_copy(spot, spot, yc_r.at[(row + d) % rows, i]).wait()
    add(part_c, came_c, mix, 0, moving)

    def pack(q):
        packed[q] = mix[tab[BACK, q]]

    unrolled(cols * cap, 8, pack)

    def push(d, carry):
        peer = (me + d) % cols
        pltpu.make_async_remote_copy(
            piece(packed, peer), piece(got, me), a2a_s, a2a_r,
            device_id=(row, peer), device_id_type=MESH,
        ).start()
        return carry

    lax.fori_loop(1, cols, push, 0)
    keep_m = pltpu.make_async_copy(piece(packed, me), piece(got, me), loc.at[2])
    keep_m.start()
    for d in order:
        spot = came_o.at[(row + d) % rows]
        pltpu.make_async_copy(spot, spot, yo_r.at[(row + d) % rows]).wait()
    add(part_o, came_o, mix_o, moving, resting)
    keep_m.wait()
    pltpu.make_async_copy(got.at[others], got.at[others], a2a_r).wait()

    def unpack(s):
        moved = tab[MOVED, s].astype(f32)
        away = got[tab[FROM_MSG, s]].astype(f32)
        here = mix_o[tab[FROM_MIX, s]].astype(f32)
        mixed[s] = jnp.where(moved > 0.5, away, here).astype(bf16)

    unrolled(requests, 8, unpack)
    for k in range(rows - 1):
        pltpu.make_async_copy(ss, ss, ss_s.at[k]).wait()
        pltpu.make_async_copy(part_o.at[0], part_o.at[0], yo_s.at[k + 1]).wait()
        for i in range(held // GROUP):
            spot = part_c.at[0, pl.ds(i * TOK, TOK)]
            pltpu.make_async_copy(spot, spot, yc_s.at[k + 1, i]).wait()
    pltpu.make_async_copy(got.at[others], got.at[others], a2a_s).wait()
    keep_x.wait()
    keep_e.wait()

    for ref, s_, r_ in ((xgot, x_s, x_r), (egot, e_s, e_r)):
        pltpu.make_async_copy(ref.at[others], ref.at[others], r_).wait()
        pltpu.make_async_copy(ref.at[others], ref.at[others], s_).wait()

    @pl.loop(0, held)
    def _(s):
        store(s).wait()


def mixer(tab, hid_c, hidden, fw, w_out, vectors, prev, pex, peb, rows, cols, cap):
    requests, _, model = hidden.shape
    held = hid_c.shape[0]
    tokens = requests * LEN
    depth, inner = w_out.shape
    width = model // rows
    slots = cols * cap
    rest = requests - held
    dt = hidden.dtype
    f32 = jnp.float32
    vmem = pl.BlockSpec(memory_space=pltpu.VMEM)
    hbm = pl.BlockSpec(memory_space=pltpu.HBM)
    dma = pltpu.SemaphoreType.DMA

    def body(*refs):
        mixer_kernel(rows, cols, cap, held, *refs)

    wide = inner + 2 * STATE
    return pl.pallas_call(
        body,
        out_shape=(
            jax.ShapeDtypeStruct((requests, LEN, width), dt),
            jax.ShapeDtypeStruct((held, inner, STATE), dt),
            jax.ShapeDtypeStruct((held, 4, wide), dt),
            jax.ShapeDtypeStruct((slots, LEN, inner + STATE), dt),
            jax.ShapeDtypeStruct((slots, 4, wide), dt),
        ),
        in_specs=[hbm] * (8 + len(vectors)),
        out_specs=(vmem, hbm, vmem, hbm, hbm),
        scratch_shapes=[
            pltpu.SMEM(tab.shape, jnp.int32),
            *[pltpu.VMEM(v.shape, v.dtype) for v in vectors],
            pltpu.VMEM(pex.shape, dt),
            pltpu.VMEM(peb.shape, dt),
            pltpu.VMEM((requests, LEN, model), dt),
            pltpu.VMEM((requests, LEN, model), dt),
            pltpu.VMEM((model, 2 * inner), dt),
            pltpu.VMEM((model, fw.shape[1] - 2 * inner), dt),
            pltpu.VMEM((model, inner), dt),
            pltpu.VMEM((held, inner, STATE), dt),
            pltpu.VMEM((tokens, inner), dt),
            pltpu.VMEM((tokens, inner), dt),
            pltpu.VMEM((tokens, 2 * STATE), dt),
            pltpu.VMEM((tokens, 128), f32),
            pltpu.VMEM((tokens, inner), dt),
            pltpu.VMEM((8, 128), f32),
            pltpu.VMEM((GROUP, 32, inner), f32),
            pltpu.VMEM((GROUP, 32, 2 * STATE), f32),
            pltpu.VMEM((3, held, inner), f32),
            pltpu.VMEM((3, held, 2 * STATE), f32),
            pltpu.VMEM((TOK, wide), f32),
            pltpu.VMEM((held, inner, STATE), dt),
            pltpu.VMEM((rest, LEN, inner + STATE), dt),
            pltpu.VMEM((rest, 4, wide), dt),
            pltpu.VMEM((slots, LEN, inner + STATE), dt),
            pltpu.VMEM((slots, 4, wide), dt),
            pltpu.VMEM((rows, rest * LEN, width), dt),
            pltpu.VMEM((rows, held * LEN, width), dt),
            pltpu.VMEM((rows, rest * LEN, width), dt),
            pltpu.VMEM((rows, held * LEN, width), dt),
            pltpu.VMEM((rows, 8, 128), f32),
            pltpu.VMEM((tokens, 128), f32),
            pltpu.VMEM((rest, LEN, width), dt),
            pltpu.VMEM((held, LEN, width), dt),
            pltpu.VMEM((slots, LEN, width), dt),
            pltpu.VMEM((slots, LEN, width), dt),
            dma(()), dma(()), dma((2 * inner // 256 + 2,)), dma((held,)),
            dma((len(vectors) + 3,)), dma((5,)), dma((3,)), dma((rows,)),
            dma((rows,)), dma((rows,)), dma((rows, held // GROUP)), dma((rows, held // GROUP)),
            dma(()), dma(()),
            dma(()), dma(()), dma(()), dma(()),
            pltpu.VMEM(w_out.shape, dt), dma((2,)), dma((2,)), dma((2, cols)),
        ],
        compiler_params=pltpu.CompilerParams(
            collective_id=1, has_side_effects=True, vmem_limit_bytes=60 << 20
        ),
        name="mixer",
    )(tab, hid_c, hidden, fw, w_out, *vectors, prev, pex, peb)


def arrive_kernel(
    tab_in, xgot_in, egot_in, edge_in, nst_in, nst, nex, neb,
    tab, xgot, egot, edge, was, xs, bs, ex, eb, new, n_sem, m_sem, l_sem,
):
    f32, bf16 = jnp.float32, jnp.bfloat16
    count, inner = new.shape[0], new.shape[1]
    loads = [
        pltpu.make_async_copy(a, b, l_sem.at[k])
        for k, (a, b) in enumerate(
            ((tab_in, tab), (xgot_in, xgot), (nst_in, was), (egot_in, egot), (edge_in, edge))
        )
    ]
    for copy in loads:
        copy.start()
    loads[0].wait()

    def place(s):
        return pltpu.make_async_copy(was.at[s], nst.at[tab[POS, s]], m_sem.at[s])

    loads[1].wait()
    t_ids, _ = token_masks()
    none = jnp.zeros((TOK, STATE), bf16)

    def store(u):
        return pltpu.make_async_copy(new.at[u], nst.at[tab[POS_O, u]], n_sem.at[u])

    @pl.loop(0, count // GROUP)
    def _(i):
        for r in range(GROUP):
            slot = tab[PICK_O, i * GROUP + r]
            xs[r] = xgot[slot, :, :inner]
            bs[r] = xgot[slot, :, inner:]
        lhs = xs[...].reshape(TOK, inner).astype(f32).T.astype(bf16)
        b_in = bs[...].reshape(TOK, STATE)
        for pair in range(GROUP // 2):
            cut = jnp.concatenate(
                [
                    jnp.where(t_ids // LEN == r, b_in, none)
                    for r in (2 * pair, 2 * pair + 1)
                ],
                axis=1,
            )
            out = jnp.dot(lhs, cut, preferred_element_type=f32).astype(bf16)
            for k in (0, 1):
                u = i * GROUP + 2 * pair + k
                new[u] = out[:, k * STATE : (k + 1) * STATE]
                store(u).start()

    loads[2].wait()

    @pl.loop(0, count)
    def _(s):
        place(s).start()

    for copy in loads[3:]:
        copy.wait()

    def edges(u):
        for source, k, spot in (
            (egot, tab[PICK_O, u], tab[POS_O, u]), (edge, u, tab[POS, u])
        ):
            lines = source[k].astype(f32)
            at = pl.ds(spot, 1)
            for q in range(KCONV - 1):
                ex[q, at, :] = lines[q : q + 1, :inner]
                eb[q, at, :] = lines[q : q + 1, inner:]

    unrolled(count, 8, edges)
    nex[...] = ex[...].astype(bf16)
    neb[...] = eb[...].astype(bf16)

    @pl.loop(0, count)
    def _(u):
        store(u).wait()
        place(u).wait()


def arrive(tab, xgot, egot, edge, nst):
    count, inner, _ = nst.shape
    requests = 2 * count
    dt, f32 = nst.dtype, jnp.float32
    vmem = pl.BlockSpec(memory_space=pltpu.VMEM)
    hbm = pl.BlockSpec(memory_space=pltpu.HBM)
    return pl.pallas_call(
        arrive_kernel,
        out_shape=(
            jax.ShapeDtypeStruct((requests, inner, STATE), dt),
            jax.ShapeDtypeStruct((3, requests, inner), dt),
            jax.ShapeDtypeStruct((3, requests, 2 * STATE), dt),
        ),
        in_specs=[hbm] * 5,
        out_specs=(hbm, vmem, vmem),
        scratch_shapes=[
            pltpu.SMEM(tab.shape, jnp.int32),
            pltpu.VMEM(xgot.shape, dt),
            pltpu.VMEM(egot.shape, dt),
            pltpu.VMEM(edge.shape, dt),
            pltpu.VMEM(nst.shape, dt),
            pltpu.VMEM((GROUP, LEN, inner), dt),
            pltpu.VMEM((GROUP, LEN, STATE), dt),
            pltpu.VMEM((3, requests, inner), f32),
            pltpu.VMEM((3, requests, 2 * STATE), f32),
            pltpu.VMEM((count, inner, STATE), dt),
            pltpu.SemaphoreType.DMA((count,)),
            pltpu.SemaphoreType.DMA((count,)),
            pltpu.SemaphoreType.DMA((5,)),
        ],
        compiler_params=pltpu.CompilerParams(vmem_limit_bytes=60 << 20),
        name="arrive",
    )(tab, xgot, egot, edge, nst)


def per_device(
    hidden, w_zx, w_bc, w_dt, w_out, dt_bias, a_log, d_skip, conv_x_w, conv_x_b,
    conv_bc_w, conv_bc_b, norm_gain, prev_state, prev_edge_x, prev_edge_bc,
    holder, continued, owner, accepted,
):
    rows, cols = lax.axis_size("row"), lax.axis_size("col")
    tokens, model = hidden.shape
    requests = tokens // LEN
    heads = dt_bias.shape[0]
    inner = heads * HEAD_DIM
    held = prev_state.shape[0]
    cap = 2 * ((requests // 4 + cols - 1) // cols)
    code = owner + 64 * (continued == 1).astype(jnp.int32) + 128 * accepted
    code = code.reshape(cols, requests)
    hidden = hidden.reshape(requests, LEN, model)
    hid_c, fw, tab = gather_all(code, hidden, w_zx, w_bc, w_dt.T, rows, cols, cap, held)
    vectors = (
        dt_bias[None, :], a_log[None, :], d_skip[None, :],
        conv_x_w, conv_x_b[None, :], conv_bc_w, conv_bc_b[None, :], norm_gain[None, :],
    )
    mixed, moved, edge, xgot, egot = mixer(
        tab, hid_c, hidden, fw, w_out, vectors, prev_state.reshape(held, inner, STATE),
        prev_edge_x.transpose(1, 0, 2), prev_edge_bc.transpose(1, 0, 2),
        rows, cols, cap,
    )
    states, new_x, new_bc = arrive(tab, xgot, egot, edge, moved)
    return (
        mixed.reshape(tokens, model // rows),
        states.reshape(requests, heads, HEAD_DIM, STATE),
        new_x.transpose(1, 0, 2),
        new_bc.transpose(1, 0, 2),
    )


def solution(mesh):
    return jax.shard_map(
        per_device,
        mesh=mesh,
        in_specs=(
            P("col", None),
            P("col", "row"),
            P("col", None),
            P("col", "row"),
            P("col", "row"),
            P("row"),
            P("row"),
            P("row"),
            P(None, "row"),
            P("row"),
            P(),
            P(),
            P("row"),
            P("col", "row", None, None),
            P("col", None, "row"),
            P("col", None, None),
            P(),
            P(),
            P(),
            P(),
        ),
        out_specs=(
            P("col", "row"),
            P("col", "row", None, None),
            P("col", None, "row"),
            P("col", None, None),
        ),
        check_vma=False,
    )
```
